32 devices in a mesh: group: 4 (over z), ctx: 2 (over x), wshard: 4 (over y, core).
Axes of the slice: x: 2, y: 2, z: 4, core: 2. Of those that a mesh axis runs over, the one named last changes fastest.
Arguments:
- words: bfloat16 [16, 2048, 512], P(('group', 'wshard'), 'ctx'), may hold values from -6 to 6
- qkv_weight: bfloat16 [512, 1536], P('wshard'), may hold values from -0.25 to 0.25
- out_weight: bfloat16 [512, 512], P('wshard'), may hold values from -4 to 4
- up_weight: bfloat16 [512, 2048], P('wshard'), may hold values from -0.25 to 0.25
- down_weight: bfloat16 [2048, 512], P('wshard'), may hold values from -0.125 to 0.125
- norm1_gain: bfloat16 [512], P('wshard'), may hold values from 0.5 to 1.5
- norm1_bias: bfloat16 [512], P('wshard'), may hold values from -3 to 3
- norm2_gain: bfloat16 [512], P('wshard'), may hold values from 0.5 to 1.5
- norm2_bias: bfloat16 [512], P('wshard'), may hold values from -3 to 3
- up_bias: bfloat16 [2048], P('wshard'), may hold values from -3 to 3
- down_bias: bfloat16 [512], P('wshard'), may hold values from -3 to 3
- cotangent: bfloat16 [16, 2048, 512], P(('group', 'wshard'), 'ctx'), may hold values from -6 to 6
- seg_map: int32 [16, 4], P(('group', 'wshard')), may hold values from 0 to 1, as said below
- off_map: int32 [16, 4], P(('group', 'wshard')), may hold values from 0 to 1, as said below
Outputs:
- output: bfloat16 [16, 2048, 512], P(('group', 'wshard'), 'ctx')
- words_grad: float32 [16, 2048, 512], P(('group', 'wshard'), 'ctx')
- qkv_weight_grad: float32 [512, 1536], P('wshard')
- out_weight_grad: float32 [512, 512], P('wshard')
- up_weight_grad: float32 [512, 2048], P('wshard')
- down_weight_grad: float32 [2048, 512], P('wshard')
- norm1_gain_grad: float32 [512], P('wshard')
- norm1_bias_grad: float32 [512], P('wshard')
- norm2_gain_grad: float32 [512], P('wshard')
- norm2_bias_grad: float32 [512], P('wshard')
- up_bias_grad: float32 [2048], P('wshard')
- down_bias_grad: float32 [512], P('wshard')
The draws below stay inside these ranges and needn't reach their ends.
Inputs may be any that keep to these rules, and one draw needn't show every extreme that they name: `seg_map`: in each row, 2 blocks carry 0 and each of the continuations 1 to 1 has 2 blocks, placed in any order. `off_map`: the prompt's blocks carry 0 to 1, each once; each continuation's blocks carry 0 to 1, each once.
All inputs are finite; a program needn't handle non-finite values.
Results may differ from the reference program's by a relative error of at most 0.04.
Values may be sent and summed in bfloat16 or wider, within the bound.
A program may use at most 128 MiB of HBM per device.

```python
import jax
import jax.numpy as jnp
from jax import lax

D = 512
HEADS = 8
HEAD_DIM = 64
FF = 2048
BLK = 512
CONT_BLK = 2
NBLK = 4
WORDS = 2048
PROMPT_BLK = 2
PGROUPS = 16


def block_layout(key):
    base = jax.random.fold_in(key, 11)
    group_keys = jax.random.split(base, PGROUPS)
    order = jax.vmap(lambda member: jax.random.permutation(member, NBLK))(group_keys).astype(jnp.int32)
    ident = jnp.arange(NBLK, dtype=jnp.int32)
    rest = jnp.maximum(ident - PROMPT_BLK, 0)
    seg_nat = jnp.where(ident < PROMPT_BLK, 0, 1 + rest // CONT_BLK).astype(jnp.int32)
    off_nat = jnp.where(ident < PROMPT_BLK, ident, rest % CONT_BLK).astype(jnp.int32)
    return (seg_nat[order], off_nat[order])


def draw_seg_map(key, part):
    return block_layout(key)[0]


def draw_off_map(key, part):
    return block_layout(key)[1]


def block_levels(key, shape, cuts, least, top_value):
    gain = 1.0
    for position, blocks in cuts:
        heights = jax.random.uniform(jax.random.fold_in(jax.random.fold_in(key, 6), position), (blocks,), jnp.float32, least / len(cuts), top_value / len(cuts))
        gain = gain * jnp.repeat(jnp.exp(heights), shape[position] // blocks).reshape((-1,) + (1,) * (len(shape) - 1 - position))
    return gain


def bell_draw(stream_key, dims, scale, limit, cuts=(), kind=jnp.bfloat16):
    values = scale * jax.random.normal(stream_key, dims, jnp.float32)
    if cuts:
        values = values * block_levels(stream_key, dims, cuts, -0.22, 0.18)
    return jnp.clip(values, -limit, limit).astype(kind)


def setup_inputs(seed: int = 0) -> dict:
    key_list = jax.random.split(jax.random.key(seed), 15)
    return {
        "words": bell_draw(key_list[0], (PGROUPS, WORDS, D), 1.0, 6.0, ((0, 16), (1, 2))),
        "qkv_weight": bell_draw(key_list[1], (D, 3 * D), D ** -0.5, 0.25, ((0, 4),)),
        "out_weight": bell_draw(key_list[2], (D, D), 2 ** -0.5, 4.0, ((0, 4),)),
        "up_weight": bell_draw(key_list[3], (D, FF), D ** -0.5, 0.25, ((0, 4),)),
        "down_weight": bell_draw(key_list[4], (FF, D), FF ** -0.5, 0.125, ((0, 4),)),
        "norm1_gain": jnp.clip(1.0 + 0.1 * jax.random.normal(key_list[5], (D,), jnp.float32), 0.5, 1.5).astype(jnp.bfloat16),
        "norm1_bias": bell_draw(key_list[6], (D,), 0.5, 3.0, ((0, 4),)),
        "norm2_gain": jnp.clip(1.0 + 0.1 * jax.random.normal(key_list[7], (D,), jnp.float32), 0.5, 1.5).astype(jnp.bfloat16),
        "norm2_bias": bell_draw(key_list[8], (D,), 0.5, 3.0, ((0, 4),)),
        "up_bias": bell_draw(key_list[9], (FF,), 0.5, 3.0, ((0, 4),)),
        "down_bias": bell_draw(key_list[10], (D,), 0.5, 3.0, ((0, 4),)),
        "cotangent": bell_draw(key_list[11], (PGROUPS, WORDS, D), 1.0, 6.0, ((0, 16), (1, 2))),
        "seg_map": draw_seg_map(jax.random.fold_in(key_list[14], 71), 0),
        "off_map": draw_off_map(jax.random.fold_in(key_list[14], 71), 0),
    }


eps = 1e-05
highest = lax.Precision.HIGHEST

@jax.custom_vjp
def low(v):
    return lax.optimization_barrier(v.astype(jnp.bfloat16)).astype(jnp.float32)

@jax.custom_vjp
def low_back(v):
    return v

def low_keep(v):
    return (low(v), None)

def low_pass(kept, grad):
    return (grad,)

def back_keep(v):
    return (v, None)

def back_low(kept, grad):
    return (low(grad),)
low.defvjp(low_keep, low_pass)
low_back.defvjp(back_keep, back_low)

def layer_norm(features, norm_gain, norm_shift):
    row_mean = lax.optimization_barrier(jnp.mean(features, axis=-1, keepdims=True))
    centred = features - row_mean
    inv_scale = lax.rsqrt(lax.optimization_barrier(jnp.mean(centred * centred, axis=-1, keepdims=True)) + eps)
    return centred * inv_scale * norm_gain + norm_shift

def matmul(left, right):
    return jnp.dot(left, right, precision=highest)

def group_forward(params, inputs, seg_row, off_row):
    w_qkv, w_out, w_up, w_down, gain1, shift1, gain2, shift2, bias_up, bias_down = params
    act1 = low(layer_norm(inputs, gain1, shift1))
    qkv = matmul(act1, w_qkv)
    query_rows = low(low_back(qkv[:, :D])).reshape(WORDS, HEADS, HEAD_DIM)
    key_rows = low(low_back(qkv[:, D:2 * D])).reshape(WORDS, HEADS, HEAD_DIM)
    value_rows = low(low_back(qkv[:, 2 * D:])).reshape(WORDS, HEADS, HEAD_DIM)
    seg_tok = jnp.repeat(seg_row, BLK)
    pos_tok = jnp.repeat(off_row * BLK, BLK) + jnp.tile(jnp.arange(BLK, dtype=jnp.int32), NBLK)

    def attend_block(block_id):
        first = (block_id * BLK).astype(jnp.int32)
        query_tile = lax.dynamic_slice_in_dim(query_rows, first, BLK, 0)
        query_seg = lax.dynamic_slice_in_dim(seg_tok, first, BLK, 0)
        query_pos = lax.dynamic_slice_in_dim(pos_tok, first, BLK, 0)
        raw_scores = jnp.einsum('qhd,khd->hqk', query_tile, key_rows, precision=highest) * HEAD_DIM ** (-0.5)
        raw_scores = low_back(raw_scores)
        allowed = (query_seg[:, None] == seg_tok[None, :]) & (pos_tok[None, :] <= query_pos[:, None]) | (seg_tok[None, :] == 0) & (query_seg[:, None] != 0)
        masked = jnp.where(allowed[None], raw_scores, -1e+30)
        attn_probs = low(jax.nn.softmax(masked, axis=-1))
        return jnp.einsum('hqk,khd->qhd', attn_probs, value_rows, precision=highest).reshape(BLK, D)
    attended = lax.map(jax.checkpoint(attend_block), jnp.arange(NBLK, dtype=jnp.int32)).reshape(WORDS, D)
    attended = low(low_back(attended))
    middle = low_back(inputs + matmul(attended, w_out))
    act2 = low(layer_norm(middle, gain2, shift2))
    hidden = low_back(matmul(act2, w_up) + bias_up)
    gelu_out = low(jax.nn.gelu(hidden, approximate=True))
    return middle + matmul(gelu_out, w_down) + bias_down

def reference(words, qkv_weight, out_weight, up_weight, down_weight, norm1_gain, norm1_bias, norm2_gain, norm2_bias, up_bias, down_bias, cotangent, seg_map, off_map):
    params = (qkv_weight.astype(jnp.float32), out_weight.astype(jnp.float32), up_weight.astype(jnp.float32), down_weight.astype(jnp.float32), norm1_gain.astype(jnp.float32), norm1_bias.astype(jnp.float32), norm2_gain.astype(jnp.float32), norm2_bias.astype(jnp.float32), up_bias.astype(jnp.float32), down_bias.astype(jnp.float32))
    words_f = words.astype(jnp.float32)
    cot_f = cotangent.astype(jnp.float32)

    def one_group(running, member):
        inputs, upstream, seg_row, off_row = member

        def forward(param_tuple, rows):
            return group_forward(param_tuple, rows, seg_row, off_row)
        result, pull = jax.vjp(forward, params, inputs)
        grad_params, grad_inputs = pull(upstream)
        running = jax.tree.map(lambda left, right: left + right, running, grad_params)
        return (running, (result.astype(jnp.bfloat16), grad_inputs))
    zeros = jax.tree.map(jnp.zeros_like, params)
    grads, outs = lax.scan(one_group, zeros, (words_f, cot_f, seg_map, off_map))
    output, words_grad = outs
    return (output, words_grad, grads[0], grads[1], grads[2], grads[3], grads[4], grads[5], grads[6], grads[7], grads[8], grads[9])
```

```python
import functools
import jax
import jax.numpy as jnp
from jax import lax
from jax.experimental import pallas as pl
from jax.experimental.pallas import tpu as pltpu
from jax.sharding import PartitionSpec as P

BLK = 512
HD = 64
EPS = 1e-5
F32 = jnp.float32
BF16 = jnp.bfloat16
K0 = 0.7978845608
K1 = 0.044715
LIVE = ((0,), (0, 1), (0, 1, 2), (0, 1, 2, 3))
MESH = pl.DeviceIdType.MESH
VLIM = 63 * 1024 * 1024
CHUNKS = (1024, 1024, 1024, 1024, 512, 768, 768)
STARTS = (0, 1024, 2048, 3072, 4096, 4608, 5376)
ROWS = 6144


def dg(a, b, ca, cb):
    return lax.dot_general(a, b, (((ca,), (cb,)), ((), ())), preferred_element_type=F32)


def colsum(v):
    return jnp.sum(v, axis=0, keepdims=True)


def rowmean(v):
    return jnp.mean(v, axis=-1, keepdims=True)


def tri(n):
    k = lax.broadcasted_iota(jnp.int32, (n, n), 0)
    q = lax.broadcasted_iota(jnp.int32, (n, n), 1)
    return k <= q


def al(v, n):
    return pl.multiple_of(v, n)


def scratch(nz):
    ne = 2 * nz
    V = lambda *s, t=BF16: pltpu.VMEM(s, t)
    d = dict(
        xs=V(1024, 512), dys=V(1024, 512), wt=V(1536, 512), wo=V(512, 512), wu=V(4, 512, 512), wd=V(4, 512, 512),
        vec=V(4, 16, 128, t=F32), so=V(2, 8, 128, t=jnp.int32), sm=pltpu.SMEM((8, 128), jnp.int32),
        a1=V(1024, 512), qkv=V(4, 768, 512), qst=V(4, 768, 256), o=V(4, 256, 512, t=F32), lse=V(4, 8, 512, t=F32),
        ost=V(2, 256, 512), ot=V(2, 512, 512), n2=V(1024, 512, t=F32), rs=V(1024, 128, t=F32), a2=V(1024, 512),
        a2t=V(512, 1024), dyt=V(512, 1024), ya=V(1024, 512, t=F32), da=V(1024, 512, t=F32),
        act=V(1024, 512), dup=V(1024, 512), do=V(4, 256, 512), dst=V(2, 256, 512), dq=V(4, 768, 512),
        xst=V(2, 2, 384, 512), dqt=V(2, 768, 1024),
        gv=V(4, 16, 128, t=F32), gvr=V(2, 16, 128, t=F32), gvy=V(16, 128, t=F32), gva=V(ne, 16, 128, t=F32),
        gg=V(8, 512, t=F32), gbu=V(4, 8, 512, t=F32),
        D=pltpu.SemaphoreType.DMA,
    )
    for k, r in enumerate(CHUNKS):
        d[f"G{k}"] = V(4, r, 128)
        d[f"A{k}"] = V(2, r, 128)
        d[f"B{k}"] = V(r, 128)
        d[f"C{k}"] = V(ne - 1, r // ne, 128)
        d[f"S{k}"] = V(r // ne, 128)
    del d["D"]
    return d


NSEM = 224


class Sems:
    def __init__(self, send, recv):
        self.send, self.recv, self.n = send, recv, 0

    def take(self, k=1):
        i = self.n
        self.n += k
        assert self.n <= NSEM
        return i


def body(nz, names, *args):
    ins = args[:8]
    y_out, wg_out, red_out, vec_out = args[8:12]
    S = dict(zip(names, args[12:12 + len(names)]))
    send, recv = args[12 + len(names):]
    words_h, cot_h, wqt_h, wo_h, wu_h, wd_h, vec_h, so_h = ins
    (xs, dys, wt, wo, wu, wd, vec, so, sm, a1, qkv, qst, o, lse, ost, ot, n2, rs, a2, a2t, dyt, ya, da, act, dup, do,
     dst, dq, xst, dqt, gv, gvr, gvy, gva, gg, gbu) = [S[n] for n in names[:36]]
    sems = Sems(send, recv)
    ne = 2 * nz
    g, x, w = lax.axis_index("group"), lax.axis_index("ctx"), lax.axis_index("wshard")
    yi, c = w // 2, w % 2
    oc = 1 - c
    e = x * nz + g
    sib = (g, x, 2 * yi + oc)
    yn = (g, x, 2 * (1 - yi) + c)
    diag = (g, x, 2 * (1 - yi) + oc)
    sw = (g, c, 2 * yi + x)
    stay = x == c

    def peer(d):
        q = (e + d) % ne
        return q, (q % nz, q // nz, w)

    def remote(src, dst_, dev, i):
        return pltpu.make_async_remote_copy(src_ref=src, dst_ref=dst_, send_sem=send.at[i], recv_sem=recv.at[i],
                                            device_id=dev, device_id_type=MESH)

    def local(src, dst_, i):
        return pltpu.make_async_copy(src, dst_, send.at[i])

    sends = []
    locs = []

    bar = pltpu.get_barrier_semaphore()
    peers = [sib, yn, diag] + [peer(d)[1] for d in range(1, ne)]
    for p in peers:
        pl.semaphore_signal(bar, inc=1, device_id=p, device_id_type=MESH)

    @pl.when(jnp.logical_not(stay))
    def _():
        pl.semaphore_signal(bar, inc=1, device_id=sw, device_id_type=MESH)

    def swap_start(src, dst_, i):
        for t in range(4):
            rows = pl.ds(t * 256, 256)

            @pl.when(stay)
            def _():
                local(src.at[rows], dst_.at[rows], i + t).start()

            @pl.when(jnp.logical_not(stay))
            def _():
                remote(src.at[rows], dst_.at[rows], sw, i + t).start()

    def swap_piece_wait(src, dst_, i, t, send_too=False):
        rows = pl.ds(al(t * 256, 256), 256)

        @pl.when(stay)
        def _():
            local(src.at[rows], dst_.at[rows], i + t).wait()

        @pl.when(jnp.logical_not(stay))
        def _():
            remote(src.at[rows], dst_.at[rows], sw, i + t).wait()

    ix, idy = sems.take(4), sems.take(4)
    own = []
    wsl = dict(
        wt=lambda s: wt.at[:, pl.ds(al(s * 128, 128), 128)],
        wo=lambda s: wo.at[pl.ds(al(s * 128, 128), 128), :],
        wu=lambda s: wu.at[:, pl.ds(al(s * 128, 128), 128), :],
        wd=lambda s: wd.at[:, pl.ds(al(s * 128, 128), 128), :],
        vec=lambda s: vec.at[s])
    srcs = dict(wt=wqt_h, wo=wo_h, wu=wu_h, wd=wd_h, vec=vec_h)
    for n in ("wt", "wo", "wu", "wd", "vec"):
        cp = local(srcs[n], wsl[n](w), sems.take())
        cp.start()
        own.append(cp)
    so_own = local(so_h, so.at[0], sems.take())
    so_own.start()

    pl.semaphore_wait(bar, len(peers) + jnp.where(stay, 0, 1))

    gath = {}
    for n in ("wt", "wo", "wu", "wd"):
        dv = wsl[n]
        gath[n] = (remote(srcs[n], dv(w), sib, sems.take()), remote(srcs[n], dv(w), yn, sems.take()),
                   remote(dv(2 * (1 - yi) + c), dv(2 * (1 - yi) + c), sib, sems.take()))

    def g_start(n):
        gath[n][0].start()
        gath[n][1].start()

    def g_forward(n):
        gath[n][1].wait_recv()
        gath[n][2].start()

    def g_done(n):
        gath[n][0].wait()
        gath[n][1].wait_send()
        gath[n][2].wait()

    vcs = [remote(vec_h, vec.at[w], p, sems.take()) for p in (sib, yn, diag)]
    so_x = remote(so_h, so.at[1], sib, sems.take())
    g_start("wt")
    swap_start(words_h, xs, ix)
    for v in vcs:
        v.start()
    so_x.start()
    gg[...] = jnp.zeros_like(gg)
    gbu[...] = jnp.zeros_like(gbu)
    gv[...] = jnp.zeros_like(gv)
    for cp in own:
        cp.wait()
    so_own.wait()
    for v in vcs:
        v.wait()
    so_x.wait()
    so[0] = jnp.where(stay, so[0], so[1])
    so_s = local(so.at[0], sm, sems.take())
    so_s.start()

    def row(k):
        return jnp.concatenate([vec[s, k:k + 1, :] for s in range(4)], axis=1)

    g_forward("wt")
    for n in ("wo", "wu", "wd"):
        g_start(n)
    g1, b1 = row(0), row(1)
    g_done("wt")
    so_s.wait()

    iq = sems.take(4)

    def q_piece(t):
        return remote(qst.at[t], qkv.at[2 * c + t // 2, :, pl.ds(al((t % 2) * 256, 256), 256)], sib, iq + t)

    def a_tile(t, _):
        rows = pl.ds(al(t * 256, 256), 256)
        swap_piece_wait(words_h, xs, ix, t)
        xv = xs[rows, :].astype(F32)
        xc = xv - rowmean(xv)
        r = lax.rsqrt(rowmean(xc * xc) + EPS)
        av = (xc * r * g1 + b1).astype(BF16)
        a1[rows, :] = av
        for who in (1, 0):
            for hp in range(2):
                cc = oc if who else c
                res = dg(wt[pl.ds(al((hp * 2 + cc) * 384, 128), 384), :], av, 1, 1)
                res = jnp.concatenate([res[0:128] * 0.125, res[128:]], axis=0).astype(BF16)
                if who:
                    qst[t, hp * 384:(hp + 1) * 384, :] = res
                else:
                    qkv[2 * c + t // 2, hp * 384:(hp + 1) * 384, pl.ds(al((t % 2) * 256, 256), 256)] = res
            if who:
                q_piece(t).start()
        return 0

    lax.fori_loop(0, 4, a_tile, 0)
    swap_start(cot_h, dys, idy)
    canon = [sm[0, b] for b in range(4)]
    phys = [jnp.minimum(sum(jnp.where(canon[b] == k, b, 0) for b in range(1, 4)), 3) for k in range(4)]

    def canon_of(p):
        return jnp.clip(sm[0, p], 0, 3)

    def q_wait(t, _):
        q_piece(t).wait()
        return 0

    lax.fori_loop(0, 4, q_wait, 0)

    def rows_of(h, part):
        return pl.ds(al((h // 2) * 384 + part * 128 + (h % 2) * HD, HD), HD)

    def fwd_head(h, _):
        kn = [qkv[phys[j], rows_of(h, 1), :].T for j in range(4)]
        vt = [qkv[phys[j], rows_of(h, 2), :] for j in range(4)]
        for i in range(4):
            q = qkv[phys[i], rows_of(h, 0), :]
            s = []
            for j in LIVE[i]:
                sj = dg(kn[j], q, 1, 0)
                s.append(jnp.where(tri(BLK), sj, -1e30) if j == i else sj)
            m = functools.reduce(jnp.maximum, [jnp.max(sj, axis=0, keepdims=True) for sj in s])
            acc = l = None
            for j, sj in zip(LIVE[i], s):
                p = jnp.exp(sj - m)
                lj = colsum(p)
                oj = dg(vt[j], p.astype(BF16), 1, 0)
                acc = oj if acc is None else acc + oj
                l = lj if l is None else l + lj
            o[i, pl.ds(al(h * HD, HD), HD), :] = acc / l
            lse[i, pl.ds(h, 1), :] = m + jnp.log(l)

        @pl.when(h == 1)
        def _():
            g_forward("wo")

        @pl.when(h == 3)
        def _():
            g_forward("wu")
        return 0

    lax.fori_loop(0, 4, fwd_head, 0)
    ox = []
    for b in range(2):
        ost[b] = o[canon_of(2 * oc + b)].astype(BF16)
        cp = remote(ost.at[b], ot.at[b, pl.ds(al(c * 256, 256), 256), :], sib, sems.take())
        cp.start()
        ox.append(cp)
    for b in range(2):
        ot[b, pl.ds(al(c * 256, 256), 256), :] = o[canon_of(2 * c + b)].astype(BF16)
    g_forward("wd")
    for cp in ox:
        cp.wait()
    for n in ("wo", "wu", "wd"):
        g_done(n)

    isem = [sems.take(4 + 2 * (ne - 1)) for _ in CHUNKS]

    def r_core(k, q):
        return remote(S[f"G{k}"].at[2 * q + oc], S[f"A{k}"].at[q], sib, isem[k] + q)

    def r_y(k):
        return remote(S[f"G{k}"].at[2 * (1 - yi) + c], S[f"B{k}"], yn, isem[k] + 2)

    def r_rs(k):
        p = CHUNKS[k] // ne
        for d in range(1, ne):
            q, dev = peer(d)
            yield remote(S[f"G{k}"].at[w, pl.ds(al(q * p, 16), p), :], S[f"C{k}"].at[ne - 1 - d], dev, isem[k] + 3 + d)

    def r_ag(k):
        p = CHUNKS[k] // ne
        for d in range(1, ne):
            yield remote(S[f"S{k}"], red_out.at[pl.ds(al(STARTS[k] + e * p, 16), p), :], peer(d)[1],
                         isem[k] + 2 + ne + d)

    def r_mine(k):
        p = CHUNKS[k] // ne
        return local(S[f"S{k}"], red_out.at[pl.ds(al(STARTS[k] + e * p, 16), p), :], isem[k] + 3)

    def s0(k):
        for q in range(2):
            r_core(k, q).start()

    def s1(k):
        G, A = S[f"G{k}"], S[f"A{k}"]
        for q in range(2):
            r_core(k, q).wait()
        for q in range(2):
            G[2 * q + c] = (G[2 * q + c].astype(F32) + A[q].astype(F32)).astype(BF16)
        r_y(k).start()

    def s2(k):
        G, B = S[f"G{k}"], S[f"B{k}"]
        r_y(k).wait()
        G[w] = (G[w].astype(F32) + B[...].astype(F32)).astype(BF16)
        for cp in r_rs(k):
            cp.start()

    def s3(k):
        G, C, T = S[f"G{k}"], S[f"C{k}"], S[f"S{k}"]
        p = CHUNKS[k] // ne
        for cp in r_rs(k):
            cp.wait()
        tot = G[w, pl.ds(al(e * p, 16), p), :].astype(F32)
        for d in range(ne - 1):
            tot = tot + C[d].astype(F32)
        T[...] = tot.astype(BF16)
        for cp in r_ag(k):
            cp.start()
        r_mine(k).start()

    def s4(k):
        for cp in r_ag(k):
            cp.wait()
        r_mine(k).wait()

    g2, b2, bd = row(2), row(3), row(4)

    def c1(t, _):
        rows = pl.ds(al(t * 256, 256), 256)
        swap_piece_wait(cot_h, dys, idy, t)
        mid = xs[rows, :].astype(F32) + dg(ot[t // 2, :, pl.ds(al((t % 2) * 256, 256), 256)], wo[...], 0, 0)
        xc = mid - rowmean(mid)
        r = lax.rsqrt(rowmean(xc * xc) + EPS)
        nv = xc * r
        n2[rows, :] = nv
        rs[rows, :] = jnp.broadcast_to(r, (256, 128))
        av = (nv * g2 + b2).astype(BF16)
        a2[rows, :] = av
        a2t[:, rows] = av.T
        dyv = dys[rows, :]
        dyt[:, rows] = dyv.T
        gg[4:5, :] += colsum(dyv.astype(F32))
        ya[rows, :] = mid + bd
        da[rows, :] = jnp.zeros((256, 512), F32)
        return 0

    lax.fori_loop(0, 4, c1, 0)

    for f in range(4):
        bu = row(5 + f)

        def c2(t, _):
            rows = pl.ds(al(t * 256, 256), 256)
            up = dg(a2[rows, :], wu[f], 1, 0) + bu
            u2 = up * up
            th = jnp.tanh(up * (K0 + (K0 * K1) * u2))
            hp = 0.5 + 0.5 * th
            av = (up * hp).astype(BF16)
            act[rows, :] = av
            ya[rows, :] += dg(av, wd[f], 1, 0)
            dact = dg(dys[rows, :], wd[f], 1, 1)
            gp = hp + (0.5 * up) * (1.0 - th * th) * (K0 + (3 * K0 * K1) * u2)
            dv = (dact * gp).astype(BF16)
            dup[rows, :] = dv
            gbu[f, 0:1, :] += colsum(dv.astype(F32))
            da[rows, :] += dg(dv, wu[f], 1, 1)
            return 0

        lax.fori_loop(0, 4, c2, 0)
        G = S[f"G{f}"]
        gd = dg(dyt[...], act[...], 1, 0).astype(BF16)
        for s in range(4):
            G[s, 0:512, :] = gd[:, s * 128:(s + 1) * 128]
        gu = dg(a2t[...], dup[...], 1, 0).astype(BF16)
        for s in range(4):
            for b in range(4):
                G[s, 512 + b * 128:640 + b * 128, :] = gu[s * 128:(s + 1) * 128, b * 128:(b + 1) * 128]
        s0(f)
        if f >= 1:
            s1(f - 1)
        if f >= 2:
            s2(f - 2)
        if f >= 3:
            s3(f - 3)

    yst, dmid = dup, act
    iy = sems.take(4)
    idx = sems.take(4)

    def out_start(src, dst_, i, t):
        rows = pl.ds(al(t * 256, 256), 256)

        @pl.when(stay)
        def _():
            local(src.at[rows], dst_.at[rows], i + t).start()

        @pl.when(jnp.logical_not(stay))
        def _():
            remote(src.at[rows], dst_.at[rows], sw, i + t).start()

    def d_piece(t):
        cols = pl.ds(al((t % 2) * 256, 256), 256)
        return remote(dst.at[t // 2, :, cols], do.at[2 * c + t // 2, :, cols], sib, idx + t)

    def c3(t, _):
        rows = pl.ds(al(t * 256, 256), 256)
        cols = pl.ds(al((t % 2) * 256, 256), 256)
        yst[rows, :] = ya[rows, :].astype(BF16)
        out_start(yst, y_out, iy, t)
        dav, nv, r = da[rows, :], n2[rows, :], rs[rows, 0:1]
        gg[2:3, :] += colsum(dav * nv)
        gg[3:4, :] += colsum(dav)
        gr = dav * g2
        dn = r * (gr - rowmean(gr) - nv * rowmean(gr * nv))
        dm = (dys[rows, :].astype(F32) + dn).astype(BF16)
        dmid[rows, :] = dm
        dst[t // 2, :, cols] = dg(wo[pl.ds(al(oc * 256, 256), 256), :], dm, 1, 1).astype(BF16)
        d_piece(t).start()
        do[2 * c + t // 2, :, cols] = dg(wo[pl.ds(al(c * 256, 256), 256), :], dm, 1, 1).astype(BF16)
        return 0

    lax.fori_loop(0, 4, c3, 0)
    go = (dg(ot[0], dmid[0:512, :], 1, 0) + dg(ot[1], dmid[512:1024, :], 1, 0)).astype(BF16)
    for s in range(4):
        for b in range(4):
            S["G4"][s, b * 128:(b + 1) * 128, :] = go[s * 128:(s + 1) * 128, b * 128:(b + 1) * 128]
    s0(4)
    s1(3)
    s2(2)
    s3(1)

    def d_wait(t, _):
        d_piece(t).wait()
        return 0

    lax.fori_loop(0, 4, d_wait, 0)

    ixq = sems.take(4)

    def x_piece(hp, b):
        return remote(xst.at[hp, b], dqt.at[hp, pl.ds(al(c * 384, 128), 384), pl.ds(b * 512, 512)], sib, ixq + hp * 2 + b)

    def x_start(hp):
        for b in range(2):
            xst[hp, b] = dq[canon_of(2 * oc + b), hp * 384:(hp + 1) * 384, :]
            x_piece(hp, b).start()
        for b in range(2):
            dqt[hp, pl.ds(al(c * 384, 128), 384), b * 512:(b + 1) * 512] = dq[canon_of(2 * c + b), hp * 384:(hp + 1) * 384, :]

    def gq_stage(hp):
        for b in range(2):
            x_piece(hp, b).wait()
        G = S[f"G{5 + hp}"]
        gq = dg(dqt[hp], a1[...], 1, 0).astype(BF16)
        for s in range(4):
            G[s] = gq[:, s * 128:(s + 1) * 128]
        s0(5 + hp)

    def bwd_head(h, _):
        kt = [qkv[phys[j], rows_of(h, 1), :] for j in range(4)]
        kn = [kj.T for kj in kt]
        vn = [qkv[phys[j], rows_of(h, 2), :].T for j in range(4)]
        dk = [None] * 4
        dv = [None] * 4
        hr = pl.ds(al(h * HD, HD), HD)
        for i in range(4):
            q = qkv[phys[i], rows_of(h, 0), :]
            gr = do[phys[i], hr, :]
            ls = lse[i, pl.ds(h, 1), :]
            delta = colsum(gr.astype(F32) * o[i, hr, :])
            dqa = None
            for j in LIVE[i]:
                p = jnp.exp(dg(kn[j], q, 1, 0) - ls)
                if j == i:
                    p = jnp.where(tri(BLK), p, 0.0)
                dp = dg(vn[j], gr, 1, 0)
                ds = (p * (dp - delta)).astype(BF16)
                p = p.astype(BF16)
                dqj = dg(kt[j], ds, 1, 0)
                dkj = dg(q, ds, 1, 1)
                dvj = dg(gr, p, 1, 1)
                dqa = dqj if dqa is None else dqa + dqj
                dk[j] = dkj if dk[j] is None else dk[j] + dkj
                dv[j] = dvj if dv[j] is None else dv[j] + dvj
            dq[i, rows_of(h, 0), :] = (dqa * 0.125).astype(BF16)
        for j in range(4):
            dq[j, rows_of(h, 1), :] = dk[j].astype(BF16)
            dq[j, rows_of(h, 2), :] = dv[j].astype(BF16)

        @pl.when(h == 0)
        def _():
            s1(4)
            s2(3)
            s3(2)

        @pl.when(h == 1)
        def _():
            x_start(0)
            s2(4)
            s3(3)

        @pl.when(h == 2)
        def _():
            gq_stage(0)
            s3(4)

        @pl.when(h == 3)
        def _():
            s1(5)
        return 0

    lax.fori_loop(0, 4, bwd_head, 0)
    x_start(1)
    s2(5)
    gq_stage(1)
    wgst = dys
    iw = sems.take(4)

    def e_tile(t, _):
        rows = pl.ds(al(t * 256, 256), 256)
        xv = xs[rows, :].astype(F32)
        xc = xv - rowmean(xv)
        r = lax.rsqrt(rowmean(xc * xc) + EPS)
        nv = xc * r
        dav = dg(dqt[0, :, rows], wt[0:768, :], 0, 0) + dg(dqt[1, :, rows], wt[768:1536, :], 0, 0)
        gg[0:1, :] += colsum(dav * nv)
        gg[1:2, :] += colsum(dav)
        gr = dav * g1
        dn = r * (gr - rowmean(gr) - nv * rowmean(gr * nv))
        wgst[rows, :] = (dmid[rows, :].astype(F32) + dn).astype(BF16)
        out_start(wgst, wg_out, iw, t)

        @pl.when(t == 0)
        def _():
            s1(6)
        return 0

    lax.fori_loop(0, 4, e_tile, 0)
    for s in range(4):
        for k in range(5):
            gv[s, k:k + 1, :] = gg[k:k + 1, s * 128:(s + 1) * 128]
        for f in range(4):
            gv[s, 5 + f:6 + f, :] = gbu[f, 0:1, s * 128:(s + 1) * 128]
    vx = [remote(gv.at[2 * q + oc], gvr.at[q], sib, sems.take()) for q in range(2)]
    vy = remote(gv.at[2 * (1 - yi) + c], gvy, yn, sems.take())
    iv = sems.take(ne - 1)
    va = [remote(gv.at[w], gva.at[e], peer(d)[1], iv + d - 1) for d in range(1, ne)]
    for cp in vx:
        cp.start()
    s3(5)
    s2(6)
    for cp in vx:
        cp.wait()
    for q in range(2):
        gv[2 * q + c] = gv[2 * q + c] + gvr[q]
    vy.start()
    vy.wait()
    gv[w] = gv[w] + gvy[...]
    gva[e] = gv[w]
    for cp in va:
        cp.start()
    s3(6)
    for cp in va:
        cp.wait()
    tot = gva[0]
    for d in range(1, ne):
        tot = tot + gva[d]
    vec_out[...] = tot
    for k in range(len(CHUNKS)):
        s4(k)

    def fin(t, _):
        swap_piece_wait(yst, y_out, iy, t)
        swap_piece_wait(wgst, wg_out, iw, t)
        return 0

    lax.fori_loop(0, 4, fin, 0)


def mega(nz, words, cot, wqt, wo, wu, wd, vec, so):
    sc = scratch(nz)
    names = tuple(sc)
    sd = jax.ShapeDtypeStruct
    any_ = pl.BlockSpec(memory_space=pl.ANY)
    return pl.pallas_call(
        functools.partial(body, nz, names),
        out_shape=(sd((1024, 512), BF16), sd((1024, 512), BF16), sd((ROWS, 128), BF16), sd((16, 128), F32)),
        in_specs=[any_] * 8,
        out_specs=(any_, any_, any_, pl.BlockSpec(memory_space=pltpu.VMEM)),
        scratch_shapes=[sc[n] for n in names] + [pltpu.SemaphoreType.DMA((NSEM,)), pltpu.SemaphoreType.DMA((NSEM,))],
        compiler_params=pltpu.CompilerParams(collective_id=0, has_side_effects=True, vmem_limit_bytes=VLIM),
        name="layer",
    )(words, cot, wqt, wo, wu, wd, vec, so)


def on_chip(words, qkv_weight, out_weight, up_weight, down_weight, norm1_gain, norm1_bias, norm2_gain,
            norm2_bias, up_bias, down_bias, cotangent, seg_map, off_map):
    nz = lax.axis_size("group")
    wqt = qkv_weight.reshape(128, 3, 2, 2, 128).transpose(3, 2, 1, 4, 0).reshape(1536, 128)
    wu = up_weight.reshape(128, 4, 4, 128).transpose(2, 0, 1, 3).reshape(4, 128, 512)
    wd = down_weight.reshape(4, 128, 512)
    vec = jnp.concatenate([norm1_gain, norm1_bias, norm2_gain, norm2_bias, down_bias, up_bias]).astype(F32)
    vec = jnp.pad(vec.reshape(9, 128), ((0, 7), (0, 0)))
    so = jnp.pad(seg_map * 2 + off_map, ((0, 7), (0, 124)))
    y, wg, red, gvec = mega(nz, words[0], cotangent[0], wqt, out_weight, wu, wd, vec, so)
    red = red.astype(F32)
    ff = red[:4096].reshape(4, 1024, 128)
    gdown = ff[:, :512].transpose(0, 2, 1).reshape(512, 512)
    gup = ff[:, 512:].reshape(4, 4, 128, 128).transpose(2, 1, 0, 3).reshape(128, 2048)
    gout = red[4096:4608].reshape(4, 128, 128).transpose(1, 0, 2).reshape(128, 512)
    gqkv = red[4608:].reshape(2, 2, 3, 128, 128).transpose(4, 2, 1, 0, 3).reshape(128, 1536)
    return (y[None], wg.astype(F32)[None], gqkv, gout, gup, gdown, gvec[0], gvec[1], gvec[2], gvec[3],
            gvec[5:9].reshape(512), gvec[4])


HEADS = 8
HEAD_DIM = 64


eps = 1e-05
neg_big = -1e30


def passed_along(value, axis, by):
    peers = lax.axis_size(axis)
    return lax.ppermute(value, axis, [(i, (i + by) % peers) for i in range(peers)])


def layer_norm(features, norm_gain, norm_shift):
    row_mean = jnp.mean(features, axis=-1, keepdims=True)
    centred = features - row_mean
    inv_scale = lax.rsqrt(jnp.mean(centred * centred, axis=-1, keepdims=True) + eps)
    return centred * inv_scale * norm_gain + norm_shift


def gelu_tanh(features):
    return jax.nn.gelu(features, approximate=True)


def rows_of(array, block_id):
    return lax.dynamic_slice_in_dim(array, block_id * BLK, BLK, 0)


def cols_of(array, block_id):
    return lax.dynamic_slice_in_dim(array, block_id * BLK, BLK, 1)


def add_rows(array, update, block_id):
    return lax.dynamic_update_slice_in_dim(
        array, rows_of(array, block_id) + update, block_id * BLK, 0
    )


def put_rows(array, update, block_id):
    return lax.dynamic_update_slice_in_dim(array, update, block_id * BLK, 0)


def put_cols(array, update, block_id):
    return lax.dynamic_update_slice_in_dim(array, update, block_id * BLK, 1)


def block_info(seg_row, off_row, block_id):
    segment = lax.dynamic_index_in_dim(seg_row, block_id, 0, keepdims=False)
    position = lax.dynamic_index_in_dim(off_row, block_id, 0, keepdims=False)
    return (segment, position)


def pair_live(seg_row, off_row, query_block, key_block):
    query_seg, query_offset = block_info(seg_row, off_row, query_block)
    key_seg, key_offset = block_info(seg_row, off_row, key_block)
    return (query_seg == key_seg) & (key_offset <= query_offset) | (key_seg == 0) & (query_seg != 0)


def pair_mask(seg_row, off_row, query_block, key_block):
    query_seg, query_offset = block_info(seg_row, off_row, query_block)
    key_seg, key_offset = block_info(seg_row, off_row, key_block)
    row_ids = lax.broadcasted_iota(jnp.int32, (BLK, BLK), 0)
    col_ids = lax.broadcasted_iota(jnp.int32, (BLK, BLK), 1)
    query_pos = query_offset * BLK + row_ids
    key_pos = key_offset * BLK + col_ids
    return (query_seg == key_seg) & (key_pos <= query_pos) | (key_seg == 0) & (query_seg != 0)


def split_heads(tile_rows):
    return tile_rows.reshape(tile_rows.shape[0], HEADS, HEAD_DIM)


def tile_scores(query_tile, key_tile, allowed):
    raw_scores = jnp.einsum(
        "qhd,khd->hqk",
        split_heads(query_tile),
        split_heads(key_tile),
        preferred_element_type=jnp.float32,
    )
    return jnp.where(allowed[None], raw_scores * HEAD_DIM ** (-0.5), neg_big)


def tile_back(query_tile, key_tile, value_tile, grad_tile, norm_tile, delta_tile, allowed):
    scores = tile_scores(query_tile, key_tile, allowed)
    exp_terms = jnp.where(allowed[None], jnp.exp(scores - norm_tile[:, :, None]), 0.0)
    d_probs = jnp.einsum(
        "qhd,khd->hqk",
        split_heads(grad_tile),
        split_heads(value_tile),
        preferred_element_type=jnp.float32,
    )
    d_scores = (exp_terms * (d_probs - delta_tile[:, :, None])).astype(jnp.bfloat16)
    return (exp_terms.astype(jnp.bfloat16), d_scores)


def query_grad(d_scores, key_tile):
    part_rows = jnp.einsum(
        "hqk,khd->qhd", d_scores, split_heads(key_tile), preferred_element_type=jnp.float32
    )
    return part_rows.reshape(BLK, -1) * HEAD_DIM ** (-0.5)


def key_grad(d_scores, query_tile):
    part_rows = jnp.einsum(
        "hqk,qhd->khd", d_scores, split_heads(query_tile), preferred_element_type=jnp.float32
    )
    return part_rows.reshape(BLK, -1) * HEAD_DIM ** (-0.5)


def value_grad(probs_low, grad_tile):
    part_rows = jnp.einsum(
        "hqk,qhd->khd", probs_low, split_heads(grad_tile), preferred_element_type=jnp.float32
    )
    return part_rows.reshape(BLK, -1)


def unchanged(running):
    return running


def on_device(
    words,
    qkv_weight,
    out_weight,
    up_weight,
    down_weight,
    norm1_gain,
    norm1_bias,
    norm2_gain,
    norm2_bias,
    up_bias,
    down_bias,
    cotangent,
    seg_map,
    off_map,
):
    gathered = (
        lax.all_gather(qkv_weight, "wshard", axis=0, tiled=True),
        lax.all_gather(out_weight, "wshard", axis=0, tiled=True),
        lax.all_gather(up_weight, "wshard", axis=0, tiled=True),
        lax.all_gather(down_weight, "wshard", axis=0, tiled=True),
        lax.all_gather(norm1_gain, "wshard", axis=0, tiled=True),
        lax.all_gather(norm1_bias, "wshard", axis=0, tiled=True),
        lax.all_gather(norm2_gain, "wshard", axis=0, tiled=True),
        lax.all_gather(norm2_bias, "wshard", axis=0, tiled=True),
        lax.all_gather(up_bias, "wshard", axis=0, tiled=True),
        lax.all_gather(down_bias, "wshard", axis=0, tiled=True),
    )
    w_qkv, w_out, w_up, w_down = (gathered[0], gathered[1], gathered[2], gathered[3])
    gain1 = gathered[4].astype(jnp.float32)
    shift1 = gathered[5].astype(jnp.float32)
    gain2 = gathered[6].astype(jnp.float32)
    shift2 = gathered[7].astype(jnp.float32)
    bias_up = gathered[8].astype(jnp.float32)
    bias_down = gathered[9].astype(jnp.float32)
    seg_row = seg_map[0]
    off_row = off_map[0]
    cycle_place = lax.axis_index("ctx")
    cycle_count = lax.axis_size("ctx")
    inputs = words[0].astype(jnp.float32)
    local_rows = inputs.shape[0]
    local_blocks = local_rows // BLK
    first_block = cycle_place * local_blocks
    width = inputs.shape[1]
    normed1, pull_norm1 = jax.vjp(layer_norm, inputs, gain1, shift1)
    act1 = normed1.astype(jnp.bfloat16)
    qkv = jnp.dot(act1, w_qkv, preferred_element_type=jnp.float32)
    query_rows = qkv[:, :width].astype(jnp.bfloat16)
    key_rows = qkv[:, width : 2 * width].astype(jnp.bfloat16)
    value_rows = qkv[:, 2 * width :].astype(jnp.bfloat16)
    start_state = (
        jnp.full((HEADS, local_rows), neg_big, jnp.float32),
        jnp.zeros((HEADS, local_rows), jnp.float32),
        jnp.zeros((local_rows, width), jnp.float32),
    )
    shard_keys = lax.all_gather(key_rows, "ctx", axis=0, tiled=True)
    shard_values = lax.all_gather(value_rows, "ctx", axis=0, tiled=True)
    key_blocks = shard_keys.shape[0] // BLK

    def online_visit_pair(pair_index, state):
        row_block = pair_index // key_blocks
        col_block = pair_index % key_blocks
        query_block = first_block + row_block
        key_block = col_block

        def online_update_tile(state):
            run_max, run_sum, accum = state
            allowed = pair_mask(seg_row, off_row, query_block, key_block)
            scores = tile_scores(
                rows_of(query_rows, row_block), rows_of(shard_keys, col_block), allowed
            )
            old_max = cols_of(run_max, row_block)
            old_sum = cols_of(run_sum, row_block)
            new_max = jnp.maximum(old_max, jnp.max(scores, axis=-1))
            exp_terms = jnp.where(allowed[None], jnp.exp(scores - new_max[:, :, None]), 0.0)
            factor = jnp.exp(old_max - new_max)
            new_sum = old_sum * factor + jnp.sum(exp_terms, axis=-1)
            part_rows = jnp.einsum(
                "hqk,khd->qhd",
                exp_terms.astype(jnp.bfloat16),
                split_heads(rows_of(shard_values, col_block)),
                preferred_element_type=jnp.float32,
            )
            old_rows = rows_of(accum, row_block).reshape(BLK, HEADS, HEAD_DIM)
            new_rows = (old_rows * factor.T[:, :, None] + part_rows).reshape(BLK, -1)
            return (
                put_cols(run_max, new_max, row_block),
                put_cols(run_sum, new_sum, row_block),
                put_rows(accum, new_rows, row_block),
            )

        return lax.cond(
            pair_live(seg_row, off_row, query_block, key_block),
            online_update_tile,
            unchanged,
            state,
        )

    run_max, run_sum, accum = lax.fori_loop(
        0, local_blocks * key_blocks, online_visit_pair, start_state
    )
    log_norm = run_max + jnp.log(run_sum)
    attended = (accum.reshape(local_rows, HEADS, HEAD_DIM) / run_sum.T[:, :, None]).reshape(
        local_rows, width
    )
    attended_low = attended.astype(jnp.bfloat16)
    middle = inputs + jnp.dot(attended_low, w_out, preferred_element_type=jnp.float32)
    normed2, pull_norm2 = jax.vjp(layer_norm, middle, gain2, shift2)
    act2 = normed2.astype(jnp.bfloat16)
    hidden = jnp.dot(act2, w_up, preferred_element_type=jnp.float32) + bias_up
    gelu_out, pull_gelu = jax.vjp(gelu_tanh, hidden)
    gelu_low = gelu_out.astype(jnp.bfloat16)
    output = (
        middle + jnp.dot(gelu_low, w_down, preferred_element_type=jnp.float32) + bias_down
    ).astype(jnp.bfloat16)
    upstream = cotangent[0]
    upstream_f = upstream.astype(jnp.float32)
    grad_down = jnp.einsum("nf,nd->fd", gelu_low, upstream, preferred_element_type=jnp.float32)
    grad_bias_down = jnp.sum(upstream_f, axis=0)
    d_gelu = jnp.einsum("nd,fd->nf", upstream, w_down, preferred_element_type=jnp.float32)
    d_hidden = pull_gelu(d_gelu)[0].astype(jnp.bfloat16)
    grad_up = jnp.einsum("nd,nf->df", act2, d_hidden, preferred_element_type=jnp.float32)
    grad_bias_up = jnp.sum(d_hidden.astype(jnp.float32), axis=0)
    d_act2 = jnp.einsum("nf,df->nd", d_hidden, w_up, preferred_element_type=jnp.float32)
    d_middle_norm, grad_gain2, grad_shift2 = pull_norm2(d_act2)
    d_middle = (upstream_f + d_middle_norm).astype(jnp.bfloat16)
    grad_out = jnp.einsum("nd,ne->de", attended_low, d_middle, preferred_element_type=jnp.float32)
    d_attended = jnp.einsum(
        "ne,de->nd", d_middle, w_out, preferred_element_type=jnp.float32
    ).astype(jnp.bfloat16)
    row_delta = jnp.sum(
        (d_attended.astype(jnp.float32) * attended).reshape(local_rows, HEADS, HEAD_DIM), axis=-1
    ).T
    zero_rows = jnp.zeros((local_rows, width), jnp.float32)

    def attend_back(cycle_turn, cycle_state):
        held_keys, held_values, held_dk, held_dv, d_query = cycle_state
        source = (cycle_place - cycle_turn) % cycle_count

        def attend_visit_pair(pair_index, partial_value):
            row_block = pair_index // local_blocks
            col_block = pair_index % local_blocks
            query_block = first_block + row_block
            key_block = source * local_blocks + col_block

            def attend_update_tile(partial_value):
                dk_acc, dv_acc, dq_acc = partial_value
                query_tile = rows_of(query_rows, row_block)
                key_tile = rows_of(held_keys, col_block)
                grad_tile = rows_of(d_attended, row_block)
                allowed = pair_mask(seg_row, off_row, query_block, key_block)
                probs_low, d_scores = tile_back(
                    query_tile,
                    key_tile,
                    rows_of(held_values, col_block),
                    grad_tile,
                    cols_of(log_norm, row_block),
                    cols_of(row_delta, row_block),
                    allowed,
                )
                dq_acc = add_rows(dq_acc, query_grad(d_scores, key_tile), row_block)
                dk_acc = add_rows(dk_acc, key_grad(d_scores, query_tile), col_block)
                dv_acc = add_rows(dv_acc, value_grad(probs_low, grad_tile), col_block)
                return (dk_acc, dv_acc, dq_acc)

            return lax.cond(
                pair_live(seg_row, off_row, query_block, key_block),
                attend_update_tile,
                unchanged,
                partial_value,
            )

        held_dk, held_dv, d_query = lax.fori_loop(
            0, local_blocks * local_blocks, attend_visit_pair, (held_dk, held_dv, d_query)
        )
        return (held_keys, held_values, held_dk, held_dv, d_query)

    def pass_grads(held_dk, held_dv):
        return (
            passed_along(held_dk.astype(jnp.bfloat16), "ctx", 1).astype(held_dk.dtype),
            passed_along(held_dv.astype(jnp.bfloat16), "ctx", 1).astype(held_dv.dtype),
        )

    def turn_step(cycle_turn, cycle_state):
        held_keys, held_values, held_dk, held_dv, d_query = attend_back(cycle_turn, cycle_state)
        held_keys, held_values = passed_along((held_keys, held_values), "ctx", 1)
        held_dk, held_dv = pass_grads(held_dk, held_dv)
        return (held_keys, held_values, held_dk, held_dv, d_query)

    cycle_state = lax.fori_loop(
        0, cycle_count - 1, turn_step, (key_rows, value_rows, zero_rows, zero_rows, zero_rows)
    )
    cycle_state = attend_back(cycle_count - 1, cycle_state)
    d_keys, d_values = pass_grads(cycle_state[2], cycle_state[3])
    d_query = cycle_state[4]
    d_qkv = jnp.concatenate(
        [d_query.astype(jnp.bfloat16), d_keys.astype(jnp.bfloat16), d_values.astype(jnp.bfloat16)],
        axis=1,
    )
    grad_qkv = jnp.einsum("nd,nf->df", act1, d_qkv, preferred_element_type=jnp.float32)
    d_act1 = jnp.einsum("nf,df->nd", d_qkv, w_qkv, preferred_element_type=jnp.float32)
    d_inputs_norm, grad_gain1, grad_shift1 = pull_norm1(d_act1)
    words_grad = d_middle.astype(jnp.float32) + d_inputs_norm
    shards = (
        lax.psum_scatter(
            grad_qkv.astype(jnp.bfloat16), "wshard", scatter_dimension=0, tiled=True
        ).astype(jnp.float32),
        lax.psum_scatter(
            grad_out.astype(jnp.bfloat16), "wshard", scatter_dimension=0, tiled=True
        ).astype(jnp.float32),
        lax.psum_scatter(
            grad_up.astype(jnp.bfloat16), "wshard", scatter_dimension=0, tiled=True
        ).astype(jnp.float32),
        lax.psum_scatter(
            grad_down.astype(jnp.bfloat16), "wshard", scatter_dimension=0, tiled=True
        ).astype(jnp.float32),
        lax.psum_scatter(
            grad_gain1.astype(jnp.bfloat16), "wshard", scatter_dimension=0, tiled=True
        ).astype(jnp.float32),
        lax.psum_scatter(
            grad_shift1.astype(jnp.bfloat16), "wshard", scatter_dimension=0, tiled=True
        ).astype(jnp.float32),
        lax.psum_scatter(
            grad_gain2.astype(jnp.bfloat16), "wshard", scatter_dimension=0, tiled=True
        ).astype(jnp.float32),
        lax.psum_scatter(
            grad_shift2.astype(jnp.bfloat16), "wshard", scatter_dimension=0, tiled=True
        ).astype(jnp.float32),
        lax.psum_scatter(
            grad_bias_up.astype(jnp.bfloat16), "wshard", scatter_dimension=0, tiled=True
        ).astype(jnp.float32),
        lax.psum_scatter(
            grad_bias_down.astype(jnp.bfloat16), "wshard", scatter_dimension=0, tiled=True
        ).astype(jnp.float32),
    )
    totals = lax.psum(
        (
            shards[0],
            shards[1],
            shards[2],
            shards[3],
            shards[4],
            shards[5],
            shards[6],
            shards[7],
            shards[8],
            shards[9],
        ),
        ("group", "ctx"),
    )
    return (
        output[None],
        words_grad[None],
        totals[0],
        totals[1],
        totals[2],
        totals[3],
        totals[4],
        totals[5],
        totals[6],
        totals[7],
        totals[8],
        totals[9],
    )


def solution(mesh):
    chip = mesh.shape["ctx"] == 2 and mesh.shape["wshard"] == 4
    return jax.shard_map(
        on_chip if chip else on_device,
        mesh=mesh,
        in_specs=(
            P(("group", "wshard"), "ctx", None),
            P("wshard", None),
            P("wshard", None),
            P("wshard", None),
            P("wshard", None),
            P("wshard"),
            P("wshard"),
            P("wshard"),
            P("wshard"),
            P("wshard"),
            P("wshard"),
            P(("group", "wshard"), "ctx", None),
            P(("group", "wshard"), None),
            P(("group", "wshard"), None),
        ),
        out_specs=(
            P(("group", "wshard"), "ctx", None),
            P(("group", "wshard"), "ctx", None),
            P("wshard", None),
            P("wshard", None),
            P("wshard", None),
            P("wshard", None),
            P("wshard"),
            P("wshard"),
            P("wshard"),
            P("wshard"),
            P("wshard"),
            P("wshard"),
        ),
        check_vma=False,
    )
```

```python
import functools
import jax
import jax.numpy as jnp
from jax import lax
from jax.experimental import pallas as pl
from jax.experimental.pallas import tpu as pltpu
from jax.sharding import PartitionSpec as P

BLK = 512
HD = 64
EPS = 1e-5
F32 = jnp.float32
BF16 = jnp.bfloat16
K0 = 0.7978845608
K1 = 0.044715
MESH = pl.DeviceIdType.MESH
VLIM = 63 * 1024 * 1024
FROWS, OROWS, QROWS = 1024, 512, 384
OSTART, QSTART, ROWS = 4096, 4608, 6144
NSEM = 240


def dg(a, b, ca, cb):
    return lax.dot_general(a, b, (((ca,), (cb,)), ((), ())), preferred_element_type=F32)


def colsum(v):
    return jnp.sum(v, axis=0, keepdims=True)


def rowmean(v):
    return jnp.mean(v, axis=-1, keepdims=True)


def key_le_query(n, key_axis):
    k = lax.broadcasted_iota(jnp.int32, (n, n), key_axis)
    q = lax.broadcasted_iota(jnp.int32, (n, n), 1 - key_axis)
    return k <= q


def al(v, n):
    return pl.multiple_of(v, n)


def scratch(nz):
    ne = 2 * nz
    V = lambda *s, t=BF16: pltpu.VMEM(s, t)
    return dict(
        xs=V(1024, 512), dys=V(1024, 512), wqr=V(128, 1536), wur=V(128, 2048), wt=V(1536, 512), wo=V(512, 512),
        wu=V(4, 512, 512), wd=V(4, 512, 512), vown=V(16, 128, t=F32), vec=V(4, 16, 128, t=F32),
        so=V(2, 8, 128, t=jnp.int32), sm=pltpu.SMEM((8, 128), jnp.int32),
        a1=V(4, 512, 512), qkv=V(4, 768, 512), o=V(4, 256, 512, t=F32), lse=V(4, 8, 512, t=F32),
        ost=V(2, 256, 512), ot=V(2, 512, 512), n2=V(1024, 512, t=F32), rs=V(1024, 128, t=F32), a2=V(1024, 512),
        a2t=V(512, 1024), dyt=V(512, 1024), ya=V(1024, 512, t=F32), da=V(1024, 512, t=F32),
        act=V(1024, 512), dup=V(1024, 512), do=V(4, 256, 512), dst=V(2, 256, 512), dq=V(4, 768, 512),
        dkv=V(128, 2048, t=F32), xst=V(4, 2, 192, 512), dqt=V(1536, 1024),
        gv=V(4, 16, 128, t=F32), gvr=V(2, 16, 128, t=F32), gvy=V(16, 128, t=F32), gva=V(ne, 16, 128, t=F32),
        gg=V(8, 512, t=F32), gbu=V(4, 8, 512, t=F32),
        FG=V(4, 4, FROWS, 128), FA=V(4, 2, FROWS, 128), FB=V(4, FROWS, 128), FX=V(4, FROWS // 2, 128),
        FZ=V(4, nz - 1, FROWS // ne, 128), FT=V(4, FROWS // ne, 128), FH=V(4, FROWS // 2, 128),
        OG=V(1, 4, OROWS, 128), OA=V(1, 2, OROWS, 128), OB=V(1, OROWS, 128), OX=V(1, OROWS // 2, 128),
        OZ=V(1, nz - 1, OROWS // ne, 128), OT=V(1, OROWS // ne, 128), OH=V(1, OROWS // 2, 128),
        QS=V(4, 4, 192, 128), QG=V(4, 2, QROWS, 128), QB=V(4, QROWS, 128), QC=V(4, ne - 1, QROWS // ne, 128),
        QT=V(4, QROWS // ne, 128),
    )


class Count:
    def __init__(self):
        self.n = 0

    def take(self, k=1):
        self.n += k
        assert self.n <= NSEM
        return self.n - k


class Ns:
    def __init__(self, d):
        self.__dict__.update(d)


def body(nz, names, *args):
    (words_h, cot_h, wq_h, wo_h, wu_h, wd_h, n1g, n1b, n2g, n2b, bdr, bur, seg_r, off_r) = args[:14]
    y_out, wg_out, red_out, vec_out = args[14:18]
    m = Ns(dict(zip(names, args[18:18 + len(names)])))
    send, recv = args[18 + len(names):]
    ct = Count()
    ne = 2 * nz
    g, x, w = lax.axis_index("group"), lax.axis_index("ctx"), lax.axis_index("wshard")
    yi, c = w // 2, w % 2
    oc, oy, ox = 1 - c, 1 - yi, 1 - x
    e = x * nz + g
    sib = (g, x, 2 * yi + oc)
    yn = (g, x, 2 * oy + c)
    diag = (g, x, 2 * oy + oc)
    xn = (g, ox, w)
    zp = (g + 1 - 2 * (g % 2), x, w)
    sw = (g, c, 2 * yi + x)
    stay = x == c
    moves = jnp.logical_not(stay)

    def peer(d):
        q = (e + d) % ne
        return q, (q % nz, q // nz, w)

    def zpeer(d):
        q = (g + d) % nz
        return q, (q, x, w)

    def remote(src, dst_, dev, i):
        return pltpu.make_async_remote_copy(src_ref=src, dst_ref=dst_, send_sem=send.at[i], recv_sem=recv.at[i],
                                            device_id=dev, device_id_type=MESH)

    def local(src, dst_, i):
        return pltpu.make_async_copy(src, dst_, send.at[i])

    def begin(src, dst_):
        cp = local(src, dst_, ct.take())
        cp.start()
        return cp

    l_wq = begin(wq_h, m.wqr)
    l_wo = begin(wo_h, m.wo.at[pl.ds(al(w * 128, 128), 128), :])
    l_wu = begin(wu_h, m.wur)
    l_wd = begin(wd_h, m.wd.at[:, pl.ds(al(w * 128, 128), 128), :])
    bar = pltpu.get_barrier_semaphore()
    peers = [sib, yn, diag] + [peer(d)[1] for d in range(1, ne)]
    for p in peers:
        pl.semaphore_signal(bar, inc=1, device_id=p, device_id_type=MESH)

    @pl.when(moves)
    def _():
        pl.semaphore_signal(bar, inc=1, device_id=sw, device_id_type=MESH)

    m.vown[...] = jnp.zeros_like(m.vown)
    for k, r in enumerate((n1g, n1b, n2g, n2b, bdr)):
        m.vown[k:k + 1, :] = r[...].astype(F32)
    m.vown[5:9, :] = bur[...].astype(F32)
    m.so[0] = jnp.zeros((8, 128), jnp.int32)
    m.so[0, 0:1, 0:4] = seg_r[...] * 2 + off_r[...]
    m.gg[...] = jnp.zeros_like(m.gg)
    m.gbu[...] = jnp.zeros_like(m.gbu)
    m.gv[...] = jnp.zeros_like(m.gv)
    pl.semaphore_wait(bar, len(peers) + jnp.where(stay, 0, 1))

    def swap(src, dst_, i, t, what):
        rows = pl.ds(al(t * 256, 256), 256)

        @pl.when(stay)
        def _():
            cp = local(src.at[rows], dst_.at[rows], i + t)
            cp.start() if what == "start" else cp.wait()

        @pl.when(moves)
        def _():
            cp = remote(src.at[rows], dst_.at[rows], sw, i + t)
            cp.start() if what == "start" else cp.wait()

    ix, idy, iy, iw = ct.take(4), ct.take(4), ct.take(4), ct.take(4)
    for t in range(4):
        swap(words_h, m.xs, ix, t, "start")
    so_x = remote(m.so.at[0], m.so.at[1], sib, ct.take())
    so_x.start()
    vcs = [remote(m.vown, m.vec.at[w], p, ct.take()) for p in (sib, yn, diag)]
    for v in vcs:
        v.start()
    m.vec[w] = m.vown[...]

    mine = pl.ds(al(w * 128, 128), 128)
    l_wq.wait()
    for cc in range(2):
        for hp in range(2):
            for part in range(3):
                b = (part * 4 + cc * 2 + hp) * 128
                blk = m.wqr[:, b:b + 128].T
                if part == 0:
                    blk = (blk.astype(F32) * 0.125).astype(BF16)
                r = cc * 768 + hp * 384 + part * 64
                m.wt[r:r + 64, mine] = blk[:64]
                m.wt[r + 192:r + 256, mine] = blk[64:]

    other = 2 * oy + c
    hs = g % 2
    sl = dict(
        wt=lambda s, f=None: m.wt.at[:, pl.ds(al(s * 128, 128), 128)],
        wo=lambda s, f=None: m.wo.at[pl.ds(al(s * 128, 128), 128), :],
        wu=lambda s, f=None: m.wu.at[:, pl.ds(al(s * 128, 128), 128), :] if f is None else
        m.wu.at[pl.ds(2 * f, 2), pl.ds(al(s * 128, 128), 128), :],
        wd=lambda s, f=None: m.wd.at[:, pl.ds(al(s * 128, 128), 128), :] if f is None else
        m.wd.at[pl.ds(2 * f, 2), pl.ds(al(s * 128, 128), 128), :])
    gath = {}
    for n in ("wt", "wo"):
        gath[n] = [remote(sl[n](w), sl[n](w), sib, ct.take()), remote(sl[n](w), sl[n](w), yn, ct.take()),
                   remote(sl[n](other), sl[n](other), sib, ct.take())]
    for n in ("wu", "wd"):
        gath[n] = [remote(sl[n](w), sl[n](w), sib, ct.take()), remote(sl[n](w, hs), sl[n](w, hs), yn, ct.take()),
                   remote(sl[n](other, hs), sl[n](other, hs), zp, ct.take()),
                   remote(sl[n](other), sl[n](other), sib, ct.take())]

    def g_start(n):
        gath[n][0].start()
        gath[n][1].start()

    def g_z(n):
        gath[n][1].wait_recv()
        gath[n][2].start()

    def g_forward(n):
        gath[n][-2].wait_recv()
        gath[n][-1].start()

    def g_done(n):
        gath[n][0].wait()
        gath[n][1].wait_send()
        if len(gath[n]) == 4:
            gath[n][2].wait_send()
        gath[n][-1].wait()

    g_start("wt")
    l_wu.wait()
    for f in range(4):
        for s in range(4):
            m.wu[f, mine, s * 128:(s + 1) * 128] = m.wur[:, s * 512 + f * 128:s * 512 + (f + 1) * 128]
    l_wo.wait()
    l_wd.wait()
    for v in vcs:
        v.wait()
    so_x.wait()
    m.so[0] = jnp.where(stay, m.so[0], m.so[1])
    so_s = local(m.so.at[0], m.sm, ct.take())
    so_s.start()

    def row(k):
        return jnp.concatenate([m.vec[s, k:k + 1, :] for s in range(4)], axis=1)

    g1, b1 = row(0), row(1)

    ia = ct.take(4)

    def a_slot(core, t):
        return m.a1.at[2 * core + t // 2, pl.ds(al((t % 2) * 256, 256), 256), :]

    def a_piece(t):
        return remote(a_slot(c, t), a_slot(c, t), sib, ia + t)

    def norm1(t, _=0):
        rows = pl.ds(al(t * 256, 256), 256)
        swap(words_h, m.xs, ix, t, "wait")
        xv = m.xs[rows, :].astype(F32)
        xc = xv - rowmean(xv)
        r = lax.rsqrt(rowmean(xc * xc) + EPS)
        a_slot(c, t)[...] = (xc * r * g1 + b1).astype(BF16)
        a_piece(t).start()
        return 0

    wrows = pl.ds(al(c * 768, 256), 768)

    def project(t, _=0):
        a_piece(t).wait()
        cols = pl.ds(al((t % 2) * 256, 256), 256)
        av = jnp.concatenate([a_slot(0, t)[...], a_slot(1, t)[...]], axis=0)
        res = dg(m.wt[wrows, :], av, 1, 1).astype(BF16)
        m.qkv[t // 2, :, cols] = res[:, :256]
        m.qkv[2 + t // 2, :, cols] = res[:, 256:]
        return 0

    lax.fori_loop(0, 3, norm1, 0)
    g_forward("wt")
    g_start("wo")
    g_start("wu")
    g_done("wt")
    lax.fori_loop(0, 2, project, 0)
    norm1(3)
    lax.fori_loop(2, 4, project, 0)
    for t in range(4):
        swap(cot_h, m.dys, idy, t, "start")
    so_s.wait()
    canon = [m.sm[0, b] for b in range(4)]
    phys = [jnp.minimum(sum(jnp.where(canon[b] == k, b, 0) for b in range(1, 4)), 3) for k in range(4)]

    def canon_of(p):
        return jnp.clip(m.sm[0, p], 0, 3)

    def rows_of(h, part):
        return pl.ds(al(h * 192 + part * 64, 64), 64)

    def fwd_head(h, _):
        kn = [m.qkv[phys[j], rows_of(h, 1), :].T for j in range(4)]
        q = jnp.concatenate([m.qkv[phys[j], rows_of(h, 0), :] for j in range(4)], axis=1)
        tri = key_le_query(BLK, 0)
        s = []
        for j in range(4):
            sj = dg(kn[j], q[:, j * BLK:], 1, 0)
            sd = jnp.where(tri, sj[:, :BLK], -1e30)
            s.append(sd if j == 3 else jnp.concatenate([sd, sj[:, BLK:]], axis=1))
        mx = [jnp.max(sj, axis=0, keepdims=True) for sj in s]
        top = mx[0]
        for j in range(1, 4):
            top = jnp.concatenate([top[:, :j * BLK], jnp.maximum(top[:, j * BLK:], mx[j])], axis=1)
        acc = tot = None
        for j in range(4):
            p = jnp.exp(s[j] - top[:, j * BLK:])
            lj = colsum(p)
            a = dg(m.qkv[phys[j], rows_of(h, 2), :], p.astype(BF16), 1, 0)
            acc = a if acc is None else jnp.concatenate([acc[:, :j * BLK], acc[:, j * BLK:] + a], axis=1)
            tot = lj if tot is None else jnp.concatenate([tot[:, :j * BLK], tot[:, j * BLK:] + lj], axis=1)
        ov = acc * (1.0 / tot)
        ls = top + jnp.log(tot)
        for i in range(4):
            m.o[i, pl.ds(al(h * HD, HD), HD), :] = ov[:, i * BLK:(i + 1) * BLK]
            m.lse[i, pl.ds(h, 1), :] = ls[:, i * BLK:(i + 1) * BLK]

        @pl.when(h == 0)
        def _():
            g_forward("wo")
            g_start("wd")

        @pl.when(h == 2)
        def _():
            g_z("wu")

        @pl.when(h == 3)
        def _():
            g_z("wd")
        return 0

    lax.fori_loop(0, 4, fwd_head, 0)
    oxc = []
    for b in range(2):
        m.ost[b] = m.o[canon_of(2 * oc + b)].astype(BF16)
        cp = remote(m.ost.at[b], m.ot.at[b, pl.ds(al(c * 256, 256), 256), :], sib, ct.take())
        cp.start()
        oxc.append(cp)
    for b in range(2):
        m.ot[b, pl.ds(al(c * 256, 256), 256), :] = m.o[canon_of(2 * c + b)].astype(BF16)
    g_forward("wu")
    g_done("wo")
    for cp in oxc:
        cp.wait()

    class Chunk:
        def __init__(self, tag, rows, start, count):
            for q in "GABXZTH":
                setattr(self, q, getattr(m, tag + q))
            self.rows, self.start, self.half, self.p = rows, start, rows // 2, rows // ne
            self.n = 6 + 2 * nz
            self.i = ct.take(self.n * count)

        def core(self, k, q):
            return remote(self.G.at[k, 2 * q + oc], self.A.at[k, q], sib, self.i + k * self.n + q)

        def y(self, k):
            return remote(self.G.at[k, other], self.B.at[k], yn, self.i + k * self.n + 2)

        def x(self, k):
            return remote(self.G.at[k, w, pl.ds(al(ox * self.half, 64), self.half), :], self.X.at[k], xn,
                          self.i + k * self.n + 3)

        def z(self, k, d):
            q, dev = zpeer(d)
            return remote(self.G.at[k, w, pl.ds(al(x * self.half + q * self.p, 16), self.p), :],
                          self.Z.at[k, nz - 1 - d], dev, self.i + k * self.n + 3 + d)

        def back(self, k, d):
            return remote(self.T.at[k], self.H.at[k, pl.ds(al(g * self.p, 16), self.p), :], zpeer(d)[1],
                          self.i + k * self.n + 2 + nz + d)

        def at(self, k):
            return red_out.at[pl.ds(al(self.start + k * self.rows + x * self.half, 16), self.half), :]

        def xback(self, k):
            return remote(self.H.at[k], self.at(k), xn, self.i + k * self.n + 2 + 2 * nz)

        def keep(self, k):
            return local(self.H.at[k], self.at(k), self.i + k * self.n + 3 + 2 * nz)

        def s0(self, k):
            for q in range(2):
                self.core(k, q).start()

        def s1(self, k):
            for q in range(2):
                self.core(k, q).wait()
            self.G[k, other] = (self.G[k, other].astype(F32) + self.A[k, oy].astype(F32)).astype(BF16)
            self.y(k).start()
            self.G[k, w] = (self.G[k, w].astype(F32) + self.A[k, yi].astype(F32)).astype(BF16)

        def s2(self, k):
            self.y(k).wait()
            self.G[k, w] = (self.G[k, w].astype(F32) + self.B[k].astype(F32)).astype(BF16)
            self.x(k).start()

        def s3(self, k):
            self.x(k).wait()
            hrows = pl.ds(al(x * self.half, 64), self.half)
            self.G[k, w, hrows, :] = (self.G[k, w, hrows, :].astype(F32) + self.X[k].astype(F32)).astype(BF16)
            for d in range(1, nz):
                self.z(k, d).start()

        def s4(self, k):
            for d in range(1, nz):
                self.z(k, d).wait()
            tot = self.G[k, w, pl.ds(al(x * self.half + g * self.p, 16), self.p), :].astype(F32)
            for d in range(nz - 1):
                tot = tot + self.Z[k, d].astype(F32)
            tot = tot.astype(BF16)
            self.T[k] = tot
            self.H[k, pl.ds(al(g * self.p, 16), self.p), :] = tot
            for d in range(1, nz):
                self.back(k, d).start()

        def s5(self, k):
            for d in range(1, nz):
                self.back(k, d).wait()
            self.xback(k).start()
            self.keep(k).start()

        def s6(self, k):
            self.xback(k).wait()
            self.keep(k).wait()

    qi = ct.take(4 * (4 + 2 * ne))
    qn, qp = 4 + 2 * ne, QROWS // ne

    def q_core(k, q):
        return remote(m.QS.at[k, 2 * q + oc], m.QG.at[k, q, pl.ds(al(c * 192, 64), 192), :], sib, qi + k * qn + q)

    def q_y(k):
        return remote(m.QG.at[k, oy], m.QB.at[k], yn, qi + k * qn + 2)

    def q_rs(k, d):
        q, dev = peer(d)
        return remote(m.QG.at[k, yi, pl.ds(al(q * qp, 16), qp), :], m.QC.at[k, ne - 1 - d], dev, qi + k * qn + 3 + d)

    def q_at(k):
        return red_out.at[pl.ds(al(QSTART + k * QROWS + e * qp, 16), qp), :]

    def q_ag(k, d):
        return remote(m.QT.at[k], q_at(k), peer(d)[1], qi + k * qn + 2 + ne + d)

    def q_keep(k):
        return local(m.QT.at[k], q_at(k), qi + k * qn + 3)

    def q0(k):
        for q in range(2):
            q_core(k, q).start()
        for q in range(2):
            m.QG[k, q, pl.ds(al(c * 192, 64), 192), :] = m.QS[k, 2 * q + c]

    def q1(k):
        for q in range(2):
            q_core(k, q).wait()
        q_y(k).start()

    def q2(k):
        q_y(k).wait()
        m.QG[k, yi] = (m.QG[k, yi].astype(F32) + m.QB[k].astype(F32)).astype(BF16)
        for d in range(1, ne):
            q_rs(k, d).start()

    def q3(k):
        for d in range(1, ne):
            q_rs(k, d).wait()
        tot = m.QG[k, yi, pl.ds(al(e * qp, 16), qp), :].astype(F32)
        for d in range(ne - 1):
            tot = tot + m.QC[k, d].astype(F32)
        m.QT[k] = tot.astype(BF16)
        for d in range(1, ne):
            q_ag(k, d).start()
        q_keep(k).start()

    def q4(k):
        for d in range(1, ne):
            q_ag(k, d).wait()
        q_keep(k).wait()

    FC = Chunk("F", FROWS, 0, 4)
    OC = Chunk("O", OROWS, OSTART, 1)

    g2, b2, bd = row(2), row(3), row(4)

    def c1(t, _):
        rows = pl.ds(al(t * 512, 512), 512)
        for u in range(2):
            swap(cot_h, m.dys, idy, 2 * t + u, "wait")
        mid = m.xs[rows, :].astype(F32) + dg(m.ot[t], m.wo[...], 0, 0)
        xc = mid - rowmean(mid)
        r = lax.rsqrt(rowmean(xc * xc) + EPS)
        nv = xc * r
        m.n2[rows, :] = nv
        m.rs[rows, :] = jnp.broadcast_to(r, (512, 128))
        av = (nv * g2 + b2).astype(BF16)
        m.a2[rows, :] = av
        m.a2t[:, rows] = av.T
        dyv = m.dys[rows, :]
        m.dyt[:, rows] = dyv.T
        m.gg[4:5, :] += colsum(dyv.astype(F32))
        m.ya[rows, :] = mid + bd
        m.da[rows, :] = jnp.zeros((512, 512), F32)
        return 0

    lax.fori_loop(0, 2, c1, 0)
    g_forward("wd")
    g_done("wu")
    g_done("wd")

    def c2(f, _):
        bu = jnp.concatenate([m.vec[s, pl.ds(5 + f, 1), :] for s in range(4)], axis=1)
        wuf, wdf = m.wu[f], m.wd[f]
        up = dg(m.a2[...], wuf, 1, 0) + bu
        u2 = up * up
        th = jnp.tanh(up * (K0 + (K0 * K1) * u2))
        hp = 0.5 + 0.5 * th
        av = (up * hp).astype(BF16)
        m.act[...] = av
        m.ya[...] += dg(av, wdf, 1, 0)
        dact = dg(m.dys[...], wdf, 1, 1)
        gp = hp + (0.5 * up) * (1.0 - th * th) * (K0 + (3 * K0 * K1) * u2)
        dv = (dact * gp).astype(BF16)
        m.dup[...] = dv
        m.gbu[f, 0:1, :] = colsum(dv.astype(F32))
        m.da[...] += dg(dv, wuf, 1, 1)

        @pl.when(f > 0)
        def _():
            FC.s1(f - 1)

        @pl.when(f == 3)
        def _():
            FC.s2(0)

        gd = dg(m.dyt[...], m.act[...], 1, 0).astype(BF16)
        for s in range(4):
            m.FG[f, s, 0:512, :] = gd[:, s * 128:(s + 1) * 128]
        gu = dg(m.a2t[...], m.dup[...], 1, 0).astype(BF16)
        for s in range(4):
            for b in range(4):
                m.FG[f, s, 512 + b * 128:640 + b * 128, :] = gu[s * 128:(s + 1) * 128, b * 128:(b + 1) * 128]
        FC.s0(f)
        return 0

    lax.fori_loop(0, 4, c2, 0)
    yst, dmid = m.dup, m.act
    idx = ct.take(2)

    def d_piece(t):
        return remote(m.dst.at[t], m.do.at[2 * c + t], sib, idx + t)

    def c3(t, _):
        rows = pl.ds(al(t * 512, 512), 512)
        yst[rows, :] = m.ya[rows, :].astype(BF16)
        for u in range(2):
            swap(yst, y_out, iy, 2 * t + u, "start")
        dav, nv, r = m.da[rows, :], m.n2[rows, :], m.rs[rows, 0:1]
        m.gg[2:3, :] += colsum(dav * nv)
        m.gg[3:4, :] += colsum(dav)
        gr = dav * g2
        dn = r * (gr - rowmean(gr) - nv * rowmean(gr * nv))
        dm = (m.dys[rows, :].astype(F32) + dn).astype(BF16)
        dmid[rows, :] = dm
        m.dst[t] = dg(m.wo[pl.ds(al(oc * 256, 256), 256), :], dm, 1, 1).astype(BF16)
        d_piece(t).start()
        m.do[2 * c + t] = dg(m.wo[pl.ds(al(c * 256, 256), 256), :], dm, 1, 1).astype(BF16)

        @pl.when(t == 0)
        def _():
            FC.s1(3)
        return 0

    lax.fori_loop(0, 2, c3, 0)
    go = (dg(m.ot[0], dmid[0:512, :], 1, 0) + dg(m.ot[1], dmid[512:1024, :], 1, 0)).astype(BF16)
    for s in range(4):
        for b in range(4):
            m.OG[0, s, b * 128:(b + 1) * 128, :] = go[s * 128:(s + 1) * 128, b * 128:(b + 1) * 128]
    OC.s0(0)
    FC.s2(1)
    FC.s3(0)
    for t in range(2):
        d_piece(t).wait()

    ixq = ct.take(8)

    def x_piece(h, b):
        return remote(m.xst.at[h, b], m.dqt.at[pl.ds(al(c * 768 + h * 192, 64), 192), pl.ds(b * 512, 512)], sib,
                      ixq + h * 2 + b)

    def x_start(h):
        hrows = pl.ds(al(h * 192, 64), 192)
        for b in range(2):
            m.xst[h, b] = m.dq[canon_of(2 * oc + b), hrows, :]
            x_piece(h, b).start()
        for b in range(2):
            m.dqt[pl.ds(al(c * 768 + h * 192, 64), 192), b * 512:(b + 1) * 512] = m.dq[canon_of(2 * c + b), hrows, :]

    def q_grad(h):
        hrows = pl.ds(al(h * 192, 64), 192)
        gq = None
        for i in range(4):
            part = dg(m.dq[i, hrows, :], m.a1[phys[i]], 1, 0)
            gq = part if gq is None else gq + part
        gq = gq.astype(BF16)
        for s in range(4):
            m.QS[h, s] = gq[:, s * 128:(s + 1) * 128]
        q0(h)

    def bwd_head(h, _):
        hr = pl.ds(al(h * HD, HD), HD)
        kt = jnp.concatenate([m.qkv[phys[j], rows_of(h, 1), :] for j in range(4)], axis=1)
        vt = jnp.concatenate([m.qkv[phys[j], rows_of(h, 2), :] for j in range(4)], axis=1)
        kn = kt.T
        tri = key_le_query(256, 1)
        for i in reversed(range(8)):
            L, b, cs = (i + 1) * 256, i // 2, slice((i % 2) * 256, (i % 2) * 256 + 256)
            q = m.qkv[phys[b], rows_of(h, 0), cs]
            gr = m.do[phys[b], hr, cs]
            ls = m.lse[b, pl.ds(h, 1), cs]
            delta = colsum(gr.astype(F32) * m.o[b, hr, cs])
            lsb = jnp.broadcast_to(ls, (128, 256)).T[:, 0:1]
            deb = jnp.broadcast_to(delta, (128, 256)).T[:, 0:1]
            p = jnp.exp(dg(q.T, kt[:, :L], 1, 0) - lsb)
            pd = jnp.where(tri, p[:, L - 256:], 0.0)
            p = jnp.concatenate([p[:, :L - 256], pd], axis=1) if i else pd
            dp = dg(gr.T, vt[:, :L], 1, 0)
            ds = (p * (dp - deb)).astype(BF16)
            p = p.astype(BF16)
            m.dq[b, rows_of(h, 0), cs] = dg(ds, kn[:L], 1, 0).T.astype(BF16)
            dk, dv = dg(q, ds, 1, 0), dg(gr, p, 1, 0)
            if i == 7:
                m.dkv[0:64, :] = dk
                m.dkv[64:128, :] = dv
            else:
                m.dkv[0:64, :L] += dk
                m.dkv[64:128, :L] += dv
        for j in range(4):
            m.dq[j, rows_of(h, 1), :] = m.dkv[0:64, j * BLK:(j + 1) * BLK].astype(BF16)
            m.dq[j, rows_of(h, 2), :] = m.dkv[64:128, j * BLK:(j + 1) * BLK].astype(BF16)
        x_start(h)
        q_grad(h)

        @pl.when(h > 0)
        def _():
            FC.s5(h - 1)
            q1(h - 1)

        FC.s4(h)

        @pl.when(h < 3)
        def _():
            FC.s3(h + 1)

        @pl.when(h < 2)
        def _():
            FC.s2(h + 2)

        @pl.when(h > 1)
        def _():
            q2(h - 2)

        @pl.when(h == 0)
        def _():
            OC.s1(0)

        @pl.when(h == 1)
        def _():
            OC.s2(0)

        @pl.when(h == 2)
        def _():
            OC.s3(0)

        @pl.when(h == 3)
        def _():
            OC.s4(0)
            q3(0)
        return 0

    lax.fori_loop(0, 4, bwd_head, 0)

    def e0(t, _):
        rows = pl.ds(al(t * 256, 256), 256)
        xv = m.xs[rows, :].astype(F32)
        xc = xv - rowmean(xv)
        r = lax.rsqrt(rowmean(xc * xc) + EPS)
        m.n2[rows, :] = xc * r
        m.rs[rows, :] = jnp.broadcast_to(r, (256, 128))
        return 0

    lax.fori_loop(0, 4, e0, 0)
    q1(3)

    def x_wait(h, _):
        for b in range(2):
            x_piece(h, b).wait()
        return 0

    lax.fori_loop(0, 4, x_wait, 0)
    wgst = m.dys

    def e1(t, _):
        rows = pl.ds(al(t * 256, 256), 256)
        dav = dg(m.dqt[:, rows], m.wt[...], 0, 0)
        nv, r = m.n2[rows, :], m.rs[rows, 0:1]
        m.gg[0:1, :] += colsum(dav * nv)
        m.gg[1:2, :] += colsum(dav)
        gr = dav * g1
        dn = r * (gr - rowmean(gr) - nv * rowmean(gr * nv))
        wgst[rows, :] = (dmid[rows, :].astype(F32) + dn).astype(BF16)
        swap(wgst, wg_out, iw, t, "start")

        @pl.when(t == 0)
        def _():
            q2(2)
            q3(1)

        @pl.when(t == 1)
        def _():
            FC.s5(3)
            OC.s5(0)

        @pl.when(t == 2)
        def _():
            q2(3)
            q3(2)
        return 0

    lax.fori_loop(0, 4, e1, 0)
    for s in range(4):
        for k in range(5):
            m.gv[s, k:k + 1, :] = m.gg[k:k + 1, s * 128:(s + 1) * 128]
        for f in range(4):
            m.gv[s, 5 + f:6 + f, :] = m.gbu[f, 0:1, s * 128:(s + 1) * 128]
    vx = [remote(m.gv.at[2 * q + oc], m.gvr.at[q], sib, ct.take()) for q in range(2)]
    vy = remote(m.gv.at[other], m.gvy, yn, ct.take())
    iv = ct.take(ne - 1)
    va = [remote(m.gv.at[w], m.gva.at[e], peer(d)[1], iv + d - 1) for d in range(1, ne)]
    for cp in vx:
        cp.start()
    for cp in vx:
        cp.wait()
    for q in range(2):
        m.gv[2 * q + c] = m.gv[2 * q + c] + m.gvr[q]
    vy.start()
    q3(3)
    vy.wait()
    m.gv[w] = m.gv[w] + m.gvy[...]
    m.gva[e] = m.gv[w]
    for cp in va:
        cp.start()
    for cp in va:
        cp.wait()
    tot = m.gva[0]
    for d in range(1, ne):
        tot = tot + m.gva[d]
    vec_out[...] = tot
    OC.s6(0)

    def fin(t, _):
        FC.s6(t)
        q4(t)
        swap(yst, y_out, iy, t, "wait")
        swap(wgst, wg_out, iw, t, "wait")
        return 0

    lax.fori_loop(0, 4, fin, 0)


def layer(nz, *ops):
    sc = scratch(nz)
    names = tuple(sc)
    sd = jax.ShapeDtypeStruct
    any_ = pl.BlockSpec(memory_space=pl.ANY)
    vm = pl.BlockSpec(memory_space=pltpu.VMEM)
    return pl.pallas_call(
        functools.partial(body, nz, names),
        out_shape=(sd((1024, 512), BF16), sd((1024, 512), BF16), sd((ROWS, 128), BF16), sd((16, 128), F32)),
        in_specs=[any_] * 6 + [vm] * 8,
        out_specs=(any_, any_, any_, vm),
        scratch_shapes=[sc[n] for n in names] + [pltpu.SemaphoreType.DMA((NSEM,)), pltpu.SemaphoreType.DMA((NSEM,))],
        compiler_params=pltpu.CompilerParams(collective_id=0, has_side_effects=True, vmem_limit_bytes=VLIM),
        name="layer",
    )(*ops)


def finish_body(y_h, wg_h, red_h, v, yo_h, wgo_h, gq_h, go_h, gu_h, gd_h, v1, v2, v3, v4, vu, vd,
                wg, red, wgo, yv, gq, go, gu, gd, sem):
    def cp(a, b, i):
        return pltpu.make_async_copy(a, b, sem.at[i])

    def red_in(k):
        return cp(red_h.at[pl.ds(k * 1024, 1024)], red.at[pl.ds(k * 1024, 1024)], k)

    def wg_in(k):
        return cp(wg_h.at[pl.ds(k * 256, 256)], wg.at[pl.ds(k * 256, 256)], 6 + k)

    outs = []

    def put(a, b):
        o = cp(a, b, 10 + len(outs))
        o.start()
        outs.append(o)

    def y_in(k):
        return cp(y_h.at[pl.ds(k * 512, 512)], yv.at[pl.ds(k * 512, 512)], 22 + k)

    for k in range(4):
        wg_in(k).start()
    for k in range(2):
        y_in(k).start()
    for k in range(6):
        red_in(k).start()
    for r, k in ((v1, 0), (v2, 1), (v3, 2), (v4, 3), (vd, 4)):
        r[...] = v[k:k + 1, :]
    vu[...] = v[5:9, :]
    for k in range(4):
        wg_in(k).wait()
        rows = slice(k * 256, (k + 1) * 256)
        wgo[rows, :] = wg[rows, :].astype(F32)
        put(wgo.at[rows], wgo_h.at[rows])
    for k in range(2):
        y_in(k).wait()
        put(yv.at[pl.ds(k * 512, 512)], yo_h.at[pl.ds(k * 512, 512)])
    for f in range(4):
        red_in(f).wait()
        gd[f * 128:(f + 1) * 128, :] = red[f * 1024:f * 1024 + 512, :].astype(F32).T
        put(gd.at[f * 128:(f + 1) * 128], gd_h.at[f * 128:(f + 1) * 128])
        for s in range(4):
            gu[:, s * 512 + f * 128:s * 512 + (f + 1) * 128] = red[f * 1024 + 512 + s * 128:f * 1024 + 640 + s * 128, :].astype(F32)
    put(gu, gu_h)
    red_in(4).wait()
    for b in range(4):
        go[:, b * 128:(b + 1) * 128] = red[OSTART + b * 128:OSTART + (b + 1) * 128, :].astype(F32)
    put(go, go_h)
    red_in(5).wait()
    for hp in range(2):
        for cc in range(2):
            for part in range(3):
                r = QSTART + hp * 768 + cc * 192 + part * 64
                blk = jnp.concatenate([red[r:r + 64, :], red[r + 384:r + 448, :]], axis=0).astype(F32).T
                if part == 0:
                    blk = blk * 0.125
                k = part * 512 + cc * 256 + hp * 128
                gq[:, k:k + 128] = blk
    put(gq, gq_h)
    for o in outs:
        o.wait()


def finish(y, wg, red, v):
    sd = jax.ShapeDtypeStruct
    any_ = pl.BlockSpec(memory_space=pl.ANY)
    vm = pl.BlockSpec(memory_space=pltpu.VMEM)
    one = sd((1, 128), F32)
    big = (sd((128, 1536), F32), sd((128, 512), F32), sd((128, 2048), F32), sd((512, 512), F32))
    return pl.pallas_call(
        finish_body,
        out_shape=(sd((1024, 512), BF16), sd((1024, 512), F32)) + big + (one, one, one, one, sd((4, 128), F32), one),
        in_specs=[any_] * 3 + [vm],
        out_specs=(any_,) * 6 + (vm,) * 6,
        scratch_shapes=[pltpu.VMEM((1024, 512), BF16), pltpu.VMEM((ROWS, 128), BF16), pltpu.VMEM((1024, 512), F32),
                        pltpu.VMEM((1024, 512), BF16)]
        + [pltpu.VMEM(b.shape, F32) for b in big] + [pltpu.SemaphoreType.DMA((24,))],
        compiler_params=pltpu.CompilerParams(vmem_limit_bytes=VLIM), name="finish",
    )(y, wg, red, v)


def on_chip(words, qkv_weight, out_weight, up_weight, down_weight, norm1_gain, norm1_bias, norm2_gain,
            norm2_bias, up_bias, down_bias, cotangent, seg_map, off_map):
    nz = lax.axis_size("group")
    r = lambda v: v.reshape(-1, 128)
    y, wg, red, v = layer(nz, words[0], cotangent[0], qkv_weight, out_weight, up_weight, down_weight.reshape(4, 128, 512),
                          r(norm1_gain), r(norm1_bias), r(norm2_gain), r(norm2_bias), r(down_bias), r(up_bias),
                          seg_map, off_map)
    y, wg, gq, go, gu, gd, v1, v2, v3, v4, vu, vd = finish(y, wg, red, v)
    f = lambda t: t.reshape(-1)
    return y[None], wg[None], gq, go, gu, gd, f(v1), f(v2), f(v3), f(v4), f(vu), f(vd)


HEADS = 8
HEAD_DIM = 64


eps = 1e-05
neg_big = -1e30


def passed_along(value, axis, by):
    peers = lax.axis_size(axis)
    return lax.ppermute(value, axis, [(i, (i + by) % peers) for i in range(peers)])


def layer_norm(features, norm_gain, norm_shift):
    row_mean = jnp.mean(features, axis=-1, keepdims=True)
    centred = features - row_mean
    inv_scale = lax.rsqrt(jnp.mean(centred * centred, axis=-1, keepdims=True) + eps)
    return centred * inv_scale * norm_gain + norm_shift


def gelu_tanh(features):
    return jax.nn.gelu(features, approximate=True)


def rows_of(array, block_id):
    return lax.dynamic_slice_in_dim(array, block_id * BLK, BLK, 0)


def cols_of(array, block_id):
    return lax.dynamic_slice_in_dim(array, block_id * BLK, BLK, 1)


def add_rows(array, update, block_id):
    return lax.dynamic_update_slice_in_dim(
        array, rows_of(array, block_id) + update, block_id * BLK, 0
    )


def put_rows(array, update, block_id):
    return lax.dynamic_update_slice_in_dim(array, update, block_id * BLK, 0)


def put_cols(array, update, block_id):
    return lax.dynamic_update_slice_in_dim(array, update, block_id * BLK, 1)


def block_info(seg_row, off_row, block_id):
    segment = lax.dynamic_index_in_dim(seg_row, block_id, 0, keepdims=False)
    position = lax.dynamic_index_in_dim(off_row, block_id, 0, keepdims=False)
    return (segment, position)


def pair_live(seg_row, off_row, query_block, key_block):
    query_seg, query_offset = block_info(seg_row, off_row, query_block)
    key_seg, key_offset = block_info(seg_row, off_row, key_block)
    return (query_seg == key_seg) & (key_offset <= query_offset) | (key_seg == 0) & (query_seg != 0)


def pair_mask(seg_row, off_row, query_block, key_block):
    query_seg, query_offset = block_info(seg_row, off_row, query_block)
    key_seg, key_offset = block_info(seg_row, off_row, key_block)
    row_ids = lax.broadcasted_iota(jnp.int32, (BLK, BLK), 0)
    col_ids = lax.broadcasted_iota(jnp.int32, (BLK, BLK), 1)
    query_pos = query_offset * BLK + row_ids
    key_pos = key_offset * BLK + col_ids
    return (query_seg == key_seg) & (key_pos <= query_pos) | (key_seg == 0) & (query_seg != 0)


def split_heads(tile_rows):
    return tile_rows.reshape(tile_rows.shape[0], HEADS, HEAD_DIM)


def tile_scores(query_tile, key_tile, allowed):
    raw_scores = jnp.einsum(
        "qhd,khd->hqk",
        split_heads(query_tile),
        split_heads(key_tile),
        preferred_element_type=jnp.float32,
    )
    return jnp.where(allowed[None], raw_scores * HEAD_DIM ** (-0.5), neg_big)


def tile_back(query_tile, key_tile, value_tile, grad_tile, norm_tile, delta_tile, allowed):
    scores = tile_scores(query_tile, key_tile, allowed)
    exp_terms = jnp.where(allowed[None], jnp.exp(scores - norm_tile[:, :, None]), 0.0)
    d_probs = jnp.einsum(
        "qhd,khd->hqk",
        split_heads(grad_tile),
        split_heads(value_tile),
        preferred_element_type=jnp.float32,
    )
    d_scores = (exp_terms * (d_probs - delta_tile[:, :, None])).astype(jnp.bfloat16)
    return (exp_terms.astype(jnp.bfloat16), d_scores)


def query_grad(d_scores, key_tile):
    part_rows = jnp.einsum(
        "hqk,khd->qhd", d_scores, split_heads(key_tile), preferred_element_type=jnp.float32
    )
    return part_rows.reshape(BLK, -1) * HEAD_DIM ** (-0.5)


def key_grad(d_scores, query_tile):
    part_rows = jnp.einsum(
        "hqk,qhd->khd", d_scores, split_heads(query_tile), preferred_element_type=jnp.float32
    )
    return part_rows.reshape(BLK, -1) * HEAD_DIM ** (-0.5)


def value_grad(probs_low, grad_tile):
    part_rows = jnp.einsum(
        "hqk,qhd->khd", probs_low, split_heads(grad_tile), preferred_element_type=jnp.float32
    )
    return part_rows.reshape(BLK, -1)


def unchanged(running):
    return running


def on_device(
    words,
    qkv_weight,
    out_weight,
    up_weight,
    down_weight,
    norm1_gain,
    norm1_bias,
    norm2_gain,
    norm2_bias,
    up_bias,
    down_bias,
    cotangent,
    seg_map,
    off_map,
):
    gathered = (
        lax.all_gather(qkv_weight, "wshard", axis=0, tiled=True),
        lax.all_gather(out_weight, "wshard", axis=0, tiled=True),
        lax.all_gather(up_weight, "wshard", axis=0, tiled=True),
        lax.all_gather(down_weight, "wshard", axis=0, tiled=True),
        lax.all_gather(norm1_gain, "wshard", axis=0, tiled=True),
        lax.all_gather(norm1_bias, "wshard", axis=0, tiled=True),
        lax.all_gather(norm2_gain, "wshard", axis=0, tiled=True),
        lax.all_gather(norm2_bias, "wshard", axis=0, tiled=True),
        lax.all_gather(up_bias, "wshard", axis=0, tiled=True),
        lax.all_gather(down_bias, "wshard", axis=0, tiled=True),
    )
    w_qkv, w_out, w_up, w_down = (gathered[0], gathered[1], gathered[2], gathered[3])
    gain1 = gathered[4].astype(jnp.float32)
    shift1 = gathered[5].astype(jnp.float32)
    gain2 = gathered[6].astype(jnp.float32)
    shift2 = gathered[7].astype(jnp.float32)
    bias_up = gathered[8].astype(jnp.float32)
    bias_down = gathered[9].astype(jnp.float32)
    seg_row = seg_map[0]
    off_row = off_map[0]
    cycle_place = lax.axis_index("ctx")
    cycle_count = lax.axis_size("ctx")
    inputs = words[0].astype(jnp.float32)
    local_rows = inputs.shape[0]
    local_blocks = local_rows // BLK
    first_block = cycle_place * local_blocks
    width = inputs.shape[1]
    normed1, pull_norm1 = jax.vjp(layer_norm, inputs, gain1, shift1)
    act1 = normed1.astype(jnp.bfloat16)
    qkv = jnp.dot(act1, w_qkv, preferred_element_type=jnp.float32)
    query_rows = qkv[:, :width].astype(jnp.bfloat16)
    key_rows = qkv[:, width : 2 * width].astype(jnp.bfloat16)
    value_rows = qkv[:, 2 * width :].astype(jnp.bfloat16)
    start_state = (
        jnp.full((HEADS, local_rows), neg_big, jnp.float32),
        jnp.zeros((HEADS, local_rows), jnp.float32),
        jnp.zeros((local_rows, width), jnp.float32),
    )
    shard_keys = lax.all_gather(key_rows, "ctx", axis=0, tiled=True)
    shard_values = lax.all_gather(value_rows, "ctx", axis=0, tiled=True)
    key_blocks = shard_keys.shape[0] // BLK

    def online_visit_pair(pair_index, state):
        row_block = pair_index // key_blocks
        col_block = pair_index % key_blocks
        query_block = first_block + row_block
        key_block = col_block

        def online_update_tile(state):
            run_max, run_sum, accum = state
            allowed = pair_mask(seg_row, off_row, query_block, key_block)
            scores = tile_scores(
                rows_of(query_rows, row_block), rows_of(shard_keys, col_block), allowed
            )
            old_max = cols_of(run_max, row_block)
            old_sum = cols_of(run_sum, row_block)
            new_max = jnp.maximum(old_max, jnp.max(scores, axis=-1))
            exp_terms = jnp.where(allowed[None], jnp.exp(scores - new_max[:, :, None]), 0.0)
            factor = jnp.exp(old_max - new_max)
            new_sum = old_sum * factor + jnp.sum(exp_terms, axis=-1)
            part_rows = jnp.einsum(
                "hqk,khd->qhd",
                exp_terms.astype(jnp.bfloat16),
                split_heads(rows_of(shard_values, col_block)),
                preferred_element_type=jnp.float32,
            )
            old_rows = rows_of(accum, row_block).reshape(BLK, HEADS, HEAD_DIM)
            new_rows = (old_rows * factor.T[:, :, None] + part_rows).reshape(BLK, -1)
            return (
                put_cols(run_max, new_max, row_block),
                put_cols(run_sum, new_sum, row_block),
                put_rows(accum, new_rows, row_block),
            )

        return lax.cond(
            pair_live(seg_row, off_row, query_block, key_block),
            online_update_tile,
            unchanged,
            state,
        )

    run_max, run_sum, accum = lax.fori_loop(
        0, local_blocks * key_blocks, online_visit_pair, start_state
    )
    log_norm = run_max + jnp.log(run_sum)
    attended = (accum.reshape(local_rows, HEADS, HEAD_DIM) / run_sum.T[:, :, None]).reshape(
        local_rows, width
    )
    attended_low = attended.astype(jnp.bfloat16)
    middle = inputs + jnp.dot(attended_low, w_out, preferred_element_type=jnp.float32)
    normed2, pull_norm2 = jax.vjp(layer_norm, middle, gain2, shift2)
    act2 = normed2.astype(jnp.bfloat16)
    hidden = jnp.dot(act2, w_up, preferred_element_type=jnp.float32) + bias_up
    gelu_out, pull_gelu = jax.vjp(gelu_tanh, hidden)
    gelu_low = gelu_out.astype(jnp.bfloat16)
    output = (
        middle + jnp.dot(gelu_low, w_down, preferred_element_type=jnp.float32) + bias_down
    ).astype(jnp.bfloat16)
    upstream = cotangent[0]
    upstream_f = upstream.astype(jnp.float32)
    grad_down = jnp.einsum("nf,nd->fd", gelu_low, upstream, preferred_element_type=jnp.float32)
    grad_bias_down = jnp.sum(upstream_f, axis=0)
    d_gelu = jnp.einsum("nd,fd->nf", upstream, w_down, preferred_element_type=jnp.float32)
    d_hidden = pull_gelu(d_gelu)[0].astype(jnp.bfloat16)
    grad_up = jnp.einsum("nd,nf->df", act2, d_hidden, preferred_element_type=jnp.float32)
    grad_bias_up = jnp.sum(d_hidden.astype(jnp.float32), axis=0)
    d_act2 = jnp.einsum("nf,df->nd", d_hidden, w_up, preferred_element_type=jnp.float32)
    d_middle_norm, grad_gain2, grad_shift2 = pull_norm2(d_act2)
    d_middle = (upstream_f + d_middle_norm).astype(jnp.bfloat16)
    grad_out = jnp.einsum("nd,ne->de", attended_low, d_middle, preferred_element_type=jnp.float32)
    d_attended = jnp.einsum(
        "ne,de->nd", d_middle, w_out, preferred_element_type=jnp.float32
    ).astype(jnp.bfloat16)
    row_delta = jnp.sum(
        (d_attended.astype(jnp.float32) * attended).reshape(local_rows, HEADS, HEAD_DIM), axis=-1
    ).T
    zero_rows = jnp.zeros((local_rows, width), jnp.float32)

    def attend_back(cycle_turn, cycle_state):
        held_keys, held_values, held_dk, held_dv, d_query = cycle_state
        source = (cycle_place - cycle_turn) % cycle_count

        def attend_visit_pair(pair_index, partial_value):
            row_block = pair_index // local_blocks
            col_block = pair_index % local_blocks
            query_block = first_block + row_block
            key_block = source * local_blocks + col_block

            def attend_update_tile(partial_value):
                dk_acc, dv_acc, dq_acc = partial_value
                query_tile = rows_of(query_rows, row_block)
                key_tile = rows_of(held_keys, col_block)
                grad_tile = rows_of(d_attended, row_block)
                allowed = pair_mask(seg_row, off_row, query_block, key_block)
                probs_low, d_scores = tile_back(
                    query_tile,
                    key_tile,
                    rows_of(held_values, col_block),
                    grad_tile,
                    cols_of(log_norm, row_block),
                    cols_of(row_delta, row_block),
                    allowed,
                )
                dq_acc = add_rows(dq_acc, query_grad(d_scores, key_tile), row_block)
                dk_acc = add_rows(dk_acc, key_grad(d_scores, query_tile), col_block)
                dv_acc = add_rows(dv_acc, value_grad(probs_low, grad_tile), col_block)
                return (dk_acc, dv_acc, dq_acc)

            return lax.cond(
                pair_live(seg_row, off_row, query_block, key_block),
                attend_update_tile,
                unchanged,
                partial_value,
            )

        held_dk, held_dv, d_query = lax.fori_loop(
            0, local_blocks * local_blocks, attend_visit_pair, (held_dk, held_dv, d_query)
        )
        return (held_keys, held_values, held_dk, held_dv, d_query)

    def pass_grads(held_dk, held_dv):
        return (
            passed_along(held_dk.astype(jnp.bfloat16), "ctx", 1).astype(held_dk.dtype),
            passed_along(held_dv.astype(jnp.bfloat16), "ctx", 1).astype(held_dv.dtype),
        )

    def turn_step(cycle_turn, cycle_state):
        held_keys, held_values, held_dk, held_dv, d_query = attend_back(cycle_turn, cycle_state)
        held_keys, held_values = passed_along((held_keys, held_values), "ctx", 1)
        held_dk, held_dv = pass_grads(held_dk, held_dv)
        return (held_keys, held_values, held_dk, held_dv, d_query)

    cycle_state = lax.fori_loop(
        0, cycle_count - 1, turn_step, (key_rows, value_rows, zero_rows, zero_rows, zero_rows)
    )
    cycle_state = attend_back(cycle_count - 1, cycle_state)
    d_keys, d_values = pass_grads(cycle_state[2], cycle_state[3])
    d_query = cycle_state[4]
    d_qkv = jnp.concatenate(
        [d_query.astype(jnp.bfloat16), d_keys.astype(jnp.bfloat16), d_values.astype(jnp.bfloat16)],
        axis=1,
    )
    grad_qkv = jnp.einsum("nd,nf->df", act1, d_qkv, preferred_element_type=jnp.float32)
    d_act1 = jnp.einsum("nf,df->nd", d_qkv, w_qkv, preferred_element_type=jnp.float32)
    d_inputs_norm, grad_gain1, grad_shift1 = pull_norm1(d_act1)
    words_grad = d_middle.astype(jnp.float32) + d_inputs_norm
    shards = (
        lax.psum_scatter(
            grad_qkv.astype(jnp.bfloat16), "wshard", scatter_dimension=0, tiled=True
        ).astype(jnp.float32),
        lax.psum_scatter(
            grad_out.astype(jnp.bfloat16), "wshard", scatter_dimension=0, tiled=True
        ).astype(jnp.float32),
        lax.psum_scatter(
            grad_up.astype(jnp.bfloat16), "wshard", scatter_dimension=0, tiled=True
        ).astype(jnp.float32),
        lax.psum_scatter(
            grad_down.astype(jnp.bfloat16), "wshard", scatter_dimension=0, tiled=True
        ).astype(jnp.float32),
        lax.psum_scatter(
            grad_gain1.astype(jnp.bfloat16), "wshard", scatter_dimension=0, tiled=True
        ).astype(jnp.float32),
        lax.psum_scatter(
            grad_shift1.astype(jnp.bfloat16), "wshard", scatter_dimension=0, tiled=True
        ).astype(jnp.float32),
        lax.psum_scatter(
            grad_gain2.astype(jnp.bfloat16), "wshard", scatter_dimension=0, tiled=True
        ).astype(jnp.float32),
        lax.psum_scatter(
            grad_shift2.astype(jnp.bfloat16), "wshard", scatter_dimension=0, tiled=True
        ).astype(jnp.float32),
        lax.psum_scatter(
            grad_bias_up.astype(jnp.bfloat16), "wshard", scatter_dimension=0, tiled=True
        ).astype(jnp.float32),
        lax.psum_scatter(
            grad_bias_down.astype(jnp.bfloat16), "wshard", scatter_dimension=0, tiled=True
        ).astype(jnp.float32),
    )
    totals = lax.psum(
        (
            shards[0],
            shards[1],
            shards[2],
            shards[3],
            shards[4],
            shards[5],
            shards[6],
            shards[7],
            shards[8],
            shards[9],
        ),
        ("group", "ctx"),
    )
    return (
        output[None],
        words_grad[None],
        totals[0],
        totals[1],
        totals[2],
        totals[3],
        totals[4],
        totals[5],
        totals[6],
        totals[7],
        totals[8],
        totals[9],
    )


def solution(mesh):
    chip = mesh.shape["ctx"] == 2 and mesh.shape["wshard"] == 4 and mesh.shape["group"] in (2, 4)
    return jax.shard_map(
        on_chip if chip else on_device,
        mesh=mesh,
        in_specs=(
            P(("group", "wshard"), "ctx", None),
            P("wshard", None),
            P("wshard", None),
            P("wshard", None),
            P("wshard", None),
            P("wshard"),
            P("wshard"),
            P("wshard"),
            P("wshard"),
            P("wshard"),
            P("wshard"),
            P(("group", "wshard"), "ctx", None),
            P(("group", "wshard"), None),
            P(("group", "wshard"), None),
        ),
        out_specs=(
            P(("group", "wshard"), "ctx", None),
            P(("group", "wshard"), "ctx", None),
            P("wshard", None),
            P("wshard", None),
            P("wshard", None),
            P("wshard", None),
            P("wshard"),
            P("wshard"),
            P("wshard"),
            P("wshard"),
            P("wshard"),
            P("wshard"),
        ),
        check_vma=False,
    )
```

```python
import functools
import jax
import jax.numpy as jnp
from jax import lax
from jax.experimental import pallas as pl
from jax.experimental.pallas import tpu as pltpu
from jax.sharding import PartitionSpec as P

BLK = 512
HD = 64
EPS = 1e-5
F32 = jnp.float32
BF16 = jnp.bfloat16
K0 = 0.7978845608
K1 = 0.044715
MESH = pl.DeviceIdType.MESH
VLIM = 63 * 1024 * 1024
FROWS, OROWS, QROWS = 1024, 512, 384
OSTART, QSTART, ROWS = 4096, 4608, 6144
NSEM = 280
CHUNKS = (("F0", FROWS, "xyz"), ("F1", FROWS, "xyz"), ("F2", FROWS, "yxz"), ("F3", FROWS, "yz"), ("O", OROWS, "yz"))


PLAN = {
    ("g", 0): ((0, 0),),
    ("f", 1): ((0, 1),),
    ("g", 1): ((1, 0),),
    ("f", 2): ((1, 1),),
    ("g", 2): ((2, 0),),
    ("f", 3): ((0, 2), (2, 1),),
    ("g", 3): ((3, 0),),
    ("c", 0): ((1, 2), (9, 0),),
    ("c", 1): ((3, 1), (0, 3), (9, 1),),
    "go": ((4, 0), (9, 2),),
    ("d", 0): ((4, 1), (2, 2), (9, 3),),
    ("D", 0): ((0, 4), (1, 3), (9, 4),),
    ("e", 0): ((9, 5),),
    ("q", 0): ((5, 0), (2, 3),),
    ("d", 1): ((3, 2), (0, 5), (5, 1), (9, 6),),
    ("D", 1): ((4, 2), (1, 4), (9, 7),),
    ("e", 1): ((2, 4), (5, 2),),
    ("q", 1): ((6, 0),),
    ("d", 2): ((6, 1),),
    ("D", 2): ((3, 3),),
    ("e", 2): ((4, 3),),
    ("q", 2): ((7, 0), (6, 2), (3, 4), (1, 5),),
    ("d", 3): ((4, 4), (7, 1), (2, 5),),
    ("D", 3): ((5, 3),),
    ("e", 3): ((6, 3), (7, 2),),
    ("q", 3): ((8, 0),),
    ("w", 0): ((8, 1),),
    ("w", 1): ((3, 5),),
    ("w", 2): ((4, 5),),
    ("w", 3): ((8, 2),),
}


def dg(a, b, ca, cb):
    return lax.dot_general(a, b, (((ca,), (cb,)), ((), ())), preferred_element_type=F32)


def colsum(v):
    return jnp.sum(v, axis=0, keepdims=True)


def rowmean(v):
    return jnp.mean(v, axis=-1, keepdims=True)


def key_le_query(n, key_axis):
    k = lax.broadcasted_iota(jnp.int32, (n, n), key_axis)
    q = lax.broadcasted_iota(jnp.int32, (n, n), 1 - key_axis)
    return k <= q


def al(v, n):
    return pl.multiple_of(v, n)


def chunk_scratch(nz, rows, kind):
    V = lambda *s: pltpu.VMEM(s, BF16)
    held = rows if kind == "yz" else rows // 2
    return dict(A=V(2, rows, 128), B=V(held if kind == "xyz" else rows, 128),
                X=V(held // nz, 128) if kind == "yz" else V(2 if kind == "xyz" else 1, held, 128),
                Z=V(nz - 1, held // nz, 128), T=V(held // nz, 128), H=V(held, 128))


def scratch(nz):
    ne = 2 * nz
    V = lambda *s, t=BF16: pltpu.VMEM(s, t)
    return dict(
        xs=V(1024, 512), dys=V(1024, 512), wqr=V(128, 1536), wur=V(128, 2048), wt=V(1536, 512), wo=V(512, 512),
        wu=V(4, 512, 512), wd=V(4, 512, 512), vown=V(16, 128, t=F32), vec=V(4, 16, 128, t=F32),
        so=V(2, 8, 128, t=jnp.int32), sm=pltpu.SMEM((8, 128), jnp.int32),
        a1=V(4, 512, 512), qkv=V(4, 768, 512), o=V(4, 256, 512, t=F32), lse=V(4, 8, 512, t=F32),
        ost=V(2, 256, 512), ot=V(2, 512, 512), n2=V(1024, 512, t=F32), rs=V(1024, 128, t=F32), a2=V(1024, 512),
        a2t=V(512, 1024), dyt=V(512, 1024), ya=V(1024, 512, t=F32), da=V(1024, 512, t=F32),
        act=V(1024, 512), dup=V(1024, 512), do=V(4, 256, 512), dst=V(2, 256, 512), dq=V(4, 768, 512),
        dkv=V(128, 2048, t=F32), xst=V(4, 2, 192, 512), dqt=V(1536, 1024),
        gv=V(4, 16, 128, t=F32), gvr=V(2, 16, 128, t=F32), gvy=V(16, 128, t=F32), gva=V(ne, 16, 128, t=F32),
        gg=V(8, 512, t=F32), gbu=V(4, 8, 512, t=F32),
        FG=V(4, 4, FROWS, 128), OG=V(4, OROWS, 128),
        **{f"{t}{q}": v for t, rows, kind in CHUNKS for q, v in chunk_scratch(nz, rows, kind).items()},
        QS=V(4, 4, 192, 128), QG=V(4, 2, QROWS, 128), QB=V(4, QROWS, 128), QC=V(4, ne - 1, QROWS // ne, 128),
        QT=V(4, QROWS // ne, 128),
    )


class Count:
    def __init__(self):
        self.n = 0

    def take(self, k=1):
        self.n += k
        assert self.n <= NSEM
        return self.n - k


class Ns:
    def __init__(self, d):
        self.__dict__.update(d)


def body(nz, names, *args):
    (words_h, cot_h, wq_h, wo_h, wu_h, wd_h, n1g, n1b, n2g, n2b, bdr, bur, seg_r, off_r) = args[:14]
    y_out, wg_out, red_out, vec_out = args[14:18]
    m = Ns(dict(zip(names, args[18:18 + len(names)])))
    send, recv = args[18 + len(names):]
    ct = Count()
    ne = 2 * nz
    g, x, w = lax.axis_index("group"), lax.axis_index("ctx"), lax.axis_index("wshard")
    yi, c = w // 2, w % 2
    oc, oy, ox = 1 - c, 1 - yi, 1 - x
    e = x * nz + g
    sib = (g, x, 2 * yi + oc)
    yn = (g, x, 2 * oy + c)
    diag = (g, x, 2 * oy + oc)
    xn = (g, ox, w)
    zp = (g + 1 - 2 * (g % 2), x, w)
    sw = (g, c, 2 * yi + x)
    stay = x == c
    moves = jnp.logical_not(stay)

    def peer(d):
        q = (e + d) % ne
        return q, (q % nz, q // nz, w)

    def zpeer(d):
        q = (g + d) % nz
        return q, (q, x, w)

    def remote(src, dst_, dev, i):
        return pltpu.make_async_remote_copy(src_ref=src, dst_ref=dst_, send_sem=send.at[i], recv_sem=recv.at[i],
                                            device_id=dev, device_id_type=MESH)

    def local(src, dst_, i):
        return pltpu.make_async_copy(src, dst_, send.at[i])

    def begin(src, dst_):
        cp = local(src, dst_, ct.take())
        cp.start()
        return cp

    l_wq = begin(wq_h, m.wqr)
    l_wo = begin(wo_h, m.wo.at[pl.ds(al(w * 128, 128), 128), :])
    l_wu = begin(wu_h, m.wur)
    l_wd = begin(wd_h, m.wd.at[:, pl.ds(al(w * 128, 128), 128), :])
    bar = pltpu.get_barrier_semaphore()
    peers = [sib, yn, diag] + [peer(d)[1] for d in range(1, ne)]
    for p in peers:
        pl.semaphore_signal(bar, inc=1, device_id=p, device_id_type=MESH)

    @pl.when(moves)
    def _():
        pl.semaphore_signal(bar, inc=1, device_id=sw, device_id_type=MESH)

    m.vown[...] = jnp.zeros_like(m.vown)
    for k, r in enumerate((n1g, n1b, n2g, n2b, bdr)):
        m.vown[k:k + 1, :] = r[...].astype(F32)
    m.vown[5:9, :] = bur[...].astype(F32)
    m.so[0] = jnp.zeros((8, 128), jnp.int32)
    m.so[0, 0:1, 0:4] = seg_r[...] * 2 + off_r[...]
    m.gg[...] = jnp.zeros_like(m.gg)
    m.gbu[...] = jnp.zeros_like(m.gbu)
    m.gv[...] = jnp.zeros_like(m.gv)
    pl.semaphore_wait(bar, len(peers) + jnp.where(stay, 0, 1))

    def swap(src, dst_, i, t, what, n=256):
        rows = pl.ds(al(t * n, n), n)

        @pl.when(stay)
        def _():
            cp = local(src.at[rows], dst_.at[rows], i + t)
            cp.start() if what == "start" else cp.wait()

        @pl.when(moves)
        def _():
            cp = remote(src.at[rows], dst_.at[rows], sw, i + t)
            cp.start() if what == "start" else cp.wait()

    ix, idy, iy, iw = ct.take(4), ct.take(4), ct.take(8), ct.take(8)
    for t in range(4):
        swap(words_h, m.xs, ix, t, "start")
    so_x = remote(m.so.at[0], m.so.at[1], sib, ct.take())
    so_x.start()
    vcs = [remote(m.vown, m.vec.at[w], p, ct.take()) for p in (sib, yn, diag)]
    for v in vcs:
        v.start()
    m.vec[w] = m.vown[...]

    mine = pl.ds(al(w * 128, 128), 128)
    l_wq.wait()
    for cc in range(2):
        for hp in range(2):
            for part in range(3):
                b = (part * 4 + cc * 2 + hp) * 128
                blk = m.wqr[:, b:b + 128].T
                if part == 0:
                    blk = (blk.astype(F32) * 0.125).astype(BF16)
                r = cc * 768 + hp * 384 + part * 64
                m.wt[r:r + 64, mine] = blk[:64]
                m.wt[r + 192:r + 256, mine] = blk[64:]

    other = 2 * oy + c

    def shard(n, s, f):
        v = pl.ds(al(s * 128, 128), 128)
        if n == "wt":
            return m.wt.at[:, v]
        if n == "wo":
            return m.wo.at[v, :]
        return (m.wu if n == "wu" else m.wd).at[f, v, :]

    pieces = [("wt", 0), ("wo", 0)] + [(n, f) for f in range(4) for n in ("wu", "wd")]
    ig = {p: ct.take(3) for p in pieces}

    def g_sib(p):
        return remote(shard(p[0], w, p[1]), shard(p[0], w, p[1]), sib, ig[p])

    def g_y(p):
        return remote(shard(p[0], w, p[1]), shard(p[0], w, p[1]), yn, ig[p] + 1)

    def g_fwd(p):
        return remote(shard(p[0], other, p[1]), shard(p[0], other, p[1]), sib, ig[p] + 2)

    def g_forward(*ps):
        for p in ps:
            g_y(p).wait_recv()
            g_fwd(p).start()

    g_y(("wt", 0)).start()
    g_sib(("wt", 0)).start()
    l_wu.wait()
    for f in range(4):
        for s in range(4):
            m.wu[f, mine, s * 128:(s + 1) * 128] = m.wur[:, s * 512 + f * 128:s * 512 + (f + 1) * 128]
    l_wo.wait()
    l_wd.wait()
    for p in pieces[1:]:
        g_y(p).start()
    for p in pieces[1:]:
        g_sib(p).start()
    for v in vcs:
        v.wait()
    so_x.wait()
    m.so[0] = jnp.where(stay, m.so[0], m.so[1])
    so_s = local(m.so.at[0], m.sm, ct.take())
    so_s.start()

    def row(k):
        return jnp.concatenate([m.vec[s, k:k + 1, :] for s in range(4)], axis=1)

    g1, b1 = row(0), row(1)

    ia = ct.take(4)

    def a_slot(core, t):
        return m.a1.at[2 * core + t // 2, pl.ds(al((t % 2) * 256, 256), 256), :]

    def a_piece(t):
        return remote(a_slot(c, t), a_slot(c, t), sib, ia + t)

    def norm1(t, _=0):
        rows = pl.ds(al(t * 256, 256), 256)
        swap(words_h, m.xs, ix, t, "wait")
        xv = m.xs[rows, :].astype(F32)
        xc = xv - rowmean(xv)
        r = lax.rsqrt(rowmean(xc * xc) + EPS)
        a_slot(c, t)[...] = (xc * r * g1 + b1).astype(BF16)
        a_piece(t).start()
        return 0

    wrows = pl.ds(al(c * 768, 256), 768)

    near, far = pl.ds(al(yi * 256, 256), 256), pl.ds(al(oy * 256, 256), 256)
    part_of = (m.ya, m.da)

    def words_of(t, feats):
        half = pl.ds(al((t % 2) * 256, 256), 256)
        return jnp.concatenate([m.a1[t // 2, half, feats], m.a1[2 + t // 2, half, feats]], axis=0)

    def project(t, part=None):
        cols = pl.ds(al((t % 2) * 256, 256), 256)
        res = dg(m.wt[wrows, far], words_of(t, far), 1, 1)
        res = res + (dg(m.wt[wrows, near], words_of(t, near), 1, 1) if part is None else part[0:768, :])
        res = res.astype(BF16)
        m.qkv[t // 2, :, cols] = res[:, :256]
        m.qkv[2 + t // 2, :, cols] = res[:, 256:]

    norm1(0)
    g_sib(("wt", 0)).wait()
    for t in range(2):
        norm1(t + 1)
        a_piece(t).wait()
        part_of[t][0:768, :] = dg(m.wt[wrows, near], words_of(t, near), 1, 1)
    g_forward(("wt", 0))
    g_fwd(("wt", 0)).wait()
    project(0, m.ya)
    project(1, m.da)
    norm1(3)
    for t in range(2, 4):
        a_piece(t).wait()
        project(t)
    for t in range(4):
        swap(cot_h, m.dys, idy, t, "start")
    so_s.wait()
    canon = [m.sm[0, b] for b in range(4)]
    phys = [jnp.minimum(sum(jnp.where(canon[b] == k, b, 0) for b in range(1, 4)), 3) for k in range(4)]

    def canon_of(p):
        return jnp.clip(m.sm[0, p], 0, 3)

    def rows_of(h, part):
        return pl.ds(al(h * 192 + part * 64, 64), 64)

    def fwd_head(h, _):
        kn = [m.qkv[phys[j], rows_of(h, 1), :].T for j in range(4)]
        q = jnp.concatenate([m.qkv[phys[j], rows_of(h, 0), :] for j in range(4)], axis=1)
        tri = key_le_query(BLK, 0)
        s = []
        for j in range(4):
            sj = dg(kn[j], q[:, j * BLK:], 1, 0)
            sd = jnp.where(tri, sj[:, :BLK], -1e30)
            s.append(sd if j == 3 else jnp.concatenate([sd, sj[:, BLK:]], axis=1))
        mx = [jnp.max(sj, axis=0, keepdims=True) for sj in s]
        top = mx[0]
        for j in range(1, 4):
            top = jnp.concatenate([top[:, :j * BLK], jnp.maximum(top[:, j * BLK:], mx[j])], axis=1)
        acc = tot = None
        for j in range(4):
            p = jnp.exp(s[j] - top[:, j * BLK:])
            lj = colsum(p)
            a = dg(m.qkv[phys[j], rows_of(h, 2), :], p.astype(BF16), 1, 0)
            acc = a if acc is None else jnp.concatenate([acc[:, :j * BLK], acc[:, j * BLK:] + a], axis=1)
            tot = lj if tot is None else jnp.concatenate([tot[:, :j * BLK], tot[:, j * BLK:] + lj], axis=1)
        ov = acc * (1.0 / tot)
        ls = top + jnp.log(tot)
        for i in range(4):
            m.o[i, pl.ds(al(h * HD, HD), HD), :] = ov[:, i * BLK:(i + 1) * BLK]
            m.lse[i, pl.ds(h, 1), :] = ls[:, i * BLK:(i + 1) * BLK]

        @pl.when(h == 0)
        def _():
            g_forward(*pieces[1:4])

        @pl.when(h == 2)
        def _():
            g_forward(*pieces[4:6])

        @pl.when(h == 3)
        def _():
            g_forward(*pieces[6:8])
        return 0

    lax.fori_loop(0, 4, fwd_head, 0)
    oxc = []
    for b in range(2):
        m.ost[b] = m.o[canon_of(2 * oc + b)].astype(BF16)
        cp = remote(m.ost.at[b], m.ot.at[b, pl.ds(al(c * 256, 256), 256), :], sib, ct.take())
        cp.start()
        oxc.append(cp)
    for b in range(2):
        m.ot[b, pl.ds(al(c * 256, 256), 256), :] = m.o[canon_of(2 * c + b)].astype(BF16)
    g_fwd(("wo", 0)).wait()
    g_sib(("wo", 0)).wait()
    for cp in oxc:
        cp.wait()

    class Chunk:
        def __init__(self, k):
            tag, self.rows, self.kind = CHUNKS[k]
            self.G = m.FG.at[k] if k < 4 else m.OG
            for q in "ABXZTH":
                setattr(self, q, getattr(m, tag + q))
            self.start = k * FROWS
            self.held = self.rows if self.kind == "yz" else self.rows // 2
            self.p = self.held // nz
            self.lo = 0 if self.kind == "yz" else x * self.held
            self.slots = (w, other) if self.kind == "xyz" else (w,)
            self.i = ct.take(8 + 2 * nz)

        def r(self, off, n):
            return pl.ds(al(off, 16), n)

        def core(self, q):
            return remote(self.G.at[2 * q + oc], self.A.at[q], sib, self.i + q)

        def y(self):
            if self.kind == "xyz":
                return remote(self.G.at[other, self.r(self.lo, self.held), :], self.B, yn, self.i + 2)
            return remote(self.G.at[other], self.B, yn, self.i + 2)

        def xs(self):
            if self.kind == "yz":
                return [remote(self.T, self.X, xn, self.i + 3)]
            return [remote(self.G.at[v, self.r(ox * self.held, self.held), :], self.X.at[n], xn, self.i + 3 + n)
                    for n, v in enumerate(self.slots)]

        def z(self, d):
            q, dev = zpeer(d)
            return remote(self.G.at[w, self.r(self.lo + q * self.p, self.p), :], self.Z.at[nz - 1 - d], dev,
                          self.i + 4 + d)

        def back(self, d):
            return remote(self.T, self.H.at[self.r(g * self.p, self.p), :], zpeer(d)[1], self.i + 3 + nz + d)

        def at(self):
            return red_out.at[self.r(self.start + self.lo, self.held), :]

        def xback(self):
            return remote(self.H, self.at(), xn, self.i + 3 + 2 * nz)

        def keep(self):
            return local(self.H, self.at(), self.i + 4 + 2 * nz)

        def add(self, slot, rows, v):
            self.G[slot, rows, :] = (self.G[slot, rows, :].astype(F32) + v.astype(F32)).astype(BF16)

        def begin(self):
            for q in range(2):
                self.core(q).start()

        def add_core(self):
            for q in range(2):
                self.core(q).wait()
            whole = slice(0, self.rows)
            self.add(other, whole, self.A[oy])
            if self.kind != "xyz":
                self.y().start()
            self.add(w, whole, self.A[yi])
            if self.kind == "xyz":
                self.x_go()

        def x_go(self):
            for cp in self.xs():
                cp.start()

        def x_add(self):
            for cp in self.xs():
                cp.wait()
            for n, v in reversed(list(enumerate(self.slots))):
                self.add(v, self.r(self.lo, self.held), self.X[n])
                if n == 1:
                    self.y().start()

        def y_add(self):
            self.y().wait()
            if self.kind == "xyz":
                self.add(w, self.r(self.lo, self.held), self.B[...])
            else:
                self.add(w, slice(0, self.rows), self.B[...])

        def z_go(self):
            for d in range(1, nz):
                self.z(d).start()

        def z_sum(self):
            for d in range(1, nz):
                self.z(d).wait()
            tot = self.G[w, self.r(self.lo + g * self.p, self.p), :].astype(F32)
            for d in range(nz - 1):
                tot = tot + self.Z[d].astype(F32)
            return tot.astype(BF16)

        def z_back(self, tot):
            self.T[...] = tot
            self.H[self.r(g * self.p, self.p), :] = tot
            for d in range(1, nz):
                self.back(d).start()

        def step(self, n):
            if n == 0:
                self.begin()
            elif n == 1:
                self.add_core()
            elif n == 2:
                if self.kind == "xyz":
                    self.x_add()
                else:
                    self.y_add()
                    self.x_go() if self.kind == "yxz" else self.z_go()
            elif n == 3:
                if self.kind == "xyz":
                    self.y_add()
                    self.z_go()
                elif self.kind == "yxz":
                    self.x_add()
                    self.z_go()
                else:
                    self.T[...] = self.z_sum()
                    self.x_go()
            elif n == 4:
                if self.kind == "yz":
                    for cp in self.xs():
                        cp.wait()
                    self.z_back((self.T[...].astype(F32) + self.X[...].astype(F32)).astype(BF16))
                else:
                    self.z_back(self.z_sum())
            elif n == 5:
                for d in range(1, nz):
                    self.back(d).wait()
                if self.kind != "yz":
                    self.xback().start()
                self.keep().start()
            else:
                if self.kind != "yz":
                    self.xback().wait()
                self.keep().wait()

    qi = ct.take(4 * (4 + 2 * ne))
    qn, qp = 4 + 2 * ne, QROWS // ne

    def q_core(k, q):
        return remote(m.QS.at[k, 2 * q + oc], m.QG.at[k, q, pl.ds(al(c * 192, 64), 192), :], sib, qi + k * qn + q)

    def q_y(k):
        return remote(m.QG.at[k, oy], m.QB.at[k], yn, qi + k * qn + 2)

    def q_rs(k, d):
        q, dev = peer(d)
        return remote(m.QG.at[k, yi, pl.ds(al(q * qp, 16), qp), :], m.QC.at[k, ne - 1 - d], dev, qi + k * qn + 3 + d)

    def q_at(k):
        return red_out.at[pl.ds(al(QSTART + k * QROWS + e * qp, 16), qp), :]

    def q_ag(k, d):
        return remote(m.QT.at[k], q_at(k), peer(d)[1], qi + k * qn + 2 + ne + d)

    def q_keep(k):
        return local(m.QT.at[k], q_at(k), qi + k * qn + 3)

    def q0(k):
        for q in range(2):
            q_core(k, q).start()
        for q in range(2):
            m.QG[k, q, pl.ds(al(c * 192, 64), 192), :] = m.QS[k, 2 * q + c]

    def q1(k):
        for q in range(2):
            q_core(k, q).wait()
        q_y(k).start()

    def q2(k):
        q_y(k).wait()
        m.QG[k, yi] = (m.QG[k, yi].astype(F32) + m.QB[k].astype(F32)).astype(BF16)
        for d in range(1, ne):
            q_rs(k, d).start()

    def q3(k):
        for d in range(1, ne):
            q_rs(k, d).wait()
        tot = m.QG[k, yi, pl.ds(al(e * qp, 16), qp), :].astype(F32)
        for d in range(ne - 1):
            tot = tot + m.QC[k, d].astype(F32)
        m.QT[k] = tot.astype(BF16)
        for d in range(1, ne):
            q_ag(k, d).start()
        q_keep(k).start()

    def q4(k):
        for d in range(1, ne):
            q_ag(k, d).wait()
        q_keep(k).wait()

    chunks = [Chunk(k) for k in range(5)]
    chain = (q0, q1, q2, q3, q4)

    def events(key):
        for k, n in PLAN.get(key, ()):
            if k == 9:
                swap(m.dup, y_out, iy, n, "start", 128)
            elif k < 5:
                chunks[k].step(n)
            else:
                chain[n](k - 5)

    def when_events(tag, v, values):
        for u in values:
            if (tag, u) in PLAN:
                @pl.when(v == u)
                def _():
                    events((tag, u))

    g2, b2, bd = row(2), row(3), row(4)

    def c1(t, _):
        rows = pl.ds(al(t * 512, 512), 512)
        for u in range(2):
            swap(cot_h, m.dys, idy, 2 * t + u, "wait")
        mid = m.xs[rows, :].astype(F32) + dg(m.ot[t], m.wo[...], 0, 0)
        xc = mid - rowmean(mid)
        r = lax.rsqrt(rowmean(xc * xc) + EPS)
        nv = xc * r
        m.n2[rows, :] = nv
        m.rs[rows, :] = jnp.broadcast_to(r, (512, 128))
        av = (nv * g2 + b2).astype(BF16)
        m.a2[rows, :] = av
        m.a2t[:, rows] = av.T
        dyv = m.dys[rows, :]
        m.dyt[:, rows] = dyv.T
        m.gg[4:5, :] += colsum(dyv.astype(F32))
        m.ya[rows, :] = mid + bd
        m.da[rows, :] = jnp.zeros((512, 512), F32)
        return 0

    lax.fori_loop(0, 2, c1, 0)
    g_forward(*pieces[8:])
    for p in pieces[2:]:
        g_sib(p).wait()
        g_fwd(p).wait()
    for p in pieces:
        g_y(p).wait_send()

    def c2(f, _):
        bu = jnp.concatenate([m.vec[s, pl.ds(5 + f, 1), :] for s in range(4)], axis=1)
        wuf, wdf = m.wu[f], m.wd[f]
        up = dg(m.a2[...], wuf, 1, 0) + bu
        u2 = up * up
        th = jnp.tanh(up * (K0 + (K0 * K1) * u2))
        hp = 0.5 + 0.5 * th
        av = (up * hp).astype(BF16)
        m.act[...] = av
        m.ya[...] += dg(av, wdf, 1, 0)
        dact = dg(m.dys[...], wdf, 1, 1)
        gp = hp + (0.5 * up) * (1.0 - th * th) * (K0 + (3 * K0 * K1) * u2)
        dv = (dact * gp).astype(BF16)
        m.dup[...] = dv
        m.gbu[f, 0:1, :] = colsum(dv.astype(F32))
        m.da[...] += dg(dv, wuf, 1, 1)

        when_events("f", f, range(4))
        gd = dg(m.dyt[...], m.act[...], 1, 0).astype(BF16)
        for s in range(4):
            m.FG[f, s, 0:512, :] = gd[:, s * 128:(s + 1) * 128]
        gu = dg(m.a2t[...], m.dup[...], 1, 0).astype(BF16)
        for s in range(4):
            for b in range(4):
                m.FG[f, s, 512 + b * 128:640 + b * 128, :] = gu[s * 128:(s + 1) * 128, b * 128:(b + 1) * 128]
        when_events("g", f, range(4))
        return 0

    lax.fori_loop(0, 4, c2, 0)
    yst, dmid = m.dup, m.act
    idx = ct.take(2)

    def d_piece(t):
        return remote(m.dst.at[t], m.do.at[2 * c + t], sib, idx + t)

    def c3(t, _):
        rows = pl.ds(al(t * 512, 512), 512)
        yst[rows, :] = m.ya[rows, :].astype(BF16)
        dav, nv, r = m.da[rows, :], m.n2[rows, :], m.rs[rows, 0:1]
        m.gg[2:3, :] += colsum(dav * nv)
        m.gg[3:4, :] += colsum(dav)
        gr = dav * g2
        dn = r * (gr - rowmean(gr) - nv * rowmean(gr * nv))
        dm = (m.dys[rows, :].astype(F32) + dn).astype(BF16)
        dmid[rows, :] = dm
        m.dst[t] = dg(m.wo[pl.ds(al(oc * 256, 256), 256), :], dm, 1, 1).astype(BF16)
        d_piece(t).start()
        m.do[2 * c + t] = dg(m.wo[pl.ds(al(c * 256, 256), 256), :], dm, 1, 1).astype(BF16)

        when_events("c", t, range(2))
        return 0

    lax.fori_loop(0, 2, c3, 0)
    go = (dg(m.ot[0], dmid[0:512, :], 1, 0) + dg(m.ot[1], dmid[512:1024, :], 1, 0)).astype(BF16)
    for s in range(4):
        for b in range(4):
            m.OG[s, b * 128:(b + 1) * 128, :] = go[s * 128:(s + 1) * 128, b * 128:(b + 1) * 128]
    events("go")
    for t in range(2):
        d_piece(t).wait()

    ixq = ct.take(8)

    def x_piece(h, b):
        return remote(m.xst.at[h, b], m.dqt.at[pl.ds(al(c * 768 + h * 192, 64), 192), pl.ds(b * 512, 512)], sib,
                      ixq + h * 2 + b)

    def x_start(h):
        hrows = pl.ds(al(h * 192, 64), 192)
        for b in range(2):
            m.xst[h, b] = m.dq[canon_of(2 * oc + b), hrows, :]
            x_piece(h, b).start()
        for b in range(2):
            m.dqt[pl.ds(al(c * 768 + h * 192, 64), 192), b * 512:(b + 1) * 512] = m.dq[canon_of(2 * c + b), hrows, :]

    def q_grad(h):
        hrows = pl.ds(al(h * 192, 64), 192)
        gq = None
        for i in range(4):
            part = dg(m.dq[i, hrows, :], m.a1[phys[i]], 1, 0)
            gq = part if gq is None else gq + part
        gq = gq.astype(BF16)
        for s in range(4):
            m.QS[h, s] = gq[:, s * 128:(s + 1) * 128]

    def bwd_head(h, _):
        hr = pl.ds(al(h * HD, HD), HD)
        kt = jnp.concatenate([m.qkv[phys[j], rows_of(h, 1), :] for j in range(4)], axis=1)
        vt = jnp.concatenate([m.qkv[phys[j], rows_of(h, 2), :] for j in range(4)], axis=1)
        kn = kt.T
        tri = key_le_query(256, 1)
        for i in reversed(range(8)):
            L, b, cs = (i + 1) * 256, i // 2, slice((i % 2) * 256, (i % 2) * 256 + 256)
            q = m.qkv[phys[b], rows_of(h, 0), cs]
            gr = m.do[phys[b], hr, cs]
            ls = m.lse[b, pl.ds(h, 1), cs]
            delta = colsum(gr.astype(F32) * m.o[b, hr, cs])
            lsb = jnp.broadcast_to(ls, (128, 256)).T[:, 0:1]
            deb = jnp.broadcast_to(delta, (128, 256)).T[:, 0:1]
            p = jnp.exp(dg(q.T, kt[:, :L], 1, 0) - lsb)
            pd = jnp.where(tri, p[:, L - 256:], 0.0)
            p = jnp.concatenate([p[:, :L - 256], pd], axis=1) if i else pd
            dp = dg(gr.T, vt[:, :L], 1, 0)
            ds = (p * (dp - deb)).astype(BF16)
            p = p.astype(BF16)
            m.dq[b, rows_of(h, 0), cs] = dg(ds, kn[:L], 1, 0).T.astype(BF16)
            dk, dv = dg(q, ds, 1, 0), dg(gr, p, 1, 0)
            if i == 7:
                m.dkv[0:64, :] = dk
                m.dkv[64:128, :] = dv
            else:
                m.dkv[0:64, :L] += dk
                m.dkv[64:128, :L] += dv
            if i in (6, 4):
                when_events("dD"[i == 4], h, range(4))
        for j in range(4):
            m.dq[j, rows_of(h, 1), :] = m.dkv[0:64, j * BLK:(j + 1) * BLK].astype(BF16)
            m.dq[j, rows_of(h, 2), :] = m.dkv[64:128, j * BLK:(j + 1) * BLK].astype(BF16)
        x_start(h)
        when_events("e", h, range(4))
        q_grad(h)
        when_events("q", h, range(4))
        return 0

    lax.fori_loop(0, 4, bwd_head, 0)

    def x_wait(h, _):
        for b in range(2):
            x_piece(h, b).wait()
        return 0

    lax.fori_loop(0, 4, x_wait, 0)
    wgst = m.dys

    def e1(t, _):
        rows = pl.ds(al(t * 256, 256), 256)
        xv = m.xs[rows, :].astype(F32)
        xc = xv - rowmean(xv)
        r = lax.rsqrt(rowmean(xc * xc) + EPS)
        nv = xc * r
        dav = dg(m.dqt[:, rows], m.wt[...], 0, 0)
        m.gg[0:1, :] += colsum(dav * nv)
        m.gg[1:2, :] += colsum(dav)
        gr = dav * g1
        dn = r * (gr - rowmean(gr) - nv * rowmean(gr * nv))
        wgst[rows, :] = (dmid[rows, :].astype(F32) + dn).astype(BF16)
        swap(wgst, wg_out, iw, t, "start", 128)
        when_events("w", t, range(4))
        return 0

    lax.fori_loop(0, 4, e1, 0)
    for s in range(4):
        for k in range(5):
            m.gv[s, k:k + 1, :] = m.gg[k:k + 1, s * 128:(s + 1) * 128]
        for f in range(4):
            m.gv[s, 5 + f:6 + f, :] = m.gbu[f, 0:1, s * 128:(s + 1) * 128]
    vx = [remote(m.gv.at[2 * q + oc], m.gvr.at[q], sib, ct.take()) for q in range(2)]
    vy = remote(m.gv.at[other], m.gvy, yn, ct.take())
    iv = ct.take(ne - 1)
    va = [remote(m.gv.at[w], m.gva.at[e], peer(d)[1], iv + d - 1) for d in range(1, ne)]
    for cp in vx:
        cp.start()
    for t in range(4, 6):
        swap(wgst, wg_out, iw, t, "start", 128)
    for cp in vx:
        cp.wait()
    for q in range(2):
        m.gv[2 * q + c] = m.gv[2 * q + c] + m.gvr[q]
    vy.start()
    q3(2)
    vy.wait()
    m.gv[w] = m.gv[w] + m.gvy[...]
    m.gva[e] = m.gv[w]
    for cp in va:
        cp.start()
    q3(3)
    for t in range(6, 8):
        swap(wgst, wg_out, iw, t, "start", 128)
    for cp in va:
        cp.wait()
    tot = m.gva[0]
    for d in range(1, ne):
        tot = tot + m.gva[d]
    vec_out[...] = tot
    for k in range(5):
        chunks[k].step(6)

    def fin(t, _):
        q4(t)
        for u in range(2):
            swap(m.dup, y_out, iy, 2 * t + u, "wait", 128)
            swap(wgst, wg_out, iw, 2 * t + u, "wait", 128)
        return 0

    lax.fori_loop(0, 4, fin, 0)


def layer(nz, *ops):
    sc = scratch(nz)
    names = tuple(sc)
    sd = jax.ShapeDtypeStruct
    any_ = pl.BlockSpec(memory_space=pl.ANY)
    vm = pl.BlockSpec(memory_space=pltpu.VMEM)
    return pl.pallas_call(
        functools.partial(body, nz, names),
        out_shape=(sd((1024, 512), BF16), sd((1024, 512), BF16), sd((ROWS, 128), BF16), sd((16, 128), F32)),
        in_specs=[any_] * 6 + [vm] * 8,
        out_specs=(any_, any_, any_, vm),
        scratch_shapes=[sc[n] for n in names] + [pltpu.SemaphoreType.DMA((NSEM,)), pltpu.SemaphoreType.DMA((NSEM,))],
        compiler_params=pltpu.CompilerParams(collective_id=0, has_side_effects=True, vmem_limit_bytes=VLIM),
        name="layer",
    )(*ops)


def finish_body(y_h, wg_h, red_h, v, yo_h, wgo_h, gq_h, go_h, gu_h, gd_h, v1, v2, v3, v4, vu, vd,
                wg, red, wgo, yv, gq, go, gu, gd, sem):
    def cp(a, b, i):
        return pltpu.make_async_copy(a, b, sem.at[i])

    def red_in(k):
        return cp(red_h.at[pl.ds(k * 1024, 1024)], red.at[pl.ds(k * 1024, 1024)], k)

    def wg_in(k):
        return cp(wg_h.at[pl.ds(k * 256, 256)], wg.at[pl.ds(k * 256, 256)], 6 + k)

    outs = []

    def put(a, b):
        o = cp(a, b, 10 + len(outs))
        o.start()
        outs.append(o)

    def y_in(k):
        return cp(y_h.at[pl.ds(k * 512, 512)], yv.at[pl.ds(k * 512, 512)], 22 + k)

    for k in range(4):
        wg_in(k).start()
    for k in range(2):
        y_in(k).start()
    for k in range(6):
        red_in(k).start()
    for r, k in ((v1, 0), (v2, 1), (v3, 2), (v4, 3), (vd, 4)):
        r[...] = v[k:k + 1, :]
    vu[...] = v[5:9, :]
    for k in range(4):
        wg_in(k).wait()
        rows = slice(k * 256, (k + 1) * 256)
        wgo[rows, :] = wg[rows, :].astype(F32)
        put(wgo.at[rows], wgo_h.at[rows])
    for k in range(2):
        y_in(k).wait()
        put(yv.at[pl.ds(k * 512, 512)], yo_h.at[pl.ds(k * 512, 512)])
    for f in range(4):
        red_in(f).wait()
        gd[f * 128:(f + 1) * 128, :] = red[f * 1024:f * 1024 + 512, :].astype(F32).T
        put(gd.at[f * 128:(f + 1) * 128], gd_h.at[f * 128:(f + 1) * 128])
        for s in range(4):
            gu[:, s * 512 + f * 128:s * 512 + (f + 1) * 128] = red[f * 1024 + 512 + s * 128:f * 1024 + 640 + s * 128, :].astype(F32)
    put(gu, gu_h)
    red_in(4).wait()
    for b in range(4):
        go[:, b * 128:(b + 1) * 128] = red[OSTART + b * 128:OSTART + (b + 1) * 128, :].astype(F32)
    put(go, go_h)
    red_in(5).wait()
    for hp in range(2):
        for cc in range(2):
            for part in range(3):
                r = QSTART + hp * 768 + cc * 192 + part * 64
                blk = jnp.concatenate([red[r:r + 64, :], red[r + 384:r + 448, :]], axis=0).astype(F32).T
                if part == 0:
                    blk = blk * 0.125
                k = part * 512 + cc * 256 + hp * 128
                gq[:, k:k + 128] = blk
    put(gq, gq_h)
    for o in outs:
        o.wait()


def finish(y, wg, red, v):
    sd = jax.ShapeDtypeStruct
    any_ = pl.BlockSpec(memory_space=pl.ANY)
    vm = pl.BlockSpec(memory_space=pltpu.VMEM)
    one = sd((1, 128), F32)
    big = (sd((128, 1536), F32), sd((128, 512), F32), sd((128, 2048), F32), sd((512, 512), F32))
    return pl.pallas_call(
        finish_body,
        out_shape=(sd((1024, 512), BF16), sd((1024, 512), F32)) + big + (one, one, one, one, sd((4, 128), F32), one),
        in_specs=[any_] * 3 + [vm],
        out_specs=(any_,) * 6 + (vm,) * 6,
        scratch_shapes=[pltpu.VMEM((1024, 512), BF16), pltpu.VMEM((ROWS, 128), BF16), pltpu.VMEM((1024, 512), F32),
                        pltpu.VMEM((1024, 512), BF16)]
        + [pltpu.VMEM(b.shape, F32) for b in big] + [pltpu.SemaphoreType.DMA((24,))],
        compiler_params=pltpu.CompilerParams(vmem_limit_bytes=VLIM), name="finish",
    )(y, wg, red, v)


def on_chip(words, qkv_weight, out_weight, up_weight, down_weight, norm1_gain, norm1_bias, norm2_gain,
            norm2_bias, up_bias, down_bias, cotangent, seg_map, off_map):
    nz = lax.axis_size("group")
    r = lambda v: v.reshape(-1, 128)
    y, wg, red, v = layer(nz, words[0], cotangent[0], qkv_weight, out_weight, up_weight, down_weight.reshape(4, 128, 512),
                          r(norm1_gain), r(norm1_bias), r(norm2_gain), r(norm2_bias), r(down_bias), r(up_bias),
                          seg_map, off_map)
    y, wg, gq, go, gu, gd, v1, v2, v3, v4, vu, vd = finish(y, wg, red, v)
    f = lambda t: t.reshape(-1)
    return y[None], wg[None], gq, go, gu, gd, f(v1), f(v2), f(v3), f(v4), f(vu), f(vd)


HEADS = 8
HEAD_DIM = 64


eps = 1e-05
neg_big = -1e30


def passed_along(value, axis, by):
    peers = lax.axis_size(axis)
    return lax.ppermute(value, axis, [(i, (i + by) % peers) for i in range(peers)])


def layer_norm(features, norm_gain, norm_shift):
    row_mean = jnp.mean(features, axis=-1, keepdims=True)
    centred = features - row_mean
    inv_scale = lax.rsqrt(jnp.mean(centred * centred, axis=-1, keepdims=True) + eps)
    return centred * inv_scale * norm_gain + norm_shift


def gelu_tanh(features):
    return jax.nn.gelu(features, approximate=True)


def rows_of(array, block_id):
    return lax.dynamic_slice_in_dim(array, block_id * BLK, BLK, 0)


def cols_of(array, block_id):
    return lax.dynamic_slice_in_dim(array, block_id * BLK, BLK, 1)


def add_rows(array, update, block_id):
    return lax.dynamic_update_slice_in_dim(
        array, rows_of(array, block_id) + update, block_id * BLK, 0
    )


def put_rows(array, update, block_id):
    return lax.dynamic_update_slice_in_dim(array, update, block_id * BLK, 0)


def put_cols(array, update, block_id):
    return lax.dynamic_update_slice_in_dim(array, update, block_id * BLK, 1)


def block_info(seg_row, off_row, block_id):
    segment = lax.dynamic_index_in_dim(seg_row, block_id, 0, keepdims=False)
    position = lax.dynamic_index_in_dim(off_row, block_id, 0, keepdims=False)
    return (segment, position)


def pair_live(seg_row, off_row, query_block, key_block):
    query_seg, query_offset = block_info(seg_row, off_row, query_block)
    key_seg, key_offset = block_info(seg_row, off_row, key_block)
    return (query_seg == key_seg) & (key_offset <= query_offset) | (key_seg == 0) & (query_seg != 0)


def pair_mask(seg_row, off_row, query_block, key_block):
    query_seg, query_offset = block_info(seg_row, off_row, query_block)
    key_seg, key_offset = block_info(seg_row, off_row, key_block)
    row_ids = lax.broadcasted_iota(jnp.int32, (BLK, BLK), 0)
    col_ids = lax.broadcasted_iota(jnp.int32, (BLK, BLK), 1)
    query_pos = query_offset * BLK + row_ids
    key_pos = key_offset * BLK + col_ids
    return (query_seg == key_seg) & (key_pos <= query_pos) | (key_seg == 0) & (query_seg != 0)


def split_heads(tile_rows):
    return tile_rows.reshape(tile_rows.shape[0], HEADS, HEAD_DIM)


def tile_scores(query_tile, key_tile, allowed):
    raw_scores = jnp.einsum(
        "qhd,khd->hqk",
        split_heads(query_tile),
        split_heads(key_tile),
        preferred_element_type=jnp.float32,
    )
    return jnp.where(allowed[None], raw_scores * HEAD_DIM ** (-0.5), neg_big)


def tile_back(query_tile, key_tile, value_tile, grad_tile, norm_tile, delta_tile, allowed):
    scores = tile_scores(query_tile, key_tile, allowed)
    exp_terms = jnp.where(allowed[None], jnp.exp(scores - norm_tile[:, :, None]), 0.0)
    d_probs = jnp.einsum(
        "qhd,khd->hqk",
        split_heads(grad_tile),
        split_heads(value_tile),
        preferred_element_type=jnp.float32,
    )
    d_scores = (exp_terms * (d_probs - delta_tile[:, :, None])).astype(jnp.bfloat16)
    return (exp_terms.astype(jnp.bfloat16), d_scores)


def query_grad(d_scores, key_tile):
    part_rows = jnp.einsum(
        "hqk,khd->qhd", d_scores, split_heads(key_tile), preferred_element_type=jnp.float32
    )
    return part_rows.reshape(BLK, -1) * HEAD_DIM ** (-0.5)


def key_grad(d_scores, query_tile):
    part_rows = jnp.einsum(
        "hqk,qhd->khd", d_scores, split_heads(query_tile), preferred_element_type=jnp.float32
    )
    return part_rows.reshape(BLK, -1) * HEAD_DIM ** (-0.5)


def value_grad(probs_low, grad_tile):
    part_rows = jnp.einsum(
        "hqk,qhd->khd", probs_low, split_heads(grad_tile), preferred_element_type=jnp.float32
    )
    return part_rows.reshape(BLK, -1)


def unchanged(running):
    return running


def on_device(
    words,
    qkv_weight,
    out_weight,
    up_weight,
    down_weight,
    norm1_gain,
    norm1_bias,
    norm2_gain,
    norm2_bias,
    up_bias,
    down_bias,
    cotangent,
    seg_map,
    off_map,
):
    gathered = (
        lax.all_gather(qkv_weight, "wshard", axis=0, tiled=True),
        lax.all_gather(out_weight, "wshard", axis=0, tiled=True),
        lax.all_gather(up_weight, "wshard", axis=0, tiled=True),
        lax.all_gather(down_weight, "wshard", axis=0, tiled=True),
        lax.all_gather(norm1_gain, "wshard", axis=0, tiled=True),
        lax.all_gather(norm1_bias, "wshard", axis=0, tiled=True),
        lax.all_gather(norm2_gain, "wshard", axis=0, tiled=True),
        lax.all_gather(norm2_bias, "wshard", axis=0, tiled=True),
        lax.all_gather(up_bias, "wshard", axis=0, tiled=True),
        lax.all_gather(down_bias, "wshard", axis=0, tiled=True),
    )
    w_qkv, w_out, w_up, w_down = (gathered[0], gathered[1], gathered[2], gathered[3])
    gain1 = gathered[4].astype(jnp.float32)
    shift1 = gathered[5].astype(jnp.float32)
    gain2 = gathered[6].astype(jnp.float32)
    shift2 = gathered[7].astype(jnp.float32)
    bias_up = gathered[8].astype(jnp.float32)
    bias_down = gathered[9].astype(jnp.float32)
    seg_row = seg_map[0]
    off_row = off_map[0]
    cycle_place = lax.axis_index("ctx")
    cycle_count = lax.axis_size("ctx")
    inputs = words[0].astype(jnp.float32)
    local_rows = inputs.shape[0]
    local_blocks = local_rows // BLK
    first_block = cycle_place * local_blocks
    width = inputs.shape[1]
    normed1, pull_norm1 = jax.vjp(layer_norm, inputs, gain1, shift1)
    act1 = normed1.astype(jnp.bfloat16)
    qkv = jnp.dot(act1, w_qkv, preferred_element_type=jnp.float32)
    query_rows = qkv[:, :width].astype(jnp.bfloat16)
    key_rows = qkv[:, width : 2 * width].astype(jnp.bfloat16)
    value_rows = qkv[:, 2 * width :].astype(jnp.bfloat16)
    start_state = (
        jnp.full((HEADS, local_rows), neg_big, jnp.float32),
        jnp.zeros((HEADS, local_rows), jnp.float32),
        jnp.zeros((local_rows, width), jnp.float32),
    )
    shard_keys = lax.all_gather(key_rows, "ctx", axis=0, tiled=True)
    shard_values = lax.all_gather(value_rows, "ctx", axis=0, tiled=True)
    key_blocks = shard_keys.shape[0] // BLK

    def online_visit_pair(pair_index, state):
        row_block = pair_index // key_blocks
        col_block = pair_index % key_blocks
        query_block = first_block + row_block
        key_block = col_block

        def online_update_tile(state):
            run_max, run_sum, accum = state
            allowed = pair_mask(seg_row, off_row, query_block, key_block)
            scores = tile_scores(
                rows_of(query_rows, row_block), rows_of(shard_keys, col_block), allowed
            )
            old_max = cols_of(run_max, row_block)
            old_sum = cols_of(run_sum, row_block)
            new_max = jnp.maximum(old_max, jnp.max(scores, axis=-1))
            exp_terms = jnp.where(allowed[None], jnp.exp(scores - new_max[:, :, None]), 0.0)
            factor = jnp.exp(old_max - new_max)
            new_sum = old_sum * factor + jnp.sum(exp_terms, axis=-1)
            part_rows = jnp.einsum(
                "hqk,khd->qhd",
                exp_terms.astype(jnp.bfloat16),
                split_heads(rows_of(shard_values, col_block)),
                preferred_element_type=jnp.float32,
            )
            old_rows = rows_of(accum, row_block).reshape(BLK, HEADS, HEAD_DIM)
            new_rows = (old_rows * factor.T[:, :, None] + part_rows).reshape(BLK, -1)
            return (
                put_cols(run_max, new_max, row_block),
                put_cols(run_sum, new_sum, row_block),
                put_rows(accum, new_rows, row_block),
            )

        return lax.cond(
            pair_live(seg_row, off_row, query_block, key_block),
            online_update_tile,
            unchanged,
            state,
        )

    run_max, run_sum, accum = lax.fori_loop(
        0, local_blocks * key_blocks, online_visit_pair, start_state
    )
    log_norm = run_max + jnp.log(run_sum)
    attended = (accum.reshape(local_rows, HEADS, HEAD_DIM) / run_sum.T[:, :, None]).reshape(
        local_rows, width
    )
    attended_low = attended.astype(jnp.bfloat16)
    middle = inputs + jnp.dot(attended_low, w_out, preferred_element_type=jnp.float32)
    normed2, pull_norm2 = jax.vjp(layer_norm, middle, gain2, shift2)
    act2 = normed2.astype(jnp.bfloat16)
    hidden = jnp.dot(act2, w_up, preferred_element_type=jnp.float32) + bias_up
    gelu_out, pull_gelu = jax.vjp(gelu_tanh, hidden)
    gelu_low = gelu_out.astype(jnp.bfloat16)
    output = (
        middle + jnp.dot(gelu_low, w_down, preferred_element_type=jnp.float32) + bias_down
    ).astype(jnp.bfloat16)
    upstream = cotangent[0]
    upstream_f = upstream.astype(jnp.float32)
    grad_down = jnp.einsum("nf,nd->fd", gelu_low, upstream, preferred_element_type=jnp.float32)
    grad_bias_down = jnp.sum(upstream_f, axis=0)
    d_gelu = jnp.einsum("nd,fd->nf", upstream, w_down, preferred_element_type=jnp.float32)
    d_hidden = pull_gelu(d_gelu)[0].astype(jnp.bfloat16)
    grad_up = jnp.einsum("nd,nf->df", act2, d_hidden, preferred_element_type=jnp.float32)
    grad_bias_up = jnp.sum(d_hidden.astype(jnp.float32), axis=0)
    d_act2 = jnp.einsum("nf,df->nd", d_hidden, w_up, preferred_element_type=jnp.float32)
    d_middle_norm, grad_gain2, grad_shift2 = pull_norm2(d_act2)
    d_middle = (upstream_f + d_middle_norm).astype(jnp.bfloat16)
    grad_out = jnp.einsum("nd,ne->de", attended_low, d_middle, preferred_element_type=jnp.float32)
    d_attended = jnp.einsum(
        "ne,de->nd", d_middle, w_out, preferred_element_type=jnp.float32
    ).astype(jnp.bfloat16)
    row_delta = jnp.sum(
        (d_attended.astype(jnp.float32) * attended).reshape(local_rows, HEADS, HEAD_DIM), axis=-1
    ).T
    zero_rows = jnp.zeros((local_rows, width), jnp.float32)

    def attend_back(cycle_turn, cycle_state):
        held_keys, held_values, held_dk, held_dv, d_query = cycle_state
        source = (cycle_place - cycle_turn) % cycle_count

        def attend_visit_pair(pair_index, partial_value):
            row_block = pair_index // local_blocks
            col_block = pair_index % local_blocks
            query_block = first_block + row_block
            key_block = source * local_blocks + col_block

            def attend_update_tile(partial_value):
                dk_acc, dv_acc, dq_acc = partial_value
                query_tile = rows_of(query_rows, row_block)
                key_tile = rows_of(held_keys, col_block)
                grad_tile = rows_of(d_attended, row_block)
                allowed = pair_mask(seg_row, off_row, query_block, key_block)
                probs_low, d_scores = tile_back(
                    query_tile,
                    key_tile,
                    rows_of(held_values, col_block),
                    grad_tile,
                    cols_of(log_norm, row_block),
                    cols_of(row_delta, row_block),
                    allowed,
                )
                dq_acc = add_rows(dq_acc, query_grad(d_scores, key_tile), row_block)
                dk_acc = add_rows(dk_acc, key_grad(d_scores, query_tile), col_block)
                dv_acc = add_rows(dv_acc, value_grad(probs_low, grad_tile), col_block)
                return (dk_acc, dv_acc, dq_acc)

            return lax.cond(
                pair_live(seg_row, off_row, query_block, key_block),
                attend_update_tile,
                unchanged,
                partial_value,
            )

        held_dk, held_dv, d_query = lax.fori_loop(
            0, local_blocks * local_blocks, attend_visit_pair, (held_dk, held_dv, d_query)
        )
        return (held_keys, held_values, held_dk, held_dv, d_query)

    def pass_grads(held_dk, held_dv):
        return (
            passed_along(held_dk.astype(jnp.bfloat16), "ctx", 1).astype(held_dk.dtype),
            passed_along(held_dv.astype(jnp.bfloat16), "ctx", 1).astype(held_dv.dtype),
        )

    def turn_step(cycle_turn, cycle_state):
        held_keys, held_values, held_dk, held_dv, d_query = attend_back(cycle_turn, cycle_state)
        held_keys, held_values = passed_along((held_keys, held_values), "ctx", 1)
        held_dk, held_dv = pass_grads(held_dk, held_dv)
        return (held_keys, held_values, held_dk, held_dv, d_query)

    cycle_state = lax.fori_loop(
        0, cycle_count - 1, turn_step, (key_rows, value_rows, zero_rows, zero_rows, zero_rows)
    )
    cycle_state = attend_back(cycle_count - 1, cycle_state)
    d_keys, d_values = pass_grads(cycle_state[2], cycle_state[3])
    d_query = cycle_state[4]
    d_qkv = jnp.concatenate(
        [d_query.astype(jnp.bfloat16), d_keys.astype(jnp.bfloat16), d_values.astype(jnp.bfloat16)],
        axis=1,
    )
    grad_qkv = jnp.einsum("nd,nf->df", act1, d_qkv, preferred_element_type=jnp.float32)
    d_act1 = jnp.einsum("nf,df->nd", d_qkv, w_qkv, preferred_element_type=jnp.float32)
    d_inputs_norm, grad_gain1, grad_shift1 = pull_norm1(d_act1)
    words_grad = d_middle.astype(jnp.float32) + d_inputs_norm
    shards = (
        lax.psum_scatter(
            grad_qkv.astype(jnp.bfloat16), "wshard", scatter_dimension=0, tiled=True
        ).astype(jnp.float32),
        lax.psum_scatter(
            grad_out.astype(jnp.bfloat16), "wshard", scatter_dimension=0, tiled=True
        ).astype(jnp.float32),
        lax.psum_scatter(
            grad_up.astype(jnp.bfloat16), "wshard", scatter_dimension=0, tiled=True
        ).astype(jnp.float32),
        lax.psum_scatter(
            grad_down.astype(jnp.bfloat16), "wshard", scatter_dimension=0, tiled=True
        ).astype(jnp.float32),
        lax.psum_scatter(
            grad_gain1.astype(jnp.bfloat16), "wshard", scatter_dimension=0, tiled=True
        ).astype(jnp.float32),
        lax.psum_scatter(
            grad_shift1.astype(jnp.bfloat16), "wshard", scatter_dimension=0, tiled=True
        ).astype(jnp.float32),
        lax.psum_scatter(
            grad_gain2.astype(jnp.bfloat16), "wshard", scatter_dimension=0, tiled=True
        ).astype(jnp.float32),
        lax.psum_scatter(
            grad_shift2.astype(jnp.bfloat16), "wshard", scatter_dimension=0, tiled=True
        ).astype(jnp.float32),
        lax.psum_scatter(
            grad_bias_up.astype(jnp.bfloat16), "wshard", scatter_dimension=0, tiled=True
        ).astype(jnp.float32),
        lax.psum_scatter(
            grad_bias_down.astype(jnp.bfloat16), "wshard", scatter_dimension=0, tiled=True
        ).astype(jnp.float32),
    )
    totals = lax.psum(
        (
            shards[0],
            shards[1],
            shards[2],
            shards[3],
            shards[4],
            shards[5],
            shards[6],
            shards[7],
            shards[8],
            shards[9],
        ),
        ("group", "ctx"),
    )
    return (
        output[None],
        words_grad[None],
        totals[0],
        totals[1],
        totals[2],
        totals[3],
        totals[4],
        totals[5],
        totals[6],
        totals[7],
        totals[8],
        totals[9],
    )


def solution(mesh):
    chip = mesh.shape["ctx"] == 2 and mesh.shape["wshard"] == 4 and mesh.shape["group"] in (2, 4)
    return jax.shard_map(
        on_chip if chip else on_device,
        mesh=mesh,
        in_specs=(
            P(("group", "wshard"), "ctx", None),
            P("wshard", None),
            P("wshard", None),
            P("wshard", None),
            P("wshard", None),
            P("wshard"),
            P("wshard"),
            P("wshard"),
            P("wshard"),
            P("wshard"),
            P("wshard"),
            P(("group", "wshard"), "ctx", None),
            P(("group", "wshard"), None),
            P(("group", "wshard"), None),
        ),
        out_specs=(
            P(("group", "wshard"), "ctx", None),
            P(("group", "wshard"), "ctx", None),
            P("wshard", None),
            P("wshard", None),
            P("wshard", None),
            P("wshard", None),
            P("wshard"),
            P("wshard"),
            P("wshard"),
            P("wshard"),
            P("wshard"),
            P("wshard"),
        ),
        check_vma=False,
    )
```

```python
import functools
import jax
import jax.numpy as jnp
from jax import lax
from jax.experimental import pallas as pl
from jax.experimental.pallas import tpu as pltpu
from jax.sharding import PartitionSpec as P

BLK = 512
HD = 64
EPS = 1e-5
F32 = jnp.float32
BF16 = jnp.bfloat16
K0 = 0.7978845608
K1 = 0.044715
MESH = pl.DeviceIdType.MESH
VLIM = 63 * 1024 * 1024
FROWS, OROWS, QROWS = 1024, 512, 384
OSTART, QSTART, ROWS = 4096, 4608, 6144
NSEND, NRECV = 64, 96
CHUNKS = (("F0", FROWS, "yxz"), ("F1", FROWS, "yxz"), ("F2", FROWS, "yxz"), ("F3", FROWS, "yxz"), ("O", OROWS, "yxz"))


PLAN = {
    ("g", 0): ((0, 0),),
    ("f", 1): ((0, 1),),
    ("g", 1): ((1, 0),),
    ("f", 2): ((1, 1),),
    ("g", 2): ((2, 0),),
    ("f", 3): ((0, 2), (2, 1),),
    ("g", 3): ((3, 0),),
    ("c", 0): ((1, 2), (9, 0),),
    ("c", 1): ((3, 1), (0, 3), (9, 1),),
    "go": ((4, 0), (9, 2),),
    ("d", 0): ((2, 2), (1, 3), (4, 1), (0, 4), (9, 3),),
    ("D", 0): ((9, 4),),
    ("e", 0): ((3, 2), (9, 5),),
    ("q", 0): ((5, 0), (2, 3), (1, 4), (4, 2),),
    ("d", 1): ((5, 1), (0, 5), (9, 6),),
    ("D", 1): ((3, 3), (2, 4), (9, 7),),
    ("e", 1): ((4, 3), (5, 2), (1, 5),),
    ("q", 1): ((6, 0),),
    ("d", 2): ((3, 4), (6, 1),),
    ("D", 2): ((2, 5), (4, 4),),
    ("e", 2): ((5, 3), (6, 2),),
    ("q", 2): ((7, 0),),
    ("d", 3): ((3, 5), (7, 1), (4, 5),),
    ("e", 3): ((6, 3),),
    ("q", 3): ((8, 0), (7, 2),),
    ("w", 0): ((8, 1),),
    ("w", 2): ((7, 3),),
    ("w", 3): ((8, 2),),
    "tail": ((8, 3),),
}


def dg(a, b, ca, cb):
    return lax.dot_general(a, b, (((ca,), (cb,)), ((), ())), preferred_element_type=F32)


def colsum(v):
    return jnp.sum(v, axis=0, keepdims=True)


def rowmean(v):
    return jnp.mean(v, axis=-1, keepdims=True)


def key_le_query(n, key_axis):
    k = lax.broadcasted_iota(jnp.int32, (n, n), key_axis)
    q = lax.broadcasted_iota(jnp.int32, (n, n), 1 - key_axis)
    return k <= q


def al(v, n):
    return pl.multiple_of(v, n)


def chunk_scratch(nz, rows, kind):
    V = lambda *s: pltpu.VMEM(s, BF16)
    held = rows if kind == "yz" else rows // 2
    return dict(A=V(2, rows, 128), B=V(held if kind == "xyz" else rows, 128),
                X=V(held // nz, 128) if kind == "yz" else V(2 if kind == "xyz" else 1, held, 128),
                Z=V(nz - 1, held // nz, 128), T=V(held // nz, 128), H=V(held, 128))


def scratch(nz):
    ne = 2 * nz
    V = lambda *s, t=BF16: pltpu.VMEM(s, t)
    return dict(
        xs=V(1024, 512), dys=V(1024, 512), wqr=V(128, 1536), wur=V(128, 2048), wt=V(1536, 512), wo=V(512, 512),
        wu=V(4, 512, 512), wd=V(4, 512, 512), vown=V(16, 128, t=F32), vec=V(4, 16, 128, t=F32),
        so=V(2, 8, 128, t=jnp.int32), sseg=V(1, 4, t=jnp.int32), soff=V(1, 4, t=jnp.int32),
        s1g=V(1, 128), s1b=V(1, 128), s2g=V(1, 128), s2b=V(1, 128), sbd=V(1, 128), sbu=V(4, 128), sm=pltpu.SMEM((8, 128), jnp.int32),
        a1=V(4, 512, 512), qkv=V(4, 768, 512), o=V(4, 256, 512, t=F32), lse=V(4, 8, 512, t=F32),
        ost=V(2, 256, 512), ot=V(2, 512, 512), n2=V(1024, 512, t=F32), rs=V(1024, 128, t=F32), a2=V(1024, 512),
        a2t=V(512, 1024), dyt=V(512, 1024), ya=V(1024, 512, t=F32), da=V(1024, 512, t=F32),
        act=V(1024, 512), dup=V(1024, 512), do=V(4, 256, 512), dst=V(2, 256, 512), dq=V(4, 768, 512),
        dkv=V(128, 2048, t=F32), xst=V(4, 2, 192, 512), dqt=V(1536, 1024),
        gv=V(4, 16, 128, t=F32), gvr=V(2, 16, 128, t=F32), gvy=V(16, 128, t=F32), gva=V(ne, 16, 128, t=F32),
        gg=V(8, 512, t=F32), gbu=V(4, 8, 512, t=F32),
        FG=V(4, 4, FROWS, 128), OG=V(4, OROWS, 128),
        **{f"{t}{q}": v for t, rows, kind in CHUNKS for q, v in chunk_scratch(nz, rows, kind).items()},
        QS=V(4, 4, 192, 128), QG=V(4, 2, QROWS, 128), QB=V(4, QROWS, 128), QC=V(4, ne - 1, QROWS // ne, 128),
        QT=V(4, QROWS // ne, 128),
    )


class Count:
    def __init__(self, most):
        self.n, self.most = 0, most

    def take(self, k=1):
        self.n += k
        assert self.n <= self.most
        return self.n - k


class Ns:
    def __init__(self, d):
        self.__dict__.update(d)


def body(nz, names, *args):
    (words_h, cot_h, wq_h, wo_h, wu_h, wd_h, n1g, n1b, n2g, n2b, bdr, bur, seg_r, off_r) = args[:14]
    y_out, wg_out, red_out, vec_out = args[14:18]
    m = Ns(dict(zip(names, args[18:18 + len(names)])))
    send, recv = args[18 + len(names):]
    cs, cr = Count(NSEND), Count(NRECV)
    ne = 2 * nz
    g, x, w = lax.axis_index("group"), lax.axis_index("ctx"), lax.axis_index("wshard")
    yi, c = w // 2, w % 2
    oc, oy, ox = 1 - c, 1 - yi, 1 - x
    e = x * nz + g
    sib = (g, x, 2 * yi + oc)
    yn = (g, x, 2 * oy + c)
    diag = (g, x, 2 * oy + oc)
    xn = (g, ox, w)
    zp = (g + 1 - 2 * (g % 2), x, w)
    sw = (g, c, 2 * yi + x)
    stay = x == c
    moves = jnp.logical_not(stay)

    def peer(d):
        q = (e + d) % ne
        return q, (q % nz, q // nz, w)

    def zpeer(d):
        q = (g + d) % nz
        return q, (q, x, w)

    def remote(src, dst_, dev, i, j):
        return pltpu.make_async_remote_copy(src_ref=src, dst_ref=dst_, send_sem=send.at[i], recv_sem=recv.at[j],
                                            device_id=dev, device_id_type=MESH)

    def local(src, dst_, i):
        return pltpu.make_async_copy(src, dst_, send.at[i])

    def sent(ref, i):
        pltpu.make_async_copy(ref, ref, send.at[i]).wait()

    def got(ref, j):
        pltpu.make_async_copy(ref, ref, recv.at[j]).wait()

    def begin(src, dst_):
        cp = local(src, dst_, cs.take())
        cp.start()
        return cp

    bar = pltpu.get_barrier_semaphore()
    peers = [sib, yn, diag] + [peer(d)[1] for d in range(1, ne)]
    for p in peers:
        pl.semaphore_signal(bar, inc=1, device_id=p, device_id_type=MESH)

    @pl.when(moves)
    def _():
        pl.semaphore_signal(bar, inc=1, device_id=sw, device_id_type=MESH)

    l_wq = begin(wq_h, m.wqr)
    l_small = [begin(a, b) for a, b in zip((n1g, n1b, n2g, n2b, bdr, bur, seg_r, off_r),
                                           (m.s1g, m.s1b, m.s2g, m.s2b, m.sbd, m.sbu, m.sseg, m.soff))]
    l_wo = begin(wo_h, m.wo.at[pl.ds(al(w * 128, 128), 128), :])
    l_wu = begin(wu_h, m.wur)
    l_wd = begin(wd_h, m.wd.at[:, pl.ds(al(w * 128, 128), 128), :])
    m.vown[...] = jnp.zeros_like(m.vown)
    m.so[0] = jnp.zeros((8, 128), jnp.int32)
    m.gg[...] = jnp.zeros_like(m.gg)
    m.gbu[...] = jnp.zeros_like(m.gbu)
    m.gv[...] = jnp.zeros_like(m.gv)
    pl.semaphore_wait(bar, len(peers) + jnp.where(stay, 0, 1))

    def swap_go(src, dst_, ij, t, n, k=0):
        rows = pl.ds(al(t * n, n), n)

        @pl.when(stay)
        def _():
            local(src.at[rows], dst_.at[rows], ij[0] + k).start()

        @pl.when(moves)
        def _():
            remote(src.at[rows], dst_.at[rows], sw, ij[0] + k, ij[1] + k).start()

    def swap_wait(ref, ij, k=0):
        sent(ref, ij[0] + k)

        @pl.when(moves)
        def _():
            got(ref, ij[1] + k)

    def pair(k=1):
        return cs.take(k), cr.take(k)

    ix, idy, iy, iw = pair(4), pair(), pair(), pair()
    for t in range(4):
        swap_go(words_h, m.xs, ix, t, 256, t)
    for cp in l_small:
        cp.wait()
    for k, r in enumerate((m.s1g, m.s1b, m.s2g, m.s2b, m.sbd)):
        m.vown[k:k + 1, :] = r[...].astype(F32)
    m.vown[5:9, :] = m.sbu[...].astype(F32)
    m.so[0, 0:1, 0:4] = m.sseg[...] * 2 + m.soff[...]
    so_x = remote(m.so.at[0], m.so.at[1], sib, *pair())
    ivc = pair()
    vcs = [remote(m.vown, m.vec.at[w], p, *ivc) for p in (sib, yn, diag)]
    m.vec[w] = m.vown[...]

    mine = pl.ds(al(w * 128, 128), 128)
    l_wq.wait()
    for cc in range(2):
        for hp in range(2):
            for part in range(3):
                b = (part * 4 + cc * 2 + hp) * 128
                blk = m.wqr[:, b:b + 128].T
                if part == 0:
                    blk = (blk.astype(F32) * 0.125).astype(BF16)
                r = cc * 768 + hp * 384 + part * 64
                m.wt[r:r + 64, mine] = blk[:64]
                m.wt[r + 192:r + 256, mine] = blk[64:]

    other = 2 * oy + c

    def shard(n, s, f):
        v = pl.ds(al(s * 128, 128), 128)
        if n == "wt":
            return m.wt.at[:, v]
        if n == "wo":
            return m.wo.at[v, :]
        return (m.wu if n == "wu" else m.wd).at[f, v, :]

    pieces = [("wt", 0), ("wo", 0)] + [(n, f) for f in range(4) for n in ("wu", "wd")]
    big2 = m.wu.at[0:2, 0:128, :]
    big8 = m.wu.at[:, 0:256, :]
    ig = dict(wt=(pair(3)), wo=(pair(3)))
    isib, iys, ifs = pair(), cs.take(), cs.take()
    iyr, ifr = cr.take(4), cr.take(4)

    def g_sems(p, k):
        n, f = p
        if n in ig:
            return ig[n][0] + k, ig[n][1] + k
        return (isib, (iys, iyr + f), (ifs, ifr + f))[k]

    def g_sib(p):
        return remote(shard(p[0], w, p[1]), shard(p[0], w, p[1]), sib, *g_sems(p, 0))

    def g_y(p):
        return remote(shard(p[0], w, p[1]), shard(p[0], w, p[1]), yn, *g_sems(p, 1))

    def g_fwd(p):
        return remote(shard(p[0], other, p[1]), shard(p[0], other, p[1]), sib, *g_sems(p, 2))

    def g_forward(*ps):
        for p in ps:
            if p[0] in ig:
                g_y(p).wait_recv()
            elif p[0] == "wu":
                got(big2, iyr + p[1])
            g_fwd(p).start()

    g_y(("wt", 0)).start()
    g_sib(("wt", 0)).start()
    for v in vcs:
        v.start()
    so_x.start()
    l_wu.wait()
    for f in range(4):
        for s in range(4):
            m.wu[f, mine, s * 128:(s + 1) * 128] = m.wur[:, s * 512 + f * 128:s * 512 + (f + 1) * 128]
    l_wo.wait()
    l_wd.wait()
    for p in pieces[1:]:
        g_y(p).start()
    for p in pieces[1:]:
        g_sib(p).start()
    sent(m.vec.at[0:3], ivc[0])
    got(m.vec.at[0:3], ivc[1])
    so_x.wait()
    m.so[0] = jnp.where(stay, m.so[0], m.so[1])
    so_s = local(m.so.at[0], m.sm, cs.take())
    so_s.start()

    def row(k):
        return jnp.concatenate([m.vec[s, k:k + 1, :] for s in range(4)], axis=1)

    g1, b1 = row(0), row(1)

    ia = pair(4)

    def a_slot(core, t):
        return m.a1.at[2 * core + t // 2, pl.ds(al((t % 2) * 256, 256), 256), :]

    def a_piece(t):
        return remote(a_slot(c, t), a_slot(c, t), sib, ia[0] + t, ia[1] + t)

    def norm1(t, _=0):
        rows = pl.ds(al(t * 256, 256), 256)
        swap_wait(m.xs.at[rows], ix, t)
        xv = m.xs[rows, :].astype(F32)
        xc = xv - rowmean(xv)
        r = lax.rsqrt(rowmean(xc * xc) + EPS)
        a_slot(c, t)[...] = (xc * r * g1 + b1).astype(BF16)
        a_piece(t).start()
        return 0

    wrows = pl.ds(al(c * 768, 256), 768)

    near, far = pl.ds(al(yi * 256, 256), 256), pl.ds(al(oy * 256, 256), 256)
    part_of = (m.ya, m.da)

    def words_of(t, feats):
        half = pl.ds(al((t % 2) * 256, 256), 256)
        return jnp.concatenate([m.a1[t // 2, half, feats], m.a1[2 + t // 2, half, feats]], axis=0)

    def project(t, part=None):
        cols = pl.ds(al((t % 2) * 256, 256), 256)
        res = dg(m.wt[wrows, far], words_of(t, far), 1, 1)
        res = res + (dg(m.wt[wrows, near], words_of(t, near), 1, 1) if part is None else part[0:768, :])
        res = res.astype(BF16)
        m.qkv[t // 2, :, cols] = res[:, :256]
        m.qkv[2 + t // 2, :, cols] = res[:, 256:]

    norm1(0)
    g_sib(("wt", 0)).wait()
    for t in range(2):
        norm1(t + 1)
        a_piece(t).wait()
        part_of[t][0:768, :] = dg(m.wt[wrows, near], words_of(t, near), 1, 1)
    g_forward(("wt", 0))
    g_fwd(("wt", 0)).wait()
    project(0, m.ya)
    project(1, m.da)
    norm1(3)
    for t in range(2, 4):
        a_piece(t).wait()
        project(t)
    for t in range(4):
        swap_go(cot_h, m.dys, idy, t, 256)
    so_s.wait()
    canon = [m.sm[0, b] for b in range(4)]
    phys = [jnp.minimum(sum(jnp.where(canon[b] == k, b, 0) for b in range(1, 4)), 3) for k in range(4)]

    def canon_of(p):
        return jnp.clip(m.sm[0, p], 0, 3)

    def rows_of(h, part):
        return pl.ds(al(h * 192 + part * 64, 64), 64)

    def fwd_head(h, _):
        kn = [m.qkv[phys[j], rows_of(h, 1), :].T for j in range(4)]
        q = jnp.concatenate([m.qkv[phys[j], rows_of(h, 0), :] for j in range(4)], axis=1)
        tri = key_le_query(BLK, 0)
        s = []
        for j in range(4):
            sj = dg(kn[j], q[:, j * BLK:], 1, 0)
            sd = jnp.where(tri, sj[:, :BLK], -1e30)
            s.append(sd if j == 3 else jnp.concatenate([sd, sj[:, BLK:]], axis=1))
        mx = [jnp.max(sj, axis=0, keepdims=True) for sj in s]
        top = mx[0]
        for j in range(1, 4):
            top = jnp.concatenate([top[:, :j * BLK], jnp.maximum(top[:, j * BLK:], mx[j])], axis=1)
        acc = tot = None
        for j in range(4):
            p = jnp.exp(s[j] - top[:, j * BLK:])
            lj = colsum(p)
            a = dg(m.qkv[phys[j], rows_of(h, 2), :], p.astype(BF16), 1, 0)
            acc = a if acc is None else jnp.concatenate([acc[:, :j * BLK], acc[:, j * BLK:] + a], axis=1)
            tot = lj if tot is None else jnp.concatenate([tot[:, :j * BLK], tot[:, j * BLK:] + lj], axis=1)
        ov = acc * (1.0 / tot)
        ls = top + jnp.log(tot)
        for i in range(4):
            m.o[i, pl.ds(al(h * HD, HD), HD), :] = ov[:, i * BLK:(i + 1) * BLK]
            m.lse[i, pl.ds(h, 1), :] = ls[:, i * BLK:(i + 1) * BLK]

        @pl.when(h == 0)
        def _():
            g_forward(*pieces[1:4])

        @pl.when(h == 2)
        def _():
            g_forward(*pieces[4:6])

        @pl.when(h == 3)
        def _():
            g_forward(*pieces[6:8])
        return 0

    lax.fori_loop(0, 4, fwd_head, 0)
    iox = pair()
    for b in range(2):
        m.ost[b] = m.o[canon_of(2 * oc + b)].astype(BF16)
        remote(m.ost.at[b], m.ot.at[b, pl.ds(al(c * 256, 256), 256), :], sib, *iox).start()
    for b in range(2):
        m.ot[b, pl.ds(al(c * 256, 256), 256), :] = m.o[canon_of(2 * c + b)].astype(BF16)
    g_fwd(("wo", 0)).wait()
    g_sib(("wo", 0)).wait()
    sent(m.ost, iox[0])
    got(m.ost, iox[1])

    class Chunk:
        def __init__(self, k):
            tag, self.rows, self.kind = CHUNKS[k]
            self.G = m.FG.at[k] if k < 4 else m.OG
            for q in "ABXZTH":
                setattr(self, q, getattr(m, tag + q))
            self.start = k * FROWS
            self.held = self.rows if self.kind == "yz" else self.rows // 2
            self.p = self.held // nz
            self.lo = 0 if self.kind == "yz" else x * self.held
            self.slots = (w, other) if self.kind == "xyz" else (w,)
            self.i, self.keeping = cs.take(), cs.take()
            self.j = cr.take(6)

        def r(self, off, n):
            return pl.ds(al(off, 16), n)

        def core(self, q):
            return remote(self.G.at[2 * q + oc], self.A.at[q], sib, self.i, self.j)

        def y(self):
            if self.kind == "xyz":
                return remote(self.G.at[other, self.r(self.lo, self.held), :], self.B, yn, self.i, self.j + 1)
            return remote(self.G.at[other], self.B, yn, self.i, self.j + 1)

        def xs(self):
            if self.kind == "yz":
                return [remote(self.T, self.X, xn, self.i, self.j + 2)]
            return [remote(self.G.at[v, self.r(ox * self.held, self.held), :], self.X.at[n], xn, self.i, self.j + 2)
                    for n, v in enumerate(self.slots)]

        def z(self, d):
            q, dev = zpeer(d)
            return remote(self.G.at[w, self.r(self.lo + q * self.p, self.p), :], self.Z.at[nz - 1 - d], dev,
                          self.i, self.j + 3)

        def back(self, d):
            return remote(self.T, self.H.at[self.r(g * self.p, self.p), :], zpeer(d)[1], self.i, self.j + 4)

        def at(self):
            return red_out.at[self.r(self.start + self.lo, self.held), :]

        def xback(self):
            return remote(self.H, self.at(), xn, self.i, self.j + 5)

        def keep(self):
            return local(self.H, self.at(), self.keeping)

        def add(self, slot, rows, v):
            self.G[slot, rows, :] = (self.G[slot, rows, :].astype(F32) + v.astype(F32)).astype(BF16)

        def begin(self):
            for q in range(2):
                self.core(q).start()

        def add_core(self):
            sent(self.A, self.i)
            got(self.A, self.j)
            whole = slice(0, self.rows)
            self.add(other, whole, self.A[oy])
            if self.kind != "xyz":
                self.y().start()
            self.add(w, whole, self.A[yi])
            if self.kind == "xyz":
                self.x_go()

        def x_go(self):
            for cp in self.xs():
                cp.start()

        def x_wait(self):
            sent(self.X, self.i)
            got(self.X, self.j + 2)

        def x_add(self):
            self.x_wait()
            for n, v in reversed(list(enumerate(self.slots))):
                self.add(v, self.r(self.lo, self.held), self.X[n])
                if n == 1:
                    self.y().start()

        def y_add(self):
            self.y().wait()
            if self.kind == "xyz":
                self.add(w, self.r(self.lo, self.held), self.B[...])
            else:
                self.add(w, slice(0, self.rows), self.B[...])

        def z_go(self):
            for d in range(1, nz):
                self.z(d).start()

        def z_sum(self):
            sent(self.Z, self.i)
            got(self.Z, self.j + 3)
            tot = self.G[w, self.r(self.lo + g * self.p, self.p), :].astype(F32)
            for d in range(nz - 1):
                tot = tot + self.Z[d].astype(F32)
            return tot.astype(BF16)

        def z_back(self, tot):
            self.T[...] = tot
            self.H[self.r(g * self.p, self.p), :] = tot
            for d in range(1, nz):
                self.back(d).start()

        def step(self, n):
            if n == 0:
                self.begin()
            elif n == 1:
                self.add_core()
            elif n == 2:
                if self.kind == "xyz":
                    self.x_add()
                else:
                    self.y_add()
                    self.x_go() if self.kind == "yxz" else self.z_go()
            elif n == 3:
                if self.kind == "xyz":
                    self.y_add()
                    self.z_go()
                elif self.kind == "yxz":
                    self.x_add()
                    self.z_go()
                else:
                    self.T[...] = self.z_sum()
                    self.x_go()
            elif n == 4:
                if self.kind == "yz":
                    self.x_wait()
                    self.z_back((self.T[...].astype(F32) + self.X[...].astype(F32)).astype(BF16))
                else:
                    self.z_back(self.z_sum())
            elif n == 5:
                sent(self.Z, self.i)
                got(self.Z, self.j + 4)
                if self.kind != "yz":
                    self.xback().start()
                self.keep().start()
            else:
                if self.kind != "yz":
                    self.xback().wait()
                self.keep().wait()

    qs, qk, qr, qp = cs.take(4), cs.take(4), cr.take(16), QROWS // ne

    def q_core(k, q):
        return remote(m.QS.at[k, 2 * q + oc], m.QG.at[k, q, pl.ds(al(c * 192, 64), 192), :], sib, qs + k, qr + 4 * k)

    def q_y(k):
        return remote(m.QG.at[k, oy], m.QB.at[k], yn, qs + k, qr + 4 * k + 1)

    def q_rs(k, d):
        q, dev = peer(d)
        return remote(m.QG.at[k, yi, pl.ds(al(q * qp, 16), qp), :], m.QC.at[k, ne - 1 - d], dev, qs + k, qr + 4 * k + 2)

    def q_at(k):
        return red_out.at[pl.ds(al(QSTART + k * QROWS + e * qp, 16), qp), :]

    def q_ag(k, d):
        return remote(m.QT.at[k], q_at(k), peer(d)[1], qs + k, qr + 4 * k + 3)

    def q_keep(k):
        return local(m.QT.at[k], q_at(k), qk + k)

    def q0(k):
        for q in range(2):
            q_core(k, q).start()
        for q in range(2):
            m.QG[k, q, pl.ds(al(c * 192, 64), 192), :] = m.QS[k, 2 * q + c]

    def q1(k):
        half = m.QG.at[k, :, 0:192, :]
        sent(half, qs + k)
        got(half, qr + 4 * k)
        q_y(k).start()

    def q2(k):
        q_y(k).wait()
        m.QG[k, yi] = (m.QG[k, yi].astype(F32) + m.QB[k].astype(F32)).astype(BF16)
        for d in range(1, ne):
            q_rs(k, d).start()

    def q3(k):
        sent(m.QC.at[k], qs + k)
        got(m.QC.at[k], qr + 4 * k + 2)
        tot = m.QG[k, yi, pl.ds(al(e * qp, 16), qp), :].astype(F32)
        for d in range(ne - 1):
            tot = tot + m.QC[k, d].astype(F32)
        m.QT[k] = tot.astype(BF16)
        for d in range(1, ne):
            q_ag(k, d).start()
        q_keep(k).start()

    def q4(k):
        sent(m.QC.at[k], qs + k)
        got(m.QC.at[k], qr + 4 * k + 3)
        q_keep(k).wait()

    chunks = [Chunk(k) for k in range(5)]
    chain = (q0, q1, q2, q3, q4)

    def events(key):
        for k, n in PLAN.get(key, ()):
            if k == 9:
                swap_go(m.dup, y_out, iy, n, 128)
            elif k < 5:
                chunks[k].step(n)
            else:
                chain[n](k - 5)

    def when_events(tag, v, values):
        for u in values:
            if (tag, u) in PLAN:
                @pl.when(v == u)
                def _():
                    events((tag, u))

    g2, b2, bd = row(2), row(3), row(4)

    def c1(t, _):
        rows = pl.ds(al(t * 512, 512), 512)
        mid = m.xs[rows, :].astype(F32) + dg(m.ot[t], m.wo[...], 0, 0)
        xc = mid - rowmean(mid)
        r = lax.rsqrt(rowmean(xc * xc) + EPS)
        nv = xc * r
        m.n2[rows, :] = nv
        m.rs[rows, :] = jnp.broadcast_to(r, (512, 128))
        av = (nv * g2 + b2).astype(BF16)
        m.a2[rows, :] = av
        m.a2t[:, rows] = av.T
        dyv = m.dys[rows, :]
        m.dyt[:, rows] = dyv.T
        m.gg[4:5, :] += colsum(dyv.astype(F32))
        m.ya[rows, :] = mid + bd
        m.da[rows, :] = jnp.zeros((512, 512), F32)
        return 0

    swap_wait(m.dys, idy)
    lax.fori_loop(0, 2, c1, 0)

    def c2(f, _):
        for u in range(4):
            @pl.when(f == u)
            def _():
                if u == 0:
                    sent(big8, isib[0])
                    got(big8, isib[1])
                got(big2, ifr + u)
        bu = jnp.concatenate([m.vec[s, pl.ds(5 + f, 1), :] for s in range(4)], axis=1)
        wuf, wdf = m.wu[f], m.wd[f]
        up = dg(m.a2[...], wuf, 1, 0) + bu
        u2 = up * up
        th = jnp.tanh(up * (K0 + (K0 * K1) * u2))
        hp = 0.5 + 0.5 * th
        av = (up * hp).astype(BF16)
        m.act[...] = av
        m.ya[...] += dg(av, wdf, 1, 0)
        dact = dg(m.dys[...], wdf, 1, 1)
        gp = hp + (0.5 * up) * (1.0 - th * th) * (K0 + (3 * K0 * K1) * u2)
        dv = (dact * gp).astype(BF16)
        m.dup[...] = dv
        m.gbu[f, 0:1, :] = colsum(dv.astype(F32))
        m.da[...] += dg(dv, wuf, 1, 1)

        @pl.when(f == 0)
        def _():
            g_forward(*pieces[8:])

        when_events("f", f, range(4))
        gd = dg(m.dyt[...], m.act[...], 1, 0).astype(BF16)
        for s in range(4):
            m.FG[f, s, 0:512, :] = gd[:, s * 128:(s + 1) * 128]
        gu = dg(m.a2t[...], m.dup[...], 1, 0).astype(BF16)
        for s in range(4):
            for b in range(4):
                m.FG[f, s, 512 + b * 128:640 + b * 128, :] = gu[s * 128:(s + 1) * 128, b * 128:(b + 1) * 128]
        when_events("g", f, range(4))
        return 0

    lax.fori_loop(0, 4, c2, 0)
    for p in pieces[:2]:
        g_y(p).wait_send()
    sent(big8, iys)
    sent(big8, ifs)
    yst, dmid = m.dup, m.act
    idx = pair()

    def d_piece(t):
        return remote(m.dst.at[t], m.do.at[2 * c + t], sib, *idx)

    def c3(t, _):
        rows = pl.ds(al(t * 512, 512), 512)
        yst[rows, :] = m.ya[rows, :].astype(BF16)
        dav, nv, r = m.da[rows, :], m.n2[rows, :], m.rs[rows, 0:1]
        m.gg[2:3, :] += colsum(dav * nv)
        m.gg[3:4, :] += colsum(dav)
        gr = dav * g2
        dn = r * (gr - rowmean(gr) - nv * rowmean(gr * nv))
        dm = (m.dys[rows, :].astype(F32) + dn).astype(BF16)
        dmid[rows, :] = dm
        m.dst[t] = dg(m.wo[pl.ds(al(oc * 256, 256), 256), :], dm, 1, 1).astype(BF16)
        d_piece(t).start()
        m.do[2 * c + t] = dg(m.wo[pl.ds(al(c * 256, 256), 256), :], dm, 1, 1).astype(BF16)

        when_events("c", t, range(2))
        return 0

    lax.fori_loop(0, 2, c3, 0)
    go = (dg(m.ot[0], dmid[0:512, :], 1, 0) + dg(m.ot[1], dmid[512:1024, :], 1, 0)).astype(BF16)
    for s in range(4):
        for b in range(4):
            m.OG[s, b * 128:(b + 1) * 128, :] = go[s * 128:(s + 1) * 128, b * 128:(b + 1) * 128]
    events("go")
    sent(m.dst, idx[0])
    got(m.dst, idx[1])

    ixq = pair()

    def x_piece(h, b):
        return remote(m.xst.at[h, b], m.dqt.at[pl.ds(al(c * 768 + h * 192, 64), 192), pl.ds(b * 512, 512)], sib,
                      *ixq)

    def x_start(h):
        hrows = pl.ds(al(h * 192, 64), 192)
        for b in range(2):
            m.xst[h, b] = m.dq[canon_of(2 * oc + b), hrows, :]
            x_piece(h, b).start()
        for b in range(2):
            m.dqt[pl.ds(al(c * 768 + h * 192, 64), 192), b * 512:(b + 1) * 512] = m.dq[canon_of(2 * c + b), hrows, :]

    def q_grad(h):
        hrows = pl.ds(al(h * 192, 64), 192)
        gq = None
        for i in range(4):
            part = dg(m.dq[i, hrows, :], m.a1[phys[i]], 1, 0)
            gq = part if gq is None else gq + part
        gq = gq.astype(BF16)
        for s in range(4):
            m.QS[h, s] = gq[:, s * 128:(s + 1) * 128]

    def bwd_head(h, _):
        hr = pl.ds(al(h * HD, HD), HD)
        kt = jnp.concatenate([m.qkv[phys[j], rows_of(h, 1), :] for j in range(4)], axis=1)
        vt = jnp.concatenate([m.qkv[phys[j], rows_of(h, 2), :] for j in range(4)], axis=1)
        kn = kt.T
        tri = key_le_query(256, 1)
        for i in reversed(range(8)):
            L, b, cs = (i + 1) * 256, i // 2, slice((i % 2) * 256, (i % 2) * 256 + 256)
            q = m.qkv[phys[b], rows_of(h, 0), cs]
            gr = m.do[phys[b], hr, cs]
            ls = m.lse[b, pl.ds(h, 1), cs]
            delta = colsum(gr.astype(F32) * m.o[b, hr, cs])
            lsb = jnp.broadcast_to(ls, (128, 256)).T[:, 0:1]
            deb = jnp.broadcast_to(delta, (128, 256)).T[:, 0:1]
            p = jnp.exp(dg(q.T, kt[:, :L], 1, 0) - lsb)
            pd = jnp.where(tri, p[:, L - 256:], 0.0)
            p = jnp.concatenate([p[:, :L - 256], pd], axis=1) if i else pd
            dp = dg(gr.T, vt[:, :L], 1, 0)
            ds = (p * (dp - deb)).astype(BF16)
            p = p.astype(BF16)
            m.dq[b, rows_of(h, 0), cs] = dg(ds, kn[:L], 1, 0).T.astype(BF16)
            dk, dv = dg(q, ds, 1, 0), dg(gr, p, 1, 0)
            if i == 7:
                m.dkv[0:64, :] = dk
                m.dkv[64:128, :] = dv
            else:
                m.dkv[0:64, :L] += dk
                m.dkv[64:128, :L] += dv
            if i in (6, 4):
                when_events("dD"[i == 4], h, range(4))
        for j in range(4):
            m.dq[j, rows_of(h, 1), :] = m.dkv[0:64, j * BLK:(j + 1) * BLK].astype(BF16)
            m.dq[j, rows_of(h, 2), :] = m.dkv[64:128, j * BLK:(j + 1) * BLK].astype(BF16)
        x_start(h)
        when_events("e", h, range(4))
        q_grad(h)
        when_events("q", h, range(4))
        return 0

    lax.fori_loop(0, 4, bwd_head, 0)

    sent(m.xst, ixq[0])
    got(m.xst, ixq[1])
    wgst = m.dys

    def e1(t, _):
        rows = pl.ds(al(t * 256, 256), 256)
        xv = m.xs[rows, :].astype(F32)
        xc = xv - rowmean(xv)
        r = lax.rsqrt(rowmean(xc * xc) + EPS)
        nv = xc * r
        dav = dg(m.dqt[:, rows], m.wt[...], 0, 0)
        m.gg[0:1, :] += colsum(dav * nv)
        m.gg[1:2, :] += colsum(dav)
        gr = dav * g1
        dn = r * (gr - rowmean(gr) - nv * rowmean(gr * nv))
        wgst[rows, :] = (dmid[rows, :].astype(F32) + dn).astype(BF16)
        swap_go(wgst, wg_out, iw, t, 128)
        when_events("w", t, range(4))
        return 0

    lax.fori_loop(0, 4, e1, 0)
    for s in range(4):
        for k in range(5):
            m.gv[s, k:k + 1, :] = m.gg[k:k + 1, s * 128:(s + 1) * 128]
        for f in range(4):
            m.gv[s, 5 + f:6 + f, :] = m.gbu[f, 0:1, s * 128:(s + 1) * 128]
    ivx, ivy, iva = pair(), pair(), pair()
    vx = [remote(m.gv.at[2 * q + oc], m.gvr.at[q], sib, *ivx) for q in range(2)]
    vy = remote(m.gv.at[other], m.gvy, yn, *ivy)
    va = [remote(m.gv.at[w], m.gva.at[e], peer(d)[1], *iva) for d in range(1, ne)]
    for cp in vx:
        cp.start()
    for t in range(4, 6):
        swap_go(wgst, wg_out, iw, t, 128)
    sent(m.gvr, ivx[0])
    got(m.gvr, ivx[1])
    for q in range(2):
        m.gv[2 * q + c] = m.gv[2 * q + c] + m.gvr[q]
    vy.start()
    events("tail")
    vy.wait()
    m.gv[w] = m.gv[w] + m.gvy[...]
    m.gva[e] = m.gv[w]
    for cp in va:
        cp.start()
    for t in range(6, 8):
        swap_go(wgst, wg_out, iw, t, 128)
    sent(m.gva.at[0:ne - 1], iva[0])
    got(m.gva.at[0:ne - 1], iva[1])
    tot = m.gva[0]
    for d in range(1, ne):
        tot = tot + m.gva[d]
    vec_out[...] = tot
    for k in range(5):
        chunks[k].step(6)

    def fin(t, _):
        q4(t)
        return 0

    lax.fori_loop(0, 4, fin, 0)
    swap_wait(m.dup, iy)
    swap_wait(wgst, iw)


def layer(nz, *ops):
    sc = scratch(nz)
    names = tuple(sc)
    sd = jax.ShapeDtypeStruct
    any_ = pl.BlockSpec(memory_space=pl.ANY)
    vm = pl.BlockSpec(memory_space=pltpu.VMEM)
    return pl.pallas_call(
        functools.partial(body, nz, names),
        out_shape=(sd((1024, 512), BF16), sd((1024, 512), BF16), sd((ROWS, 128), BF16), sd((16, 128), F32)),
        in_specs=[any_] * 14,
        out_specs=(any_, any_, any_, vm),
        scratch_shapes=[sc[n] for n in names] + [pltpu.SemaphoreType.DMA((NSEND,)), pltpu.SemaphoreType.DMA((NRECV,))],
        compiler_params=pltpu.CompilerParams(collective_id=0, has_side_effects=True, vmem_limit_bytes=VLIM),
        name="layer",
    )(*ops)


def finish_body(y_h, wg_h, red_h, v, yo_h, wgo_h, gq_h, go_h, gu_h, gd_h, v1, v2, v3, v4, vu, vd,
                wg, red, wgo, yv, gq, go, gu, gd, sem):
    def cp(a, b, i):
        return pltpu.make_async_copy(a, b, sem.at[i])

    def red_in(k):
        return cp(red_h.at[pl.ds(k * 1024, 1024)], red.at[pl.ds(k * 1024, 1024)], k)

    def wg_in(k):
        return cp(wg_h.at[pl.ds(k * 256, 256)], wg.at[pl.ds(k * 256, 256)], 6 + k)

    outs = []

    def put(a, b):
        o = cp(a, b, 10 + len(outs))
        o.start()
        outs.append(o)

    def y_in(k):
        return cp(y_h.at[pl.ds(k * 512, 512)], yv.at[pl.ds(k * 512, 512)], 22 + k)

    for k in range(4):
        wg_in(k).start()
    for k in range(2):
        y_in(k).start()
    for k in range(6):
        red_in(k).start()
    for r, k in ((v1, 0), (v2, 1), (v3, 2), (v4, 3), (vd, 4)):
        r[...] = v[k:k + 1, :]
    vu[...] = v[5:9, :]
    for k in range(4):
        wg_in(k).wait()
        rows = slice(k * 256, (k + 1) * 256)
        wgo[rows, :] = wg[rows, :].astype(F32)
        put(wgo.at[rows], wgo_h.at[rows])
    for k in range(2):
        y_in(k).wait()
        put(yv.at[pl.ds(k * 512, 512)], yo_h.at[pl.ds(k * 512, 512)])
    for f in range(4):
        red_in(f).wait()
        gd[f * 128:(f + 1) * 128, :] = red[f * 1024:f * 1024 + 512, :].astype(F32).T
        put(gd.at[f * 128:(f + 1) * 128], gd_h.at[f * 128:(f + 1) * 128])
        for s in range(4):
            gu[:, s * 512 + f * 128:s * 512 + (f + 1) * 128] = red[f * 1024 + 512 + s * 128:f * 1024 + 640 + s * 128, :].astype(F32)
    put(gu, gu_h)
    red_in(4).wait()
    for b in range(4):
        go[:, b * 128:(b + 1) * 128] = red[OSTART + b * 128:OSTART + (b + 1) * 128, :].astype(F32)
    put(go, go_h)
    red_in(5).wait()
    for hp in range(2):
        for cc in range(2):
            for part in range(3):
                r = QSTART + hp * 768 + cc * 192 + part * 64
                blk = jnp.concatenate([red[r:r + 64, :], red[r + 384:r + 448, :]], axis=0).astype(F32).T
                if part == 0:
                    blk = blk * 0.125
                k = part * 512 + cc * 256 + hp * 128
                gq[:, k:k + 128] = blk
    put(gq, gq_h)
    for o in outs:
        o.wait()


def finish(y, wg, red, v):
    sd = jax.ShapeDtypeStruct
    any_ = pl.BlockSpec(memory_space=pl.ANY)
    vm = pl.BlockSpec(memory_space=pltpu.VMEM)
    one = sd((1, 128), F32)
    big = (sd((128, 1536), F32), sd((128, 512), F32), sd((128, 2048), F32), sd((512, 512), F32))
    return pl.pallas_call(
        finish_body,
        out_shape=(sd((1024, 512), BF16), sd((1024, 512), F32)) + big + (one, one, one, one, sd((4, 128), F32), one),
        in_specs=[any_] * 3 + [vm],
        out_specs=(any_,) * 6 + (vm,) * 6,
        scratch_shapes=[pltpu.VMEM((1024, 512), BF16), pltpu.VMEM((ROWS, 128), BF16), pltpu.VMEM((1024, 512), F32),
                        pltpu.VMEM((1024, 512), BF16)]
        + [pltpu.VMEM(b.shape, F32) for b in big] + [pltpu.SemaphoreType.DMA((24,))],
        compiler_params=pltpu.CompilerParams(vmem_limit_bytes=VLIM), name="finish",
    )(y, wg, red, v)


def on_chip(words, qkv_weight, out_weight, up_weight, down_weight, norm1_gain, norm1_bias, norm2_gain,
            norm2_bias, up_bias, down_bias, cotangent, seg_map, off_map):
    nz = lax.axis_size("group")
    r = lambda v: v.reshape(-1, 128)
    y, wg, red, v = layer(nz, words[0], cotangent[0], qkv_weight, out_weight, up_weight, down_weight.reshape(4, 128, 512),
                          r(norm1_gain), r(norm1_bias), r(norm2_gain), r(norm2_bias), r(down_bias), r(up_bias),
                          seg_map, off_map)
    y, wg, gq, go, gu, gd, v1, v2, v3, v4, vu, vd = finish(y, wg, red, v)
    f = lambda t: t.reshape(-1)
    return y[None], wg[None], gq, go, gu, gd, f(v1), f(v2), f(v3), f(v4), f(vu), f(vd)


HEADS = 8
HEAD_DIM = 64


eps = 1e-05
neg_big = -1e30


def passed_along(value, axis, by):
    peers = lax.axis_size(axis)
    return lax.ppermute(value, axis, [(i, (i + by) % peers) for i in range(peers)])


def layer_norm(features, norm_gain, norm_shift):
    row_mean = jnp.mean(features, axis=-1, keepdims=True)
    centred = features - row_mean
    inv_scale = lax.rsqrt(jnp.mean(centred * centred, axis=-1, keepdims=True) + eps)
    return centred * inv_scale * norm_gain + norm_shift


def gelu_tanh(features):
    return jax.nn.gelu(features, approximate=True)


def rows_of(array, block_id):
    return lax.dynamic_slice_in_dim(array, block_id * BLK, BLK, 0)


def cols_of(array, block_id):
    return lax.dynamic_slice_in_dim(array, block_id * BLK, BLK, 1)


def add_rows(array, update, block_id):
    return lax.dynamic_update_slice_in_dim(
        array, rows_of(array, block_id) + update, block_id * BLK, 0
    )


def put_rows(array, update, block_id):
    return lax.dynamic_update_slice_in_dim(array, update, block_id * BLK, 0)


def put_cols(array, update, block_id):
    return lax.dynamic_update_slice_in_dim(array, update, block_id * BLK, 1)


def block_info(seg_row, off_row, block_id):
    segment = lax.dynamic_index_in_dim(seg_row, block_id, 0, keepdims=False)
    position = lax.dynamic_index_in_dim(off_row, block_id, 0, keepdims=False)
    return (segment, position)


def pair_live(seg_row, off_row, query_block, key_block):
    query_seg, query_offset = block_info(seg_row, off_row, query_block)
    key_seg, key_offset = block_info(seg_row, off_row, key_block)
    return (query_seg == key_seg) & (key_offset <= query_offset) | (key_seg == 0) & (query_seg != 0)


def pair_mask(seg_row, off_row, query_block, key_block):
    query_seg, query_offset = block_info(seg_row, off_row, query_block)
    key_seg, key_offset = block_info(seg_row, off_row, key_block)
    row_ids = lax.broadcasted_iota(jnp.int32, (BLK, BLK), 0)
    col_ids = lax.broadcasted_iota(jnp.int32, (BLK, BLK), 1)
    query_pos = query_offset * BLK + row_ids
    key_pos = key_offset * BLK + col_ids
    return (query_seg == key_seg) & (key_pos <= query_pos) | (key_seg == 0) & (query_seg != 0)


def split_heads(tile_rows):
    return tile_rows.reshape(tile_rows.shape[0], HEADS, HEAD_DIM)


def tile_scores(query_tile, key_tile, allowed):
    raw_scores = jnp.einsum(
        "qhd,khd->hqk",
        split_heads(query_tile),
        split_heads(key_tile),
        preferred_element_type=jnp.float32,
    )
    return jnp.where(allowed[None], raw_scores * HEAD_DIM ** (-0.5), neg_big)


def tile_back(query_tile, key_tile, value_tile, grad_tile, norm_tile, delta_tile, allowed):
    scores = tile_scores(query_tile, key_tile, allowed)
    exp_terms = jnp.where(allowed[None], jnp.exp(scores - norm_tile[:, :, None]), 0.0)
    d_probs = jnp.einsum(
        "qhd,khd->hqk",
        split_heads(grad_tile),
        split_heads(value_tile),
        preferred_element_type=jnp.float32,
    )
    d_scores = (exp_terms * (d_probs - delta_tile[:, :, None])).astype(jnp.bfloat16)
    return (exp_terms.astype(jnp.bfloat16), d_scores)


def query_grad(d_scores, key_tile):
    part_rows = jnp.einsum(
        "hqk,khd->qhd", d_scores, split_heads(key_tile), preferred_element_type=jnp.float32
    )
    return part_rows.reshape(BLK, -1) * HEAD_DIM ** (-0.5)


def key_grad(d_scores, query_tile):
    part_rows = jnp.einsum(
        "hqk,qhd->khd", d_scores, split_heads(query_tile), preferred_element_type=jnp.float32
    )
    return part_rows.reshape(BLK, -1) * HEAD_DIM ** (-0.5)


def value_grad(probs_low, grad_tile):
    part_rows = jnp.einsum(
        "hqk,qhd->khd", probs_low, split_heads(grad_tile), preferred_element_type=jnp.float32
    )
    return part_rows.reshape(BLK, -1)


def unchanged(running):
    return running


def on_device(
    words,
    qkv_weight,
    out_weight,
    up_weight,
    down_weight,
    norm1_gain,
    norm1_bias,
    norm2_gain,
    norm2_bias,
    up_bias,
    down_bias,
    cotangent,
    seg_map,
    off_map,
):
    gathered = (
        lax.all_gather(qkv_weight, "wshard", axis=0, tiled=True),
        lax.all_gather(out_weight, "wshard", axis=0, tiled=True),
        lax.all_gather(up_weight, "wshard", axis=0, tiled=True),
        lax.all_gather(down_weight, "wshard", axis=0, tiled=True),
        lax.all_gather(norm1_gain, "wshard", axis=0, tiled=True),
        lax.all_gather(norm1_bias, "wshard", axis=0, tiled=True),
        lax.all_gather(norm2_gain, "wshard", axis=0, tiled=True),
        lax.all_gather(norm2_bias, "wshard", axis=0, tiled=True),
        lax.all_gather(up_bias, "wshard", axis=0, tiled=True),
        lax.all_gather(down_bias, "wshard", axis=0, tiled=True),
    )
    w_qkv, w_out, w_up, w_down = (gathered[0], gathered[1], gathered[2], gathered[3])
    gain1 = gathered[4].astype(jnp.float32)
    shift1 = gathered[5].astype(jnp.float32)
    gain2 = gathered[6].astype(jnp.float32)
    shift2 = gathered[7].astype(jnp.float32)
    bias_up = gathered[8].astype(jnp.float32)
    bias_down = gathered[9].astype(jnp.float32)
    seg_row = seg_map[0]
    off_row = off_map[0]
    cycle_place = lax.axis_index("ctx")
    cycle_count = lax.axis_size("ctx")
    inputs = words[0].astype(jnp.float32)
    local_rows = inputs.shape[0]
    local_blocks = local_rows // BLK
    first_block = cycle_place * local_blocks
    width = inputs.shape[1]
    normed1, pull_norm1 = jax.vjp(layer_norm, inputs, gain1, shift1)
    act1 = normed1.astype(jnp.bfloat16)
    qkv = jnp.dot(act1, w_qkv, preferred_element_type=jnp.float32)
    query_rows = qkv[:, :width].astype(jnp.bfloat16)
    key_rows = qkv[:, width : 2 * width].astype(jnp.bfloat16)
    value_rows = qkv[:, 2 * width :].astype(jnp.bfloat16)
    start_state = (
        jnp.full((HEADS, local_rows), neg_big, jnp.float32),
        jnp.zeros((HEADS, local_rows), jnp.float32),
        jnp.zeros((local_rows, width), jnp.float32),
    )
    shard_keys = lax.all_gather(key_rows, "ctx", axis=0, tiled=True)
    shard_values = lax.all_gather(value_rows, "ctx", axis=0, tiled=True)
    key_blocks = shard_keys.shape[0] // BLK

    def online_visit_pair(pair_index, state):
        row_block = pair_index // key_blocks
        col_block = pair_index % key_blocks
        query_block = first_block + row_block
        key_block = col_block

        def online_update_tile(state):
            run_max, run_sum, accum = state
            allowed = pair_mask(seg_row, off_row, query_block, key_block)
            scores = tile_scores(
                rows_of(query_rows, row_block), rows_of(shard_keys, col_block), allowed
            )
            old_max = cols_of(run_max, row_block)
            old_sum = cols_of(run_sum, row_block)
            new_max = jnp.maximum(old_max, jnp.max(scores, axis=-1))
            exp_terms = jnp.where(allowed[None], jnp.exp(scores - new_max[:, :, None]), 0.0)
            factor = jnp.exp(old_max - new_max)
            new_sum = old_sum * factor + jnp.sum(exp_terms, axis=-1)
            part_rows = jnp.einsum(
                "hqk,khd->qhd",
                exp_terms.astype(jnp.bfloat16),
                split_heads(rows_of(shard_values, col_block)),
                preferred_element_type=jnp.float32,
            )
            old_rows = rows_of(accum, row_block).reshape(BLK, HEADS, HEAD_DIM)
            new_rows = (old_rows * factor.T[:, :, None] + part_rows).reshape(BLK, -1)
            return (
                put_cols(run_max, new_max, row_block),
                put_cols(run_sum, new_sum, row_block),
                put_rows(accum, new_rows, row_block),
            )

        return lax.cond(
            pair_live(seg_row, off_row, query_block, key_block),
            online_update_tile,
            unchanged,
            state,
        )

    run_max, run_sum, accum = lax.fori_loop(
        0, local_blocks * key_blocks, online_visit_pair, start_state
    )
    log_norm = run_max + jnp.log(run_sum)
    attended = (accum.reshape(local_rows, HEADS, HEAD_DIM) / run_sum.T[:, :, None]).reshape(
        local_rows, width
    )
    attended_low = attended.astype(jnp.bfloat16)
    middle = inputs + jnp.dot(attended_low, w_out, preferred_element_type=jnp.float32)
    normed2, pull_norm2 = jax.vjp(layer_norm, middle, gain2, shift2)
    act2 = normed2.astype(jnp.bfloat16)
    hidden = jnp.dot(act2, w_up, preferred_element_type=jnp.float32) + bias_up
    gelu_out, pull_gelu = jax.vjp(gelu_tanh, hidden)
    gelu_low = gelu_out.astype(jnp.bfloat16)
    output = (
        middle + jnp.dot(gelu_low, w_down, preferred_element_type=jnp.float32) + bias_down
    ).astype(jnp.bfloat16)
    upstream = cotangent[0]
    upstream_f = upstream.astype(jnp.float32)
    grad_down = jnp.einsum("nf,nd->fd", gelu_low, upstream, preferred_element_type=jnp.float32)
    grad_bias_down = jnp.sum(upstream_f, axis=0)
    d_gelu = jnp.einsum("nd,fd->nf", upstream, w_down, preferred_element_type=jnp.float32)
    d_hidden = pull_gelu(d_gelu)[0].astype(jnp.bfloat16)
    grad_up = jnp.einsum("nd,nf->df", act2, d_hidden, preferred_element_type=jnp.float32)
    grad_bias_up = jnp.sum(d_hidden.astype(jnp.float32), axis=0)
    d_act2 = jnp.einsum("nf,df->nd", d_hidden, w_up, preferred_element_type=jnp.float32)
    d_middle_norm, grad_gain2, grad_shift2 = pull_norm2(d_act2)
    d_middle = (upstream_f + d_middle_norm).astype(jnp.bfloat16)
    grad_out = jnp.einsum("nd,ne->de", attended_low, d_middle, preferred_element_type=jnp.float32)
    d_attended = jnp.einsum(
        "ne,de->nd", d_middle, w_out, preferred_element_type=jnp.float32
    ).astype(jnp.bfloat16)
    row_delta = jnp.sum(
        (d_attended.astype(jnp.float32) * attended).reshape(local_rows, HEADS, HEAD_DIM), axis=-1
    ).T
    zero_rows = jnp.zeros((local_rows, width), jnp.float32)

    def attend_back(cycle_turn, cycle_state):
        held_keys, held_values, held_dk, held_dv, d_query = cycle_state
        source = (cycle_place - cycle_turn) % cycle_count

        def attend_visit_pair(pair_index, partial_value):
            row_block = pair_index // local_blocks
            col_block = pair_index % local_blocks
            query_block = first_block + row_block
            key_block = source * local_blocks + col_block

            def attend_update_tile(partial_value):
                dk_acc, dv_acc, dq_acc = partial_value
                query_tile = rows_of(query_rows, row_block)
                key_tile = rows_of(held_keys, col_block)
                grad_tile = rows_of(d_attended, row_block)
                allowed = pair_mask(seg_row, off_row, query_block, key_block)
                probs_low, d_scores = tile_back(
                    query_tile,
                    key_tile,
                    rows_of(held_values, col_block),
                    grad_tile,
                    cols_of(log_norm, row_block),
                    cols_of(row_delta, row_block),
                    allowed,
                )
                dq_acc = add_rows(dq_acc, query_grad(d_scores, key_tile), row_block)
                dk_acc = add_rows(dk_acc, key_grad(d_scores, query_tile), col_block)
                dv_acc = add_rows(dv_acc, value_grad(probs_low, grad_tile), col_block)
                return (dk_acc, dv_acc, dq_acc)

            return lax.cond(
                pair_live(seg_row, off_row, query_block, key_block),
                attend_update_tile,
                unchanged,
                partial_value,
            )

        held_dk, held_dv, d_query = lax.fori_loop(
            0, local_blocks * local_blocks, attend_visit_pair, (held_dk, held_dv, d_query)
        )
        return (held_keys, held_values, held_dk, held_dv, d_query)

    def pass_grads(held_dk, held_dv):
        return (
            passed_along(held_dk.astype(jnp.bfloat16), "ctx", 1).astype(held_dk.dtype),
            passed_along(held_dv.astype(jnp.bfloat16), "ctx", 1).astype(held_dv.dtype),
        )

    def turn_step(cycle_turn, cycle_state):
        held_keys, held_values, held_dk, held_dv, d_query = attend_back(cycle_turn, cycle_state)
        held_keys, held_values = passed_along((held_keys, held_values), "ctx", 1)
        held_dk, held_dv = pass_grads(held_dk, held_dv)
        return (held_keys, held_values, held_dk, held_dv, d_query)

    cycle_state = lax.fori_loop(
        0, cycle_count - 1, turn_step, (key_rows, value_rows, zero_rows, zero_rows, zero_rows)
    )
    cycle_state = attend_back(cycle_count - 1, cycle_state)
    d_keys, d_values = pass_grads(cycle_state[2], cycle_state[3])
    d_query = cycle_state[4]
    d_qkv = jnp.concatenate(
        [d_query.astype(jnp.bfloat16), d_keys.astype(jnp.bfloat16), d_values.astype(jnp.bfloat16)],
        axis=1,
    )
    grad_qkv = jnp.einsum("nd,nf->df", act1, d_qkv, preferred_element_type=jnp.float32)
    d_act1 = jnp.einsum("nf,df->nd", d_qkv, w_qkv, preferred_element_type=jnp.float32)
    d_inputs_norm, grad_gain1, grad_shift1 = pull_norm1(d_act1)
    words_grad = d_middle.astype(jnp.float32) + d_inputs_norm
    shards = (
        lax.psum_scatter(
            grad_qkv.astype(jnp.bfloat16), "wshard", scatter_dimension=0, tiled=True
        ).astype(jnp.float32),
        lax.psum_scatter(
            grad_out.astype(jnp.bfloat16), "wshard", scatter_dimension=0, tiled=True
        ).astype(jnp.float32),
        lax.psum_scatter(
            grad_up.astype(jnp.bfloat16), "wshard", scatter_dimension=0, tiled=True
        ).astype(jnp.float32),
        lax.psum_scatter(
            grad_down.astype(jnp.bfloat16), "wshard", scatter_dimension=0, tiled=True
        ).astype(jnp.float32),
        lax.psum_scatter(
            grad_gain1.astype(jnp.bfloat16), "wshard", scatter_dimension=0, tiled=True
        ).astype(jnp.float32),
        lax.psum_scatter(
            grad_shift1.astype(jnp.bfloat16), "wshard", scatter_dimension=0, tiled=True
        ).astype(jnp.float32),
        lax.psum_scatter(
            grad_gain2.astype(jnp.bfloat16), "wshard", scatter_dimension=0, tiled=True
        ).astype(jnp.float32),
        lax.psum_scatter(
            grad_shift2.astype(jnp.bfloat16), "wshard", scatter_dimension=0, tiled=True
        ).astype(jnp.float32),
        lax.psum_scatter(
            grad_bias_up.astype(jnp.bfloat16), "wshard", scatter_dimension=0, tiled=True
        ).astype(jnp.float32),
        lax.psum_scatter(
            grad_bias_down.astype(jnp.bfloat16), "wshard", scatter_dimension=0, tiled=True
        ).astype(jnp.float32),
    )
    totals = lax.psum(
        (
            shards[0],
            shards[1],
            shards[2],
            shards[3],
            shards[4],
            shards[5],
            shards[6],
            shards[7],
            shards[8],
            shards[9],
        ),
        ("group", "ctx"),
    )
    return (
        output[None],
        words_grad[None],
        totals[0],
        totals[1],
        totals[2],
        totals[3],
        totals[4],
        totals[5],
        totals[6],
        totals[7],
        totals[8],
        totals[9],
    )


def solution(mesh):
    chip = mesh.shape["ctx"] == 2 and mesh.shape["wshard"] == 4 and mesh.shape["group"] in (2, 4)
    return jax.shard_map(
        on_chip if chip else on_device,
        mesh=mesh,
        in_specs=(
            P(("group", "wshard"), "ctx", None),
            P("wshard", None),
            P("wshard", None),
            P("wshard", None),
            P("wshard", None),
            P("wshard"),
            P("wshard"),
            P("wshard"),
            P("wshard"),
            P("wshard"),
            P("wshard"),
            P(("group", "wshard"), "ctx", None),
            P(("group", "wshard"), None),
            P(("group", "wshard"), None),
        ),
        out_specs=(
            P(("group", "wshard"), "ctx", None),
            P(("group", "wshard"), "ctx", None),
            P("wshard", None),
            P("wshard", None),
            P("wshard", None),
            P("wshard", None),
            P("wshard"),
            P("wshard"),
            P("wshard"),
            P("wshard"),
            P("wshard"),
            P("wshard"),
        ),
        check_vma=False,
    )
```

```python
import functools
import jax
import jax.numpy as jnp
from jax import lax
from jax.experimental import pallas as pl
from jax.experimental.pallas import tpu as pltpu
from jax.sharding import PartitionSpec as P

BLK = 512
HD = 64
EPS = 1e-5
F32 = jnp.float32
BF16 = jnp.bfloat16
K0 = 0.7978845608
K1 = 0.044715
MESH = pl.DeviceIdType.MESH
VLIM = 63 * 1024 * 1024
FROWS, OROWS, QROWS = 1024, 512, 384
OSTART, QSTART, ROWS = 4096, 4608, 6144
NSEND, NRECV = 64, 96
CHUNKS = (("F0", FROWS, "xyz"), ("F1", FROWS, "yxz"), ("F2", FROWS, "xyz"), ("F3", FROWS, "yxz"), ("O", OROWS, "yxz"))


PLAN = {
    ("g", 0): ((0, 0),),
    ("f", 1): ((0, 1),),
    ("g", 1): ((1, 0),),
    ("f", 2): ((1, 1),),
    ("g", 2): ((2, 0),),
    ("f", 3): ((0, 2), (2, 1),),
    ("g", 3): ((3, 0),),
    ("c", 0): ((1, 2), (3, 1), (9, 0),),
    ("c", 1): ((0, 3), (9, 1),),
    "go": ((4, 0), (9, 2),),
    ("d", 0): ((2, 2), (4, 1), (1, 3), (0, 4), (9, 3),),
    ("D", 0): ((3, 2), (9, 4),),
    ("e", 0): ((9, 5),),
    ("q", 0): ((5, 0), (2, 3), (1, 4),),
    ("d", 1): ((5, 1), (4, 2), (0, 5), (9, 6),),
    ("D", 1): ((3, 3), (9, 7),),
    ("e", 1): ((2, 4),),
    ("q", 1): ((6, 0), (5, 2), (4, 3), (1, 5),),
    ("d", 2): ((6, 1), (3, 4),),
    ("e", 2): ((2, 5),),
    ("q", 2): ((7, 0), (6, 2), (5, 3),),
    ("d", 3): ((4, 4), (7, 1),),
    ("D", 3): ((3, 5),),
    ("e", 3): ((6, 3),),
    ("q", 3): ((8, 0), (7, 2),),
    "x": ((4, 5), (8, 1),),
    ("w", 1): ((8, 2),),
    ("w", 2): ((7, 3),),
    "tail": ((8, 3),),
}


def dg(a, b, ca, cb):
    return lax.dot_general(a, b, (((ca,), (cb,)), ((), ())), preferred_element_type=F32)


def colsum(v):
    return jnp.sum(v, axis=0, keepdims=True)


def rowmean(v):
    return jnp.mean(v, axis=-1, keepdims=True)


def key_le_query(n, key_axis):
    k = lax.broadcasted_iota(jnp.int32, (n, n), key_axis)
    q = lax.broadcasted_iota(jnp.int32, (n, n), 1 - key_axis)
    return k <= q


def al(v, n):
    return pl.multiple_of(v, n)


def chunk_scratch(nz, rows, kind):
    V = lambda *s: pltpu.VMEM(s, BF16)
    held = rows if kind == "yz" else rows // 2
    return dict(A=V(2, rows, 128), B=V(held if kind == "xyz" else rows, 128),
                X=V(held // nz, 128) if kind == "yz" else V(2 if kind == "xyz" else 1, held, 128),
                Z=V(nz - 1, held // nz, 128), T=V(held // nz, 128), H=V(held, 128))


def scratch(nz):
    ne = 2 * nz
    V = lambda *s, t=BF16: pltpu.VMEM(s, t)
    return dict(
        xs=V(1024, 512), dys=V(1024, 512), wqr=V(128, 1536), wur=V(128, 2048), wt=V(1536, 512), wo=V(512, 512),
        wu=V(4, 512, 512), wd=V(4, 512, 512), vown=V(16, 128, t=F32), vec=V(4, 16, 128, t=F32),
        so=V(2, 8, 128, t=jnp.int32), sseg=V(1, 4, t=jnp.int32), soff=V(1, 4, t=jnp.int32),
        s1g=V(1, 128), s1b=V(1, 128), s2g=V(1, 128), s2b=V(1, 128), sbd=V(1, 128), sbu=V(4, 128), sm=pltpu.SMEM((8, 128), jnp.int32),
        a1=V(4, 512, 512), qkv=V(4, 768, 512), o=V(4, 256, 512, t=F32), lse=V(4, 8, 512, t=F32),
        ost=V(2, 256, 512), ot=V(2, 512, 512), n2=V(1024, 512, t=F32), rs=V(1024, 128, t=F32), a2=V(1024, 512),
        a2t=V(512, 1024), dyt=V(512, 1024), ya=V(1024, 512, t=F32), da=V(1024, 512, t=F32),
        act=V(1024, 512), dup=V(1024, 512), do=V(4, 256, 512), dst=V(2, 256, 512), dq=V(4, 768, 512),
        dkv=V(128, 2048, t=F32), xst=V(4, 2, 192, 512), dqt=V(1536, 1024),
        gv=V(4, 16, 128, t=F32), gvr=V(2, 16, 128, t=F32), gvy=V(16, 128, t=F32), gva=V(ne, 16, 128, t=F32),
        gg=V(8, 512, t=F32), gbu=V(4, 8, 512, t=F32),
        FG=V(4, 4, FROWS, 128), OG=V(4, OROWS, 128),
        **{f"{t}{q}": v for t, rows, kind in CHUNKS for q, v in chunk_scratch(nz, rows, kind).items()},
        QS=V(4, 4, 192, 128), QG=V(4, 2, QROWS, 128), QB=V(4, QROWS, 128), QC=V(4, ne - 1, QROWS // ne, 128),
        QT=V(4, QROWS // ne, 128),
    )


class Count:
    def __init__(self, most):
        self.n, self.most = 0, most

    def take(self, k=1):
        self.n += k
        assert self.n <= self.most
        return self.n - k


class Ns:
    def __init__(self, d):
        self.__dict__.update(d)


def body(nz, names, *args):
    (words_h, cot_h, wq_h, wo_h, wu_h, wd_h, n1g, n1b, n2g, n2b, bdr, bur, seg_r, off_r) = args[:14]
    y_out, wg_out, red_out, vec_out = args[14:18]
    m = Ns(dict(zip(names, args[18:18 + len(names)])))
    send, recv = args[18 + len(names):]
    cs, cr = Count(NSEND), Count(NRECV)
    ne = 2 * nz
    g, x, w = lax.axis_index("group"), lax.axis_index("ctx"), lax.axis_index("wshard")
    yi, c = w // 2, w % 2
    oc, oy, ox = 1 - c, 1 - yi, 1 - x
    e = x * nz + g
    sib = (g, x, 2 * yi + oc)
    yn = (g, x, 2 * oy + c)
    diag = (g, x, 2 * oy + oc)
    xn = (g, ox, w)
    zp = (g + 1 - 2 * (g % 2), x, w)
    sw = (g, c, 2 * yi + x)
    stay = x == c
    moves = jnp.logical_not(stay)

    def peer(d):
        q = (e + d) % ne
        return q, (q % nz, q // nz, w)

    def zpeer(d):
        q = (g + d) % nz
        return q, (q, x, w)

    def remote(src, dst_, dev, i, j):
        return pltpu.make_async_remote_copy(src_ref=src, dst_ref=dst_, send_sem=send.at[i], recv_sem=recv.at[j],
                                            device_id=dev, device_id_type=MESH)

    def local(src, dst_, i):
        return pltpu.make_async_copy(src, dst_, send.at[i])

    def sent(ref, i):
        pltpu.make_async_copy(ref, ref, send.at[i]).wait()

    def got(ref, j):
        pltpu.make_async_copy(ref, ref, recv.at[j]).wait()

    def begin(src, dst_):
        cp = local(src, dst_, cs.take())
        cp.start()
        return cp

    bar = pltpu.get_barrier_semaphore()
    peers = [sib, yn, diag] + [peer(d)[1] for d in range(1, ne)]
    for p in peers:
        pl.semaphore_signal(bar, inc=1, device_id=p, device_id_type=MESH)

    @pl.when(moves)
    def _():
        pl.semaphore_signal(bar, inc=1, device_id=sw, device_id_type=MESH)

    l_wq = begin(wq_h, m.wqr)
    l_small = [begin(a, b) for a, b in zip((n1g, n1b, n2g, n2b, bdr, bur, seg_r, off_r),
                                           (m.s1g, m.s1b, m.s2g, m.s2b, m.sbd, m.sbu, m.sseg, m.soff))]
    l_wo = begin(wo_h, m.wo.at[pl.ds(al(w * 128, 128), 128), :])
    l_wu = begin(wu_h, m.wur)
    l_wd = begin(wd_h, m.wd.at[:, pl.ds(al(w * 128, 128), 128), :])
    m.vown[...] = jnp.zeros_like(m.vown)
    m.so[0] = jnp.zeros((8, 128), jnp.int32)
    m.gg[...] = jnp.zeros_like(m.gg)
    m.gbu[...] = jnp.zeros_like(m.gbu)
    m.gv[...] = jnp.zeros_like(m.gv)
    pl.semaphore_wait(bar, len(peers) + jnp.where(stay, 0, 1))

    def swap_go(src, dst_, ij, t, n, k=0):
        rows = pl.ds(al(t * n, n), n)

        @pl.when(stay)
        def _():
            local(src.at[rows], dst_.at[rows], ij[0] + k).start()

        @pl.when(moves)
        def _():
            remote(src.at[rows], dst_.at[rows], sw, ij[0] + k, ij[1] + k).start()

    def swap_wait(ref, ij, k=0):
        sent(ref, ij[0] + k)

        @pl.when(moves)
        def _():
            got(ref, ij[1] + k)

    def pair(k=1):
        return cs.take(k), cr.take(k)

    ix, idy, iy, iw = pair(4), pair(), pair(), pair()
    for t in range(4):
        swap_go(words_h, m.xs, ix, t, 256, t)
    for cp in l_small:
        cp.wait()
    for k, r in enumerate((m.s1g, m.s1b, m.s2g, m.s2b, m.sbd)):
        m.vown[k:k + 1, :] = r[...].astype(F32)
    m.vown[5:9, :] = m.sbu[...].astype(F32)
    m.so[0, 0:1, 0:4] = m.sseg[...] * 2 + m.soff[...]
    so_x = remote(m.so.at[0], m.so.at[1], sib, *pair())
    ivc = pair()
    vcs = [remote(m.vown, m.vec.at[w], p, *ivc) for p in (sib, yn, diag)]
    m.vec[w] = m.vown[...]

    mine = pl.ds(al(w * 128, 128), 128)
    l_wq.wait()
    for cc in range(2):
        for hp in range(2):
            for part in range(3):
                b = (part * 4 + cc * 2 + hp) * 128
                blk = m.wqr[:, b:b + 128].T
                if part == 0:
                    blk = (blk.astype(F32) * 0.125).astype(BF16)
                r = cc * 768 + hp * 384 + part * 64
                m.wt[r:r + 64, mine] = blk[:64]
                m.wt[r + 192:r + 256, mine] = blk[64:]

    other = 2 * oy + c

    def shard(n, s, f):
        v = pl.ds(al(s * 128, 128), 128)
        if n == "wt":
            return m.wt.at[:, v]
        if n == "wo":
            return m.wo.at[v, :]
        return (m.wu if n == "wu" else m.wd).at[f, v, :]

    pieces = [("wt", 0), ("wo", 0)] + [(n, f) for f in range(4) for n in ("wu", "wd")]
    big2 = m.wu.at[0:2, 0:128, :]
    big8 = m.wu.at[:, 0:256, :]
    ig = dict(wt=(pair(3)), wo=(pair(3)))
    isib, iys, ifs = pair(), cs.take(), cs.take()
    iyr, ifr = cr.take(4), cr.take(4)

    def g_sems(p, k):
        n, f = p
        if n in ig:
            return ig[n][0] + k, ig[n][1] + k
        return (isib, (iys, iyr + f), (ifs, ifr + f))[k]

    def g_sib(p):
        return remote(shard(p[0], w, p[1]), shard(p[0], w, p[1]), sib, *g_sems(p, 0))

    def g_y(p):
        return remote(shard(p[0], w, p[1]), shard(p[0], w, p[1]), yn, *g_sems(p, 1))

    def g_fwd(p):
        return remote(shard(p[0], other, p[1]), shard(p[0], other, p[1]), sib, *g_sems(p, 2))

    def g_forward(*ps):
        for p in ps:
            if p[0] in ig:
                g_y(p).wait_recv()
            elif p[0] == "wu":
                got(big2, iyr + p[1])
            g_fwd(p).start()

    g_y(("wt", 0)).start()
    g_sib(("wt", 0)).start()
    for v in vcs:
        v.start()
    so_x.start()
    l_wu.wait()
    for f in range(4):
        for s in range(4):
            m.wu[f, mine, s * 128:(s + 1) * 128] = m.wur[:, s * 512 + f * 128:s * 512 + (f + 1) * 128]
    l_wo.wait()
    l_wd.wait()
    for p in pieces[1:]:
        g_y(p).start()
    for p in pieces[1:]:
        g_sib(p).start()
    sent(m.vec.at[0:3], ivc[0])
    got(m.vec.at[0:3], ivc[1])
    so_x.wait()
    m.so[0] = jnp.where(stay, m.so[0], m.so[1])
    so_s = local(m.so.at[0], m.sm, cs.take())
    so_s.start()

    def row(k):
        return jnp.concatenate([m.vec[s, k:k + 1, :] for s in range(4)], axis=1)

    g1, b1 = row(0), row(1)

    ia = pair(4)

    def a_slot(core, t):
        return m.a1.at[2 * core + t // 2, pl.ds(al((t % 2) * 256, 256), 256), :]

    def a_piece(t):
        return remote(a_slot(c, t), a_slot(c, t), sib, ia[0] + t, ia[1] + t)

    def norm1(t, _=0):
        rows = pl.ds(al(t * 256, 256), 256)
        swap_wait(m.xs.at[rows], ix, t)
        xv = m.xs[rows, :].astype(F32)
        xc = xv - rowmean(xv)
        r = lax.rsqrt(rowmean(xc * xc) + EPS)
        a_slot(c, t)[...] = (xc * r * g1 + b1).astype(BF16)
        a_piece(t).start()
        return 0

    wrows = pl.ds(al(c * 768, 256), 768)

    near, far = pl.ds(al(yi * 256, 256), 256), pl.ds(al(oy * 256, 256), 256)
    part_of = (m.ya, m.da)

    def words_of(t, feats):
        half = pl.ds(al((t % 2) * 256, 256), 256)
        return jnp.concatenate([m.a1[t // 2, half, feats], m.a1[2 + t // 2, half, feats]], axis=0)

    def project(t, part=None):
        cols = pl.ds(al((t % 2) * 256, 256), 256)
        res = dg(m.wt[wrows, far], words_of(t, far), 1, 1)
        res = res + (dg(m.wt[wrows, near], words_of(t, near), 1, 1) if part is None else part[0:768, :])
        res = res.astype(BF16)
        m.qkv[t // 2, :, cols] = res[:, :256]
        m.qkv[2 + t // 2, :, cols] = res[:, 256:]

    norm1(0)
    g_sib(("wt", 0)).wait()
    for t in range(2):
        norm1(t + 1)
        a_piece(t).wait()
        part_of[t][0:768, :] = dg(m.wt[wrows, near], words_of(t, near), 1, 1)
    g_forward(("wt", 0))
    g_fwd(("wt", 0)).wait()
    project(0, m.ya)
    project(1, m.da)
    norm1(3)
    for t in range(2, 4):
        a_piece(t).wait()
        project(t)
    for t in range(4):
        swap_go(cot_h, m.dys, idy, t, 256)
    so_s.wait()
    canon = [m.sm[0, b] for b in range(4)]
    phys = [jnp.minimum(sum(jnp.where(canon[b] == k, b, 0) for b in range(1, 4)), 3) for k in range(4)]

    def canon_of(p):
        return jnp.clip(m.sm[0, p], 0, 3)

    def rows_of(h, part):
        return pl.ds(al(h * 192 + part * 64, 64), 64)

    def fwd_head(h, _):
        kn = [m.qkv[phys[j], rows_of(h, 1), :].T for j in range(4)]
        q = jnp.concatenate([m.qkv[phys[j], rows_of(h, 0), :] for j in range(4)], axis=1)
        tri = key_le_query(BLK, 0)
        s = []
        for j in range(4):
            sj = dg(kn[j], q[:, j * BLK:], 1, 0)
            sd = jnp.where(tri, sj[:, :BLK], -1e30)
            s.append(sd if j == 3 else jnp.concatenate([sd, sj[:, BLK:]], axis=1))
        mx = [jnp.max(sj, axis=0, keepdims=True) for sj in s]
        top = mx[0]
        for j in range(1, 4):
            top = jnp.concatenate([top[:, :j * BLK], jnp.maximum(top[:, j * BLK:], mx[j])], axis=1)
        acc = tot = None
        for j in range(4):
            p = jnp.exp(s[j] - top[:, j * BLK:])
            lj = colsum(p)
            a = dg(m.qkv[phys[j], rows_of(h, 2), :], p.astype(BF16), 1, 0)
            acc = a if acc is None else jnp.concatenate([acc[:, :j * BLK], acc[:, j * BLK:] + a], axis=1)
            tot = lj if tot is None else jnp.concatenate([tot[:, :j * BLK], tot[:, j * BLK:] + lj], axis=1)
        ov = acc * (1.0 / tot)
        ls = top + jnp.log(tot)
        for i in range(4):
            m.o[i, pl.ds(al(h * HD, HD), HD), :] = ov[:, i * BLK:(i + 1) * BLK]
            m.lse[i, pl.ds(h, 1), :] = ls[:, i * BLK:(i + 1) * BLK]

        @pl.when(h == 0)
        def _():
            g_forward(*pieces[1:4])

        @pl.when(h == 2)
        def _():
            g_forward(*pieces[4:6])

        @pl.when(h == 3)
        def _():
            g_forward(*pieces[6:8])
        return 0

    lax.fori_loop(0, 4, fwd_head, 0)
    iox = pair()
    for b in range(2):
        m.ost[b] = m.o[canon_of(2 * oc + b)].astype(BF16)
        remote(m.ost.at[b], m.ot.at[b, pl.ds(al(c * 256, 256), 256), :], sib, *iox).start()
    for b in range(2):
        m.ot[b, pl.ds(al(c * 256, 256), 256), :] = m.o[canon_of(2 * c + b)].astype(BF16)
    g_fwd(("wo", 0)).wait()
    g_sib(("wo", 0)).wait()
    sent(m.ost, iox[0])
    got(m.ost, iox[1])

    class Chunk:
        def __init__(self, k):
            tag, self.rows, self.kind = CHUNKS[k]
            self.G = m.FG.at[k] if k < 4 else m.OG
            for q in "ABXZTH":
                setattr(self, q, getattr(m, tag + q))
            self.start = k * FROWS
            self.held = self.rows if self.kind == "yz" else self.rows // 2
            self.p = self.held // nz
            self.lo = 0 if self.kind == "yz" else x * self.held
            self.slots = (w, other) if self.kind == "xyz" else (w,)
            self.i, self.keeping = cs.take(), cs.take()
            self.j = cr.take(6)

        def r(self, off, n):
            return pl.ds(al(off, 16), n)

        def core(self, q):
            return remote(self.G.at[2 * q + oc], self.A.at[q], sib, self.i, self.j)

        def y(self):
            if self.kind == "xyz":
                return remote(self.G.at[other, self.r(self.lo, self.held), :], self.B, yn, self.i, self.j + 1)
            return remote(self.G.at[other], self.B, yn, self.i, self.j + 1)

        def xs(self):
            if self.kind == "yz":
                return [remote(self.T, self.X, xn, self.i, self.j + 2)]
            return [remote(self.G.at[v, self.r(ox * self.held, self.held), :], self.X.at[n], xn, self.i, self.j + 2)
                    for n, v in enumerate(self.slots)]

        def z(self, d):
            q, dev = zpeer(d)
            return remote(self.G.at[w, self.r(self.lo + q * self.p, self.p), :], self.Z.at[nz - 1 - d], dev,
                          self.i, self.j + 3)

        def back(self, d):
            return remote(self.T, self.H.at[self.r(g * self.p, self.p), :], zpeer(d)[1], self.i, self.j + 4)

        def at(self):
            return red_out.at[self.r(self.start + self.lo, self.held), :]

        def xback(self):
            return remote(self.H, self.at(), xn, self.i, self.j + 5)

        def keep(self):
            return local(self.H, self.at(), self.keeping)

        def add(self, slot, rows, v):
            self.G[slot, rows, :] = (self.G[slot, rows, :].astype(F32) + v.astype(F32)).astype(BF16)

        def begin(self):
            for q in range(2):
                self.core(q).start()

        def add_core(self):
            sent(self.A, self.i)
            got(self.A, self.j)
            whole = slice(0, self.rows)
            self.add(other, whole, self.A[oy])
            if self.kind != "xyz":
                self.y().start()
            self.add(w, whole, self.A[yi])
            if self.kind == "xyz":
                self.x_go()

        def x_go(self):
            for cp in self.xs():
                cp.start()

        def x_wait(self):
            sent(self.X, self.i)
            got(self.X, self.j + 2)

        def x_add(self):
            self.x_wait()
            for n, v in reversed(list(enumerate(self.slots))):
                self.add(v, self.r(self.lo, self.held), self.X[n])
                if n == 1:
                    self.y().start()

        def y_add(self):
            self.y().wait()
            if self.kind == "xyz":
                self.add(w, self.r(self.lo, self.held), self.B[...])
            else:
                self.add(w, slice(0, self.rows), self.B[...])

        def z_go(self):
            for d in range(1, nz):
                self.z(d).start()

        def z_sum(self):
            sent(self.Z, self.i)
            got(self.Z, self.j + 3)
            tot = self.G[w, self.r(self.lo + g * self.p, self.p), :].astype(F32)
            for d in range(nz - 1):
                tot = tot + self.Z[d].astype(F32)
            return tot.astype(BF16)

        def z_back(self, tot):
            self.T[...] = tot
            self.H[self.r(g * self.p, self.p), :] = tot
            for d in range(1, nz):
                self.back(d).start()

        def step(self, n):
            if n == 0:
                self.begin()
            elif n == 1:
                self.add_core()
            elif n == 2:
                if self.kind == "xyz":
                    self.x_add()
                else:
                    self.y_add()
                    self.x_go() if self.kind == "yxz" else self.z_go()
            elif n == 3:
                if self.kind == "xyz":
                    self.y_add()
                    self.z_go()
                elif self.kind == "yxz":
                    self.x_add()
                    self.z_go()
                else:
                    self.T[...] = self.z_sum()
                    self.x_go()
            elif n == 4:
                if self.kind == "yz":
                    self.x_wait()
                    self.z_back((self.T[...].astype(F32) + self.X[...].astype(F32)).astype(BF16))
                else:
                    self.z_back(self.z_sum())
            elif n == 5:
                sent(self.Z, self.i)
                got(self.Z, self.j + 4)
                if self.kind != "yz":
                    self.xback().start()
                self.keep().start()
            else:
                if self.kind != "yz":
                    self.xback().wait()
                self.keep().wait()

    qs, qk, qr, qp = cs.take(4), cs.take(4), cr.take(16), QROWS // ne

    def q_core(k, q):
        return remote(m.QS.at[k, 2 * q + oc], m.QG.at[k, q, pl.ds(al(c * 192, 64), 192), :], sib, qs + k, qr + 4 * k)

    def q_y(k):
        return remote(m.QG.at[k, oy], m.QB.at[k], yn, qs + k, qr + 4 * k + 1)

    def q_rs(k, d):
        q, dev = peer(d)
        return remote(m.QG.at[k, yi, pl.ds(al(q * qp, 16), qp), :], m.QC.at[k, ne - 1 - d], dev, qs + k, qr + 4 * k + 2)

    def q_at(k):
        return red_out.at[pl.ds(al(QSTART + k * QROWS + e * qp, 16), qp), :]

    def q_ag(k, d):
        return remote(m.QT.at[k], q_at(k), peer(d)[1], qs + k, qr + 4 * k + 3)

    def q_keep(k):
        return local(m.QT.at[k], q_at(k), qk + k)

    def q0(k):
        for q in range(2):
            q_core(k, q).start()
        for q in range(2):
            m.QG[k, q, pl.ds(al(c * 192, 64), 192), :] = m.QS[k, 2 * q + c]

    def q1(k):
        half = m.QG.at[k, :, 0:192, :]
        sent(half, qs + k)
        got(half, qr + 4 * k)
        q_y(k).start()

    def q2(k):
        q_y(k).wait()
        m.QG[k, yi] = (m.QG[k, yi].astype(F32) + m.QB[k].astype(F32)).astype(BF16)
        for d in range(1, ne):
            q_rs(k, d).start()

    def q3(k):
        sent(m.QC.at[k], qs + k)
        got(m.QC.at[k], qr + 4 * k + 2)
        tot = m.QG[k, yi, pl.ds(al(e * qp, 16), qp), :].astype(F32)
        for d in range(ne - 1):
            tot = tot + m.QC[k, d].astype(F32)
        m.QT[k] = tot.astype(BF16)
        for d in range(1, ne):
            q_ag(k, d).start()
        q_keep(k).start()

    def q4(k):
        sent(m.QC.at[k], qs + k)
        got(m.QC.at[k], qr + 4 * k + 3)
        q_keep(k).wait()

    chunks = [Chunk(k) for k in range(5)]
    chain = (q0, q1, q2, q3, q4)

    def events(key):
        for k, n in PLAN.get(key, ()):
            if k == 9:
                swap_go(m.dup, y_out, iy, n, 128)
            elif k < 5:
                chunks[k].step(n)
            else:
                chain[n](k - 5)

    def when_events(tag, v, values):
        for u in values:
            if (tag, u) in PLAN:
                @pl.when(v == u)
                def _():
                    events((tag, u))

    g2, b2, bd = row(2), row(3), row(4)

    def c1(t, _):
        rows = pl.ds(al(t * 512, 512), 512)
        mid = m.xs[rows, :].astype(F32) + dg(m.ot[t], m.wo[...], 0, 0)
        xc = mid - rowmean(mid)
        r = lax.rsqrt(rowmean(xc * xc) + EPS)
        nv = xc * r
        m.n2[rows, :] = nv
        m.rs[rows, :] = jnp.broadcast_to(r, (512, 128))
        av = (nv * g2 + b2).astype(BF16)
        m.a2[rows, :] = av
        m.a2t[:, rows] = av.T
        dyv = m.dys[rows, :]
        m.dyt[:, rows] = dyv.T
        m.gg[4:5, :] += colsum(dyv.astype(F32))
        m.ya[rows, :] = mid + bd
        m.da[rows, :] = jnp.zeros((512, 512), F32)
        return 0

    swap_wait(m.dys, idy)
    lax.fori_loop(0, 2, c1, 0)

    def c2(f, _):
        for u in range(4):
            @pl.when(f == u)
            def _():
                if u == 0:
                    sent(big8, isib[0])
                    got(big8, isib[1])
                got(big2, ifr + u)
        bu = jnp.concatenate([m.vec[s, pl.ds(5 + f, 1), :] for s in range(4)], axis=1)
        wuf, wdf = m.wu[f], m.wd[f]
        up = dg(m.a2[...], wuf, 1, 0) + bu
        u2 = up * up
        th = jnp.tanh(up * (K0 + (K0 * K1) * u2))
        hp = 0.5 + 0.5 * th
        av = (up * hp).astype(BF16)
        m.act[...] = av
        m.ya[...] += dg(av, wdf, 1, 0)
        dact = dg(m.dys[...], wdf, 1, 1)
        gp = hp + (0.5 * up) * (1.0 - th * th) * (K0 + (3 * K0 * K1) * u2)
        dv = (dact * gp).astype(BF16)
        m.dup[...] = dv
        m.gbu[f, 0:1, :] = colsum(dv.astype(F32))
        m.da[...] += dg(dv, wuf, 1, 1)

        @pl.when(f == 0)
        def _():
            g_forward(*pieces[8:])

        when_events("f", f, range(4))
        gd = dg(m.dyt[...], m.act[...], 1, 0).astype(BF16)
        for s in range(4):
            m.FG[f, s, 0:512, :] = gd[:, s * 128:(s + 1) * 128]
        gu = dg(m.a2t[...], m.dup[...], 1, 0).astype(BF16)
        for s in range(4):
            for b in range(4):
                m.FG[f, s, 512 + b * 128:640 + b * 128, :] = gu[s * 128:(s + 1) * 128, b * 128:(b + 1) * 128]
        when_events("g", f, range(4))
        return 0

    lax.fori_loop(0, 4, c2, 0)
    for p in pieces[:2]:
        g_y(p).wait_send()
    sent(big8, iys)
    sent(big8, ifs)
    yst, dmid = m.dup, m.act
    idx = pair()

    def d_piece(t):
        return remote(m.dst.at[t], m.do.at[2 * c + t], sib, *idx)

    def c3(t, _):
        rows = pl.ds(al(t * 512, 512), 512)
        yst[rows, :] = m.ya[rows, :].astype(BF16)
        dav, nv, r = m.da[rows, :], m.n2[rows, :], m.rs[rows, 0:1]
        m.gg[2:3, :] += colsum(dav * nv)
        m.gg[3:4, :] += colsum(dav)
        gr = dav * g2
        dn = r * (gr - rowmean(gr) - nv * rowmean(gr * nv))
        dm = (m.dys[rows, :].astype(F32) + dn).astype(BF16)
        dmid[rows, :] = dm
        m.dst[t] = dg(m.wo[pl.ds(al(oc * 256, 256), 256), :], dm, 1, 1).astype(BF16)
        d_piece(t).start()
        m.do[2 * c + t] = dg(m.wo[pl.ds(al(c * 256, 256), 256), :], dm, 1, 1).astype(BF16)

        when_events("c", t, range(2))
        return 0

    lax.fori_loop(0, 2, c3, 0)
    go = (dg(m.ot[0], dmid[0:512, :], 1, 0) + dg(m.ot[1], dmid[512:1024, :], 1, 0)).astype(BF16)
    for s in range(4):
        for b in range(4):
            m.OG[s, b * 128:(b + 1) * 128, :] = go[s * 128:(s + 1) * 128, b * 128:(b + 1) * 128]
    events("go")
    sent(m.dst, idx[0])
    got(m.dst, idx[1])

    ixq = pair()

    def x_piece(h, b):
        return remote(m.xst.at[h, b], m.dqt.at[pl.ds(al(c * 768 + h * 192, 64), 192), pl.ds(b * 512, 512)], sib,
                      *ixq)

    def x_start(h):
        hrows = pl.ds(al(h * 192, 64), 192)
        for b in range(2):
            m.xst[h, b] = m.dq[canon_of(2 * oc + b), hrows, :]
            x_piece(h, b).start()
        for b in range(2):
            m.dqt[pl.ds(al(c * 768 + h * 192, 64), 192), b * 512:(b + 1) * 512] = m.dq[canon_of(2 * c + b), hrows, :]

    def q_grad(h):
        hrows = pl.ds(al(h * 192, 64), 192)
        gq = None
        for i in range(4):
            part = dg(m.dq[i, hrows, :], m.a1[phys[i]], 1, 0)
            gq = part if gq is None else gq + part
        gq = gq.astype(BF16)
        for s in range(4):
            m.QS[h, s] = gq[:, s * 128:(s + 1) * 128]

    def bwd_head(h, _):
        hr = pl.ds(al(h * HD, HD), HD)
        kt = jnp.concatenate([m.qkv[phys[j], rows_of(h, 1), :] for j in range(4)], axis=1)
        vt = jnp.concatenate([m.qkv[phys[j], rows_of(h, 2), :] for j in range(4)], axis=1)
        kn = kt.T
        tri = key_le_query(256, 1)
        for i in reversed(range(8)):
            L, b, cs = (i + 1) * 256, i // 2, slice((i % 2) * 256, (i % 2) * 256 + 256)
            q = m.qkv[phys[b], rows_of(h, 0), cs]
            gr = m.do[phys[b], hr, cs]
            ls = m.lse[b, pl.ds(h, 1), cs]
            delta = colsum(gr.astype(F32) * m.o[b, hr, cs])
            lsb = jnp.broadcast_to(ls, (128, 256)).T[:, 0:1]
            deb = jnp.broadcast_to(delta, (128, 256)).T[:, 0:1]
            p = jnp.exp(dg(q.T, kt[:, :L], 1, 0) - lsb)
            pd = jnp.where(tri, p[:, L - 256:], 0.0)
            p = jnp.concatenate([p[:, :L - 256], pd], axis=1) if i else pd
            dp = dg(gr.T, vt[:, :L], 1, 0)
            ds = (p * (dp - deb)).astype(BF16)
            p = p.astype(BF16)
            m.dq[b, rows_of(h, 0), cs] = dg(ds, kn[:L], 1, 0).T.astype(BF16)
            dk, dv = dg(q, ds, 1, 0), dg(gr, p, 1, 0)
            if i == 7:
                m.dkv[0:64, :] = dk
                m.dkv[64:128, :] = dv
            else:
                m.dkv[0:64, :L] += dk
                m.dkv[64:128, :L] += dv
            if i in (6, 4):
                when_events("dD"[i == 4], h, range(4))
        for j in range(4):
            m.dq[j, rows_of(h, 1), :] = m.dkv[0:64, j * BLK:(j + 1) * BLK].astype(BF16)
            m.dq[j, rows_of(h, 2), :] = m.dkv[64:128, j * BLK:(j + 1) * BLK].astype(BF16)
        x_start(h)
        when_events("e", h, range(4))
        q_grad(h)
        when_events("q", h, range(4))
        return 0

    lax.fori_loop(0, 4, bwd_head, 0)

    sent(m.xst, ixq[0])
    got(m.xst, ixq[1])
    events("x")
    wgst = m.dys

    def e1(t, _):
        rows = pl.ds(al(t * 256, 256), 256)
        xv = m.xs[rows, :].astype(F32)
        xc = xv - rowmean(xv)
        r = lax.rsqrt(rowmean(xc * xc) + EPS)
        nv = xc * r
        dav = dg(m.dqt[:, rows], m.wt[...], 0, 0)
        m.gg[0:1, :] += colsum(dav * nv)
        m.gg[1:2, :] += colsum(dav)
        gr = dav * g1
        dn = r * (gr - rowmean(gr) - nv * rowmean(gr * nv))
        wgst[rows, :] = (dmid[rows, :].astype(F32) + dn).astype(BF16)
        swap_go(wgst, wg_out, iw, t, 128)
        when_events("w", t, range(4))
        return 0

    lax.fori_loop(0, 4, e1, 0)
    for s in range(4):
        for k in range(5):
            m.gv[s, k:k + 1, :] = m.gg[k:k + 1, s * 128:(s + 1) * 128]
        for f in range(4):
            m.gv[s, 5 + f:6 + f, :] = m.gbu[f, 0:1, s * 128:(s + 1) * 128]
    ivx, ivy, iva = pair(), pair(), pair()
    vx = [remote(m.gv.at[2 * q + oc], m.gvr.at[q], sib, *ivx) for q in range(2)]
    vy = remote(m.gv.at[other], m.gvy, yn, *ivy)
    va = [remote(m.gv.at[w], m.gva.at[e], peer(d)[1], *iva) for d in range(1, ne)]
    for cp in vx:
        cp.start()
    for t in range(4, 6):
        swap_go(wgst, wg_out, iw, t, 128)
    sent(m.gvr, ivx[0])
    got(m.gvr, ivx[1])
    for q in range(2):
        m.gv[2 * q + c] = m.gv[2 * q + c] + m.gvr[q]
    vy.start()
    events("tail")
    vy.wait()
    m.gv[w] = m.gv[w] + m.gvy[...]
    m.gva[e] = m.gv[w]
    for cp in va:
        cp.start()
    for t in range(6, 8):
        swap_go(wgst, wg_out, iw, t, 128)
    sent(m.gva.at[0:ne - 1], iva[0])
    got(m.gva.at[0:ne - 1], iva[1])
    tot = m.gva[0]
    for d in range(1, ne):
        tot = tot + m.gva[d]
    vec_out[...] = tot
    for k in range(5):
        chunks[k].step(6)

    def fin(t, _):
        q4(t)
        return 0

    lax.fori_loop(0, 4, fin, 0)
    swap_wait(m.dup, iy)
    swap_wait(wgst, iw)


def layer(nz, *ops):
    sc = scratch(nz)
    names = tuple(sc)
    sd = jax.ShapeDtypeStruct
    any_ = pl.BlockSpec(memory_space=pl.ANY)
    vm = pl.BlockSpec(memory_space=pltpu.VMEM)
    return pl.pallas_call(
        functools.partial(body, nz, names),
        out_shape=(sd((1024, 512), BF16), sd((1024, 512), BF16), sd((ROWS, 128), BF16), sd((16, 128), F32)),
        in_specs=[any_] * 14,
        out_specs=(any_, any_, any_, vm),
        scratch_shapes=[sc[n] for n in names] + [pltpu.SemaphoreType.DMA((NSEND,)), pltpu.SemaphoreType.DMA((NRECV,))],
        compiler_params=pltpu.CompilerParams(collective_id=0, has_side_effects=True, vmem_limit_bytes=VLIM),
        name="layer",
    )(*ops)


def finish_body(y_h, wg_h, red_h, v, yo_h, wgo_h, gq_h, go_h, gu_h, gd_h, v1, v2, v3, v4, vu, vd,
                wg, red, wgo, yv, gq, go, gu, gd, sem):
    def cp(a, b, i):
        return pltpu.make_async_copy(a, b, sem.at[i])

    def red_in(k):
        return cp(red_h.at[pl.ds(k * 1024, 1024)], red.at[pl.ds(k * 1024, 1024)], k)

    def wg_in(k):
        return cp(wg_h.at[pl.ds(k * 256, 256)], wg.at[pl.ds(k * 256, 256)], 6 + k)

    outs = []

    def put(a, b):
        o = cp(a, b, 10 + len(outs))
        o.start()
        outs.append(o)

    def y_in(k):
        return cp(y_h.at[pl.ds(k * 512, 512)], yv.at[pl.ds(k * 512, 512)], 22 + k)

    for k in range(4):
        wg_in(k).start()
    for k in range(2):
        y_in(k).start()
    for k in range(6):
        red_in(k).start()
    for r, k in ((v1, 0), (v2, 1), (v3, 2), (v4, 3), (vd, 4)):
        r[...] = v[k:k + 1, :]
    vu[...] = v[5:9, :]
    for k in range(4):
        wg_in(k).wait()
        rows = slice(k * 256, (k + 1) * 256)
        wgo[rows, :] = wg[rows, :].astype(F32)
        put(wgo.at[rows], wgo_h.at[rows])
    for k in range(2):
        y_in(k).wait()
        put(yv.at[pl.ds(k * 512, 512)], yo_h.at[pl.ds(k * 512, 512)])
    for f in range(4):
        red_in(f).wait()
        gd[f * 128:(f + 1) * 128, :] = red[f * 1024:f * 1024 + 512, :].astype(F32).T
        put(gd.at[f * 128:(f + 1) * 128], gd_h.at[f * 128:(f + 1) * 128])
        for s in range(4):
            gu[:, s * 512 + f * 128:s * 512 + (f + 1) * 128] = red[f * 1024 + 512 + s * 128:f * 1024 + 640 + s * 128, :].astype(F32)
    put(gu, gu_h)
    red_in(4).wait()
    for b in range(4):
        go[:, b * 128:(b + 1) * 128] = red[OSTART + b * 128:OSTART + (b + 1) * 128, :].astype(F32)
    put(go, go_h)
    red_in(5).wait()
    for hp in range(2):
        for cc in range(2):
            for part in range(3):
                r = QSTART + hp * 768 + cc * 192 + part * 64
                blk = jnp.concatenate([red[r:r + 64, :], red[r + 384:r + 448, :]], axis=0).astype(F32).T
                if part == 0:
                    blk = blk * 0.125
                k = part * 512 + cc * 256 + hp * 128
                gq[:, k:k + 128] = blk
    put(gq, gq_h)
    for o in outs:
        o.wait()


def finish(y, wg, red, v):
    sd = jax.ShapeDtypeStruct
    any_ = pl.BlockSpec(memory_space=pl.ANY)
    vm = pl.BlockSpec(memory_space=pltpu.VMEM)
    one = sd((1, 128), F32)
    big = (sd((128, 1536), F32), sd((128, 512), F32), sd((128, 2048), F32), sd((512, 512), F32))
    return pl.pallas_call(
        finish_body,
        out_shape=(sd((1024, 512), BF16), sd((1024, 512), F32)) + big + (one, one, one, one, sd((4, 128), F32), one),
        in_specs=[any_] * 3 + [vm],
        out_specs=(any_,) * 6 + (vm,) * 6,
        scratch_shapes=[pltpu.VMEM((1024, 512), BF16), pltpu.VMEM((ROWS, 128), BF16), pltpu.VMEM((1024, 512), F32),
                        pltpu.VMEM((1024, 512), BF16)]
        + [pltpu.VMEM(b.shape, F32) for b in big] + [pltpu.SemaphoreType.DMA((24,))],
        compiler_params=pltpu.CompilerParams(vmem_limit_bytes=VLIM), name="finish",
    )(y, wg, red, v)


def on_chip(words, qkv_weight, out_weight, up_weight, down_weight, norm1_gain, norm1_bias, norm2_gain,
            norm2_bias, up_bias, down_bias, cotangent, seg_map, off_map):
    nz = lax.axis_size("group")
    r = lambda v: v.reshape(-1, 128)
    y, wg, red, v = layer(nz, words[0], cotangent[0], qkv_weight, out_weight, up_weight, down_weight.reshape(4, 128, 512),
                          r(norm1_gain), r(norm1_bias), r(norm2_gain), r(norm2_bias), r(down_bias), r(up_bias),
                          seg_map, off_map)
    y, wg, gq, go, gu, gd, v1, v2, v3, v4, vu, vd = finish(y, wg, red, v)
    f = lambda t: t.reshape(-1)
    return y[None], wg[None], gq, go, gu, gd, f(v1), f(v2), f(v3), f(v4), f(vu), f(vd)


HEADS = 8
HEAD_DIM = 64


eps = 1e-05
neg_big = -1e30


def passed_along(value, axis, by):
    peers = lax.axis_size(axis)
    return lax.ppermute(value, axis, [(i, (i + by) % peers) for i in range(peers)])


def layer_norm(features, norm_gain, norm_shift):
    row_mean = jnp.mean(features, axis=-1, keepdims=True)
    centred = features - row_mean
    inv_scale = lax.rsqrt(jnp.mean(centred * centred, axis=-1, keepdims=True) + eps)
    return centred * inv_scale * norm_gain + norm_shift


def gelu_tanh(features):
    return jax.nn.gelu(features, approximate=True)


def rows_of(array, block_id):
    return lax.dynamic_slice_in_dim(array, block_id * BLK, BLK, 0)


def cols_of(array, block_id):
    return lax.dynamic_slice_in_dim(array, block_id * BLK, BLK, 1)


def add_rows(array, update, block_id):
    return lax.dynamic_update_slice_in_dim(
        array, rows_of(array, block_id) + update, block_id * BLK, 0
    )


def put_rows(array, update, block_id):
    return lax.dynamic_update_slice_in_dim(array, update, block_id * BLK, 0)


def put_cols(array, update, block_id):
    return lax.dynamic_update_slice_in_dim(array, update, block_id * BLK, 1)


def block_info(seg_row, off_row, block_id):
    segment = lax.dynamic_index_in_dim(seg_row, block_id, 0, keepdims=False)
    position = lax.dynamic_index_in_dim(off_row, block_id, 0, keepdims=False)
    return (segment, position)


def pair_live(seg_row, off_row, query_block, key_block):
    query_seg, query_offset = block_info(seg_row, off_row, query_block)
    key_seg, key_offset = block_info(seg_row, off_row, key_block)
    return (query_seg == key_seg) & (key_offset <= query_offset) | (key_seg == 0) & (query_seg != 0)


def pair_mask(seg_row, off_row, query_block, key_block):
    query_seg, query_offset = block_info(seg_row, off_row, query_block)
    key_seg, key_offset = block_info(seg_row, off_row, key_block)
    row_ids = lax.broadcasted_iota(jnp.int32, (BLK, BLK), 0)
    col_ids = lax.broadcasted_iota(jnp.int32, (BLK, BLK), 1)
    query_pos = query_offset * BLK + row_ids
    key_pos = key_offset * BLK + col_ids
    return (query_seg == key_seg) & (key_pos <= query_pos) | (key_seg == 0) & (query_seg != 0)


def split_heads(tile_rows):
    return tile_rows.reshape(tile_rows.shape[0], HEADS, HEAD_DIM)


def tile_scores(query_tile, key_tile, allowed):
    raw_scores = jnp.einsum(
        "qhd,khd->hqk",
        split_heads(query_tile),
        split_heads(key_tile),
        preferred_element_type=jnp.float32,
    )
    return jnp.where(allowed[None], raw_scores * HEAD_DIM ** (-0.5), neg_big)


def tile_back(query_tile, key_tile, value_tile, grad_tile, norm_tile, delta_tile, allowed):
    scores = tile_scores(query_tile, key_tile, allowed)
    exp_terms = jnp.where(allowed[None], jnp.exp(scores - norm_tile[:, :, None]), 0.0)
    d_probs = jnp.einsum(
        "qhd,khd->hqk",
        split_heads(grad_tile),
        split_heads(value_tile),
        preferred_element_type=jnp.float32,
    )
    d_scores = (exp_terms * (d_probs - delta_tile[:, :, None])).astype(jnp.bfloat16)
    return (exp_terms.astype(jnp.bfloat16), d_scores)


def query_grad(d_scores, key_tile):
    part_rows = jnp.einsum(
        "hqk,khd->qhd", d_scores, split_heads(key_tile), preferred_element_type=jnp.float32
    )
    return part_rows.reshape(BLK, -1) * HEAD_DIM ** (-0.5)


def key_grad(d_scores, query_tile):
    part_rows = jnp.einsum(
        "hqk,qhd->khd", d_scores, split_heads(query_tile), preferred_element_type=jnp.float32
    )
    return part_rows.reshape(BLK, -1) * HEAD_DIM ** (-0.5)


def value_grad(probs_low, grad_tile):
    part_rows = jnp.einsum(
        "hqk,qhd->khd", probs_low, split_heads(grad_tile), preferred_element_type=jnp.float32
    )
    return part_rows.reshape(BLK, -1)


def unchanged(running):
    return running


def on_device(
    words,
    qkv_weight,
    out_weight,
    up_weight,
    down_weight,
    norm1_gain,
    norm1_bias,
    norm2_gain,
    norm2_bias,
    up_bias,
    down_bias,
    cotangent,
    seg_map,
    off_map,
):
    gathered = (
        lax.all_gather(qkv_weight, "wshard", axis=0, tiled=True),
        lax.all_gather(out_weight, "wshard", axis=0, tiled=True),
        lax.all_gather(up_weight, "wshard", axis=0, tiled=True),
        lax.all_gather(down_weight, "wshard", axis=0, tiled=True),
        lax.all_gather(norm1_gain, "wshard", axis=0, tiled=True),
        lax.all_gather(norm1_bias, "wshard", axis=0, tiled=True),
        lax.all_gather(norm2_gain, "wshard", axis=0, tiled=True),
        lax.all_gather(norm2_bias, "wshard", axis=0, tiled=True),
        lax.all_gather(up_bias, "wshard", axis=0, tiled=True),
        lax.all_gather(down_bias, "wshard", axis=0, tiled=True),
    )
    w_qkv, w_out, w_up, w_down = (gathered[0], gathered[1], gathered[2], gathered[3])
    gain1 = gathered[4].astype(jnp.float32)
    shift1 = gathered[5].astype(jnp.float32)
    gain2 = gathered[6].astype(jnp.float32)
    shift2 = gathered[7].astype(jnp.float32)
    bias_up = gathered[8].astype(jnp.float32)
    bias_down = gathered[9].astype(jnp.float32)
    seg_row = seg_map[0]
    off_row = off_map[0]
    cycle_place = lax.axis_index("ctx")
    cycle_count = lax.axis_size("ctx")
    inputs = words[0].astype(jnp.float32)
    local_rows = inputs.shape[0]
    local_blocks = local_rows // BLK
    first_block = cycle_place * local_blocks
    width = inputs.shape[1]
    normed1, pull_norm1 = jax.vjp(layer_norm, inputs, gain1, shift1)
    act1 = normed1.astype(jnp.bfloat16)
    qkv = jnp.dot(act1, w_qkv, preferred_element_type=jnp.float32)
    query_rows = qkv[:, :width].astype(jnp.bfloat16)
    key_rows = qkv[:, width : 2 * width].astype(jnp.bfloat16)
    value_rows = qkv[:, 2 * width :].astype(jnp.bfloat16)
    start_state = (
        jnp.full((HEADS, local_rows), neg_big, jnp.float32),
        jnp.zeros((HEADS, local_rows), jnp.float32),
        jnp.zeros((local_rows, width), jnp.float32),
    )
    shard_keys = lax.all_gather(key_rows, "ctx", axis=0, tiled=True)
    shard_values = lax.all_gather(value_rows, "ctx", axis=0, tiled=True)
    key_blocks = shard_keys.shape[0] // BLK

    def online_visit_pair(pair_index, state):
        row_block = pair_index // key_blocks
        col_block = pair_index % key_blocks
        query_block = first_block + row_block
        key_block = col_block

        def online_update_tile(state):
            run_max, run_sum, accum = state
            allowed = pair_mask(seg_row, off_row, query_block, key_block)
            scores = tile_scores(
                rows_of(query_rows, row_block), rows_of(shard_keys, col_block), allowed
            )
            old_max = cols_of(run_max, row_block)
            old_sum = cols_of(run_sum, row_block)
            new_max = jnp.maximum(old_max, jnp.max(scores, axis=-1))
            exp_terms = jnp.where(allowed[None], jnp.exp(scores - new_max[:, :, None]), 0.0)
            factor = jnp.exp(old_max - new_max)
            new_sum = old_sum * factor + jnp.sum(exp_terms, axis=-1)
            part_rows = jnp.einsum(
                "hqk,khd->qhd",
                exp_terms.astype(jnp.bfloat16),
                split_heads(rows_of(shard_values, col_block)),
                preferred_element_type=jnp.float32,
            )
            old_rows = rows_of(accum, row_block).reshape(BLK, HEADS, HEAD_DIM)
            new_rows = (old_rows * factor.T[:, :, None] + part_rows).reshape(BLK, -1)
            return (
                put_cols(run_max, new_max, row_block),
                put_cols(run_sum, new_sum, row_block),
                put_rows(accum, new_rows, row_block),
            )

        return lax.cond(
            pair_live(seg_row, off_row, query_block, key_block),
            online_update_tile,
            unchanged,
            state,
        )

    run_max, run_sum, accum = lax.fori_loop(
        0, local_blocks * key_blocks, online_visit_pair, start_state
    )
    log_norm = run_max + jnp.log(run_sum)
    attended = (accum.reshape(local_rows, HEADS, HEAD_DIM) / run_sum.T[:, :, None]).reshape(
        local_rows, width
    )
    attended_low = attended.astype(jnp.bfloat16)
    middle = inputs + jnp.dot(attended_low, w_out, preferred_element_type=jnp.float32)
    normed2, pull_norm2 = jax.vjp(layer_norm, middle, gain2, shift2)
    act2 = normed2.astype(jnp.bfloat16)
    hidden = jnp.dot(act2, w_up, preferred_element_type=jnp.float32) + bias_up
    gelu_out, pull_gelu = jax.vjp(gelu_tanh, hidden)
    gelu_low = gelu_out.astype(jnp.bfloat16)
    output = (
        middle + jnp.dot(gelu_low, w_down, preferred_element_type=jnp.float32) + bias_down
    ).astype(jnp.bfloat16)
    upstream = cotangent[0]
    upstream_f = upstream.astype(jnp.float32)
    grad_down = jnp.einsum("nf,nd->fd", gelu_low, upstream, preferred_element_type=jnp.float32)
    grad_bias_down = jnp.sum(upstream_f, axis=0)
    d_gelu = jnp.einsum("nd,fd->nf", upstream, w_down, preferred_element_type=jnp.float32)
    d_hidden = pull_gelu(d_gelu)[0].astype(jnp.bfloat16)
    grad_up = jnp.einsum("nd,nf->df", act2, d_hidden, preferred_element_type=jnp.float32)
    grad_bias_up = jnp.sum(d_hidden.astype(jnp.float32), axis=0)
    d_act2 = jnp.einsum("nf,df->nd", d_hidden, w_up, preferred_element_type=jnp.float32)
    d_middle_norm, grad_gain2, grad_shift2 = pull_norm2(d_act2)
    d_middle = (upstream_f + d_middle_norm).astype(jnp.bfloat16)
    grad_out = jnp.einsum("nd,ne->de", attended_low, d_middle, preferred_element_type=jnp.float32)
    d_attended = jnp.einsum(
        "ne,de->nd", d_middle, w_out, preferred_element_type=jnp.float32
    ).astype(jnp.bfloat16)
    row_delta = jnp.sum(
        (d_attended.astype(jnp.float32) * attended).reshape(local_rows, HEADS, HEAD_DIM), axis=-1
    ).T
    zero_rows = jnp.zeros((local_rows, width), jnp.float32)

    def attend_back(cycle_turn, cycle_state):
        held_keys, held_values, held_dk, held_dv, d_query = cycle_state
        source = (cycle_place - cycle_turn) % cycle_count

        def attend_visit_pair(pair_index, partial_value):
            row_block = pair_index // local_blocks
            col_block = pair_index % local_blocks
            query_block = first_block + row_block
            key_block = source * local_blocks + col_block

            def attend_update_tile(partial_value):
                dk_acc, dv_acc, dq_acc = partial_value
                query_tile = rows_of(query_rows, row_block)
                key_tile = rows_of(held_keys, col_block)
                grad_tile = rows_of(d_attended, row_block)
                allowed = pair_mask(seg_row, off_row, query_block, key_block)
                probs_low, d_scores = tile_back(
                    query_tile,
                    key_tile,
                    rows_of(held_values, col_block),
                    grad_tile,
                    cols_of(log_norm, row_block),
                    cols_of(row_delta, row_block),
                    allowed,
                )
                dq_acc = add_rows(dq_acc, query_grad(d_scores, key_tile), row_block)
                dk_acc = add_rows(dk_acc, key_grad(d_scores, query_tile), col_block)
                dv_acc = add_rows(dv_acc, value_grad(probs_low, grad_tile), col_block)
                return (dk_acc, dv_acc, dq_acc)

            return lax.cond(
                pair_live(seg_row, off_row, query_block, key_block),
                attend_update_tile,
                unchanged,
                partial_value,
            )

        held_dk, held_dv, d_query = lax.fori_loop(
            0, local_blocks * local_blocks, attend_visit_pair, (held_dk, held_dv, d_query)
        )
        return (held_keys, held_values, held_dk, held_dv, d_query)

    def pass_grads(held_dk, held_dv):
        return (
            passed_along(held_dk.astype(jnp.bfloat16), "ctx", 1).astype(held_dk.dtype),
            passed_along(held_dv.astype(jnp.bfloat16), "ctx", 1).astype(held_dv.dtype),
        )

    def turn_step(cycle_turn, cycle_state):
        held_keys, held_values, held_dk, held_dv, d_query = attend_back(cycle_turn, cycle_state)
        held_keys, held_values = passed_along((held_keys, held_values), "ctx", 1)
        held_dk, held_dv = pass_grads(held_dk, held_dv)
        return (held_keys, held_values, held_dk, held_dv, d_query)

    cycle_state = lax.fori_loop(
        0, cycle_count - 1, turn_step, (key_rows, value_rows, zero_rows, zero_rows, zero_rows)
    )
    cycle_state = attend_back(cycle_count - 1, cycle_state)
    d_keys, d_values = pass_grads(cycle_state[2], cycle_state[3])
    d_query = cycle_state[4]
    d_qkv = jnp.concatenate(
        [d_query.astype(jnp.bfloat16), d_keys.astype(jnp.bfloat16), d_values.astype(jnp.bfloat16)],
        axis=1,
    )
    grad_qkv = jnp.einsum("nd,nf->df", act1, d_qkv, preferred_element_type=jnp.float32)
    d_act1 = jnp.einsum("nf,df->nd", d_qkv, w_qkv, preferred_element_type=jnp.float32)
    d_inputs_norm, grad_gain1, grad_shift1 = pull_norm1(d_act1)
    words_grad = d_middle.astype(jnp.float32) + d_inputs_norm
    shards = (
        lax.psum_scatter(
            grad_qkv.astype(jnp.bfloat16), "wshard", scatter_dimension=0, tiled=True
        ).astype(jnp.float32),
        lax.psum_scatter(
            grad_out.astype(jnp.bfloat16), "wshard", scatter_dimension=0, tiled=True
        ).astype(jnp.float32),
        lax.psum_scatter(
            grad_up.astype(jnp.bfloat16), "wshard", scatter_dimension=0, tiled=True
        ).astype(jnp.float32),
        lax.psum_scatter(
            grad_down.astype(jnp.bfloat16), "wshard", scatter_dimension=0, tiled=True
        ).astype(jnp.float32),
        lax.psum_scatter(
            grad_gain1.astype(jnp.bfloat16), "wshard", scatter_dimension=0, tiled=True
        ).astype(jnp.float32),
        lax.psum_scatter(
            grad_shift1.astype(jnp.bfloat16), "wshard", scatter_dimension=0, tiled=True
        ).astype(jnp.float32),
        lax.psum_scatter(
            grad_gain2.astype(jnp.bfloat16), "wshard", scatter_dimension=0, tiled=True
        ).astype(jnp.float32),
        lax.psum_scatter(
            grad_shift2.astype(jnp.bfloat16), "wshard", scatter_dimension=0, tiled=True
        ).astype(jnp.float32),
        lax.psum_scatter(
            grad_bias_up.astype(jnp.bfloat16), "wshard", scatter_dimension=0, tiled=True
        ).astype(jnp.float32),
        lax.psum_scatter(
            grad_bias_down.astype(jnp.bfloat16), "wshard", scatter_dimension=0, tiled=True
        ).astype(jnp.float32),
    )
    totals = lax.psum(
        (
            shards[0],
            shards[1],
            shards[2],
            shards[3],
            shards[4],
            shards[5],
            shards[6],
            shards[7],
            shards[8],
            shards[9],
        ),
        ("group", "ctx"),
    )
    return (
        output[None],
        words_grad[None],
        totals[0],
        totals[1],
        totals[2],
        totals[3],
        totals[4],
        totals[5],
        totals[6],
        totals[7],
        totals[8],
        totals[9],
    )


def solution(mesh):
    chip = mesh.shape["ctx"] == 2 and mesh.shape["wshard"] == 4 and mesh.shape["group"] in (2, 4)
    return jax.shard_map(
        on_chip if chip else on_device,
        mesh=mesh,
        in_specs=(
            P(("group", "wshard"), "ctx", None),
            P("wshard", None),
            P("wshard", None),
            P("wshard", None),
            P("wshard", None),
            P("wshard"),
            P("wshard"),
            P("wshard"),
            P("wshard"),
            P("wshard"),
            P("wshard"),
            P(("group", "wshard"), "ctx", None),
            P(("group", "wshard"), None),
            P(("group", "wshard"), None),
        ),
        out_specs=(
            P(("group", "wshard"), "ctx", None),
            P(("group", "wshard"), "ctx", None),
            P("wshard", None),
            P("wshard", None),
            P("wshard", None),
            P("wshard", None),
            P("wshard"),
            P("wshard"),
            P("wshard"),
            P("wshard"),
            P("wshard"),
            P("wshard"),
        ),
        check_vma=False,
    )
```

```python
import functools
import jax
import jax.numpy as jnp
from jax import lax
from jax.experimental import pallas as pl
from jax.experimental.pallas import tpu as pltpu
from jax.sharding import PartitionSpec as P

BLK = 512
HD = 64
EPS = 1e-5
F32 = jnp.float32
BF16 = jnp.bfloat16
K0 = 0.7978845608
K1 = 0.044715
MESH = pl.DeviceIdType.MESH
VLIM = 63 * 1024 * 1024
FROWS, OROWS, QROWS = 1024, 512, 384
OSTART, QSTART, ROWS = 4096, 4608, 6144
NSEND, NRECV = 66, 90
CHUNKS = (("F0", FROWS, "xyz"), ("F1", FROWS, "yxz"), ("F2", FROWS, "xyz"), ("F3", FROWS, "yxz"), ("O", OROWS, "yxz"))


PLAN = {
    ("g", 0): ((0, 0),),
    ("f", 1): ((0, 1),),
    ("g", 1): ((1, 0),),
    ("f", 2): ((1, 1),),
    ("g", 2): ((2, 0),),
    ("f", 3): ((0, 2), (2, 1),),
    ("g", 3): ((3, 0),),
    ("c", 0): ((1, 2), (3, 1), (9, 0),),
    ("c", 1): ((0, 3), (9, 1),),
    "go": ((4, 0), (9, 2),),
    ("d", 0): ((2, 2), (4, 1), (1, 3), (0, 4), (9, 3),),
    ("D", 0): ((3, 2), (9, 4),),
    ("e", 0): ((9, 5),),
    ("q", 0): ((5, 0), (2, 3), (1, 4),),
    ("d", 1): ((5, 1), (4, 2), (0, 5), (3, 3), (9, 6),),
    ("D", 1): ((9, 7),),
    ("e", 1): ((2, 4),),
    ("q", 1): ((6, 0), (5, 2), (4, 3), (1, 5),),
    ("d", 2): ((6, 1), (3, 4),),
    ("e", 2): ((2, 5),),
    ("q", 2): ((7, 0), (6, 2), (5, 3),),
    ("d", 3): ((4, 4), (7, 1),),
    ("D", 3): ((3, 5),),
    ("e", 3): ((6, 3),),
    ("q", 3): ((8, 0), (7, 2),),
    "x": ((4, 5), (8, 1),),
    ("w", 1): ((8, 2),),
    ("w", 2): ((7, 3),),
    "tail": ((8, 3),),
}


def dg(a, b, ca, cb):
    return lax.dot_general(a, b, (((ca,), (cb,)), ((), ())), preferred_element_type=F32)


def colsum(v):
    return jnp.sum(v, axis=0, keepdims=True)


def rowmean(v):
    return jnp.mean(v, axis=-1, keepdims=True)


def key_le_query(n, key_axis):
    k = lax.broadcasted_iota(jnp.int32, (n, n), key_axis)
    q = lax.broadcasted_iota(jnp.int32, (n, n), 1 - key_axis)
    return k <= q


def al(v, n):
    return pl.multiple_of(v, n)


def chunk_scratch(nz, rows, kind):
    V = lambda *s: pltpu.VMEM(s, BF16)
    held = rows if kind == "yz" else rows // 2
    return dict(A=V(2, rows, 128), B=V(held if kind == "xyz" else rows, 128),
                X=V(held // nz, 128) if kind == "yz" else V(2 if kind == "xyz" else 1, held, 128),
                Z=V(nz - 1, held // nz, 128), T=V(held // nz, 128), H=V(held, 128))


def scratch(nz):
    ne = 2 * nz
    V = lambda *s, t=BF16: pltpu.VMEM(s, t)
    return dict(
        xs=V(1024, 512), dys=V(1024, 512), wt=V(1536, 512), wo=V(512, 512),
        wu=V(4, 512, 512), wd=V(4, 512, 512), vown=V(16, 128, t=F32), vec=V(4, 16, 128, t=F32),
        so=V(2, 8, 128, t=jnp.int32), sseg=V(1, 4, t=jnp.int32), soff=V(1, 4, t=jnp.int32),
        s1g=V(1, 128), s1b=V(1, 128), s2g=V(1, 128), s2b=V(1, 128), sbd=V(1, 128), sbu=V(4, 128), sm=pltpu.SMEM((8, 128), jnp.int32),
        a1=V(4, 512, 512), qkv=V(4, 768, 512), o=V(4, 256, 512, t=F32), lse=V(4, 8, 512, t=F32),
        ost=V(2, 256, 512), ot=V(2, 512, 512), n2=V(1024, 512, t=F32), rs=V(1024, 128, t=F32), a2=V(1024, 512),
        a2t=V(512, 1024), dyt=V(512, 1024), ya=V(1024, 512, t=F32), da=V(1024, 512, t=F32),
        act=V(1024, 512), dup=V(1024, 512), do=V(4, 256, 512), dst=V(2, 256, 512), dq=V(4, 768, 512),
        dkv=V(128, 2048, t=F32), xst=V(4, 2, 192, 512), dqt=V(1536, 1024),
        gv=V(4, 16, 128, t=F32), gvr=V(2, 16, 128, t=F32), gvy=V(16, 128, t=F32), gva=V(ne, 16, 128, t=F32),
        n1=V(1024, 512, t=F32), r1=V(1024, 128, t=F32), gg=V(8, 512, t=F32), gbu=V(4, 8, 512, t=F32),
        FG=V(4, 4, FROWS, 128), OG=V(4, OROWS, 128),
        **{f"{t}{q}": v for t, rows, kind in CHUNKS for q, v in chunk_scratch(nz, rows, kind).items()},
        QS=V(4, 4, 192, 128), QG=V(4, 2, QROWS, 128), QB=V(4, QROWS, 128), QC=V(4, ne - 1, QROWS // ne, 128),
        QT=V(4, QROWS // ne, 128),
    )


class Count:
    def __init__(self, most):
        self.n, self.most = 0, most

    def take(self, k=1):
        self.n += k
        assert self.n <= self.most
        return self.n - k


class Ns:
    def __init__(self, d):
        self.__dict__.update(d)


def body(nz, names, *args):
    (words_h, cot_h, wq_h, wo_h, wu_h, wd_h, n1g, n1b, n2g, n2b, bdr, bur, seg_r, off_r) = args[:14]
    y_out, wg_out, red_out, vec_out = args[14:18]
    m = Ns(dict(zip(names, args[18:18 + len(names)])))
    send, recv = args[18 + len(names):]
    cs, cr = Count(NSEND), Count(NRECV)
    ne = 2 * nz
    g, x, w = lax.axis_index("group"), lax.axis_index("ctx"), lax.axis_index("wshard")
    yi, c = w // 2, w % 2
    oc, oy, ox = 1 - c, 1 - yi, 1 - x
    e = x * nz + g
    sib = (g, x, 2 * yi + oc)
    yn = (g, x, 2 * oy + c)
    diag = (g, x, 2 * oy + oc)
    xn = (g, ox, w)
    zp = (g + 1 - 2 * (g % 2), x, w)
    sw = (g, c, 2 * yi + x)
    stay = x == c
    moves = jnp.logical_not(stay)

    def peer(d):
        q = (e + d) % ne
        return q, (q % nz, q // nz, w)

    def zpeer(d):
        q = (g + d) % nz
        return q, (q, x, w)

    def remote(src, dst_, dev, i, j):
        return pltpu.make_async_remote_copy(src_ref=src, dst_ref=dst_, send_sem=send.at[i], recv_sem=recv.at[j],
                                            device_id=dev, device_id_type=MESH)

    def local(src, dst_, i):
        return pltpu.make_async_copy(src, dst_, send.at[i])

    def sent(ref, i):
        pltpu.make_async_copy(ref, ref, send.at[i]).wait()

    def got(ref, j):
        pltpu.make_async_copy(ref, ref, recv.at[j]).wait()

    def begin(src, dst_):
        cp = local(src, dst_, cs.take())
        cp.start()
        return cp

    bar = pltpu.get_barrier_semaphore()
    peers = [sib, yn, diag] + [peer(d)[1] for d in range(1, ne)]
    for p in peers:
        pl.semaphore_signal(bar, inc=1, device_id=p, device_id_type=MESH)

    @pl.when(moves)
    def _():
        pl.semaphore_signal(bar, inc=1, device_id=sw, device_id_type=MESH)

    l_wq = [begin(wq_h.at[:, pl.ds(k * 512, 512)], m.act.at[pl.ds(k * 128, 128), :]) for k in range(3)]
    l_small = [begin(a, b) for a, b in zip((n1g, n1b, n2g, n2b, bdr, bur, seg_r, off_r),
                                           (m.s1g, m.s1b, m.s2g, m.s2b, m.sbd, m.sbu, m.sseg, m.soff))]
    l_wo = begin(wo_h, m.wo.at[pl.ds(al(w * 128, 128), 128), :])
    l_wu = [begin(wu_h.at[:, pl.ds(k * 512, 512)], m.dup.at[pl.ds(k * 128, 128), :]) for k in range(4)]
    l_wd = begin(wd_h, m.wd.at[:, pl.ds(al(w * 128, 128), 128), :])
    m.vown[...] = jnp.zeros_like(m.vown)
    m.so[0] = jnp.zeros((8, 128), jnp.int32)
    m.gg[...] = jnp.zeros_like(m.gg)
    m.gbu[...] = jnp.zeros_like(m.gbu)
    m.gv[...] = jnp.zeros_like(m.gv)
    pl.semaphore_wait(bar, len(peers) + jnp.where(stay, 0, 1))

    def swap_go(src, dst_, ij, t, n, k=0):
        rows = pl.ds(al(t * n, n), n)

        @pl.when(stay)
        def _():
            local(src.at[rows], dst_.at[rows], ij[0] + k).start()

        @pl.when(moves)
        def _():
            remote(src.at[rows], dst_.at[rows], sw, ij[0] + k, ij[1] + k).start()

    def swap_wait(ref, ij, k=0):
        sent(ref, ij[0] + k)

        @pl.when(moves)
        def _():
            got(ref, ij[1] + k)

    def pair(k=1):
        return cs.take(k), cr.take(k)

    ix, idy, iy, iw = pair(4), pair(), pair(), pair()
    for t in range(4):
        swap_go(words_h, m.xs, ix, t, 256, t)
    for cp in l_small:
        cp.wait()
    for k, r in enumerate((m.s1g, m.s1b, m.s2g, m.s2b, m.sbd)):
        m.vown[k:k + 1, :] = r[...].astype(F32)
    m.vown[5:9, :] = m.sbu[...].astype(F32)
    m.so[0, 0:1, 0:4] = m.sseg[...] * 2 + m.soff[...]
    so_x = remote(m.so.at[0], m.so.at[1], sib, *pair())
    ivc = pair()
    vcs = [remote(m.vown, m.vec.at[w], p, *ivc) for p in (sib, yn, diag)]
    m.vec[w] = m.vown[...]

    mine = pl.ds(al(w * 128, 128), 128)
    for cp in l_wq:
        cp.wait()
    for cc in range(2):
        for hp in range(2):
            for part in range(3):
                b = (part * 4 + cc * 2 + hp) * 128
                blk = m.act[part * 128:(part + 1) * 128, b - part * 512:b - part * 512 + 128].T
                if part == 0:
                    blk = (blk.astype(F32) * 0.125).astype(BF16)
                r = cc * 768 + hp * 384 + part * 64
                m.wt[r:r + 64, mine] = blk[:64]
                m.wt[r + 192:r + 256, mine] = blk[64:]

    other = 2 * oy + c

    def shard(n, s, f):
        v = pl.ds(al(s * 128, 128), 128)
        if n == "wt":
            return m.wt.at[:, v]
        if n == "wo":
            return m.wo.at[v, :]
        return (m.wu if n == "wu" else m.wd).at[f, v, :]

    pieces = [("wt", 0), ("wo", 0)] + [(n, f) for f in range(4) for n in ("wu", "wd")]
    big2 = m.wu.at[0:2, 0:128, :]
    big8 = m.wu.at[:, 0:256, :]
    ig = dict(wt=(pair(3)), wo=(pair(3)))
    isib, iys, ifs = pair(), cs.take(), cs.take()
    iyr, ifr = cr.take(4), cr.take(4)

    def g_sems(p, k):
        n, f = p
        if n in ig:
            return ig[n][0] + k, ig[n][1] + k
        return (isib, (iys, iyr + f), (ifs, ifr + f))[k]

    def g_sib(p):
        return remote(shard(p[0], w, p[1]), shard(p[0], w, p[1]), sib, *g_sems(p, 0))

    def g_y(p):
        return remote(shard(p[0], w, p[1]), shard(p[0], w, p[1]), yn, *g_sems(p, 1))

    def g_fwd(p):
        return remote(shard(p[0], other, p[1]), shard(p[0], other, p[1]), sib, *g_sems(p, 2))

    def g_forward(*ps):
        for p in ps:
            if p[0] in ig:
                g_y(p).wait_recv()
            elif p[0] == "wu":
                got(big2, iyr + p[1])
            g_fwd(p).start()

    g_y(("wt", 0)).start()
    g_sib(("wt", 0)).start()
    for v in vcs:
        v.start()
    so_x.start()
    for cp in l_wu:
        cp.wait()
    for f in range(4):
        for s in range(4):
            m.wu[f, mine, s * 128:(s + 1) * 128] = m.dup[s * 128:(s + 1) * 128, f * 128:(f + 1) * 128]
    l_wo.wait()
    l_wd.wait()
    for p in pieces[1:]:
        g_y(p).start()
    for p in pieces[1:]:
        g_sib(p).start()
    sent(m.vec.at[0:3], ivc[0])
    got(m.vec.at[0:3], ivc[1])
    so_x.wait()
    m.so[0] = jnp.where(stay, m.so[0], m.so[1])
    so_s = local(m.so.at[0], m.sm, cs.take())
    so_s.start()

    def row(k):
        return jnp.concatenate([m.vec[s, k:k + 1, :] for s in range(4)], axis=1)

    g1, b1 = row(0), row(1)

    ia = pair(4)

    def a_slot(core, t):
        return m.a1.at[2 * core + t // 2, pl.ds(al((t % 2) * 256, 256), 256), :]

    def a_piece(t):
        return remote(a_slot(c, t), a_slot(c, t), sib, ia[0] + t, ia[1] + t)

    def norm1(t, _=0):
        rows = pl.ds(al(t * 256, 256), 256)
        swap_wait(m.xs.at[rows], ix, t)
        xv = m.xs[rows, :].astype(F32)
        xc = xv - rowmean(xv)
        r = lax.rsqrt(rowmean(xc * xc) + EPS)
        nv = xc * r
        a_slot(c, t)[...] = (nv * g1 + b1).astype(BF16)
        a_piece(t).start()
        m.n1[rows, :] = nv
        m.r1[rows, :] = jnp.broadcast_to(r, (256, 128))
        return 0

    wrows = pl.ds(al(c * 768, 256), 768)

    near, far = pl.ds(al(yi * 256, 256), 256), pl.ds(al(oy * 256, 256), 256)
    part_of = (m.ya, m.da)

    def words_of(t, feats):
        half = pl.ds(al((t % 2) * 256, 256), 256)
        return jnp.concatenate([m.a1[t // 2, half, feats], m.a1[2 + t // 2, half, feats]], axis=0)

    def project(t, part=None):
        cols = pl.ds(al((t % 2) * 256, 256), 256)
        res = dg(m.wt[wrows, far], words_of(t, far), 1, 1)
        res = res + (dg(m.wt[wrows, near], words_of(t, near), 1, 1) if part is None else part[0:768, :])
        res = res.astype(BF16)
        m.qkv[t // 2, :, cols] = res[:, :256]
        m.qkv[2 + t // 2, :, cols] = res[:, 256:]

    norm1(0)
    g_sib(("wt", 0)).wait()
    for t in range(2):
        norm1(t + 1)
        a_piece(t).wait()
        part_of[t][0:768, :] = dg(m.wt[wrows, near], words_of(t, near), 1, 1)
    g_forward(("wt", 0))
    g_fwd(("wt", 0)).wait()
    project(0, m.ya)
    project(1, m.da)
    norm1(3)
    for t in range(2, 4):
        a_piece(t).wait()
        project(t)
    for t in range(4):
        swap_go(cot_h, m.dys, idy, t, 256)
    so_s.wait()
    canon = [m.sm[0, b] for b in range(4)]
    phys = [jnp.minimum(sum(jnp.where(canon[b] == k, b, 0) for b in range(1, 4)), 3) for k in range(4)]

    def canon_of(p):
        return jnp.clip(m.sm[0, p], 0, 3)

    def rows_of(h, part):
        return pl.ds(al(h * 192 + part * 64, 64), 64)

    def fwd_head(h, _):
        kn = [m.qkv[phys[j], rows_of(h, 1), :].T for j in range(4)]
        q = jnp.concatenate([m.qkv[phys[j], rows_of(h, 0), :] for j in range(4)], axis=1)
        tri = key_le_query(BLK, 0)
        s = []
        for j in range(4):
            sj = dg(kn[j], q[:, j * BLK:], 1, 0)
            sd = jnp.where(tri, sj[:, :BLK], -1e30)
            s.append(sd if j == 3 else jnp.concatenate([sd, sj[:, BLK:]], axis=1))
        mx = [jnp.max(sj, axis=0, keepdims=True) for sj in s]
        top = mx[0]
        for j in range(1, 4):
            top = jnp.concatenate([top[:, :j * BLK], jnp.maximum(top[:, j * BLK:], mx[j])], axis=1)
        acc = None
        for j in range(4):
            p = jnp.exp(s[j] - top[:, j * BLK:]).astype(BF16)
            a = dg(jnp.concatenate([m.qkv[phys[j], rows_of(h, 2), :], jnp.ones((16, BLK), BF16)], axis=0), p, 1, 0)
            acc = a if acc is None else jnp.concatenate([acc[:, :j * BLK], acc[:, j * BLK:] + a], axis=1)
        tot = acc[HD:HD + 1]
        ov = acc[:HD] * (1.0 / tot)
        ls = top + jnp.log(tot)
        for i in range(4):
            m.o[i, pl.ds(al(h * HD, HD), HD), :] = ov[:, i * BLK:(i + 1) * BLK]
            m.lse[i, pl.ds(h, 1), :] = ls[:, i * BLK:(i + 1) * BLK]

        @pl.when(h == 0)
        def _():
            g_forward(*pieces[1:4])

        @pl.when(h == 2)
        def _():
            g_forward(*pieces[4:6])

        @pl.when(h == 3)
        def _():
            g_forward(*pieces[6:8])
        return 0

    lax.fori_loop(0, 4, fwd_head, 0)
    iox = pair()
    for b in range(2):
        m.ost[b] = m.o[canon_of(2 * oc + b)].astype(BF16)
        remote(m.ost.at[b], m.ot.at[b, pl.ds(al(c * 256, 256), 256), :], sib, *iox).start()
    for b in range(2):
        m.ot[b, pl.ds(al(c * 256, 256), 256), :] = m.o[canon_of(2 * c + b)].astype(BF16)
    g_fwd(("wo", 0)).wait()
    g_sib(("wo", 0)).wait()
    sent(m.ost, iox[0])
    got(m.ost, iox[1])

    class Chunk:
        def __init__(self, k):
            tag, self.rows, self.kind = CHUNKS[k]
            self.G = m.FG.at[k] if k < 4 else m.OG
            for q in "ABXZTH":
                setattr(self, q, getattr(m, tag + q))
            self.start = k * FROWS
            self.held = self.rows if self.kind == "yz" else self.rows // 2
            self.p = self.held // nz
            self.lo = 0 if self.kind == "yz" else x * self.held
            self.slots = (w, other) if self.kind == "xyz" else (w,)
            self.i, self.keeping = cs.take(), cs.take()
            self.j = cr.take(6)

        def r(self, off, n):
            return pl.ds(al(off, 16), n)

        def core(self, q):
            return remote(self.G.at[2 * q + oc], self.A.at[q], sib, self.i, self.j)

        def y(self):
            if self.kind == "xyz":
                return remote(self.G.at[other, self.r(self.lo, self.held), :], self.B, yn, self.i, self.j + 1)
            return remote(self.G.at[other], self.B, yn, self.i, self.j + 1)

        def xs(self):
            if self.kind == "yz":
                return [remote(self.T, self.X, xn, self.i, self.j + 2)]
            return [remote(self.G.at[v, self.r(ox * self.held, self.held), :], self.X.at[n], xn, self.i, self.j + 2)
                    for n, v in enumerate(self.slots)]

        def z(self, d):
            q, dev = zpeer(d)
            return remote(self.G.at[w, self.r(self.lo + q * self.p, self.p), :], self.Z.at[nz - 1 - d], dev,
                          self.i, self.j + 3)

        def back(self, d):
            return remote(self.T, self.H.at[self.r(g * self.p, self.p), :], zpeer(d)[1], self.i, self.j + 4)

        def at(self):
            return red_out.at[self.r(self.start + self.lo, self.held), :]

        def xback(self):
            return remote(self.H, self.at(), xn, self.i, self.j + 5)

        def keep(self):
            return local(self.H, self.at(), self.keeping)

        def add(self, slot, rows, v):
            self.G[slot, rows, :] = (self.G[slot, rows, :].astype(F32) + v.astype(F32)).astype(BF16)

        def begin(self):
            for q in range(2):
                self.core(q).start()

        def add_core(self):
            sent(self.A, self.i)
            got(self.A, self.j)
            whole = slice(0, self.rows)
            self.add(other, whole, self.A[oy])
            if self.kind != "xyz":
                self.y().start()
            self.add(w, whole, self.A[yi])
            if self.kind == "xyz":
                self.x_go()

        def x_go(self):
            for cp in self.xs():
                cp.start()

        def x_wait(self):
            sent(self.X, self.i)
            got(self.X, self.j + 2)

        def x_add(self):
            self.x_wait()
            for n, v in reversed(list(enumerate(self.slots))):
                self.add(v, self.r(self.lo, self.held), self.X[n])
                if n == 1:
                    self.y().start()

        def y_add(self):
            self.y().wait()
            if self.kind == "xyz":
                self.add(w, self.r(self.lo, self.held), self.B[...])
            else:
                self.add(w, slice(0, self.rows), self.B[...])

        def z_go(self):
            for d in range(1, nz):
                self.z(d).start()

        def z_sum(self):
            sent(self.Z, self.i)
            got(self.Z, self.j + 3)
            tot = self.G[w, self.r(self.lo + g * self.p, self.p), :].astype(F32)
            for d in range(nz - 1):
                tot = tot + self.Z[d].astype(F32)
            return tot.astype(BF16)

        def z_back(self, tot):
            self.T[...] = tot
            self.H[self.r(g * self.p, self.p), :] = tot
            for d in range(1, nz):
                self.back(d).start()

        def step(self, n):
            if n == 0:
                self.begin()
            elif n == 1:
                self.add_core()
            elif n == 2:
                if self.kind == "xyz":
                    self.x_add()
                else:
                    self.y_add()
                    self.x_go() if self.kind == "yxz" else self.z_go()
            elif n == 3:
                if self.kind == "xyz":
                    self.y_add()
                    self.z_go()
                elif self.kind == "yxz":
                    self.x_add()
                    self.z_go()
                else:
                    self.T[...] = self.z_sum()
                    self.x_go()
            elif n == 4:
                if self.kind == "yz":
                    self.x_wait()
                    self.z_back((self.T[...].astype(F32) + self.X[...].astype(F32)).astype(BF16))
                else:
                    self.z_back(self.z_sum())
            elif n == 5:
                sent(self.Z, self.i)
                got(self.Z, self.j + 4)
                if self.kind != "yz":
                    self.xback().start()
                self.keep().start()
            else:
                if self.kind != "yz":
                    self.xback().wait()
                self.keep().wait()

    qs, qk, qr, qp = cs.take(4), cs.take(4), cr.take(16), QROWS // ne

    def q_core(k, q):
        return remote(m.QS.at[k, 2 * q + oc], m.QG.at[k, q, pl.ds(al(c * 192, 64), 192), :], sib, qs + k, qr + 4 * k)

    def q_y(k):
        return remote(m.QG.at[k, oy], m.QB.at[k], yn, qs + k, qr + 4 * k + 1)

    def q_rs(k, d):
        q, dev = peer(d)
        return remote(m.QG.at[k, yi, pl.ds(al(q * qp, 16), qp), :], m.QC.at[k, ne - 1 - d], dev, qs + k, qr + 4 * k + 2)

    def q_at(k):
        return red_out.at[pl.ds(al(QSTART + k * QROWS + e * qp, 16), qp), :]

    def q_ag(k, d):
        return remote(m.QT.at[k], q_at(k), peer(d)[1], qs + k, qr + 4 * k + 3)

    def q_keep(k):
        return local(m.QT.at[k], q_at(k), qk + k)

    def q0(k):
        for q in range(2):
            q_core(k, q).start()
        for q in range(2):
            m.QG[k, q, pl.ds(al(c * 192, 64), 192), :] = m.QS[k, 2 * q + c]

    def q1(k):
        half = m.QG.at[k, :, 0:192, :]
        sent(half, qs + k)
        got(half, qr + 4 * k)
        q_y(k).start()

    def q2(k):
        q_y(k).wait()
        m.QG[k, yi] = (m.QG[k, yi].astype(F32) + m.QB[k].astype(F32)).astype(BF16)
        for d in range(1, ne):
            q_rs(k, d).start()

    def q3(k):
        sent(m.QC.at[k], qs + k)
        got(m.QC.at[k], qr + 4 * k + 2)
        tot = m.QG[k, yi, pl.ds(al(e * qp, 16), qp), :].astype(F32)
        for d in range(ne - 1):
            tot = tot + m.QC[k, d].astype(F32)
        m.QT[k] = tot.astype(BF16)
        for d in range(1, ne):
            q_ag(k, d).start()
        q_keep(k).start()

    def q4(k):
        sent(m.QC.at[k], qs + k)
        got(m.QC.at[k], qr + 4 * k + 3)
        q_keep(k).wait()

    chunks = [Chunk(k) for k in range(5)]
    chain = (q0, q1, q2, q3, q4)

    def events(key):
        for k, n in PLAN.get(key, ()):
            if k == 9:
                swap_go(m.dup, y_out, iy, n, 128)
            elif k < 5:
                chunks[k].step(n)
            else:
                chain[n](k - 5)

    def when_events(tag, v, values):
        for u in values:
            if (tag, u) in PLAN:
                @pl.when(v == u)
                def _():
                    events((tag, u))

    g2, b2, bd = row(2), row(3), row(4)

    def c1(t, _):
        rows = pl.ds(al(t * 512, 512), 512)
        mid = m.xs[rows, :].astype(F32) + dg(m.ot[t], m.wo[...], 0, 0)
        xc = mid - rowmean(mid)
        r = lax.rsqrt(rowmean(xc * xc) + EPS)
        nv = xc * r
        m.n2[rows, :] = nv
        m.rs[rows, :] = jnp.broadcast_to(r, (512, 128))
        av = (nv * g2 + b2).astype(BF16)
        m.a2[rows, :] = av
        m.a2t[:, rows] = av.T
        dyv = m.dys[rows, :]
        m.dyt[:, rows] = dyv.T
        m.gg[4:5, :] += colsum(dyv.astype(F32))
        m.ya[rows, :] = mid + bd
        m.da[rows, :] = jnp.zeros((512, 512), F32)
        return 0

    swap_wait(m.dys, idy)
    lax.fori_loop(0, 2, c1, 0)

    def c2(f, _):
        for u in range(4):
            @pl.when(f == u)
            def _():
                if u == 0:
                    sent(big8, isib[0])
                    got(big8, isib[1])
                got(big2, ifr + u)
        bu = jnp.concatenate([m.vec[s, pl.ds(5 + f, 1), :] for s in range(4)], axis=1)
        wuf, wdf = m.wu[f], m.wd[f]
        up = dg(m.a2[...], wuf, 1, 0) + bu
        u2 = up * up
        th = jnp.tanh(up * (K0 + (K0 * K1) * u2))
        hp = 0.5 + 0.5 * th
        av = (up * hp).astype(BF16)
        m.act[...] = av
        m.ya[...] += dg(av, wdf, 1, 0)
        dact = dg(m.dys[...], wdf, 1, 1)
        gp = hp + (0.5 * up) * (1.0 - th * th) * (K0 + (3 * K0 * K1) * u2)
        dv = (dact * gp).astype(BF16)
        m.dup[...] = dv
        m.gbu[f, 0:1, :] = colsum(dv.astype(F32))
        m.da[...] += dg(dv, wuf, 1, 1)

        @pl.when(f == 0)
        def _():
            g_forward(*pieces[8:])

        when_events("f", f, range(4))
        gd = dg(m.dyt[...], m.act[...], 1, 0).astype(BF16)
        for s in range(4):
            m.FG[f, s, 0:512, :] = gd[:, s * 128:(s + 1) * 128]
        gu = dg(m.a2t[...], m.dup[...], 1, 0).astype(BF16)
        for s in range(4):
            for b in range(4):
                m.FG[f, s, 512 + b * 128:640 + b * 128, :] = gu[s * 128:(s + 1) * 128, b * 128:(b + 1) * 128]
        when_events("g", f, range(4))
        return 0

    lax.fori_loop(0, 4, c2, 0)
    for p in pieces[:2]:
        g_y(p).wait_send()
    sent(big8, iys)
    sent(big8, ifs)
    yst, dmid = m.dup, m.act
    idx = pair()

    def d_piece(t):
        return remote(m.dst.at[t], m.do.at[2 * c + t], sib, *idx)

    def c3(t, _):
        rows = pl.ds(al(t * 512, 512), 512)
        yst[rows, :] = m.ya[rows, :].astype(BF16)
        dav, nv, r = m.da[rows, :], m.n2[rows, :], m.rs[rows, 0:1]
        m.gg[2:3, :] += colsum(dav * nv)
        m.gg[3:4, :] += colsum(dav)
        gr = dav * g2
        dn = r * (gr - rowmean(gr) - nv * rowmean(gr * nv))
        dm = (m.dys[rows, :].astype(F32) + dn).astype(BF16)
        dmid[rows, :] = dm
        m.dst[t] = dg(m.wo[pl.ds(al(oc * 256, 256), 256), :], dm, 1, 1).astype(BF16)
        d_piece(t).start()
        m.do[2 * c + t] = dg(m.wo[pl.ds(al(c * 256, 256), 256), :], dm, 1, 1).astype(BF16)

        when_events("c", t, range(2))
        return 0

    lax.fori_loop(0, 2, c3, 0)
    go = (dg(m.ot[0], dmid[0:512, :], 1, 0) + dg(m.ot[1], dmid[512:1024, :], 1, 0)).astype(BF16)
    for s in range(4):
        for b in range(4):
            m.OG[s, b * 128:(b + 1) * 128, :] = go[s * 128:(s + 1) * 128, b * 128:(b + 1) * 128]
    events("go")
    sent(m.dst, idx[0])
    got(m.dst, idx[1])

    ixq = pair()

    def x_piece(h, b):
        return remote(m.xst.at[h, b], m.dqt.at[pl.ds(al(c * 768 + h * 192, 64), 192), pl.ds(b * 512, 512)], sib,
                      *ixq)

    def x_start(h):
        hrows = pl.ds(al(h * 192, 64), 192)
        for b in range(2):
            m.xst[h, b] = m.dq[canon_of(2 * oc + b), hrows, :]
            x_piece(h, b).start()
        for b in range(2):
            m.dqt[pl.ds(al(c * 768 + h * 192, 64), 192), b * 512:(b + 1) * 512] = m.dq[canon_of(2 * c + b), hrows, :]

    def q_grad(h):
        hrows = pl.ds(al(h * 192, 64), 192)
        gq = None
        for i in range(4):
            part = dg(m.dq[i, hrows, :], m.a1[phys[i]], 1, 0)
            gq = part if gq is None else gq + part
        gq = gq.astype(BF16)
        for s in range(4):
            m.QS[h, s] = gq[:, s * 128:(s + 1) * 128]

    def bwd_head(h, _):
        hr = pl.ds(al(h * HD, HD), HD)
        kt = jnp.concatenate([m.qkv[phys[j], rows_of(h, 1), :] for j in range(4)], axis=1)
        vt = jnp.concatenate([m.qkv[phys[j], rows_of(h, 2), :] for j in range(4)], axis=1)
        kn = kt.T
        tri = key_le_query(256, 1)
        for i in reversed(range(8)):
            L, b, cs = (i + 1) * 256, i // 2, slice((i % 2) * 256, (i % 2) * 256 + 256)
            q = m.qkv[phys[b], rows_of(h, 0), cs]
            gr = m.do[phys[b], hr, cs]
            ls = m.lse[b, pl.ds(h, 1), cs]
            delta = colsum(gr.astype(F32) * m.o[b, hr, cs])
            lsb = jnp.broadcast_to(ls, (128, 256)).T[:, 0:1]
            deb = jnp.broadcast_to(delta, (128, 256)).T[:, 0:1]
            p = jnp.exp(dg(q.T, kt[:, :L], 1, 0) - lsb)
            pd = jnp.where(tri, p[:, L - 256:], 0.0)
            p = jnp.concatenate([p[:, :L - 256], pd], axis=1) if i else pd
            dp = dg(gr.T, vt[:, :L], 1, 0)
            ds = (p * (dp - deb)).astype(BF16)
            p = p.astype(BF16)
            m.dq[b, rows_of(h, 0), cs] = dg(ds, kn[:L], 1, 0).T.astype(BF16)
            dk, dv = dg(q, ds, 1, 0), dg(gr, p, 1, 0)
            if i == 7:
                m.dkv[0:64, :] = dk
                m.dkv[64:128, :] = dv
            else:
                m.dkv[0:64, :L] += dk
                m.dkv[64:128, :L] += dv
            if i in (6, 4):
                when_events("dD"[i == 4], h, range(4))
        for j in range(4):
            m.dq[j, rows_of(h, 1), :] = m.dkv[0:64, j * BLK:(j + 1) * BLK].astype(BF16)
            m.dq[j, rows_of(h, 2), :] = m.dkv[64:128, j * BLK:(j + 1) * BLK].astype(BF16)
        x_start(h)
        when_events("e", h, range(4))
        q_grad(h)
        when_events("q", h, range(4))
        return 0

    lax.fori_loop(0, 4, bwd_head, 0)

    sent(m.xst, ixq[0])
    got(m.xst, ixq[1])
    events("x")
    wgst = m.dys

    def e1(t, _):
        rows = pl.ds(al(t * 256, 256), 256)
        nv, r = m.n1[rows, :], m.r1[rows, 0:1]
        dav = dg(m.dqt[:, rows], m.wt[...], 0, 0)
        m.gg[0:1, :] += colsum(dav * nv)
        m.gg[1:2, :] += colsum(dav)
        gr = dav * g1
        dn = r * (gr - rowmean(gr) - nv * rowmean(gr * nv))
        wgst[rows, :] = (dmid[rows, :].astype(F32) + dn).astype(BF16)
        swap_go(wgst, wg_out, iw, t, 128)
        when_events("w", t, range(4))
        return 0

    lax.fori_loop(0, 4, e1, 0)
    for s in range(4):
        for k in range(5):
            m.gv[s, k:k + 1, :] = m.gg[k:k + 1, s * 128:(s + 1) * 128]
        for f in range(4):
            m.gv[s, 5 + f:6 + f, :] = m.gbu[f, 0:1, s * 128:(s + 1) * 128]
    ivx, ivy, iva = pair(), pair(), pair()
    vx = [remote(m.gv.at[2 * q + oc], m.gvr.at[q], sib, *ivx) for q in range(2)]
    vy = remote(m.gv.at[other], m.gvy, yn, *ivy)
    va = [remote(m.gv.at[w], m.gva.at[e], peer(d)[1], *iva) for d in range(1, ne)]
    for cp in vx:
        cp.start()
    for t in range(4, 6):
        swap_go(wgst, wg_out, iw, t, 128)
    sent(m.gvr, ivx[0])
    got(m.gvr, ivx[1])
    for q in range(2):
        m.gv[2 * q + c] = m.gv[2 * q + c] + m.gvr[q]
    vy.start()
    events("tail")
    vy.wait()
    m.gv[w] = m.gv[w] + m.gvy[...]
    m.gva[e] = m.gv[w]
    for cp in va:
        cp.start()
    for t in range(6, 8):
        swap_go(wgst, wg_out, iw, t, 128)
    sent(m.gva.at[0:ne - 1], iva[0])
    got(m.gva.at[0:ne - 1], iva[1])
    tot = m.gva[0]
    for d in range(1, ne):
        tot = tot + m.gva[d]
    vec_out[...] = tot
    for k in range(5):
        chunks[k].step(6)

    def fin(t, _):
        q4(t)
        return 0

    lax.fori_loop(0, 4, fin, 0)
    swap_wait(m.dup, iy)
    swap_wait(wgst, iw)


def layer(nz, *ops):
    sc = scratch(nz)
    names = tuple(sc)
    sd = jax.ShapeDtypeStruct
    any_ = pl.BlockSpec(memory_space=pl.ANY)
    vm = pl.BlockSpec(memory_space=pltpu.VMEM)
    return pl.pallas_call(
        functools.partial(body, nz, names),
        out_shape=(sd((1024, 512), BF16), sd((1024, 512), BF16), sd((ROWS, 128), BF16), sd((16, 128), F32)),
        in_specs=[any_] * 14,
        out_specs=(any_, any_, any_, vm),
        scratch_shapes=[sc[n] for n in names] + [pltpu.SemaphoreType.DMA((NSEND,)), pltpu.SemaphoreType.DMA((NRECV,))],
        compiler_params=pltpu.CompilerParams(collective_id=0, has_side_effects=True, vmem_limit_bytes=VLIM),
        name="layer",
    )(*ops)


def finish_body(y_h, wg_h, red_h, v, yo_h, wgo_h, gq_h, go_h, gu_h, gd_h, v1, v2, v3, v4, vu, vd,
                wg, red, wgo, yv, gq, go, gu, gd, sem):
    def cp(a, b, i):
        return pltpu.make_async_copy(a, b, sem.at[i])

    def red_in(k):
        return cp(red_h.at[pl.ds(k * 1024, 1024)], red.at[pl.ds(k * 1024, 1024)], k)

    def wg_in(k):
        return cp(wg_h.at[pl.ds(k * 256, 256)], wg.at[pl.ds(k * 256, 256)], 6 + k)

    outs = []

    def put(a, b):
        o = cp(a, b, 10 + len(outs))
        o.start()
        outs.append(o)

    def y_in(k):
        return cp(y_h.at[pl.ds(k * 512, 512)], yv.at[pl.ds(k * 512, 512)], 22 + k)

    for k in range(4):
        wg_in(k).start()
    for k in range(2):
        y_in(k).start()
    for k in range(6):
        red_in(k).start()
    for r, k in ((v1, 0), (v2, 1), (v3, 2), (v4, 3), (vd, 4)):
        r[...] = v[k:k + 1, :]
    vu[...] = v[5:9, :]
    for k in range(4):
        wg_in(k).wait()
        rows = slice(k * 256, (k + 1) * 256)
        wgo[rows, :] = wg[rows, :].astype(F32)
        put(wgo.at[rows], wgo_h.at[rows])
    for k in range(2):
        y_in(k).wait()
        put(yv.at[pl.ds(k * 512, 512)], yo_h.at[pl.ds(k * 512, 512)])
    for f in range(4):
        red_in(f).wait()
        gd[f * 128:(f + 1) * 128, :] = red[f * 1024:f * 1024 + 512, :].astype(F32).T
        put(gd.at[f * 128:(f + 1) * 128], gd_h.at[f * 128:(f + 1) * 128])
        for s in range(4):
            gu[:, s * 512 + f * 128:s * 512 + (f + 1) * 128] = red[f * 1024 + 512 + s * 128:f * 1024 + 640 + s * 128, :].astype(F32)
    put(gu, gu_h)
    red_in(4).wait()
    for b in range(4):
        go[:, b * 128:(b + 1) * 128] = red[OSTART + b * 128:OSTART + (b + 1) * 128, :].astype(F32)
    put(go, go_h)
    red_in(5).wait()
    for hp in range(2):
        for cc in range(2):
            for part in range(3):
                r = QSTART + hp * 768 + cc * 192 + part * 64
                blk = jnp.concatenate([red[r:r + 64, :], red[r + 384:r + 448, :]], axis=0).astype(F32).T
                if part == 0:
                    blk = blk * 0.125
                k = part * 512 + cc * 256 + hp * 128
                gq[:, k:k + 128] = blk
    put(gq, gq_h)
    for o in outs:
        o.wait()


def finish(y, wg, red, v):
    sd = jax.ShapeDtypeStruct
    any_ = pl.BlockSpec(memory_space=pl.ANY)
    vm = pl.BlockSpec(memory_space=pltpu.VMEM)
    one = sd((1, 128), F32)
    big = (sd((128, 1536), F32), sd((128, 512), F32), sd((128, 2048), F32), sd((512, 512), F32))
    return pl.pallas_call(
        finish_body,
        out_shape=(sd((1024, 512), BF16), sd((1024, 512), F32)) + big + (one, one, one, one, sd((4, 128), F32), one),
        in_specs=[any_] * 3 + [vm],
        out_specs=(any_,) * 6 + (vm,) * 6,
        scratch_shapes=[pltpu.VMEM((1024, 512), BF16), pltpu.VMEM((ROWS, 128), BF16), pltpu.VMEM((1024, 512), F32),
                        pltpu.VMEM((1024, 512), BF16)]
        + [pltpu.VMEM(b.shape, F32) for b in big] + [pltpu.SemaphoreType.DMA((24,))],
        compiler_params=pltpu.CompilerParams(vmem_limit_bytes=VLIM), name="finish",
    )(y, wg, red, v)


def on_chip(words, qkv_weight, out_weight, up_weight, down_weight, norm1_gain, norm1_bias, norm2_gain,
            norm2_bias, up_bias, down_bias, cotangent, seg_map, off_map):
    nz = lax.axis_size("group")
    r = lambda v: v.reshape(-1, 128)
    y, wg, red, v = layer(nz, words[0], cotangent[0], qkv_weight, out_weight, up_weight, down_weight.reshape(4, 128, 512),
                          r(norm1_gain), r(norm1_bias), r(norm2_gain), r(norm2_bias), r(down_bias), r(up_bias),
                          seg_map, off_map)
    y, wg, gq, go, gu, gd, v1, v2, v3, v4, vu, vd = finish(y, wg, red, v)
    f = lambda t: t.reshape(-1)
    return y[None], wg[None], gq, go, gu, gd, f(v1), f(v2), f(v3), f(v4), f(vu), f(vd)


HEADS = 8
HEAD_DIM = 64


eps = 1e-05
neg_big = -1e30


def passed_along(value, axis, by):
    peers = lax.axis_size(axis)
    return lax.ppermute(value, axis, [(i, (i + by) % peers) for i in range(peers)])


def layer_norm(features, norm_gain, norm_shift):
    row_mean = jnp.mean(features, axis=-1, keepdims=True)
    centred = features - row_mean
    inv_scale = lax.rsqrt(jnp.mean(centred * centred, axis=-1, keepdims=True) + eps)
    return centred * inv_scale * norm_gain + norm_shift


def gelu_tanh(features):
    return jax.nn.gelu(features, approximate=True)


def rows_of(array, block_id):
    return lax.dynamic_slice_in_dim(array, block_id * BLK, BLK, 0)


def cols_of(array, block_id):
    return lax.dynamic_slice_in_dim(array, block_id * BLK, BLK, 1)


def add_rows(array, update, block_id):
    return lax.dynamic_update_slice_in_dim(
        array, rows_of(array, block_id) + update, block_id * BLK, 0
    )


def put_rows(array, update, block_id):
    return lax.dynamic_update_slice_in_dim(array, update, block_id * BLK, 0)


def put_cols(array, update, block_id):
    return lax.dynamic_update_slice_in_dim(array, update, block_id * BLK, 1)


def block_info(seg_row, off_row, block_id):
    segment = lax.dynamic_index_in_dim(seg_row, block_id, 0, keepdims=False)
    position = lax.dynamic_index_in_dim(off_row, block_id, 0, keepdims=False)
    return (segment, position)


def pair_live(seg_row, off_row, query_block, key_block):
    query_seg, query_offset = block_info(seg_row, off_row, query_block)
    key_seg, key_offset = block_info(seg_row, off_row, key_block)
    return (query_seg == key_seg) & (key_offset <= query_offset) | (key_seg == 0) & (query_seg != 0)


def pair_mask(seg_row, off_row, query_block, key_block):
    query_seg, query_offset = block_info(seg_row, off_row, query_block)
    key_seg, key_offset = block_info(seg_row, off_row, key_block)
    row_ids = lax.broadcasted_iota(jnp.int32, (BLK, BLK), 0)
    col_ids = lax.broadcasted_iota(jnp.int32, (BLK, BLK), 1)
    query_pos = query_offset * BLK + row_ids
    key_pos = key_offset * BLK + col_ids
    return (query_seg == key_seg) & (key_pos <= query_pos) | (key_seg == 0) & (query_seg != 0)


def split_heads(tile_rows):
    return tile_rows.reshape(tile_rows.shape[0], HEADS, HEAD_DIM)


def tile_scores(query_tile, key_tile, allowed):
    raw_scores = jnp.einsum(
        "qhd,khd->hqk",
        split_heads(query_tile),
        split_heads(key_tile),
        preferred_element_type=jnp.float32,
    )
    return jnp.where(allowed[None], raw_scores * HEAD_DIM ** (-0.5), neg_big)


def tile_back(query_tile, key_tile, value_tile, grad_tile, norm_tile, delta_tile, allowed):
    scores = tile_scores(query_tile, key_tile, allowed)
    exp_terms = jnp.where(allowed[None], jnp.exp(scores - norm_tile[:, :, None]), 0.0)
    d_probs = jnp.einsum(
        "qhd,khd->hqk",
        split_heads(grad_tile),
        split_heads(value_tile),
        preferred_element_type=jnp.float32,
    )
    d_scores = (exp_terms * (d_probs - delta_tile[:, :, None])).astype(jnp.bfloat16)
    return (exp_terms.astype(jnp.bfloat16), d_scores)


def query_grad(d_scores, key_tile):
    part_rows = jnp.einsum(
        "hqk,khd->qhd", d_scores, split_heads(key_tile), preferred_element_type=jnp.float32
    )
    return part_rows.reshape(BLK, -1) * HEAD_DIM ** (-0.5)


def key_grad(d_scores, query_tile):
    part_rows = jnp.einsum(
        "hqk,qhd->khd", d_scores, split_heads(query_tile), preferred_element_type=jnp.float32
    )
    return part_rows.reshape(BLK, -1) * HEAD_DIM ** (-0.5)


def value_grad(probs_low, grad_tile):
    part_rows = jnp.einsum(
        "hqk,qhd->khd", probs_low, split_heads(grad_tile), preferred_element_type=jnp.float32
    )
    return part_rows.reshape(BLK, -1)


def unchanged(running):
    return running


def on_device(
    words,
    qkv_weight,
    out_weight,
    up_weight,
    down_weight,
    norm1_gain,
    norm1_bias,
    norm2_gain,
    norm2_bias,
    up_bias,
    down_bias,
    cotangent,
    seg_map,
    off_map,
):
    gathered = (
        lax.all_gather(qkv_weight, "wshard", axis=0, tiled=True),
        lax.all_gather(out_weight, "wshard", axis=0, tiled=True),
        lax.all_gather(up_weight, "wshard", axis=0, tiled=True),
        lax.all_gather(down_weight, "wshard", axis=0, tiled=True),
        lax.all_gather(norm1_gain, "wshard", axis=0, tiled=True),
        lax.all_gather(norm1_bias, "wshard", axis=0, tiled=True),
        lax.all_gather(norm2_gain, "wshard", axis=0, tiled=True),
        lax.all_gather(norm2_bias, "wshard", axis=0, tiled=True),
        lax.all_gather(up_bias, "wshard", axis=0, tiled=True),
        lax.all_gather(down_bias, "wshard", axis=0, tiled=True),
    )
    w_qkv, w_out, w_up, w_down = (gathered[0], gathered[1], gathered[2], gathered[3])
    gain1 = gathered[4].astype(jnp.float32)
    shift1 = gathered[5].astype(jnp.float32)
    gain2 = gathered[6].astype(jnp.float32)
    shift2 = gathered[7].astype(jnp.float32)
    bias_up = gathered[8].astype(jnp.float32)
    bias_down = gathered[9].astype(jnp.float32)
    seg_row = seg_map[0]
    off_row = off_map[0]
    cycle_place = lax.axis_index("ctx")
    cycle_count = lax.axis_size("ctx")
    inputs = words[0].astype(jnp.float32)
    local_rows = inputs.shape[0]
    local_blocks = local_rows // BLK
    first_block = cycle_place * local_blocks
    width = inputs.shape[1]
    normed1, pull_norm1 = jax.vjp(layer_norm, inputs, gain1, shift1)
    act1 = normed1.astype(jnp.bfloat16)
    qkv = jnp.dot(act1, w_qkv, preferred_element_type=jnp.float32)
    query_rows = qkv[:, :width].astype(jnp.bfloat16)
    key_rows = qkv[:, width : 2 * width].astype(jnp.bfloat16)
    value_rows = qkv[:, 2 * width :].astype(jnp.bfloat16)
    start_state = (
        jnp.full((HEADS, local_rows), neg_big, jnp.float32),
        jnp.zeros((HEADS, local_rows), jnp.float32),
        jnp.zeros((local_rows, width), jnp.float32),
    )
    shard_keys = lax.all_gather(key_rows, "ctx", axis=0, tiled=True)
    shard_values = lax.all_gather(value_rows, "ctx", axis=0, tiled=True)
    key_blocks = shard_keys.shape[0] // BLK

    def online_visit_pair(pair_index, state):
        row_block = pair_index // key_blocks
        col_block = pair_index % key_blocks
        query_block = first_block + row_block
        key_block = col_block

        def online_update_tile(state):
            run_max, run_sum, accum = state
            allowed = pair_mask(seg_row, off_row, query_block, key_block)
            scores = tile_scores(
                rows_of(query_rows, row_block), rows_of(shard_keys, col_block), allowed
            )
            old_max = cols_of(run_max, row_block)
            old_sum = cols_of(run_sum, row_block)
            new_max = jnp.maximum(old_max, jnp.max(scores, axis=-1))
            exp_terms = jnp.where(allowed[None], jnp.exp(scores - new_max[:, :, None]), 0.0)
            factor = jnp.exp(old_max - new_max)
            new_sum = old_sum * factor + jnp.sum(exp_terms, axis=-1)
            part_rows = jnp.einsum(
                "hqk,khd->qhd",
                exp_terms.astype(jnp.bfloat16),
                split_heads(rows_of(shard_values, col_block)),
                preferred_element_type=jnp.float32,
            )
            old_rows = rows_of(accum, row_block).reshape(BLK, HEADS, HEAD_DIM)
            new_rows = (old_rows * factor.T[:, :, None] + part_rows).reshape(BLK, -1)
            return (
                put_cols(run_max, new_max, row_block),
                put_cols(run_sum, new_sum, row_block),
                put_rows(accum, new_rows, row_block),
            )

        return lax.cond(
            pair_live(seg_row, off_row, query_block, key_block),
            online_update_tile,
            unchanged,
            state,
        )

    run_max, run_sum, accum = lax.fori_loop(
        0, local_blocks * key_blocks, online_visit_pair, start_state
    )
    log_norm = run_max + jnp.log(run_sum)
    attended = (accum.reshape(local_rows, HEADS, HEAD_DIM) / run_sum.T[:, :, None]).reshape(
        local_rows, width
    )
    attended_low = attended.astype(jnp.bfloat16)
    middle = inputs + jnp.dot(attended_low, w_out, preferred_element_type=jnp.float32)
    normed2, pull_norm2 = jax.vjp(layer_norm, middle, gain2, shift2)
    act2 = normed2.astype(jnp.bfloat16)
    hidden = jnp.dot(act2, w_up, preferred_element_type=jnp.float32) + bias_up
    gelu_out, pull_gelu = jax.vjp(gelu_tanh, hidden)
    gelu_low = gelu_out.astype(jnp.bfloat16)
    output = (
        middle + jnp.dot(gelu_low, w_down, preferred_element_type=jnp.float32) + bias_down
    ).astype(jnp.bfloat16)
    upstream = cotangent[0]
    upstream_f = upstream.astype(jnp.float32)
    grad_down = jnp.einsum("nf,nd->fd", gelu_low, upstream, preferred_element_type=jnp.float32)
    grad_bias_down = jnp.sum(upstream_f, axis=0)
    d_gelu = jnp.einsum("nd,fd->nf", upstream, w_down, preferred_element_type=jnp.float32)
    d_hidden = pull_gelu(d_gelu)[0].astype(jnp.bfloat16)
    grad_up = jnp.einsum("nd,nf->df", act2, d_hidden, preferred_element_type=jnp.float32)
    grad_bias_up = jnp.sum(d_hidden.astype(jnp.float32), axis=0)
    d_act2 = jnp.einsum("nf,df->nd", d_hidden, w_up, preferred_element_type=jnp.float32)
    d_middle_norm, grad_gain2, grad_shift2 = pull_norm2(d_act2)
    d_middle = (upstream_f + d_middle_norm).astype(jnp.bfloat16)
    grad_out = jnp.einsum("nd,ne->de", attended_low, d_middle, preferred_element_type=jnp.float32)
    d_attended = jnp.einsum(
        "ne,de->nd", d_middle, w_out, preferred_element_type=jnp.float32
    ).astype(jnp.bfloat16)
    row_delta = jnp.sum(
        (d_attended.astype(jnp.float32) * attended).reshape(local_rows, HEADS, HEAD_DIM), axis=-1
    ).T
    zero_rows = jnp.zeros((local_rows, width), jnp.float32)

    def attend_back(cycle_turn, cycle_state):
        held_keys, held_values, held_dk, held_dv, d_query = cycle_state
        source = (cycle_place - cycle_turn) % cycle_count

        def attend_visit_pair(pair_index, partial_value):
            row_block = pair_index // local_blocks
            col_block = pair_index % local_blocks
            query_block = first_block + row_block
            key_block = source * local_blocks + col_block

            def attend_update_tile(partial_value):
                dk_acc, dv_acc, dq_acc = partial_value
                query_tile = rows_of(query_rows, row_block)
                key_tile = rows_of(held_keys, col_block)
                grad_tile = rows_of(d_attended, row_block)
                allowed = pair_mask(seg_row, off_row, query_block, key_block)
                probs_low, d_scores = tile_back(
                    query_tile,
                    key_tile,
                    rows_of(held_values, col_block),
                    grad_tile,
                    cols_of(log_norm, row_block),
                    cols_of(row_delta, row_block),
                    allowed,
                )
                dq_acc = add_rows(dq_acc, query_grad(d_scores, key_tile), row_block)
                dk_acc = add_rows(dk_acc, key_grad(d_scores, query_tile), col_block)
                dv_acc = add_rows(dv_acc, value_grad(probs_low, grad_tile), col_block)
                return (dk_acc, dv_acc, dq_acc)

            return lax.cond(
                pair_live(seg_row, off_row, query_block, key_block),
                attend_update_tile,
                unchanged,
                partial_value,
            )

        held_dk, held_dv, d_query = lax.fori_loop(
            0, local_blocks * local_blocks, attend_visit_pair, (held_dk, held_dv, d_query)
        )
        return (held_keys, held_values, held_dk, held_dv, d_query)

    def pass_grads(held_dk, held_dv):
        return (
            passed_along(held_dk.astype(jnp.bfloat16), "ctx", 1).astype(held_dk.dtype),
            passed_along(held_dv.astype(jnp.bfloat16), "ctx", 1).astype(held_dv.dtype),
        )

    def turn_step(cycle_turn, cycle_state):
        held_keys, held_values, held_dk, held_dv, d_query = attend_back(cycle_turn, cycle_state)
        held_keys, held_values = passed_along((held_keys, held_values), "ctx", 1)
        held_dk, held_dv = pass_grads(held_dk, held_dv)
        return (held_keys, held_values, held_dk, held_dv, d_query)

    cycle_state = lax.fori_loop(
        0, cycle_count - 1, turn_step, (key_rows, value_rows, zero_rows, zero_rows, zero_rows)
    )
    cycle_state = attend_back(cycle_count - 1, cycle_state)
    d_keys, d_values = pass_grads(cycle_state[2], cycle_state[3])
    d_query = cycle_state[4]
    d_qkv = jnp.concatenate(
        [d_query.astype(jnp.bfloat16), d_keys.astype(jnp.bfloat16), d_values.astype(jnp.bfloat16)],
        axis=1,
    )
    grad_qkv = jnp.einsum("nd,nf->df", act1, d_qkv, preferred_element_type=jnp.float32)
    d_act1 = jnp.einsum("nf,df->nd", d_qkv, w_qkv, preferred_element_type=jnp.float32)
    d_inputs_norm, grad_gain1, grad_shift1 = pull_norm1(d_act1)
    words_grad = d_middle.astype(jnp.float32) + d_inputs_norm
    shards = (
        lax.psum_scatter(
            grad_qkv.astype(jnp.bfloat16), "wshard", scatter_dimension=0, tiled=True
        ).astype(jnp.float32),
        lax.psum_scatter(
            grad_out.astype(jnp.bfloat16), "wshard", scatter_dimension=0, tiled=True
        ).astype(jnp.float32),
        lax.psum_scatter(
            grad_up.astype(jnp.bfloat16), "wshard", scatter_dimension=0, tiled=True
        ).astype(jnp.float32),
        lax.psum_scatter(
            grad_down.astype(jnp.bfloat16), "wshard", scatter_dimension=0, tiled=True
        ).astype(jnp.float32),
        lax.psum_scatter(
            grad_gain1.astype(jnp.bfloat16), "wshard", scatter_dimension=0, tiled=True
        ).astype(jnp.float32),
        lax.psum_scatter(
            grad_shift1.astype(jnp.bfloat16), "wshard", scatter_dimension=0, tiled=True
        ).astype(jnp.float32),
        lax.psum_scatter(
            grad_gain2.astype(jnp.bfloat16), "wshard", scatter_dimension=0, tiled=True
        ).astype(jnp.float32),
        lax.psum_scatter(
            grad_shift2.astype(jnp.bfloat16), "wshard", scatter_dimension=0, tiled=True
        ).astype(jnp.float32),
        lax.psum_scatter(
            grad_bias_up.astype(jnp.bfloat16), "wshard", scatter_dimension=0, tiled=True
        ).astype(jnp.float32),
        lax.psum_scatter(
            grad_bias_down.astype(jnp.bfloat16), "wshard", scatter_dimension=0, tiled=True
        ).astype(jnp.float32),
    )
    totals = lax.psum(
        (
            shards[0],
            shards[1],
            shards[2],
            shards[3],
            shards[4],
            shards[5],
            shards[6],
            shards[7],
            shards[8],
            shards[9],
        ),
        ("group", "ctx"),
    )
    return (
        output[None],
        words_grad[None],
        totals[0],
        totals[1],
        totals[2],
        totals[3],
        totals[4],
        totals[5],
        totals[6],
        totals[7],
        totals[8],
        totals[9],
    )


def solution(mesh):
    chip = mesh.shape["ctx"] == 2 and mesh.shape["wshard"] == 4 and mesh.shape["group"] in (2, 4)
    return jax.shard_map(
        on_chip if chip else on_device,
        mesh=mesh,
        in_specs=(
            P(("group", "wshard"), "ctx", None),
            P("wshard", None),
            P("wshard", None),
            P("wshard", None),
            P("wshard", None),
            P("wshard"),
            P("wshard"),
            P("wshard"),
            P("wshard"),
            P("wshard"),
            P("wshard"),
            P(("group", "wshard"), "ctx", None),
            P(("group", "wshard"), None),
            P(("group", "wshard"), None),
        ),
        out_specs=(
            P(("group", "wshard"), "ctx", None),
            P(("group", "wshard"), "ctx", None),
            P("wshard", None),
            P("wshard", None),
            P("wshard", None),
            P("wshard", None),
            P("wshard"),
            P("wshard"),
            P("wshard"),
            P("wshard"),
            P("wshard"),
            P("wshard"),
        ),
        check_vma=False,
    )
```

```python
import functools
import jax
import jax.numpy as jnp
from jax import lax
from jax.experimental import pallas as pl
from jax.experimental.pallas import tpu as pltpu
from jax.sharding import PartitionSpec as P

BLK = 512
HD = 64
EPS = 1e-5
F32 = jnp.float32
BF16 = jnp.bfloat16
K0 = 0.7978845608
K1 = 0.044715
MESH = pl.DeviceIdType.MESH
VLIM = 63 * 1024 * 1024
FROWS, OROWS, QROWS = 1024, 512, 384
OSTART, QSTART, ROWS = 4096, 4608, 6144
NSEND, NRECV = 66, 90
CHUNKS = (("F0", FROWS, "yxz"), ("F1", FROWS, "xyz"), ("F2", FROWS, "xyz"), ("F3", FROWS, "yxz"), ("O", OROWS, "yxz"))


PLAN = {
    ("g", 0): ((0, 0),),
    ("f", 1): ((0, 1),),
    ("g", 1): ((1, 0),),
    ("f", 2): ((1, 1),),
    ("g", 2): ((2, 0),),
    ("f", 3): ((0, 2), (2, 1),),
    ("g", 3): ((3, 0),),
    ("c", 0): ((1, 2), (3, 1), (9, 0),),
    ("c", 1): ((0, 3), (9, 1),),
    "go": ((4, 0), (9, 2),),
    ("d", 0): ((1, 3), (4, 1), (9, 3),),
    ("D", 0): ((0, 4), (2, 2), (9, 4),),
    ("e", 0): ((3, 2), (9, 5),),
    ("q", 0): ((5, 0), (1, 4),),
    ("d", 1): ((4, 2), (5, 1), (0, 5), (9, 6),),
    ("D", 1): ((2, 3), (9, 7),),
    ("e", 1): ((1, 5), (3, 3),),
    ("q", 1): ((6, 0), (5, 2), (4, 3),),
    ("d", 2): ((2, 4), (6, 1),),
    ("D", 2): ((3, 4),),
    ("q", 2): ((7, 0), (6, 2), (4, 4),),
    ("d", 3): ((7, 1), (5, 3), (2, 5),),
    ("e", 3): ((3, 5),),
    ("q", 3): ((8, 0), (7, 2), (6, 3),),
    "x": ((4, 5), (8, 1),),
    ("w", 1): ((7, 3), (8, 2),),
    "tail": ((8, 3),),
}


def dg(a, b, ca, cb):
    return lax.dot_general(a, b, (((ca,), (cb,)), ((), ())), preferred_element_type=F32)


def colsum(v):
    return jnp.sum(v, axis=0, keepdims=True)


def rowmean(v):
    return jnp.mean(v, axis=-1, keepdims=True)


def key_le_query(n, key_axis):
    k = lax.broadcasted_iota(jnp.int32, (n, n), key_axis)
    q = lax.broadcasted_iota(jnp.int32, (n, n), 1 - key_axis)
    return k <= q


def al(v, n):
    return pl.multiple_of(v, n)


def chunk_scratch(nz, rows, kind):
    V = lambda *s: pltpu.VMEM(s, BF16)
    held = rows if kind == "yz" else rows // 2
    return dict(A=V(2, rows, 128), B=V(held if kind == "xyz" else rows, 128),
                X=V(held // nz, 128) if kind == "yz" else V(2 if kind == "xyz" else 1, held, 128),
                Z=V(nz - 1, held // nz, 128), T=V(held // nz, 128), H=V(held, 128))


def scratch(nz):
    ne = 2 * nz
    V = lambda *s, t=BF16: pltpu.VMEM(s, t)
    return dict(
        xs=V(1024, 512), dys=V(1024, 512), wt=V(1536, 512), wo=V(512, 512),
        wu=V(4, 512, 512), wd=V(4, 512, 512), vown=V(16, 128, t=F32), vec=V(4, 16, 128, t=F32),
        so=V(2, 8, 128, t=jnp.int32), sseg=V(1, 4, t=jnp.int32), soff=V(1, 4, t=jnp.int32),
        s1g=V(1, 128), s1b=V(1, 128), s2g=V(1, 128), s2b=V(1, 128), sbd=V(1, 128), sbu=V(4, 128), sm=pltpu.SMEM((8, 128), jnp.int32),
        a1=V(4, 512, 512), qkv=V(4, 768, 512), o=V(4, 256, 512, t=F32), lse=V(4, 8, 512, t=F32),
        ost=V(2, 256, 512), ot=V(2, 512, 512), n2=V(1024, 512, t=F32), rs=V(1024, 128, t=F32), a2=V(1024, 512),
        a2t=V(512, 1024), dyt=V(512, 1024), ya=V(1024, 512, t=F32), da=V(1024, 512, t=F32),
        act=V(1024, 512), dup=V(1024, 512), do=V(4, 256, 512), dst=V(2, 256, 512), dq=V(4, 768, 512),
        dkv=V(128, 2048, t=F32), xst=V(4, 2, 192, 512), dqt=V(1536, 1024),
        gv=V(4, 16, 128, t=F32), gvr=V(2, 16, 128, t=F32), gvy=V(16, 128, t=F32), gva=V(ne, 16, 128, t=F32),
        n1=V(1024, 512, t=F32), r1=V(1024, 128, t=F32), gg=V(8, 512, t=F32), gbu=V(4, 8, 512, t=F32),
        FG=V(4, 4, FROWS, 128), OG=V(4, OROWS, 128),
        **{f"{t}{q}": v for t, rows, kind in CHUNKS for q, v in chunk_scratch(nz, rows, kind).items()},
        QS=V(4, 4, 192, 128), QG=V(4, 2, QROWS, 128), QB=V(4, QROWS, 128), QC=V(4, ne - 1, QROWS // ne, 128),
        QT=V(4, QROWS // ne, 128),
    )


class Count:
    def __init__(self, most):
        self.n, self.most = 0, most

    def take(self, k=1):
        self.n += k
        assert self.n <= self.most
        return self.n - k


class Ns:
    def __init__(self, d):
        self.__dict__.update(d)


def body(nz, names, *args):
    (words_h, cot_h, wq_h, wo_h, wu_h, wd_h, n1g, n1b, n2g, n2b, bdr, bur, seg_r, off_r) = args[:14]
    y_out, wg_out, red_out, vec_out = args[14:18]
    m = Ns(dict(zip(names, args[18:18 + len(names)])))
    send, recv = args[18 + len(names):]
    cs, cr = Count(NSEND), Count(NRECV)
    ne = 2 * nz
    g, x, w = lax.axis_index("group"), lax.axis_index("ctx"), lax.axis_index("wshard")
    yi, c = w // 2, w % 2
    oc, oy, ox = 1 - c, 1 - yi, 1 - x
    e = x * nz + g
    sib = (g, x, 2 * yi + oc)
    yn = (g, x, 2 * oy + c)
    diag = (g, x, 2 * oy + oc)
    xn = (g, ox, w)
    zp = (g + 1 - 2 * (g % 2), x, w)
    sw = (g, c, 2 * yi + x)
    stay = x == c
    moves = jnp.logical_not(stay)

    def peer(d):
        q = (e + d) % ne
        return q, (q % nz, q // nz, w)

    def zpeer(d):
        q = (g + d) % nz
        return q, (q, x, w)

    def remote(src, dst_, dev, i, j):
        return pltpu.make_async_remote_copy(src_ref=src, dst_ref=dst_, send_sem=send.at[i], recv_sem=recv.at[j],
                                            device_id=dev, device_id_type=MESH)

    def local(src, dst_, i):
        return pltpu.make_async_copy(src, dst_, send.at[i])

    def sent(ref, i):
        pltpu.make_async_copy(ref, ref, send.at[i]).wait()

    def got(ref, j):
        pltpu.make_async_copy(ref, ref, recv.at[j]).wait()

    def begin(src, dst_):
        cp = local(src, dst_, cs.take())
        cp.start()
        return cp

    bar = pltpu.get_barrier_semaphore()
    peers = [sib, yn, diag] + [peer(d)[1] for d in range(1, ne)]
    for p in peers:
        pl.semaphore_signal(bar, inc=1, device_id=p, device_id_type=MESH)

    @pl.when(moves)
    def _():
        pl.semaphore_signal(bar, inc=1, device_id=sw, device_id_type=MESH)

    l_wq = [begin(wq_h.at[:, pl.ds(k * 512, 512)], m.act.at[pl.ds(k * 128, 128), :]) for k in range(3)]
    l_small = [begin(a, b) for a, b in zip((n1g, n1b, n2g, n2b, bdr, bur, seg_r, off_r),
                                           (m.s1g, m.s1b, m.s2g, m.s2b, m.sbd, m.sbu, m.sseg, m.soff))]
    l_wo = begin(wo_h, m.wo.at[pl.ds(al(w * 128, 128), 128), :])
    l_wu = [begin(wu_h.at[:, pl.ds(k * 512, 512)], m.dup.at[pl.ds(k * 128, 128), :]) for k in range(4)]
    l_wd = begin(wd_h, m.wd.at[:, pl.ds(al(w * 128, 128), 128), :])
    m.vown[...] = jnp.zeros_like(m.vown)
    m.so[0] = jnp.zeros((8, 128), jnp.int32)
    m.gg[...] = jnp.zeros_like(m.gg)
    m.gbu[...] = jnp.zeros_like(m.gbu)
    m.gv[...] = jnp.zeros_like(m.gv)
    pl.semaphore_wait(bar, len(peers) + jnp.where(stay, 0, 1))

    def swap_go(src, dst_, ij, t, n, k=0):
        rows = pl.ds(al(t * n, n), n)

        @pl.when(stay)
        def _():
            local(src.at[rows], dst_.at[rows], ij[0] + k).start()

        @pl.when(moves)
        def _():
            remote(src.at[rows], dst_.at[rows], sw, ij[0] + k, ij[1] + k).start()

    def swap_wait(ref, ij, k=0):
        sent(ref, ij[0] + k)

        @pl.when(moves)
        def _():
            got(ref, ij[1] + k)

    def pair(k=1):
        return cs.take(k), cr.take(k)

    ix, idy, iy, iw = pair(4), pair(), pair(), pair()
    for t in range(4):
        swap_go(words_h, m.xs, ix, t, 256, t)
    for cp in l_small:
        cp.wait()
    for k, r in enumerate((m.s1g, m.s1b, m.s2g, m.s2b, m.sbd)):
        m.vown[k:k + 1, :] = r[...].astype(F32)
    m.vown[5:9, :] = m.sbu[...].astype(F32)
    m.so[0, 0:1, 0:4] = m.sseg[...] * 2 + m.soff[...]
    so_x = remote(m.so.at[0], m.so.at[1], sib, *pair())
    ivc = pair()
    vcs = [remote(m.vown, m.vec.at[w], p, *ivc) for p in (sib, yn, diag)]
    m.vec[w] = m.vown[...]

    mine = pl.ds(al(w * 128, 128), 128)
    for cp in l_wq:
        cp.wait()
    for cc in range(2):
        for hp in range(2):
            for part in range(3):
                b = (part * 4 + cc * 2 + hp) * 128
                blk = m.act[part * 128:(part + 1) * 128, b - part * 512:b - part * 512 + 128].T
                if part == 0:
                    blk = (blk.astype(F32) * 0.125).astype(BF16)
                r = cc * 768 + hp * 384 + part * 64
                m.wt[r:r + 64, mine] = blk[:64]
                m.wt[r + 192:r + 256, mine] = blk[64:]

    other = 2 * oy + c

    def shard(n, s, f):
        v = pl.ds(al(s * 128, 128), 128)
        if n == "wt":
            return m.wt.at[:, v]
        if n == "wo":
            return m.wo.at[v, :]
        return (m.wu if n == "wu" else m.wd).at[f, v, :]

    pieces = [("wt", 0), ("wo", 0)] + [(n, f) for f in range(4) for n in ("wu", "wd")]
    big2 = m.wu.at[0:2, 0:128, :]
    big8 = m.wu.at[:, 0:256, :]
    ig = dict(wt=(pair(3)), wo=(pair(3)))
    isib, iys, ifs = pair(), cs.take(), cs.take()
    iyr, ifr = cr.take(4), cr.take(4)

    def g_sems(p, k):
        n, f = p
        if n in ig:
            return ig[n][0] + k, ig[n][1] + k
        return (isib, (iys, iyr + f), (ifs, ifr + f))[k]

    def g_sib(p):
        return remote(shard(p[0], w, p[1]), shard(p[0], w, p[1]), sib, *g_sems(p, 0))

    def g_y(p):
        return remote(shard(p[0], w, p[1]), shard(p[0], w, p[1]), yn, *g_sems(p, 1))

    def g_fwd(p):
        return remote(shard(p[0], other, p[1]), shard(p[0], other, p[1]), sib, *g_sems(p, 2))

    def g_forward(*ps):
        for p in ps:
            if p[0] in ig:
                g_y(p).wait_recv()
            elif p[0] == "wu":
                got(big2, iyr + p[1])
            g_fwd(p).start()

    g_y(("wt", 0)).start()
    g_sib(("wt", 0)).start()
    for v in vcs:
        v.start()
    so_x.start()
    for cp in l_wu:
        cp.wait()
    for f in range(4):
        for s in range(4):
            m.wu[f, mine, s * 128:(s + 1) * 128] = m.dup[s * 128:(s + 1) * 128, f * 128:(f + 1) * 128]
    l_wo.wait()
    l_wd.wait()
    for p in pieces[1:]:
        g_y(p).start()
    for p in pieces[1:]:
        g_sib(p).start()
    sent(m.vec.at[0:3], ivc[0])
    got(m.vec.at[0:3], ivc[1])
    so_x.wait()
    m.so[0] = jnp.where(stay, m.so[0], m.so[1])
    so_s = local(m.so.at[0], m.sm, cs.take())
    so_s.start()

    def row(k):
        return jnp.concatenate([m.vec[s, k:k + 1, :] for s in range(4)], axis=1)

    g1, b1 = row(0), row(1)

    ia = pair(4)

    def a_slot(core, t):
        return m.a1.at[2 * core + t // 2, pl.ds(al((t % 2) * 256, 256), 256), :]

    def a_piece(t):
        return remote(a_slot(c, t), a_slot(c, t), sib, ia[0] + t, ia[1] + t)

    def norm1(t, _=0):
        rows = pl.ds(al(t * 256, 256), 256)
        swap_wait(m.xs.at[rows], ix, t)
        xv = m.xs[rows, :].astype(F32)
        xc = xv - rowmean(xv)
        r = lax.rsqrt(rowmean(xc * xc) + EPS)
        nv = xc * r
        a_slot(c, t)[...] = (nv * g1 + b1).astype(BF16)
        a_piece(t).start()
        m.n1[rows, :] = nv
        m.r1[rows, :] = jnp.broadcast_to(r, (256, 128))
        return 0

    wrows = pl.ds(al(c * 768, 256), 768)

    near, far = pl.ds(al(yi * 256, 256), 256), pl.ds(al(oy * 256, 256), 256)
    part_of = (m.ya, m.da)

    def words_of(t, feats):
        half = pl.ds(al((t % 2) * 256, 256), 256)
        return jnp.concatenate([m.a1[t // 2, half, feats], m.a1[2 + t // 2, half, feats]], axis=0)

    def project(t, part=None):
        cols = pl.ds(al((t % 2) * 256, 256), 256)
        res = dg(m.wt[wrows, far], words_of(t, far), 1, 1)
        res = res + (dg(m.wt[wrows, near], words_of(t, near), 1, 1) if part is None else part[0:768, :])
        res = res.astype(BF16)
        m.qkv[t // 2, :, cols] = res[:, :256]
        m.qkv[2 + t // 2, :, cols] = res[:, 256:]

    norm1(0)
    g_sib(("wt", 0)).wait()
    for t in range(2):
        norm1(t + 1)
        a_piece(t).wait()
        part_of[t][0:768, :] = dg(m.wt[wrows, near], words_of(t, near), 1, 1)
    g_forward(("wt", 0))
    g_fwd(("wt", 0)).wait()
    project(0, m.ya)
    project(1, m.da)
    norm1(3)
    for t in range(2, 4):
        a_piece(t).wait()
        project(t)
    for t in range(4):
        swap_go(cot_h, m.dys, idy, t, 256)
    so_s.wait()
    canon = [m.sm[0, b] for b in range(4)]
    phys = [jnp.minimum(sum(jnp.where(canon[b] == k, b, 0) for b in range(1, 4)), 3) for k in range(4)]

    def canon_of(p):
        return jnp.clip(m.sm[0, p], 0, 3)

    def rows_of(h, part):
        return pl.ds(al(h * 192 + part * 64, 64), 64)

    def fwd_head(h, _):
        kn = [m.qkv[phys[j], rows_of(h, 1), :].T for j in range(4)]
        q = jnp.concatenate([m.qkv[phys[j], rows_of(h, 0), :] for j in range(4)], axis=1)
        tri = key_le_query(BLK, 0)
        s = []
        for j in range(4):
            sj = dg(kn[j], q[:, j * BLK:], 1, 0)
            sd = jnp.where(tri, sj[:, :BLK], -1e30)
            s.append(sd if j == 3 else jnp.concatenate([sd, sj[:, BLK:]], axis=1))
        mx = [jnp.max(sj, axis=0, keepdims=True) for sj in s]
        top = mx[0]
        for j in range(1, 4):
            top = jnp.concatenate([top[:, :j * BLK], jnp.maximum(top[:, j * BLK:], mx[j])], axis=1)
        acc = None
        for j in range(4):
            p = jnp.exp(s[j] - top[:, j * BLK:]).astype(BF16)
            a = dg(jnp.concatenate([m.qkv[phys[j], rows_of(h, 2), :], jnp.ones((16, BLK), BF16)], axis=0), p, 1, 0)
            acc = a if acc is None else jnp.concatenate([acc[:, :j * BLK], acc[:, j * BLK:] + a], axis=1)
        tot = acc[HD:HD + 1]
        ov = acc[:HD] * (1.0 / tot)
        ls = top + jnp.log(tot)
        for i in range(4):
            m.o[i, pl.ds(al(h * HD, HD), HD), :] = ov[:, i * BLK:(i + 1) * BLK]
            m.lse[i, pl.ds(h, 1), :] = ls[:, i * BLK:(i + 1) * BLK]

        @pl.when(h == 0)
        def _():
            g_forward(*pieces[1:4])

        @pl.when(h == 2)
        def _():
            g_forward(*pieces[4:6])

        @pl.when(h == 3)
        def _():
            g_forward(*pieces[6:8])
        return 0

    lax.fori_loop(0, 4, fwd_head, 0)
    iox = pair()
    for b in range(2):
        m.ost[b] = m.o[canon_of(2 * oc + b)].astype(BF16)
        remote(m.ost.at[b], m.ot.at[b, pl.ds(al(c * 256, 256), 256), :], sib, *iox).start()
    for b in range(2):
        m.ot[b, pl.ds(al(c * 256, 256), 256), :] = m.o[canon_of(2 * c + b)].astype(BF16)
    g_fwd(("wo", 0)).wait()
    g_sib(("wo", 0)).wait()
    sent(m.ost, iox[0])
    got(m.ost, iox[1])

    class Chunk:
        def __init__(self, k):
            tag, self.rows, self.kind = CHUNKS[k]
            self.G = m.FG.at[k] if k < 4 else m.OG
            for q in "ABXZTH":
                setattr(self, q, getattr(m, tag + q))
            self.start = k * FROWS
            self.held = self.rows if self.kind == "yz" else self.rows // 2
            self.p = self.held // nz
            self.lo = 0 if self.kind == "yz" else x * self.held
            self.slots = (w, other) if self.kind == "xyz" else (w,)
            self.i, self.keeping = cs.take(), cs.take()
            self.j = cr.take(6)

        def r(self, off, n):
            return pl.ds(al(off, 16), n)

        def core(self, q):
            return remote(self.G.at[2 * q + oc], self.A.at[q], sib, self.i, self.j)

        def y(self):
            if self.kind == "xyz":
                return remote(self.G.at[other, self.r(self.lo, self.held), :], self.B, yn, self.i, self.j + 1)
            return remote(self.G.at[other], self.B, yn, self.i, self.j + 1)

        def xs(self):
            if self.kind == "yz":
                return [remote(self.T, self.X, xn, self.i, self.j + 2)]
            return [remote(self.G.at[v, self.r(ox * self.held, self.held), :], self.X.at[n], xn, self.i, self.j + 2)
                    for n, v in enumerate(self.slots)]

        def z(self, d):
            q, dev = zpeer(d)
            return remote(self.G.at[w, self.r(self.lo + q * self.p, self.p), :], self.Z.at[nz - 1 - d], dev,
                          self.i, self.j + 3)

        def back(self, d):
            return remote(self.T, self.H.at[self.r(g * self.p, self.p), :], zpeer(d)[1], self.i, self.j + 4)

        def at(self):
            return red_out.at[self.r(self.start + self.lo, self.held), :]

        def xback(self):
            return remote(self.H, self.at(), xn, self.i, self.j + 5)

        def keep(self):
            return local(self.H, self.at(), self.keeping)

        def add(self, slot, rows, v):
            self.G[slot, rows, :] = (self.G[slot, rows, :].astype(F32) + v.astype(F32)).astype(BF16)

        def begin(self):
            for q in range(2):
                self.core(q).start()

        def add_core(self):
            sent(self.A, self.i)
            got(self.A, self.j)
            whole = slice(0, self.rows)
            self.add(other, whole, self.A[oy])
            if self.kind != "xyz":
                self.y().start()
            self.add(w, whole, self.A[yi])
            if self.kind == "xyz":
                self.x_go()

        def x_go(self):
            for cp in self.xs():
                cp.start()

        def x_wait(self):
            sent(self.X, self.i)
            got(self.X, self.j + 2)

        def x_add(self):
            self.x_wait()
            for n, v in reversed(list(enumerate(self.slots))):
                self.add(v, self.r(self.lo, self.held), self.X[n])
                if n == 1:
                    self.y().start()

        def y_add(self):
            self.y().wait()
            if self.kind == "xyz":
                self.add(w, self.r(self.lo, self.held), self.B[...])
            else:
                self.add(w, slice(0, self.rows), self.B[...])

        def z_go(self):
            for d in range(1, nz):
                self.z(d).start()

        def z_sum(self):
            sent(self.Z, self.i)
            got(self.Z, self.j + 3)
            tot = self.G[w, self.r(self.lo + g * self.p, self.p), :].astype(F32)
            for d in range(nz - 1):
                tot = tot + self.Z[d].astype(F32)
            return tot.astype(BF16)

        def z_back(self, tot):
            self.T[...] = tot
            self.H[self.r(g * self.p, self.p), :] = tot
            for d in range(1, nz):
                self.back(d).start()

        def step(self, n):
            if n == 0:
                self.begin()
            elif n == 1:
                self.add_core()
            elif n == 2:
                if self.kind == "xyz":
                    self.x_add()
                else:
                    self.y_add()
                    self.x_go() if self.kind == "yxz" else self.z_go()
            elif n == 3:
                if self.kind == "xyz":
                    self.y_add()
                    self.z_go()
                elif self.kind == "yxz":
                    self.x_add()
                    self.z_go()
                else:
                    self.T[...] = self.z_sum()
                    self.x_go()
            elif n == 4:
                if self.kind == "yz":
                    self.x_wait()
                    self.z_back((self.T[...].astype(F32) + self.X[...].astype(F32)).astype(BF16))
                else:
                    self.z_back(self.z_sum())
            elif n == 5:
                sent(self.Z, self.i)
                got(self.Z, self.j + 4)
                if self.kind != "yz":
                    self.xback().start()
                self.keep().start()
            else:
                if self.kind != "yz":
                    self.xback().wait()
                self.keep().wait()

    qs, qk, qr, qp = cs.take(4), cs.take(4), cr.take(16), QROWS // ne

    def q_core(k, q):
        return remote(m.QS.at[k, 2 * q + oc], m.QG.at[k, q, pl.ds(al(c * 192, 64), 192), :], sib, qs + k, qr + 4 * k)

    def q_y(k):
        return remote(m.QG.at[k, oy], m.QB.at[k], yn, qs + k, qr + 4 * k + 1)

    def q_rs(k, d):
        q, dev = peer(d)
        return remote(m.QG.at[k, yi, pl.ds(al(q * qp, 16), qp), :], m.QC.at[k, ne - 1 - d], dev, qs + k, qr + 4 * k + 2)

    def q_at(k):
        return red_out.at[pl.ds(al(QSTART + k * QROWS + e * qp, 16), qp), :]

    def q_ag(k, d):
        return remote(m.QT.at[k], q_at(k), peer(d)[1], qs + k, qr + 4 * k + 3)

    def q_keep(k):
        return local(m.QT.at[k], q_at(k), qk + k)

    def q0(k):
        for q in range(2):
            q_core(k, q).start()
        for q in range(2):
            m.QG[k, q, pl.ds(al(c * 192, 64), 192), :] = m.QS[k, 2 * q + c]

    def q1(k):
        half = m.QG.at[k, :, 0:192, :]
        sent(half, qs + k)
        got(half, qr + 4 * k)
        q_y(k).start()

    def q2(k):
        q_y(k).wait()
        m.QG[k, yi] = (m.QG[k, yi].astype(F32) + m.QB[k].astype(F32)).astype(BF16)
        for d in range(1, ne):
            q_rs(k, d).start()

    def q3(k):
        sent(m.QC.at[k], qs + k)
        got(m.QC.at[k], qr + 4 * k + 2)
        tot = m.QG[k, yi, pl.ds(al(e * qp, 16), qp), :].astype(F32)
        for d in range(ne - 1):
            tot = tot + m.QC[k, d].astype(F32)
        m.QT[k] = tot.astype(BF16)
        for d in range(1, ne):
            q_ag(k, d).start()
        q_keep(k).start()

    def q4(k):
        sent(m.QC.at[k], qs + k)
        got(m.QC.at[k], qr + 4 * k + 3)
        q_keep(k).wait()

    chunks = [Chunk(k) for k in range(5)]
    chain = (q0, q1, q2, q3, q4)

    def events(key):
        for k, n in PLAN.get(key, ()):
            if k == 9:
                swap_go(m.dup, y_out, iy, n, 128)
            elif k < 5:
                chunks[k].step(n)
            else:
                chain[n](k - 5)

    def when_events(tag, v, values):
        for u in values:
            if (tag, u) in PLAN:
                @pl.when(v == u)
                def _():
                    events((tag, u))

    g2, b2, bd = row(2), row(3), row(4)

    def c1(t, _):
        rows = pl.ds(al(t * 512, 512), 512)
        mid = m.xs[rows, :].astype(F32) + dg(m.ot[t], m.wo[...], 0, 0)
        xc = mid - rowmean(mid)
        r = lax.rsqrt(rowmean(xc * xc) + EPS)
        nv = xc * r
        m.n2[rows, :] = nv
        m.rs[rows, :] = jnp.broadcast_to(r, (512, 128))
        av = (nv * g2 + b2).astype(BF16)
        m.a2[rows, :] = av
        m.a2t[:, rows] = av.T
        dyv = m.dys[rows, :]
        m.dyt[:, rows] = dyv.T
        m.gg[4:5, :] += colsum(dyv.astype(F32))
        m.ya[rows, :] = mid + bd
        m.da[rows, :] = jnp.zeros((512, 512), F32)
        return 0

    swap_wait(m.dys, idy)
    lax.fori_loop(0, 2, c1, 0)

    def c2(f, _):
        for u in range(4):
            @pl.when(f == u)
            def _():
                if u == 0:
                    sent(big8, isib[0])
                    got(big8, isib[1])
                got(big2, ifr + u)
        bu = jnp.concatenate([m.vec[s, pl.ds(5 + f, 1), :] for s in range(4)], axis=1)
        wuf, wdf = m.wu[f], m.wd[f]
        up = dg(m.a2[...], wuf, 1, 0) + bu
        u2 = up * up
        th = jnp.tanh(up * (K0 + (K0 * K1) * u2))
        hp = 0.5 + 0.5 * th
        av = (up * hp).astype(BF16)
        m.act[...] = av
        m.ya[...] += dg(av, wdf, 1, 0)
        dact = dg(m.dys[...], wdf, 1, 1)
        gp = hp + (0.5 * up) * (1.0 - th * th) * (K0 + (3 * K0 * K1) * u2)
        dv = (dact * gp).astype(BF16)
        m.dup[...] = dv
        m.gbu[f, 0:1, :] = colsum(dv.astype(F32))
        m.da[...] += dg(dv, wuf, 1, 1)

        @pl.when(f == 0)
        def _():
            g_forward(*pieces[8:])

        when_events("f", f, range(4))
        gd = dg(m.dyt[...], m.act[...], 1, 0).astype(BF16)
        for s in range(4):
            m.FG[f, s, 0:512, :] = gd[:, s * 128:(s + 1) * 128]
        gu = dg(m.a2t[...], m.dup[...], 1, 0).astype(BF16)
        for s in range(4):
            for b in range(4):
                m.FG[f, s, 512 + b * 128:640 + b * 128, :] = gu[s * 128:(s + 1) * 128, b * 128:(b + 1) * 128]
        when_events("g", f, range(4))
        return 0

    lax.fori_loop(0, 4, c2, 0)
    for p in pieces[:2]:
        g_y(p).wait_send()
    sent(big8, iys)
    sent(big8, ifs)
    yst, dmid = m.dup, m.act
    idx = pair()

    def d_piece(t):
        return remote(m.dst.at[t], m.do.at[2 * c + t], sib, *idx)

    def c3(t, _):
        rows = pl.ds(al(t * 512, 512), 512)
        yst[rows, :] = m.ya[rows, :].astype(BF16)
        dav, nv, r = m.da[rows, :], m.n2[rows, :], m.rs[rows, 0:1]
        m.gg[2:3, :] += colsum(dav * nv)
        m.gg[3:4, :] += colsum(dav)
        gr = dav * g2
        dn = r * (gr - rowmean(gr) - nv * rowmean(gr * nv))
        dm = (m.dys[rows, :].astype(F32) + dn).astype(BF16)
        dmid[rows, :] = dm
        m.dst[t] = dg(m.wo[pl.ds(al(oc * 256, 256), 256), :], dm, 1, 1).astype(BF16)
        d_piece(t).start()
        m.do[2 * c + t] = dg(m.wo[pl.ds(al(c * 256, 256), 256), :], dm, 1, 1).astype(BF16)

        when_events("c", t, range(2))
        return 0

    lax.fori_loop(0, 2, c3, 0)
    go = (dg(m.ot[0], dmid[0:512, :], 1, 0) + dg(m.ot[1], dmid[512:1024, :], 1, 0)).astype(BF16)
    for s in range(4):
        for b in range(4):
            m.OG[s, b * 128:(b + 1) * 128, :] = go[s * 128:(s + 1) * 128, b * 128:(b + 1) * 128]
    events("go")
    sent(m.dst, idx[0])
    got(m.dst, idx[1])

    ixq = pair()

    def x_piece(h, b):
        return remote(m.xst.at[h, b], m.dqt.at[pl.ds(al(c * 768 + h * 192, 64), 192), pl.ds(b * 512, 512)], sib,
                      *ixq)

    def x_start(h):
        hrows = pl.ds(al(h * 192, 64), 192)
        for b in range(2):
            m.xst[h, b] = m.dq[canon_of(2 * oc + b), hrows, :]
            x_piece(h, b).start()
        for b in range(2):
            m.dqt[pl.ds(al(c * 768 + h * 192, 64), 192), b * 512:(b + 1) * 512] = m.dq[canon_of(2 * c + b), hrows, :]

    def q_grad(h):
        hrows = pl.ds(al(h * 192, 64), 192)
        gq = None
        for i in range(4):
            part = dg(m.dq[i, hrows, :], m.a1[phys[i]], 1, 0)
            gq = part if gq is None else gq + part
        gq = gq.astype(BF16)
        for s in range(4):
            m.QS[h, s] = gq[:, s * 128:(s + 1) * 128]

    def bwd_head(h, _):
        hr = pl.ds(al(h * HD, HD), HD)
        kt = jnp.concatenate([m.qkv[phys[j], rows_of(h, 1), :] for j in range(4)], axis=1)
        vt = jnp.concatenate([m.qkv[phys[j], rows_of(h, 2), :] for j in range(4)], axis=1)
        kn = kt.T
        tri = key_le_query(256, 1)
        for i in reversed(range(8)):
            L, b, cs = (i + 1) * 256, i // 2, slice((i % 2) * 256, (i % 2) * 256 + 256)
            q = m.qkv[phys[b], rows_of(h, 0), cs]
            gr = m.do[phys[b], hr, cs]
            ls = m.lse[b, pl.ds(h, 1), cs]
            delta = colsum(gr.astype(F32) * m.o[b, hr, cs])
            lsb = jnp.broadcast_to(ls, (128, 256)).T[:, 0:1]
            deb = jnp.broadcast_to(delta, (128, 256)).T[:, 0:1]
            p = jnp.exp(dg(q.T, kt[:, :L], 1, 0) - lsb)
            pd = jnp.where(tri, p[:, L - 256:], 0.0)
            p = jnp.concatenate([p[:, :L - 256], pd], axis=1) if i else pd
            dp = dg(gr.T, vt[:, :L], 1, 0)
            ds = (p * (dp - deb)).astype(BF16)
            p = p.astype(BF16)
            m.dq[b, rows_of(h, 0), cs] = dg(ds, kn[:L], 1, 0).T.astype(BF16)
            dk, dv = dg(q, ds, 1, 0), dg(gr, p, 1, 0)
            if i == 7:
                m.dkv[0:64, :] = dk
                m.dkv[64:128, :] = dv
            else:
                m.dkv[0:64, :L] += dk
                m.dkv[64:128, :L] += dv
            if i in (6, 4):
                when_events("dD"[i == 4], h, range(4))
        for j in range(4):
            m.dq[j, rows_of(h, 1), :] = m.dkv[0:64, j * BLK:(j + 1) * BLK].astype(BF16)
            m.dq[j, rows_of(h, 2), :] = m.dkv[64:128, j * BLK:(j + 1) * BLK].astype(BF16)
        x_start(h)
        when_events("e", h, range(4))
        q_grad(h)
        when_events("q", h, range(4))
        return 0

    lax.fori_loop(0, 4, bwd_head, 0)

    sent(m.xst, ixq[0])
    got(m.xst, ixq[1])
    events("x")
    wgst = m.dys

    def e1(t, _):
        rows = pl.ds(al(t * 256, 256), 256)
        nv, r = m.n1[rows, :], m.r1[rows, 0:1]
        dav = dg(m.dqt[:, rows], m.wt[...], 0, 0)
        m.gg[0:1, :] += colsum(dav * nv)
        m.gg[1:2, :] += colsum(dav)
        gr = dav * g1
        dn = r * (gr - rowmean(gr) - nv * rowmean(gr * nv))
        wgst[rows, :] = (dmid[rows, :].astype(F32) + dn).astype(BF16)
        swap_go(wgst, wg_out, iw, t, 128)
        when_events("w", t, range(4))
        return 0

    lax.fori_loop(0, 4, e1, 0)
    for s in range(4):
        for k in range(5):
            m.gv[s, k:k + 1, :] = m.gg[k:k + 1, s * 128:(s + 1) * 128]
        for f in range(4):
            m.gv[s, 5 + f:6 + f, :] = m.gbu[f, 0:1, s * 128:(s + 1) * 128]
    ivx, ivy, iva = pair(), pair(), pair()
    vx = [remote(m.gv.at[2 * q + oc], m.gvr.at[q], sib, *ivx) for q in range(2)]
    vy = remote(m.gv.at[other], m.gvy, yn, *ivy)
    va = [remote(m.gv.at[w], m.gva.at[e], peer(d)[1], *iva) for d in range(1, ne)]
    for cp in vx:
        cp.start()
    for t in range(4, 6):
        swap_go(wgst, wg_out, iw, t, 128)
    sent(m.gvr, ivx[0])
    got(m.gvr, ivx[1])
    for q in range(2):
        m.gv[2 * q + c] = m.gv[2 * q + c] + m.gvr[q]
    vy.start()
    events("tail")
    vy.wait()
    m.gv[w] = m.gv[w] + m.gvy[...]
    m.gva[e] = m.gv[w]
    for cp in va:
        cp.start()
    for t in range(6, 8):
        swap_go(wgst, wg_out, iw, t, 128)
    sent(m.gva.at[0:ne - 1], iva[0])
    got(m.gva.at[0:ne - 1], iva[1])
    tot = m.gva[0]
    for d in range(1, ne):
        tot = tot + m.gva[d]
    vec_out[...] = tot
    for k in range(5):
        chunks[k].step(6)

    def fin(t, _):
        q4(t)
        return 0

    lax.fori_loop(0, 4, fin, 0)
    swap_wait(m.dup, iy)
    swap_wait(wgst, iw)


def layer(nz, *ops):
    sc = scratch(nz)
    names = tuple(sc)
    sd = jax.ShapeDtypeStruct
    any_ = pl.BlockSpec(memory_space=pl.ANY)
    vm = pl.BlockSpec(memory_space=pltpu.VMEM)
    return pl.pallas_call(
        functools.partial(body, nz, names),
        out_shape=(sd((1024, 512), BF16), sd((1024, 512), BF16), sd((ROWS, 128), BF16), sd((16, 128), F32)),
        in_specs=[any_] * 14,
        out_specs=(any_, any_, any_, vm),
        scratch_shapes=[sc[n] for n in names] + [pltpu.SemaphoreType.DMA((NSEND,)), pltpu.SemaphoreType.DMA((NRECV,))],
        compiler_params=pltpu.CompilerParams(collective_id=0, has_side_effects=True, vmem_limit_bytes=VLIM),
        name="layer",
    )(*ops)


def finish_body(y_h, wg_h, red_h, v, yo_h, wgo_h, gq_h, go_h, gu_h, gd_h, v1, v2, v3, v4, vu, vd,
                wg, red, wgo, yv, gq, go, gu, gd, sem):
    def cp(a, b, i):
        return pltpu.make_async_copy(a, b, sem.at[i])

    def red_in(k):
        return cp(red_h.at[pl.ds(k * 1024, 1024)], red.at[pl.ds(k * 1024, 1024)], k)

    def wg_in(k):
        return cp(wg_h.at[pl.ds(k * 256, 256)], wg.at[pl.ds(k * 256, 256)], 6 + k)

    outs = []

    def put(a, b):
        o = cp(a, b, 10 + len(outs))
        o.start()
        outs.append(o)

    def y_in(k):
        return cp(y_h.at[pl.ds(k * 512, 512)], yv.at[pl.ds(k * 512, 512)], 22 + k)

    for k in range(4):
        wg_in(k).start()
    for k in range(2):
        y_in(k).start()
    for k in range(6):
        red_in(k).start()
    for r, k in ((v1, 0), (v2, 1), (v3, 2), (v4, 3), (vd, 4)):
        r[...] = v[k:k + 1, :]
    vu[...] = v[5:9, :]
    for k in range(4):
        wg_in(k).wait()
        rows = slice(k * 256, (k + 1) * 256)
        wgo[rows, :] = wg[rows, :].astype(F32)
        put(wgo.at[rows], wgo_h.at[rows])
    for k in range(2):
        y_in(k).wait()
        put(yv.at[pl.ds(k * 512, 512)], yo_h.at[pl.ds(k * 512, 512)])
    for f in range(4):
        red_in(f).wait()
        gd[f * 128:(f + 1) * 128, :] = red[f * 1024:f * 1024 + 512, :].astype(F32).T
        put(gd.at[f * 128:(f + 1) * 128], gd_h.at[f * 128:(f + 1) * 128])
        for s in range(4):
            gu[:, s * 512 + f * 128:s * 512 + (f + 1) * 128] = red[f * 1024 + 512 + s * 128:f * 1024 + 640 + s * 128, :].astype(F32)
    put(gu, gu_h)
    red_in(4).wait()
    for b in range(4):
        go[:, b * 128:(b + 1) * 128] = red[OSTART + b * 128:OSTART + (b + 1) * 128, :].astype(F32)
    put(go, go_h)
    red_in(5).wait()
    for hp in range(2):
        for cc in range(2):
            for part in range(3):
                r = QSTART + hp * 768 + cc * 192 + part * 64
                blk = jnp.concatenate([red[r:r + 64, :], red[r + 384:r + 448, :]], axis=0).astype(F32).T
                if part == 0:
                    blk = blk * 0.125
                k = part * 512 + cc * 256 + hp * 128
                gq[:, k:k + 128] = blk
    put(gq, gq_h)
    for o in outs:
        o.wait()


def finish(y, wg, red, v):
    sd = jax.ShapeDtypeStruct
    any_ = pl.BlockSpec(memory_space=pl.ANY)
    vm = pl.BlockSpec(memory_space=pltpu.VMEM)
    one = sd((1, 128), F32)
    big = (sd((128, 1536), F32), sd((128, 512), F32), sd((128, 2048), F32), sd((512, 512), F32))
    return pl.pallas_call(
        finish_body,
        out_shape=(sd((1024, 512), BF16), sd((1024, 512), F32)) + big + (one, one, one, one, sd((4, 128), F32), one),
        in_specs=[any_] * 3 + [vm],
        out_specs=(any_,) * 6 + (vm,) * 6,
        scratch_shapes=[pltpu.VMEM((1024, 512), BF16), pltpu.VMEM((ROWS, 128), BF16), pltpu.VMEM((1024, 512), F32),
                        pltpu.VMEM((1024, 512), BF16)]
        + [pltpu.VMEM(b.shape, F32) for b in big] + [pltpu.SemaphoreType.DMA((24,))],
        compiler_params=pltpu.CompilerParams(vmem_limit_bytes=VLIM), name="finish",
    )(y, wg, red, v)


def on_chip(words, qkv_weight, out_weight, up_weight, down_weight, norm1_gain, norm1_bias, norm2_gain,
            norm2_bias, up_bias, down_bias, cotangent, seg_map, off_map):
    nz = lax.axis_size("group")
    r = lambda v: v.reshape(-1, 128)
    y, wg, red, v = layer(nz, words[0], cotangent[0], qkv_weight, out_weight, up_weight, down_weight.reshape(4, 128, 512),
                          r(norm1_gain), r(norm1_bias), r(norm2_gain), r(norm2_bias), r(down_bias), r(up_bias),
                          seg_map, off_map)
    y, wg, gq, go, gu, gd, v1, v2, v3, v4, vu, vd = finish(y, wg, red, v)
    f = lambda t: t.reshape(-1)
    return y[None], wg[None], gq, go, gu, gd, f(v1), f(v2), f(v3), f(v4), f(vu), f(vd)


HEADS = 8
HEAD_DIM = 64


eps = 1e-05
neg_big = -1e30


def passed_along(value, axis, by):
    peers = lax.axis_size(axis)
    return lax.ppermute(value, axis, [(i, (i + by) % peers) for i in range(peers)])


def layer_norm(features, norm_gain, norm_shift):
    row_mean = jnp.mean(features, axis=-1, keepdims=True)
    centred = features - row_mean
    inv_scale = lax.rsqrt(jnp.mean(centred * centred, axis=-1, keepdims=True) + eps)
    return centred * inv_scale * norm_gain + norm_shift


def gelu_tanh(features):
    return jax.nn.gelu(features, approximate=True)


def rows_of(array, block_id):
    return lax.dynamic_slice_in_dim(array, block_id * BLK, BLK, 0)


def cols_of(array, block_id):
    return lax.dynamic_slice_in_dim(array, block_id * BLK, BLK, 1)


def add_rows(array, update, block_id):
    return lax.dynamic_update_slice_in_dim(
        array, rows_of(array, block_id) + update, block_id * BLK, 0
    )


def put_rows(array, update, block_id):
    return lax.dynamic_update_slice_in_dim(array, update, block_id * BLK, 0)


def put_cols(array, update, block_id):
    return lax.dynamic_update_slice_in_dim(array, update, block_id * BLK, 1)


def block_info(seg_row, off_row, block_id):
    segment = lax.dynamic_index_in_dim(seg_row, block_id, 0, keepdims=False)
    position = lax.dynamic_index_in_dim(off_row, block_id, 0, keepdims=False)
    return (segment, position)


def pair_live(seg_row, off_row, query_block, key_block):
    query_seg, query_offset = block_info(seg_row, off_row, query_block)
    key_seg, key_offset = block_info(seg_row, off_row, key_block)
    return (query_seg == key_seg) & (key_offset <= query_offset) | (key_seg == 0) & (query_seg != 0)


def pair_mask(seg_row, off_row, query_block, key_block):
    query_seg, query_offset = block_info(seg_row, off_row, query_block)
    key_seg, key_offset = block_info(seg_row, off_row, key_block)
    row_ids = lax.broadcasted_iota(jnp.int32, (BLK, BLK), 0)
    col_ids = lax.broadcasted_iota(jnp.int32, (BLK, BLK), 1)
    query_pos = query_offset * BLK + row_ids
    key_pos = key_offset * BLK + col_ids
    return (query_seg == key_seg) & (key_pos <= query_pos) | (key_seg == 0) & (query_seg != 0)


def split_heads(tile_rows):
    return tile_rows.reshape(tile_rows.shape[0], HEADS, HEAD_DIM)


def tile_scores(query_tile, key_tile, allowed):
    raw_scores = jnp.einsum(
        "qhd,khd->hqk",
        split_heads(query_tile),
        split_heads(key_tile),
        preferred_element_type=jnp.float32,
    )
    return jnp.where(allowed[None], raw_scores * HEAD_DIM ** (-0.5), neg_big)


def tile_back(query_tile, key_tile, value_tile, grad_tile, norm_tile, delta_tile, allowed):
    scores = tile_scores(query_tile, key_tile, allowed)
    exp_terms = jnp.where(allowed[None], jnp.exp(scores - norm_tile[:, :, None]), 0.0)
    d_probs = jnp.einsum(
        "qhd,khd->hqk",
        split_heads(grad_tile),
        split_heads(value_tile),
        preferred_element_type=jnp.float32,
    )
    d_scores = (exp_terms * (d_probs - delta_tile[:, :, None])).astype(jnp.bfloat16)
    return (exp_terms.astype(jnp.bfloat16), d_scores)


def query_grad(d_scores, key_tile):
    part_rows = jnp.einsum(
        "hqk,khd->qhd", d_scores, split_heads(key_tile), preferred_element_type=jnp.float32
    )
    return part_rows.reshape(BLK, -1) * HEAD_DIM ** (-0.5)


def key_grad(d_scores, query_tile):
    part_rows = jnp.einsum(
        "hqk,qhd->khd", d_scores, split_heads(query_tile), preferred_element_type=jnp.float32
    )
    return part_rows.reshape(BLK, -1) * HEAD_DIM ** (-0.5)


def value_grad(probs_low, grad_tile):
    part_rows = jnp.einsum(
        "hqk,qhd->khd", probs_low, split_heads(grad_tile), preferred_element_type=jnp.float32
    )
    return part_rows.reshape(BLK, -1)


def unchanged(running):
    return running


def on_device(
    words,
    qkv_weight,
    out_weight,
    up_weight,
    down_weight,
    norm1_gain,
    norm1_bias,
    norm2_gain,
    norm2_bias,
    up_bias,
    down_bias,
    cotangent,
    seg_map,
    off_map,
):
    gathered = (
        lax.all_gather(qkv_weight, "wshard", axis=0, tiled=True),
        lax.all_gather(out_weight, "wshard", axis=0, tiled=True),
        lax.all_gather(up_weight, "wshard", axis=0, tiled=True),
        lax.all_gather(down_weight, "wshard", axis=0, tiled=True),
        lax.all_gather(norm1_gain, "wshard", axis=0, tiled=True),
        lax.all_gather(norm1_bias, "wshard", axis=0, tiled=True),
        lax.all_gather(norm2_gain, "wshard", axis=0, tiled=True),
        lax.all_gather(norm2_bias, "wshard", axis=0, tiled=True),
        lax.all_gather(up_bias, "wshard", axis=0, tiled=True),
        lax.all_gather(down_bias, "wshard", axis=0, tiled=True),
    )
    w_qkv, w_out, w_up, w_down = (gathered[0], gathered[1], gathered[2], gathered[3])
    gain1 = gathered[4].astype(jnp.float32)
    shift1 = gathered[5].astype(jnp.float32)
    gain2 = gathered[6].astype(jnp.float32)
    shift2 = gathered[7].astype(jnp.float32)
    bias_up = gathered[8].astype(jnp.float32)
    bias_down = gathered[9].astype(jnp.float32)
    seg_row = seg_map[0]
    off_row = off_map[0]
    cycle_place = lax.axis_index("ctx")
    cycle_count = lax.axis_size("ctx")
    inputs = words[0].astype(jnp.float32)
    local_rows = inputs.shape[0]
    local_blocks = local_rows // BLK
    first_block = cycle_place * local_blocks
    width = inputs.shape[1]
    normed1, pull_norm1 = jax.vjp(layer_norm, inputs, gain1, shift1)
    act1 = normed1.astype(jnp.bfloat16)
    qkv = jnp.dot(act1, w_qkv, preferred_element_type=jnp.float32)
    query_rows = qkv[:, :width].astype(jnp.bfloat16)
    key_rows = qkv[:, width : 2 * width].astype(jnp.bfloat16)
    value_rows = qkv[:, 2 * width :].astype(jnp.bfloat16)
    start_state = (
        jnp.full((HEADS, local_rows), neg_big, jnp.float32),
        jnp.zeros((HEADS, local_rows), jnp.float32),
        jnp.zeros((local_rows, width), jnp.float32),
    )
    shard_keys = lax.all_gather(key_rows, "ctx", axis=0, tiled=True)
    shard_values = lax.all_gather(value_rows, "ctx", axis=0, tiled=True)
    key_blocks = shard_keys.shape[0] // BLK

    def online_visit_pair(pair_index, state):
        row_block = pair_index // key_blocks
        col_block = pair_index % key_blocks
        query_block = first_block + row_block
        key_block = col_block

        def online_update_tile(state):
            run_max, run_sum, accum = state
            allowed = pair_mask(seg_row, off_row, query_block, key_block)
            scores = tile_scores(
                rows_of(query_rows, row_block), rows_of(shard_keys, col_block), allowed
            )
            old_max = cols_of(run_max, row_block)
            old_sum = cols_of(run_sum, row_block)
            new_max = jnp.maximum(old_max, jnp.max(scores, axis=-1))
            exp_terms = jnp.where(allowed[None], jnp.exp(scores - new_max[:, :, None]), 0.0)
            factor = jnp.exp(old_max - new_max)
            new_sum = old_sum * factor + jnp.sum(exp_terms, axis=-1)
            part_rows = jnp.einsum(
                "hqk,khd->qhd",
                exp_terms.astype(jnp.bfloat16),
                split_heads(rows_of(shard_values, col_block)),
                preferred_element_type=jnp.float32,
            )
            old_rows = rows_of(accum, row_block).reshape(BLK, HEADS, HEAD_DIM)
            new_rows = (old_rows * factor.T[:, :, None] + part_rows).reshape(BLK, -1)
            return (
                put_cols(run_max, new_max, row_block),
                put_cols(run_sum, new_sum, row_block),
                put_rows(accum, new_rows, row_block),
            )

        return lax.cond(
            pair_live(seg_row, off_row, query_block, key_block),
            online_update_tile,
            unchanged,
            state,
        )

    run_max, run_sum, accum = lax.fori_loop(
        0, local_blocks * key_blocks, online_visit_pair, start_state
    )
    log_norm = run_max + jnp.log(run_sum)
    attended = (accum.reshape(local_rows, HEADS, HEAD_DIM) / run_sum.T[:, :, None]).reshape(
        local_rows, width
    )
    attended_low = attended.astype(jnp.bfloat16)
    middle = inputs + jnp.dot(attended_low, w_out, preferred_element_type=jnp.float32)
    normed2, pull_norm2 = jax.vjp(layer_norm, middle, gain2, shift2)
    act2 = normed2.astype(jnp.bfloat16)
    hidden = jnp.dot(act2, w_up, preferred_element_type=jnp.float32) + bias_up
    gelu_out, pull_gelu = jax.vjp(gelu_tanh, hidden)
    gelu_low = gelu_out.astype(jnp.bfloat16)
    output = (
        middle + jnp.dot(gelu_low, w_down, preferred_element_type=jnp.float32) + bias_down
    ).astype(jnp.bfloat16)
    upstream = cotangent[0]
    upstream_f = upstream.astype(jnp.float32)
    grad_down = jnp.einsum("nf,nd->fd", gelu_low, upstream, preferred_element_type=jnp.float32)
    grad_bias_down = jnp.sum(upstream_f, axis=0)
    d_gelu = jnp.einsum("nd,fd->nf", upstream, w_down, preferred_element_type=jnp.float32)
    d_hidden = pull_gelu(d_gelu)[0].astype(jnp.bfloat16)
    grad_up = jnp.einsum("nd,nf->df", act2, d_hidden, preferred_element_type=jnp.float32)
    grad_bias_up = jnp.sum(d_hidden.astype(jnp.float32), axis=0)
    d_act2 = jnp.einsum("nf,df->nd", d_hidden, w_up, preferred_element_type=jnp.float32)
    d_middle_norm, grad_gain2, grad_shift2 = pull_norm2(d_act2)
    d_middle = (upstream_f + d_middle_norm).astype(jnp.bfloat16)
    grad_out = jnp.einsum("nd,ne->de", attended_low, d_middle, preferred_element_type=jnp.float32)
    d_attended = jnp.einsum(
        "ne,de->nd", d_middle, w_out, preferred_element_type=jnp.float32
    ).astype(jnp.bfloat16)
    row_delta = jnp.sum(
        (d_attended.astype(jnp.float32) * attended).reshape(local_rows, HEADS, HEAD_DIM), axis=-1
    ).T
    zero_rows = jnp.zeros((local_rows, width), jnp.float32)

    def attend_back(cycle_turn, cycle_state):
        held_keys, held_values, held_dk, held_dv, d_query = cycle_state
        source = (cycle_place - cycle_turn) % cycle_count

        def attend_visit_pair(pair_index, partial_value):
            row_block = pair_index // local_blocks
            col_block = pair_index % local_blocks
            query_block = first_block + row_block
            key_block = source * local_blocks + col_block

            def attend_update_tile(partial_value):
                dk_acc, dv_acc, dq_acc = partial_value
                query_tile = rows_of(query_rows, row_block)
                key_tile = rows_of(held_keys, col_block)
                grad_tile = rows_of(d_attended, row_block)
                allowed = pair_mask(seg_row, off_row, query_block, key_block)
                probs_low, d_scores = tile_back(
                    query_tile,
                    key_tile,
                    rows_of(held_values, col_block),
                    grad_tile,
                    cols_of(log_norm, row_block),
                    cols_of(row_delta, row_block),
                    allowed,
                )
                dq_acc = add_rows(dq_acc, query_grad(d_scores, key_tile), row_block)
                dk_acc = add_rows(dk_acc, key_grad(d_scores, query_tile), col_block)
                dv_acc = add_rows(dv_acc, value_grad(probs_low, grad_tile), col_block)
                return (dk_acc, dv_acc, dq_acc)

            return lax.cond(
                pair_live(seg_row, off_row, query_block, key_block),
                attend_update_tile,
                unchanged,
                partial_value,
            )

        held_dk, held_dv, d_query = lax.fori_loop(
            0, local_blocks * local_blocks, attend_visit_pair, (held_dk, held_dv, d_query)
        )
        return (held_keys, held_values, held_dk, held_dv, d_query)

    def pass_grads(held_dk, held_dv):
        return (
            passed_along(held_dk.astype(jnp.bfloat16), "ctx", 1).astype(held_dk.dtype),
            passed_along(held_dv.astype(jnp.bfloat16), "ctx", 1).astype(held_dv.dtype),
        )

    def turn_step(cycle_turn, cycle_state):
        held_keys, held_values, held_dk, held_dv, d_query = attend_back(cycle_turn, cycle_state)
        held_keys, held_values = passed_along((held_keys, held_values), "ctx", 1)
        held_dk, held_dv = pass_grads(held_dk, held_dv)
        return (held_keys, held_values, held_dk, held_dv, d_query)

    cycle_state = lax.fori_loop(
        0, cycle_count - 1, turn_step, (key_rows, value_rows, zero_rows, zero_rows, zero_rows)
    )
    cycle_state = attend_back(cycle_count - 1, cycle_state)
    d_keys, d_values = pass_grads(cycle_state[2], cycle_state[3])
    d_query = cycle_state[4]
    d_qkv = jnp.concatenate(
        [d_query.astype(jnp.bfloat16), d_keys.astype(jnp.bfloat16), d_values.astype(jnp.bfloat16)],
        axis=1,
    )
    grad_qkv = jnp.einsum("nd,nf->df", act1, d_qkv, preferred_element_type=jnp.float32)
    d_act1 = jnp.einsum("nf,df->nd", d_qkv, w_qkv, preferred_element_type=jnp.float32)
    d_inputs_norm, grad_gain1, grad_shift1 = pull_norm1(d_act1)
    words_grad = d_middle.astype(jnp.float32) + d_inputs_norm
    shards = (
        lax.psum_scatter(
            grad_qkv.astype(jnp.bfloat16), "wshard", scatter_dimension=0, tiled=True
        ).astype(jnp.float32),
        lax.psum_scatter(
            grad_out.astype(jnp.bfloat16), "wshard", scatter_dimension=0, tiled=True
        ).astype(jnp.float32),
        lax.psum_scatter(
            grad_up.astype(jnp.bfloat16), "wshard", scatter_dimension=0, tiled=True
        ).astype(jnp.float32),
        lax.psum_scatter(
            grad_down.astype(jnp.bfloat16), "wshard", scatter_dimension=0, tiled=True
        ).astype(jnp.float32),
        lax.psum_scatter(
            grad_gain1.astype(jnp.bfloat16), "wshard", scatter_dimension=0, tiled=True
        ).astype(jnp.float32),
        lax.psum_scatter(
            grad_shift1.astype(jnp.bfloat16), "wshard", scatter_dimension=0, tiled=True
        ).astype(jnp.float32),
        lax.psum_scatter(
            grad_gain2.astype(jnp.bfloat16), "wshard", scatter_dimension=0, tiled=True
        ).astype(jnp.float32),
        lax.psum_scatter(
            grad_shift2.astype(jnp.bfloat16), "wshard", scatter_dimension=0, tiled=True
        ).astype(jnp.float32),
        lax.psum_scatter(
            grad_bias_up.astype(jnp.bfloat16), "wshard", scatter_dimension=0, tiled=True
        ).astype(jnp.float32),
        lax.psum_scatter(
            grad_bias_down.astype(jnp.bfloat16), "wshard", scatter_dimension=0, tiled=True
        ).astype(jnp.float32),
    )
    totals = lax.psum(
        (
            shards[0],
            shards[1],
            shards[2],
            shards[3],
            shards[4],
            shards[5],
            shards[6],
            shards[7],
            shards[8],
            shards[9],
        ),
        ("group", "ctx"),
    )
    return (
        output[None],
        words_grad[None],
        totals[0],
        totals[1],
        totals[2],
        totals[3],
        totals[4],
        totals[5],
        totals[6],
        totals[7],
        totals[8],
        totals[9],
    )


def solution(mesh):
    chip = mesh.shape["ctx"] == 2 and mesh.shape["wshard"] == 4 and mesh.shape["group"] in (2, 4)
    return jax.shard_map(
        on_chip if chip else on_device,
        mesh=mesh,
        in_specs=(
            P(("group", "wshard"), "ctx", None),
            P("wshard", None),
            P("wshard", None),
            P("wshard", None),
            P("wshard", None),
            P("wshard"),
            P("wshard"),
            P("wshard"),
            P("wshard"),
            P("wshard"),
            P("wshard"),
            P(("group", "wshard"), "ctx", None),
            P(("group", "wshard"), None),
            P(("group", "wshard"), None),
        ),
        out_specs=(
            P(("group", "wshard"), "ctx", None),
            P(("group", "wshard"), "ctx", None),
            P("wshard", None),
            P("wshard", None),
            P("wshard", None),
            P("wshard", None),
            P("wshard"),
            P("wshard"),
            P("wshard"),
            P("wshard"),
            P("wshard"),
            P("wshard"),
        ),
        check_vma=False,
    )
```
